32 devices in a mesh: dp: 8 (over z, y), tensor: 4 (over x, core).
Axes of the slice: x: 2, y: 2, z: 4, core: 2. Of those that a mesh axis runs over, the one named last changes fastest.
Arguments:
- noisy_latents: bfloat16 [16, 256, 16], P('dp'), may hold values from -6 to 6
- noise_target: float32 [16, 256, 16], P('dp'), may hold values from -6 to 6
- timesteps: int32 [16], P('dp'), may hold values from 0 to 999
- labels: int32 [16], P('dp'), may hold values from 0 to 999
- owners: int32 [39], replicated, may hold values from 0 to 7, as said below
- step_count: int32 [1], replicated, may hold values from 2 to 20
- master_bank: float32 [64, 1024, 1024], P('dp', None, 'tensor'), may hold values from -0.1875 to 0.1875
- momentum_bank: float32 [64, 1024, 1024], P('dp', None, 'tensor'), may hold values from -0.0024414062 to 0.0024414062
- embed_tables: float32 [1288, 1024], P(None, 'tensor'), may hold values from -0.75 to 0.75
- embed_first: float32 [1288, 1024], P(None, 'tensor'), may hold values from -0.0024414062 to 0.0024414062
- embed_second: float32 [1288, 1024], P(None, 'tensor'), may hold values from 2.4414062e-08 to 9.765625e-08
Outputs:
- loss: float32 [], replicated
- master_new: float32 [64, 1024, 1024], P('dp', None, 'tensor')
- momentum_new: float32 [64, 1024, 1024], P('dp', None, 'tensor')
- embed_new: float32 [1288, 1024], P(None, 'tensor')
- first_new: float32 [1288, 1024], P(None, 'tensor')
- second_new: float32 [1288, 1024], P(None, 'tensor')
The draws below stay inside these ranges and needn't reach their ends.
Inputs may be any that keep to these rules, and one draw needn't show every extreme that they name: `owners`: each index of dp owns at most 8 units, and one owns exactly 8.
All inputs are finite; a program needn't handle non-finite values.
Results may differ from the reference program's by a relative error of at most 0.0089.
Values may be sent and summed in bfloat16 or wider, within the bound.
No kernel may reach another device: no remote copies, remote signals or barrier semaphores. Data moves between devices by JAX's collectives and lax.ppermute only.
A program may use at most 384 MiB of HBM per device.

```python
import math
import jax
import jax.numpy as jnp
from jax import lax

D = 1024
HEADS = 16
HEAD_DIM = 64
FREQ = 256
CLASSES = 1000
PV = 16
GRID = 16
LAYERS = 2
SLOTS = 8
TOKS = 256
LATENTS = 16
TOKENS = 4096
NU = 39
EROWS = 1288
BANK_ROWS = 64
N_DP = 8
N_TENSOR = 4


def draw_owners(key, part):
    key_one, key_two, key_three = jax.random.split(jax.random.fold_in(key, 11), 3)
    busiest = jax.random.randint(key_one, (), 0, N_DP)
    shuffled = jax.random.permutation(key_two, NU)
    places = jax.random.permutation(key_three, (N_DP - 1) * SLOTS)[:NU - SLOTS]
    others = places // SLOTS
    others = others + (others >= busiest).astype(jnp.int32)
    values = jnp.concatenate([jnp.full((SLOTS,), busiest, jnp.int32), others.astype(jnp.int32)])
    return jnp.zeros((NU,), jnp.int32).at[shuffled].set(values)


def set_ends(values, own_key, least, high):
    spot = [jax.random.randint(jax.random.fold_in(own_key, axis), (), 0, length) for axis, length in enumerate(values.shape)]
    longest = values.shape.index(max(values.shape))
    beside = spot[:longest] + [(spot[longest] + 1) % values.shape[longest]] + spot[longest + 1:]
    return values.at[tuple(spot)].set(least).at[tuple(beside)].set(high)


def block_scale(own_key, shape, pieces, least, high):
    factor_of = 1.0
    for dim, blocks in pieces:
        draws = jax.random.uniform(jax.random.fold_in(jax.random.fold_in(own_key, 6), dim), (blocks,), jnp.float32, least / len(pieces), high / len(pieces))
        factor_of = factor_of * jnp.repeat(jnp.exp(draws), shape[dim] // blocks).reshape((-1,) + (1,) * (len(shape) - 1 - dim))
    return factor_of


def gaussian(own_key, dims, scale, reach, cuts=(), kind=jnp.bfloat16):
    entries = jax.random.normal(own_key, dims, jnp.float32) * scale
    if len(cuts) > 0:
        entries = block_scale(own_key, dims, cuts, -0.22, 0.18) * entries
    return jnp.clip(entries, min=-reach, max=reach).astype(kind)


def setup_inputs(seed: int = 0) -> dict:
    splits = jax.random.split(jax.random.key(seed), 12)
    noisy_latents = gaussian(splits[0], (LATENTS, TOKS, PV), 1.0, 6.0, ((0, 8),))
    noise_target = gaussian(splits[1], (LATENTS, TOKS, PV), 1.0, 6.0, ((0, 8),), jnp.float32)
    timesteps = set_ends(jax.random.randint(splits[2], (LATENTS,), 0, 1000), jax.random.fold_in(splits[2], 1), 0, 999).astype(jnp.int32)
    labels = set_ends(jax.random.randint(splits[3], (LATENTS,), 0, CLASSES), jax.random.fold_in(splits[3], 1), 0, CLASSES - 1).astype(jnp.int32)
    owners = draw_owners(jax.random.fold_in(splits[11], 71), 0)
    step_count = jax.random.randint(splits[5], (1,), 2, 21).astype(jnp.int32)
    master_bank = gaussian(splits[6], (BANK_ROWS, D, D), D ** -0.5, 0.1875, ((0, 8), (2, 4)), jnp.float32)
    momentum_bank = gaussian(splits[7], (BANK_ROWS, D, D), (0.01 * TOKENS ** -0.5), 0.0024414062, ((0, 8), (2, 4)), jnp.float32)
    embed_tables = gaussian(splits[8], (EROWS, D), 0.05, 0.75, ((1, 4),), jnp.float32)
    embed_first = gaussian(splits[9], (EROWS, D), (0.01 * TOKENS ** -0.5), 0.0024414062, ((1, 4),), jnp.float32)
    embed_second = jnp.clip(jnp.exp(math.log(9.765624753299562e-08) - 1.3862944 * jax.random.uniform(splits[10], (EROWS, D), jnp.float32) ** block_scale(splits[10], (EROWS, D), ((1, 4),), -0.2, 0.2)), 2.4414061883248905e-08, 9.765624753299562e-08)
    return {"noisy_latents": noisy_latents, "noise_target": noise_target, "timesteps": timesteps, "labels": labels, "owners": owners, "step_count": step_count, "master_bank": master_bank, "momentum_bank": momentum_bank, "embed_tables": embed_tables, "embed_first": embed_first, "embed_second": embed_second}


@jax.custom_vjp
def low(v):
    return lax.optimization_barrier(v.astype(jnp.bfloat16)).astype(jnp.float32)

@jax.custom_vjp
def low_back(v):
    return v

def low_keep(v):
    return (low(v), None)

def low_pass(kept, grad):
    return (grad,)

def back_keep(v):
    return (v, None)

def back_low(kept, grad):
    return (low(grad),)
low.defvjp(low_keep, low_pass)
low_back.defvjp(back_keep, back_low)
HIGHEST_PREC = lax.Precision.HIGHEST
NS_COEF = (3.4445, -4.775, 2.0315)
LR_MUON = 0.5
LR_ADAM = 0.02
WEIGHT_DECAY = 0.1

def layer_norm(values):
    centered = values - lax.optimization_barrier(jnp.mean(values, -1, keepdims=True))
    return centered * lax.rsqrt(lax.optimization_barrier(jnp.mean(centered * centered, -1, keepdims=True)) + 1e-06)

def softmax_rows(scores):
    shifted = jnp.exp(scores - lax.optimization_barrier(jnp.max(scores, -1, keepdims=True)))
    return shifted / lax.optimization_barrier(jnp.sum(shifted, -1, keepdims=True))

def position_table():
    quarter = D // 4
    omega = jnp.exp(-math.log(10000.0) * jnp.arange(quarter, dtype=jnp.float32) / quarter)
    places = jnp.arange(GRID * GRID, dtype=jnp.int32)
    rows_at = (places // GRID).astype(jnp.float32)[:, None] * omega[None]
    cols_at = (places % GRID).astype(jnp.float32)[:, None] * omega[None]
    return jnp.concatenate([jnp.sin(rows_at), jnp.cos(rows_at), jnp.sin(cols_at), jnp.cos(cols_at)], 1)

def time_features(timesteps):
    half_freq = FREQ // 2
    rates = jnp.exp(-math.log(10000.0) * jnp.arange(half_freq, dtype=jnp.float32) / half_freq)
    angles = timesteps.astype(jnp.float32)[:, None] * rates[None]
    return jnp.concatenate([jnp.cos(angles), jnp.sin(angles)], 1)

def newton(block):
    iterate = block / (jnp.sqrt(jnp.sum(block * block)) + 1e-07)
    for sweep in range(5):
        gram_mat = jnp.dot(iterate.T, iterate, precision=HIGHEST_PREC)
        poly_mat = NS_COEF[1] * gram_mat + NS_COEF[2] * jnp.dot(gram_mat, gram_mat, precision=HIGHEST_PREC)
        iterate = NS_COEF[0] * iterate + jnp.dot(iterate, poly_mat, precision=HIGHEST_PREC)
    return iterate

def forward(unit_w, tables, noisy_in, target, timesteps, labels):
    unit_low = low(unit_w)
    tables_low = low(tables)
    patch_w = tables_low[:PV]
    time_w1 = tables_low[PV:PV + FREQ]
    class_w = tables_low[PV + FREQ:PV + FREQ + CLASSES]
    head_w = tables_low[PV + FREQ + CLASSES:]
    n_lat = noisy_in.shape[0]
    top = 18 * LAYERS
    score_scale = 1.0 / math.sqrt(HEAD_DIM)
    stream = low_back(jnp.einsum('ltp,pd->ltd', low(noisy_in), patch_w, precision=HIGHEST_PREC)) + position_table()[None]
    time_one = low_back(jnp.dot(low(time_features(timesteps)), time_w1, precision=HIGHEST_PREC))
    second = low_back(jnp.dot(low(jax.nn.silu(time_one)), unit_low[top], precision=HIGHEST_PREC))
    onehot = (labels[:, None] == jnp.arange(CLASSES, dtype=jnp.int32)[None]).astype(jnp.float32)
    condition = second + jnp.dot(onehot, class_w, precision=HIGHEST_PREC)
    cond_in = low(jax.nn.silu(condition))
    for depth_idx in range(LAYERS):
        base = 18 * depth_idx
        ada_w = jnp.concatenate([unit_low[base + 12 + j] for j in range(6)], 1)
        modulation = low_back(jnp.dot(cond_in, ada_w, precision=HIGHEST_PREC)).reshape(n_lat, 6, 1, D)
        inner_in = low(layer_norm(stream) * (1.0 + modulation[:, 1]) + modulation[:, 0])
        projected = [low(low_back(jnp.einsum('ltd,de->lte', inner_in, unit_low[base + j], precision=HIGHEST_PREC))).reshape(n_lat, TOKS, HEADS, HEAD_DIM) for j in range(3)]
        scores = low_back(jnp.einsum('lqhd,lkhd->lhqk', projected[0], projected[1], precision=HIGHEST_PREC) * score_scale)
        attn_probs = low(softmax_rows(scores))
        mixed_out = low(low_back(jnp.einsum('lhqk,lkhd->lqhd', attn_probs, projected[2], precision=HIGHEST_PREC).reshape(n_lat, TOKS, D)))
        attended = low_back(jnp.einsum('lte,de->ltd', mixed_out, unit_low[base + 3], precision=HIGHEST_PREC))
        stream = stream + modulation[:, 2] * attended
        inner_mid = low(layer_norm(stream) * (1.0 + modulation[:, 4]) + modulation[:, 3])
        up_w = jnp.concatenate([unit_low[base + 4 + j] for j in range(4)], 1)
        hidden = low_back(jnp.einsum('ltd,df->ltf', inner_mid, up_w, precision=HIGHEST_PREC))
        active = low(jax.nn.gelu(hidden, approximate=True))
        down_w = jnp.concatenate([unit_low[base + 8 + j] for j in range(4)], 1)
        branch = low_back(jnp.einsum('ltf,df->ltd', active, down_w, precision=HIGHEST_PREC))
        stream = stream + modulation[:, 5] * branch
    final_w = jnp.concatenate([unit_low[top + 1], unit_low[top + 2]], 1)
    final_mod = low_back(jnp.dot(cond_in, final_w, precision=HIGHEST_PREC)).reshape(n_lat, 2, 1, D)
    inner_out = low(layer_norm(stream) * (1.0 + final_mod[:, 1]) + final_mod[:, 0])
    output = low_back(jnp.einsum('ltd,pd->ltp', inner_out, head_w, precision=HIGHEST_PREC))
    error_out = output - target
    return jnp.sum(error_out * error_out) / (LATENTS * TOKS * PV)

def reference(noisy_latents, noise_target, timesteps, labels, owners, step_count, master_bank, momentum_bank, embed_tables, embed_first, embed_second):
    unit_order = jnp.arange(NU, dtype=jnp.int32)
    same_owner = owners[:, None] == owners[None, :]
    slot_of = lax.optimization_barrier(jnp.sum((same_owner & (unit_order[None, :] < unit_order[:, None])).astype(jnp.int32), 1))
    bank_rows = (owners * SLOTS + slot_of).astype(jnp.int32)
    unit_w = master_bank[bank_rows]
    group_size = 16 if LATENTS % 16 == 0 else LATENTS
    n_groups = LATENTS // group_size
    batches = (noisy_latents.astype(jnp.float32).reshape(n_groups, group_size, TOKS, PV), noise_target.reshape(n_groups, group_size, TOKS, PV), timesteps.reshape(n_groups, group_size), labels.reshape(n_groups, group_size))

    def one_group(carry, batch):
        loss_sum, grad_units, grad_tables = carry
        loss_part, pull = jax.vjp(lambda weights_in, tables_in: forward(weights_in, tables_in, *batch), unit_w, embed_tables)
        more_units, more_tables = pull(jnp.ones_like(loss_part))
        return ((loss_sum + loss_part, grad_units + more_units, grad_tables + more_tables), None)
    start = (jnp.zeros((), jnp.float32), jnp.zeros_like(unit_w), jnp.zeros_like(embed_tables))
    (loss, grad_units, grad_tables), unused = lax.scan(one_group, start, batches)
    momentum = 0.5 * momentum_bank[bank_rows] + grad_units
    block_w = D // N_TENSOR
    blocks = momentum.reshape(NU, D, N_TENSOR, block_w).transpose(0, 2, 1, 3).reshape(NU * N_TENSOR, D, block_w)
    ortho = lax.map(newton, blocks).reshape(NU, N_TENSOR, D, block_w).transpose(0, 2, 1, 3).reshape(NU, D, D)
    master_new = master_bank.at[bank_rows].set(unit_w - LR_MUON * ortho)
    momentum_new = momentum_bank.at[bank_rows].set(momentum)
    first_new = 0.5 * embed_first + 0.5 * grad_tables
    second_new = 0.5 * embed_second + 0.5 * grad_tables * grad_tables
    bias_fix = 1.0 - jnp.power(0.5, step_count[0].astype(jnp.float32))
    embed_new = embed_tables * (1.0 - LR_ADAM * WEIGHT_DECAY) - LR_ADAM * (first_new / bias_fix) / (jnp.sqrt(second_new / bias_fix) + 1e-08)
    return (loss, master_new, momentum_new, embed_new, first_new, second_new)
```

```python
import functools
import math

import jax
import jax.numpy as jnp
import numpy as np
from jax import lax
from jax.experimental import pallas as pl
from jax.experimental.pallas import tpu as pltpu
from jax.sharding import PartitionSpec as P

D = 1024
HEAD_DIM = 64
FREQ = 256
CLASSES = 1000
GRID = 16
LAYERS = 2
BIG = 12
SMALL = 6
N_BIG = BIG * LAYERS
TIME_AT = SMALL * LAYERS
FINAL_AT = TIME_AT + 1
SMALL_ROWS = 16

NS_COEF = (3.4445, -4.775, 2.0315)
LR_MUON = 0.5
LR_ADAM = 0.02
WEIGHT_DECAY = 0.1
SCORE_SCALE = 1.0 / math.sqrt(HEAD_DIM)
HIGHEST_PREC = lax.Precision.HIGHEST

F32 = jnp.float32
BF16 = jnp.bfloat16
VMEM_LIMIT = 56 * 1024 * 1024
GELU_C = math.sqrt(2.0 / math.pi)
GROUPS = ((0, 4), (4, 12), (12, 16), (16, 24))


def unit_tables():
    big, small = [], []
    for u in range(18 * LAYERS):
        layer, place = divmod(u, 18)
        big.append(layer * BIG + place if place < BIG else -1)
        small.append(-1 if place < BIG else layer * SMALL + place - BIG)
    return np.array(big + [-1] * 3), np.array(small + [TIME_AT, FINAL_AT, FINAL_AT + 1])


BIG_OF, SMALL_OF = unit_tables()


def params(**more):
    return pltpu.CompilerParams(vmem_limit_bytes=VMEM_LIMIT, **more)


def dot(a, b):
    return lax.dot_general(a, b, (((1,), (0,)), ((), ())), preferred_element_type=F32)


def dot_nt(a, b):
    return lax.dot_general(a, b, (((1,), (1,)), ((), ())), preferred_element_type=F32)


def dot_tn(a, b):
    return lax.dot_general(a, b, (((0,), (0,)), ((), ())), preferred_element_type=F32)


def shape(dims, kind):
    return jax.ShapeDtypeStruct(dims, kind)


def flip(values, axis, bit, size):
    return lax.ppermute(values, axis, [(i, i ^ bit) for i in range(size)])


def pick(values, axis, place):
    low, high = (lax.index_in_dim(values, i, axis, keepdims=False) for i in (0, 1))
    return jnp.where(place == 0, low, high)


def dp_sum(values, n_data):
    bit = 1
    while bit < n_data:
        values = values + flip(values, "dp", bit, n_data)
        bit *= 2
    return values


def dp_rows(values, n_data):
    bit = 1
    while bit < n_data:
        values = jnp.concatenate([values, flip(values, "dp", bit, n_data)], 0)
        bit *= 2
    return values


def core_flip(values):
    return flip(values, "tensor", 1, 4)


def x_flip(values):
    return flip(values, "tensor", 2, 4)


def gather_tokens(own):
    beside = core_flip(own)
    across = x_flip(own)
    return jnp.concatenate([own, beside, across, core_flip(across)], 0)


def scatter_tokens(keep, send):
    got = core_flip(send)
    near = keep[0] + got[0].astype(F32)
    far = (keep[1] + got[1].astype(F32)).astype(BF16)
    return near + x_flip(far).astype(F32)


def own_columns_sum(values, chip, core):
    split = values.reshape(values.shape[:-1] + (2, 2, values.shape[-1] // 4))
    axis = split.ndim - 2
    mine = pick(split, axis, core) + core_flip(pick(split, axis, 1 - core))
    axis = mine.ndim - 2
    return pick(mine, axis, chip) + x_flip(pick(mine, axis, 1 - chip))


def ring_order(n_data):
    return [0, 2, 4, 6, 7, 5, 3, 1] if n_data == 8 else list(range(n_data))


def sched_kernel(steps, depth, n_data, place_ref, own_ref, next_ref, out_ref):
    lane = lax.broadcasted_iota(jnp.int32, (n_data, 128), 1)
    row = lax.broadcasted_iota(jnp.int32, (n_data, 128), 0)
    far = jnp.int32(999)
    out_lane = lax.broadcasted_iota(jnp.int32, (1, 128), 1)

    def step(t, carry):
        line = jnp.full((1, 128), -1, jnp.int32)
        after = []
        for way in range(2):
            have, sent, *coming = carry[way]
            place = place_ref[way]
            before = jnp.where(place == 0, n_data - 1, place - 1)
            open_now = have * (1 - sent) * (1 - next_ref[way])
            first = jnp.min(jnp.where(open_now > 0, lane, far), axis=1, keepdims=True)
            chosen = (lane == first).astype(jnp.int32)
            first = jnp.broadcast_to(first, (n_data, 128))
            for k, who in enumerate((place, before)):
                index = jnp.min(jnp.where(row == who, first, far), axis=0, keepdims=True)
                index = jnp.where(index == far, -1, index)
                line = jnp.where(out_lane == 2 * way + k, index, line)
            coming = list(coming) + [pltpu.roll(chosen, 1, 0)]
            after.append((have + coming[0], sent + chosen, *coming[1:]))
        out_ref[pl.ds(t, 1), :] = line
        return tuple(after)

    none = jnp.zeros((n_data, 128), jnp.int32)
    lax.fori_loop(0, steps, step, tuple((own_ref[way], none) + (none,) * (depth - 1) for way in range(2)))


def ring_schedule(owners_big, n_data, steps, depth, my_data):
    order = np.array(ring_order(n_data))
    place_of = np.argsort(order)
    place = jnp.sum(jnp.where(jnp.arange(n_data) == my_data, place_of, 0)).astype(jnp.int32)
    at = jnp.arange(n_data)[:, None]
    owner_place = jnp.sum(jnp.where(owners_big[:, None] == jnp.arange(n_data)[None], place_of[None], 0), 1)
    owner_place = jnp.concatenate([owner_place, jnp.full((128 - N_BIG,), -9, owner_place.dtype)])[None]
    back_place = jnp.where(owner_place >= 0, n_data - 1 - owner_place, -9)
    own = jnp.stack([at == owner_place, at == back_place]).astype(jnp.int32)
    follow = (at + 1) % n_data
    nxt = jnp.stack([follow == owner_place, follow == back_place]).astype(jnp.int32)
    out = pl.pallas_call(
        functools.partial(sched_kernel, steps, depth, n_data),
        out_shape=shape((steps, 128), jnp.int32),
        in_specs=[
            pl.BlockSpec(memory_space=pltpu.SMEM),
            pl.BlockSpec(memory_space=pltpu.VMEM),
            pl.BlockSpec(memory_space=pltpu.VMEM),
        ],
        out_specs=pl.BlockSpec(memory_space=pltpu.VMEM),
    )(jnp.stack([place, n_data - 1 - place]), own, nxt)
    return out[:, :4]


def spread_init_kernel(big_ref, bank_ref, *refs):
    outs, (wide, narrow, in_sem, out_sem) = refs[: len(GROUPS)], refs[len(GROUPS) :]
    n_slots = bank_ref.shape[0]

    def load(s):
        return pltpu.make_async_copy(bank_ref.at[s], wide.at[s % 2], in_sem.at[s % 2])

    def stores(s):
        unit = big_ref[s]
        for g, (low, high) in enumerate(GROUPS):
            inside = (unit >= low) & (unit < high)
            at = jnp.clip(unit - low, 0, high - low - 1)
            yield inside, pltpu.make_async_copy(narrow.at[s % 2], outs[g].at[at], out_sem.at[s % 2])

    def wait_stores(s):
        for inside, copy in stores(s):
            pl.when(inside)(copy.wait)

    load(0).start()
    for s in range(n_slots):
        if s + 1 < n_slots:
            load(s + 1).start()
        load(s).wait()
        if s >= 2:
            wait_stores(s - 2)
        narrow[s % 2] = wide[s % 2].astype(BF16)
        for inside, copy in stores(s):
            pl.when(inside)(copy.start)
    for s in range(max(n_slots - 2, 0), n_slots):
        wait_stores(s)


def spread_init(big_slots, master_bank):
    n_slots, rows, columns = master_bank.shape
    return pl.pallas_call(
        spread_init_kernel,
        out_shape=[shape((high - low, rows, columns), BF16) for low, high in GROUPS],
        in_specs=[pl.BlockSpec(memory_space=pltpu.SMEM), pl.BlockSpec(memory_space=pl.ANY)],
        out_specs=[pl.BlockSpec(memory_space=pl.ANY)] * len(GROUPS),
        scratch_shapes=[
            pltpu.VMEM((2, rows, columns), F32),
            pltpu.VMEM((2, rows, columns), BF16),
            pltpu.SemaphoreType.DMA((2,)),
            pltpu.SemaphoreType.DMA((2,)),
        ],
        compiler_params=params(),
    )(big_slots, master_bank)


def moves(index, groups, refs, way, half):
    for ref, (low, high) in zip(refs, groups):
        inside = (index >= low) & (index < high)
        at = jnp.clip(index - low, 0, high - low - 1)
        yield inside, ref.at[at, pl.ds(way * half, half)]


def spread_kernel(groups, half, place_at, fetch_at, tab_ref, *refs):
    n = len(groups)
    refs = list(refs)
    got = [refs.pop(0) for _ in range(2)] if place_at is not None else None
    refs = refs[n:]
    held = [refs.pop(0) for _ in range(n)]
    out = [refs.pop(0) for _ in range(2)] if fetch_at is not None else None
    sem = refs.pop(0)
    if place_at is not None:
        copies = []
        for way in range(2):
            for inside, spot in moves(tab_ref[place_at, 2 * way + 1], groups, held, way, half):
                copies.append((inside, pltpu.make_async_copy(got[way], spot, sem.at[way])))
        for inside, copy in copies:
            pl.when(inside)(copy.start)
        for inside, copy in copies:
            pl.when(inside)(copy.wait)
    if fetch_at is not None:
        copies = []
        for way in range(2):
            for inside, spot in moves(tab_ref[fetch_at, 2 * way], groups, held, way, half):
                copies.append((inside, pltpu.make_async_copy(spot, out[way], sem.at[2 + way])))
        for inside, copy in copies:
            pl.when(inside)(copy.start)
        for inside, copy in copies:
            pl.when(inside)(copy.wait)


def spread_step(tab, groups, held, got, place_at, fetch_at):
    n = len(groups)
    rows, columns = held[0].shape[1:]
    half = rows // 2
    any_spec = pl.BlockSpec(memory_space=pl.ANY)
    lead = [tab] + (list(got) if place_at is not None else [])
    outs = [shape(h.shape, h.dtype) for h in held]
    if fetch_at is not None:
        outs += [shape((half, columns), BF16)] * 2
    res = pl.pallas_call(
        functools.partial(spread_kernel, groups, half, place_at, fetch_at),
        out_shape=outs,
        in_specs=[pl.BlockSpec(memory_space=pltpu.SMEM)] + [any_spec] * (len(lead) - 1 + n),
        out_specs=[any_spec] * len(outs),
        scratch_shapes=[pltpu.SemaphoreType.DMA((4,))],
        input_output_aliases={len(lead) + i: i for i in range(n)},
        compiler_params=params(),
    )(*lead, *held)
    return list(res[:n]), list(res[n:])


def ring_perms(n_data):
    order = ring_order(n_data)
    ahead = [(order[i], order[(i + 1) % n_data]) for i in range(n_data)]
    return ahead, [(b, a) for a, b in ahead]


def spread_weights(tab, held, n_data, steps, depth):
    perms = ring_perms(n_data)
    held = list(held)
    got = {}
    for t in range(steps + depth):
        place_at = t - depth if t >= depth else None
        fetch_at = t if t < steps else None
        live = [
            g
            for g, (low, high) in enumerate(GROUPS)
            if t - depth <= high - 1 + (n_data - 2) * depth
        ]
        new, sends = spread_step(
            tab, [GROUPS[g] for g in live], [held[g] for g in live], got.get(t - depth), place_at, fetch_at
        )
        for g, value in zip(live, new):
            held[g] = value
        if fetch_at is not None:
            got[t] = [lax.ppermute(sends[way], "dp", perms[way]) for way in range(2)]
    return held


def reduce_kernel(groups, half, place_at, fetch_at, tab_ref, *refs):
    n = len(groups)
    refs = list(refs)
    got = [refs.pop(0) for _ in range(2)] if place_at is not None else None
    refs = refs[n:]
    held = [refs.pop(0) for _ in range(n)]
    out = [refs.pop(0) for _ in range(2)] if fetch_at is not None else None
    total, other, sem = refs
    add = [tab_ref[place_at, 2 * way] for way in range(2)] if place_at is not None else None
    take = [tab_ref[fetch_at, 2 * way + 1] for way in range(2)] if fetch_at is not None else None
    first, second, back = [], [], []
    for way in range(2):
        if add is not None:
            for inside, spot in moves(add[way], groups, held, way, half):
                first.append((inside, pltpu.make_async_copy(spot, total.at[way], sem.at[way])))
                back.append((inside, pltpu.make_async_copy(total.at[way], spot, sem.at[4 + way])))
        if take is not None:
            for inside, spot in moves(take[way], groups, held, way, half):
                if add is not None:
                    inside = inside & (take[way] != add[way])
                second.append((inside, pltpu.make_async_copy(spot, other.at[way], sem.at[2 + way])))
    for inside, copy in first + second:
        pl.when(inside)(copy.start)
    if add is not None:
        for inside, copy in first:
            pl.when(inside)(copy.wait)
        for way in range(2):
            total[way] = total[way] + got[way][...].astype(F32)
        for inside, copy in back:
            pl.when(inside)(copy.start)
    if take is not None:
        for inside, copy in second:
            pl.when(inside)(copy.wait)
        for way in range(2):
            if add is None:
                out[way][...] = other[way].astype(BF16)
            else:
                same = take[way] == add[way]

                @pl.when(same)
                def _():
                    out[way][...] = total[way].astype(BF16)

                @pl.when(jnp.logical_not(same))
                def _():
                    out[way][...] = other[way].astype(BF16)

    if add is not None:
        for inside, copy in back:
            pl.when(inside)(copy.wait)


def reduce_step(tab, groups, held, got, place_at, fetch_at):
    n = len(groups)
    rows, columns = held[0].shape[1:]
    half = rows // 2
    any_spec = pl.BlockSpec(memory_space=pl.ANY)
    whole = pl.BlockSpec(memory_space=pltpu.VMEM)
    lead = list(got) if place_at is not None else []
    outs = [shape(h.shape, h.dtype) for h in held]
    sends = [shape((half, columns), BF16)] * 2 if fetch_at is not None else []
    res = pl.pallas_call(
        functools.partial(reduce_kernel, groups, half, place_at, fetch_at),
        out_shape=outs + sends,
        in_specs=[pl.BlockSpec(memory_space=pltpu.SMEM)] + [whole] * len(lead) + [any_spec] * n,
        out_specs=[any_spec] * n + [whole] * len(sends),
        scratch_shapes=[
            pltpu.VMEM((2, half, columns), F32),
            pltpu.VMEM((2, half, columns), F32),
            pltpu.SemaphoreType.DMA((6,)),
        ],
        input_output_aliases={1 + len(lead) + i: i for i in range(n)},
        compiler_params=params(),
    )(tab, *lead, *held)
    return list(res[:n]), list(res[n:])


class Reducer:
    def __init__(self, tab, n_data, steps, depth):
        self.tab, self.n_data, self.steps, self.depth = tab, n_data, steps, depth
        self.perms = [p for p in reversed(ring_perms(n_data))]
        self.held = {}
        self.got = {}
        self.at = 0

    def lowest(self, k):
        return (self.steps - 1 - k) - (self.n_data - 2) * self.depth

    def run(self):
        ready = min(GROUPS[g][0] for g in self.held)
        while self.at < self.steps + self.depth:
            k = self.at
            if k < self.steps and max(self.lowest(k), 0) < ready:
                return
            live = sorted(self.held)
            place_at = self.steps - 1 - (k - self.depth) if k >= self.depth else None
            fetch_at = self.steps - 1 - k if k < self.steps else None
            new, sends = reduce_step(
                self.tab,
                [GROUPS[g] for g in live],
                [self.held[g] for g in live],
                self.got.get(k - self.depth),
                place_at,
                fetch_at,
            )
            for g, value in zip(live, new):
                self.held[g] = value
            if fetch_at is not None:
                self.got[k] = [lax.ppermute(sends[way], "dp", self.perms[way]) for way in range(2)]
            self.at += 1


def split_rows(total, keep_ref, send_ref):
    rows = total.shape[0] // 4
    for i in range(2):
        keep_ref[i] = total[2 * i * rows : (2 * i + 1) * rows]
        send_ref[i] = total[(2 * i + 1) * rows : (2 * i + 2) * rows].astype(BF16)


def part_shapes(rows, width):
    return [shape((2, rows // 4, width), F32), shape((2, rows // 4, width), BF16)]


def softmax_parts(q, k):
    scores = dot_nt(q, k) * SCORE_SCALE
    expo = jnp.exp(scores - jnp.max(scores, -1, keepdims=True))
    return expo / jnp.sum(expo, -1, keepdims=True)


def attention_kernel(n_lat, x_ref, w_ref, qkv_ref, mixed_ref, keep_ref, send_ref):
    x = x_ref[...]
    for j in range(3):
        qkv_ref[j] = dot(x, w_ref[j]).astype(BF16)
    toks = x.shape[0] // n_lat
    heads = w_ref.shape[2] // HEAD_DIM
    for l in range(n_lat):
        rows = slice(l * toks, (l + 1) * toks)
        outs = []
        for h in range(heads):
            cols = slice(h * HEAD_DIM, (h + 1) * HEAD_DIM)
            q, k, v = (qkv_ref[j, rows, cols] for j in range(3))
            outs.append(dot(softmax_parts(q, k).astype(BF16), v))
        mixed_ref[rows, :] = jnp.concatenate(outs, 1).astype(BF16)
    split_rows(dot_nt(mixed_ref[...], w_ref[3]), keep_ref, send_ref)


def attention(x, w, n_lat):
    rows, width = x.shape
    columns = w.shape[2]
    return pl.pallas_call(
        functools.partial(attention_kernel, n_lat),
        out_shape=[shape((3, rows, columns), BF16), shape((rows, columns), BF16)] + part_shapes(rows, width),
        compiler_params=params(),
    )(x, w)


def gelu(x):
    return 0.5 * x * (1.0 + jnp.tanh(GELU_C * (x + 0.044715 * x * x * x)))


def gelu_grad(x):
    t = jnp.tanh(GELU_C * (x + 0.044715 * x * x * x))
    return 0.5 * (1.0 + t) + 0.5 * x * (1.0 - t * t) * (GELU_C * (1.0 + 3 * 0.044715 * x * x))


def mlp_kernel(x_ref, w_ref, hidden_ref, active_ref, keep_ref, send_ref):
    x = x_ref[...]
    total = None
    for j in range(4):
        hidden = dot(x, w_ref[j])
        hidden_ref[j] = hidden
        active = gelu(hidden).astype(BF16)
        active_ref[j] = active
        part = dot_nt(active, w_ref[4 + j])
        total = part if total is None else total + part
    split_rows(total, keep_ref, send_ref)


def mlp(x, w):
    rows, width = x.shape
    columns = w.shape[2]
    return pl.pallas_call(
        mlp_kernel,
        out_shape=[shape((4, rows, columns), F32), shape((4, rows, columns), BF16)] + part_shapes(rows, width),
        compiler_params=params(),
    )(x, w)


def mlp_back_kernel(d_ref, hidden_ref, w_ref, dh_ref, keep_ref, send_ref):
    d = d_ref[...]
    total = None
    for j in range(4):
        dh = (gelu_grad(hidden_ref[j]) * dot(d, w_ref[4 + j])).astype(BF16)
        dh_ref[j] = dh
        part = dot_nt(dh, w_ref[j])
        total = part if total is None else total + part
    split_rows(total, keep_ref, send_ref)


def mlp_back(d, hidden, w):
    rows, width = d.shape
    columns = w.shape[2]
    return pl.pallas_call(
        mlp_back_kernel,
        out_shape=[shape((4, rows, columns), BF16)] + part_shapes(rows, width),
        compiler_params=params(),
    )(d, hidden, w)


def attention_back_kernel(n_lat, d_ref, qkv_ref, w_ref, dqkv_ref, keep_ref, send_ref):
    d_mixed = dot(d_ref[...], w_ref[3]).astype(BF16)
    toks = d_mixed.shape[0] // n_lat
    heads = w_ref.shape[2] // HEAD_DIM
    for l in range(n_lat):
        rows = slice(l * toks, (l + 1) * toks)
        outs = [[], [], []]
        for h in range(heads):
            cols = slice(h * HEAD_DIM, (h + 1) * HEAD_DIM)
            q, k, v = (qkv_ref[j, rows, cols] for j in range(3))
            do = d_mixed[rows, cols]
            probs = softmax_parts(q, k)
            d_probs = dot_nt(do, v)
            d_scores = probs * (d_probs - jnp.sum(probs * d_probs, -1, keepdims=True))
            d_scores = d_scores.astype(BF16)
            outs[0].append(dot(d_scores, k) * SCORE_SCALE)
            outs[1].append(dot_tn(d_scores, q) * SCORE_SCALE)
            outs[2].append(dot_tn(probs.astype(BF16), do))
        for j in range(3):
            dqkv_ref[j, rows, :] = jnp.concatenate(outs[j], 1).astype(BF16)
    total = dot_nt(dqkv_ref[0], w_ref[0]) + dot_nt(dqkv_ref[1], w_ref[1]) + dot_nt(dqkv_ref[2], w_ref[2])
    split_rows(total, keep_ref, send_ref)


def attention_back(d, qkv, w, n_lat):
    rows, width = d.shape
    columns = w.shape[2]
    return pl.pallas_call(
        functools.partial(attention_back_kernel, n_lat),
        out_shape=[shape((3, rows, columns), BF16)] + part_shapes(rows, width),
        compiler_params=params(),
    )(d, qkv, w)


def weight_grad_kernel(counts, n_lat, *refs):
    n = len(counts)
    lefts, rights, (out_ref, mean_ref, sum_ref) = refs[:n], refs[n : 2 * n], refs[2 * n :]
    step = pl.program_id(0)
    base = 0
    for k, count in enumerate(counts):

        @pl.when((step >= base) & (step < base + count))
        def _(left=lefts[k], right=rights[k], k=k):
            a, b = left[...], right[0]
            toks = a.shape[0] // n_lat
            means, sums = [], []
            for l in range(n_lat):
                rows = slice(l * toks, (l + 1) * toks)
                means.append(jnp.sum(a[rows].astype(F32), 0, keepdims=True) * (1.0 / toks))
                sums.append(jnp.sum(b[rows].astype(F32), 0, keepdims=True))
            mean = jnp.concatenate(means + [jnp.zeros((8 - n_lat, a.shape[1]), F32)], 0).astype(BF16)
            total = jnp.concatenate(sums + [jnp.zeros((8 - n_lat, b.shape[1]), F32)], 0).astype(BF16)
            mean_ref[k] = mean.astype(F32)
            sum_ref[0] = total.astype(F32)
            out_ref[0] = dot_tn(a, b) - dot_tn(mean, total)

        base += count


def weight_grads(pairs, n_lat):
    counts = [right.shape[0] for _, right in pairs]
    total = sum(counts)
    rows, width = pairs[0][0].shape
    columns = pairs[0][1].shape[2]
    bases = np.cumsum([0] + counts)

    def right_spec(k):
        base, count = int(bases[k]), counts[k]
        return pl.BlockSpec((1, rows, columns), lambda i: (jnp.clip(i - base, 0, count - 1), 0, 0))

    return pl.pallas_call(
        functools.partial(weight_grad_kernel, counts, n_lat),
        grid=(total,),
        in_specs=[pl.BlockSpec((rows, width), lambda i: (0, 0))] * len(pairs)
        + [right_spec(k) for k in range(len(pairs))],
        out_specs=[
            pl.BlockSpec((1, width, columns), lambda i: (i, 0, 0)),
            pl.BlockSpec((len(pairs), 8, width), lambda i: (0, 0, 0)),
            pl.BlockSpec((1, 8, columns), lambda i: (i, 0, 0)),
        ],
        out_shape=[
            shape((total, width, columns), F32),
            shape((len(pairs), 8, width), F32),
            shape((total, 8, columns), F32),
        ],
        compiler_params=params(dimension_semantics=("arbitrary",)),
    )(*[left for left, _ in pairs], *[right for _, right in pairs])


def modulation_kernel(small_ref, cond_ref, bank_ref, out_ref):
    s = pl.program_id(0)

    @pl.when(s == 0)
    def _():
        out_ref[...] = jnp.zeros_like(out_ref)

    unit = small_ref[s]

    @pl.when((unit >= 0) & (unit != TIME_AT))
    def _():
        out_ref[jnp.maximum(unit, 0)] = dot(cond_ref[...], bank_ref[0].astype(BF16))


def modulations(small_slots, cond_in, bank):
    n_slots, rows, columns = bank.shape
    n_all = cond_in.shape[0]
    return pl.pallas_call(
        modulation_kernel,
        grid_spec=pltpu.PrefetchScalarGridSpec(
            num_scalar_prefetch=1,
            grid=(n_slots,),
            in_specs=[
                pl.BlockSpec((n_all, rows), lambda s, t: (0, 0)),
                pl.BlockSpec((1, rows, columns), lambda s, t: (s, 0, 0)),
            ],
            out_specs=pl.BlockSpec((SMALL_ROWS, n_all, columns), lambda s, t: (0, 0, 0)),
        ),
        out_shape=shape((SMALL_ROWS, n_all, columns), F32),
        compiler_params=params(dimension_semantics=("arbitrary",)),
    )(small_slots, cond_in, bank)


def cond_back_kernel(small_ref, d_ref, bank_ref, out_ref):
    s = pl.program_id(0)

    @pl.when(s == 0)
    def _():
        out_ref[...] = jnp.zeros_like(out_ref)

    unit = small_ref[s]

    @pl.when((unit >= 0) & (unit != TIME_AT))
    def _():
        out_ref[...] += dot_nt(d_ref[jnp.maximum(unit, 0)], bank_ref[0].astype(BF16))


def cond_back(small_slots, d_small, bank):
    n_slots, rows, columns = bank.shape
    n_all = d_small.shape[1]
    return pl.pallas_call(
        cond_back_kernel,
        grid_spec=pltpu.PrefetchScalarGridSpec(
            num_scalar_prefetch=1,
            grid=(n_slots,),
            in_specs=[
                pl.BlockSpec(d_small.shape, lambda s, t: (0, 0, 0)),
                pl.BlockSpec((1, rows, columns), lambda s, t: (s, 0, 0)),
            ],
            out_specs=pl.BlockSpec((n_all, rows), lambda s, t: (0, 0)),
        ),
        out_shape=shape((n_all, rows), F32),
        compiler_params=params(dimension_semantics=("arbitrary",)),
    )(small_slots, d_small, bank)


def halves(x):
    high = x.astype(BF16)
    return high, (x - high.astype(F32)).astype(BF16)


def newton_sweep(x):
    xh, xl = halves(x)
    cross = dot_tn(xh, xl)
    gram = dot_tn(xh, xh) + (cross + cross.T)
    gh, gl = halves(gram)
    cross = dot(gh, gl)
    square = dot(gh, gh) + (cross + cross.T)
    ph, pl_ = halves(NS_COEF[1] * gram + NS_COEF[2] * square)
    return NS_COEF[0] * x + (dot(xh, ph) + (dot(xl, ph) + dot(xh, pl_)))


def newton_kernel(
    big_ref, left_ref, right_ref, a_ref, b_ref, bank_ref, mom_ref, g0, g1, g2, g3, new_ref, mom_new_ref, grad, sem
):
    s = pl.program_id(0)
    unit, left, right = big_ref[s], left_ref[s], right_ref[s]

    @pl.when(right < 0)
    def _():
        new_ref[...] = bank_ref[...]
        mom_new_ref[...] = mom_ref[...]

    @pl.when(right >= 0)
    def _():
        copies = []
        for ref, (low, high) in zip((g0, g1, g2, g3), GROUPS):
            inside = (unit >= low) & (unit < high)
            at = jnp.clip(unit - low, 0, high - low - 1)
            copies.append((inside, pltpu.make_async_copy(ref.at[at], grad, sem.at[0])))
        for inside, copy in copies:
            pl.when(inside)(copy.start)
        some = dot_tn(a_ref[jnp.maximum(left, 0)], b_ref[jnp.maximum(right, 0)])
        for inside, copy in copies:
            pl.when(inside)(copy.wait)

        @pl.when(unit >= 0)
        def _():
            mom_new_ref[0] = 0.5 * mom_ref[0] + (some + grad[...])

        @pl.when(unit < 0)
        def _():
            mom_new_ref[0] = 0.5 * mom_ref[0] + some

        block = mom_new_ref[0]
        norm = jnp.sqrt(jnp.sum(block * block)) + 1e-07
        x = block / norm
        for _ in range(5):
            x = newton_sweep(x)
        new_ref[0] = bank_ref[0] - LR_MUON * x


def optimizer(big_slots, left_slots, right_slots, a_all, b_all, master, momentum, grads):
    n_slots, rows, columns = master.shape
    block = pl.BlockSpec((1, rows, columns), lambda s, *t: (s, 0, 0))
    any_spec = pl.BlockSpec(memory_space=pl.ANY)
    return pl.pallas_call(
        newton_kernel,
        grid_spec=pltpu.PrefetchScalarGridSpec(
            num_scalar_prefetch=3,
            grid=(n_slots,),
            in_specs=[
                pl.BlockSpec(a_all.shape, lambda s, *t: (0, 0, 0)),
                pl.BlockSpec(b_all.shape, lambda s, *t: (0, 0, 0)),
                block,
                block,
            ]
            + [any_spec] * 4,
            out_specs=[block, block],
            scratch_shapes=[pltpu.VMEM((rows, columns), F32), pltpu.SemaphoreType.DMA((1,))],
        ),
        out_shape=[shape(master.shape, F32), shape(momentum.shape, F32)],
        compiler_params=params(dimension_semantics=("arbitrary",)),
    )(big_slots, left_slots, right_slots, a_all, b_all, master, momentum, *grads)


def layer_norm(values):
    centered = values - jnp.mean(values, -1, keepdims=True)
    inv_std = lax.rsqrt(jnp.mean(centered * centered, -1, keepdims=True) + 1e-06)
    return centered * inv_std, inv_std


def norm_back(grad_out, normed, inv_std):
    return inv_std * (
        grad_out
        - jnp.mean(grad_out, -1, keepdims=True)
        - normed * jnp.mean(grad_out * normed, -1, keepdims=True)
    )


def position_rows(first, rows):
    quarter = D // 4
    omega = jnp.exp(-math.log(10000.0) * jnp.arange(quarter, dtype=F32) / quarter)
    places = first + jnp.arange(rows, dtype=jnp.int32)
    rows_at = (places // GRID).astype(F32)[:, None] * omega[None]
    cols_at = (places % GRID).astype(F32)[:, None] * omega[None]
    return jnp.concatenate([jnp.sin(rows_at), jnp.cos(rows_at), jnp.sin(cols_at), jnp.cos(cols_at)], 1)


def time_features(timesteps):
    half_freq = FREQ // 2
    rates = jnp.exp(-math.log(10000.0) * jnp.arange(half_freq, dtype=F32) / half_freq)
    angles = timesteps.astype(F32)[:, None] * rates[None]
    return jnp.concatenate([jnp.cos(angles), jnp.sin(angles)], 1)


def shards(
    noisy_latents,
    noise_target,
    timesteps,
    labels,
    owners,
    step_count,
    master_bank,
    momentum_bank,
    embed_tables,
    embed_first,
    embed_second,
):
    n_lat, n_tok, n_patch = noisy_latents.shape
    n_slots, width, columns = master_bank.shape
    n_units = owners.shape[0]
    n_data = lax.axis_size("dp")
    my_data = lax.axis_index("dp")
    my_tensor = lax.axis_index("tensor")
    chip, core = my_tensor // 2, my_tensor % 2
    n_all = n_lat * n_data
    own_rows = n_lat * n_tok // 4
    count_all = float(n_all * n_tok * n_patch)
    depth = 2 if n_data <= 8 else 1
    steps = N_BIG + (n_data - 2) * depth

    unit_order = jnp.arange(n_units, dtype=jnp.int32)
    same_owner = owners[:, None] == owners[None, :]
    slot_of = jnp.sum((same_owner & (unit_order[None, :] < unit_order[:, None])).astype(jnp.int32), 1)
    mine = (owners[None, :] == my_data) & (
        slot_of[None, :] == jnp.arange(n_slots, dtype=jnp.int32)[:, None]
    )

    def of_slot(table):
        return jnp.sum(jnp.where(mine, jnp.asarray(table + 1, jnp.int32)[None], 0), 1) - 1

    big_slots, small_slots = of_slot(BIG_OF), of_slot(SMALL_OF)
    owners_big = jnp.concatenate([owners[18 * l : 18 * l + BIG] for l in range(LAYERS)])
    tab = ring_schedule(owners_big, n_data, steps, depth, my_data)
    held = spread_init(big_slots, master_bank)
    weights = spread_weights(tab, held, n_data, steps, depth)

    ids = jnp.stack([timesteps, labels], 1)[None]
    ids = jnp.where(jnp.arange(n_data)[:, None, None] == my_data, ids, 0)
    ids = dp_sum(ids, n_data).reshape(n_all, 2)
    narrow = embed_tables.astype(BF16)
    edge_rows = lax.all_gather(
        jnp.concatenate([narrow[:n_patch], narrow[n_patch + FREQ + CLASSES :]], 0), "tensor", axis=1, tiled=True
    )
    patch_w, head_w = edge_rows[:n_patch], edge_rows[n_patch:]
    features = time_features(ids[:, 0]).astype(BF16)
    time_one = jnp.dot(features, narrow[n_patch : n_patch + FREQ], preferred_element_type=F32)
    time_act = lax.all_gather(jax.nn.silu(time_one).astype(BF16), "tensor", axis=1, tiled=True)
    time_mine = owners[18 * LAYERS] == my_data
    time_w2 = lax.dynamic_index_in_dim(master_bank, slot_of[18 * LAYERS], 0, keepdims=False).astype(BF16)
    second = jnp.dot(time_act, time_w2, preferred_element_type=F32)
    second = dp_sum(jnp.where(time_mine, second, 0.0), n_data)
    onehot = ids[:, 1:2] == jnp.arange(CLASSES, dtype=jnp.int32)[None]
    class_w = narrow[n_patch + FREQ : n_patch + FREQ + CLASSES]
    condition = second + jnp.dot(onehot.astype(BF16), class_w, preferred_element_type=F32)
    cond_in = lax.all_gather(jax.nn.silu(condition).astype(BF16), "tensor", axis=1, tiled=True)
    mods = modulations(small_slots, cond_in, master_bank)
    mods = mods.transpose(1, 0, 2).reshape(n_data, n_lat, SMALL_ROWS, columns)
    bit = n_data // 2
    while bit:
        pairs = mods.reshape((2, mods.shape[0] // 2) + mods.shape[1:])
        side = (my_data // bit) % 2
        mods = pick(pairs, 0, side) + flip(pick(pairs, 0, 1 - side), "dp", bit, n_data)
        bit //= 2
    mods = lax.all_gather(mods[0], "tensor", axis=2, tiled=True)
    mods = pick(mods, 0, chip)

    first_row = my_tensor * own_rows
    noisy_own = lax.dynamic_slice_in_dim(noisy_latents.reshape(n_lat * n_tok, n_patch), first_row, own_rows, 0)
    target_own = lax.dynamic_slice_in_dim(noise_target.reshape(n_lat * n_tok, n_patch), first_row, own_rows, 0)
    stream = jnp.dot(noisy_own, patch_w, preferred_element_type=F32) + position_rows(
        first_row % n_tok, own_rows
    )

    def modulate(values, shift, scale):
        normed, inv_std = layer_norm(values)
        return (normed * (1.0 + scale) + shift).astype(BF16), normed, inv_std

    kept = []
    for layer in range(LAYERS):
        shift_a, scale_a, gate_a, shift_m, scale_m, gate_m = (mods[SMALL * layer + i][None] for i in range(SMALL))
        w_attn, w_mlp = weights[2 * layer], weights[2 * layer + 1]
        inner, normed, inv_std = modulate(stream, shift_a, scale_a)
        inner = gather_tokens(inner)
        qkv, mixed, keep, send = attention(inner, w_attn, n_lat)
        attended = scatter_tokens(keep, send)
        stream_mid = stream + gate_a * attended
        inner_mid, normed_mid, inv_mid = modulate(stream_mid, shift_m, scale_m)
        inner_mid = gather_tokens(inner_mid)
        hidden, active, keep, send = mlp(inner_mid, w_mlp)
        branch = scatter_tokens(keep, send)
        stream = stream_mid + gate_m * branch
        kept.append(
            (inner, normed, inv_std, qkv, mixed, attended, inner_mid, normed_mid, inv_mid, hidden, active, branch)
        )
    shift_f, scale_f = mods[FINAL_AT][None], mods[FINAL_AT + 1][None]
    inner_out, normed_out, inv_out = modulate(stream, shift_f, scale_f)
    output = lax.dot_general(inner_out, head_w, (((1,), (1,)), ((), ())), preferred_element_type=F32)
    error_out = output - target_own
    loss_own = jnp.sum(error_out * error_out) / count_all
    d_output = (2.0 * error_out / count_all).astype(BF16)
    grad_head = lax.dot_general(d_output, inner_out, (((0,), (0,)), ((), ())), preferred_element_type=F32)

    d_inner = jnp.dot(d_output, head_w, preferred_element_type=F32)
    d_mods = {FINAL_AT: jnp.sum(d_inner, 0), FINAL_AT + 1: jnp.sum(d_inner * normed_out, 0)}
    grad_flow = norm_back(d_inner * (1.0 + scale_f), normed_out, inv_out)
    ring = Reducer(tab, n_data, steps, depth)
    lefts, rights = {}, {}
    for layer in reversed(range(LAYERS)):
        (inner, normed, inv_std, qkv, mixed, attended, inner_mid, normed_mid, inv_mid, hidden, active, branch) = kept[
            layer
        ]
        shift_a, scale_a, gate_a, shift_m, scale_m, gate_m = (mods[SMALL * layer + i][None] for i in range(SMALL))
        w_attn, w_mlp = weights[2 * layer], weights[2 * layer + 1]
        d_branch = gather_tokens((gate_m * grad_flow).astype(BF16))
        d_gate_m = jnp.sum(grad_flow * branch, 0)
        d_hidden, keep, send = mlp_back(d_branch, hidden, w_mlp)
        d_inner_mid = scatter_tokens(keep, send)
        grads, left, right = weight_grads([(inner_mid, d_hidden), (d_branch, active)], n_lat)
        ring.held[2 * layer + 1] = grads
        lefts[2 * layer + 1], rights[2 * layer + 1] = left, right
        ring.run()
        d_shift_m = jnp.sum(d_inner_mid, 0)
        d_scale_m = jnp.sum(d_inner_mid * normed_mid, 0)
        grad_mid = grad_flow + norm_back(d_inner_mid * (1.0 + scale_m), normed_mid, inv_mid)
        d_attended = gather_tokens((gate_a * grad_mid).astype(BF16))
        d_gate_a = jnp.sum(grad_mid * attended, 0)
        d_qkv, keep, send = attention_back(d_attended, qkv, w_attn, n_lat)
        d_inner = scatter_tokens(keep, send)
        grads, left, right = weight_grads([(inner, d_qkv), (d_attended, mixed[None])], n_lat)
        ring.held[2 * layer] = grads
        lefts[2 * layer], rights[2 * layer] = left, right
        ring.run()
        d_shift_a = jnp.sum(d_inner, 0)
        d_scale_a = jnp.sum(d_inner * normed, 0)
        grad_flow = grad_mid + norm_back(d_inner * (1.0 + scale_a), normed, inv_std)
        for i, value in enumerate((d_shift_a, d_scale_a, d_gate_a, d_shift_m, d_scale_m, d_gate_m)):
            d_mods[SMALL * layer + i] = value

    d_mods[TIME_AT] = jnp.zeros((width,), F32)
    d_mods[SMALL_ROWS - 1] = jnp.zeros((width,), F32)
    d_small = jnp.stack([d_mods[i] for i in range(SMALL_ROWS)]).reshape(SMALL_ROWS, 2, 2, columns)
    d_small = pick(d_small, 2, core) + core_flip(pick(d_small, 2, 1 - core))
    near, far = pick(d_small, 1, chip), x_flip(pick(d_small, 1, 1 - chip))
    d_small = jnp.where(
        jnp.arange(2)[:, None, None] == chip, near[None], far[None]
    ).astype(BF16)
    d_small = jnp.where(jnp.arange(n_data)[:, None, None, None] == my_data, d_small[None], jnp.zeros((), BF16))
    d_small = dp_sum(d_small, n_data).reshape(n_all, SMALL_ROWS, columns).transpose(1, 0, 2)
    d_cond = cond_back(small_slots, d_small, master_bank)
    d_cond = dp_sum(own_columns_sum(d_cond, chip, core), n_data)
    unused, silu_pull = jax.vjp(jax.nn.silu, condition)
    d_condition = silu_pull(d_cond)[0]
    d_second = d_condition.astype(BF16)
    grad_class = lax.dot_general(
        onehot.astype(F32), d_condition, (((0,), (0,)), ((), ())), precision=HIGHEST_PREC
    )
    d_time_act = lax.dot_general(d_second, time_w2, (((1,), (1,)), ((), ())), preferred_element_type=F32)
    d_time_act = jnp.where(time_mine, d_time_act, 0.0)
    d_time_act = dp_sum(own_columns_sum(d_time_act, chip, core), n_data)
    unused, time_pull = jax.vjp(jax.nn.silu, time_one)
    d_time_one = time_pull(d_time_act)[0].astype(BF16)
    grad_time_one = lax.dot_general(features, d_time_one, (((0,), (0,)), ((), ())), preferred_element_type=F32)
    d_stream = grad_flow.astype(BF16)
    grad_patch = lax.dot_general(noisy_own, d_stream, (((0,), (0,)), ((), ())), preferred_element_type=F32)
    edges = jnp.concatenate([grad_patch, grad_head, jnp.full((1, width), loss_own)], 0)
    edges = dp_sum(own_columns_sum(edges, chip, core), n_data)
    loss = edges[2 * n_patch, 0]
    grad_embed = jnp.concatenate(
        [edges[:n_patch], grad_time_one, grad_class, edges[n_patch : 2 * n_patch]], 0
    )

    a_rows, b_rows = [], []
    for g in range(len(GROUPS)):
        a_rows.append(lefts[g][:, :n_lat].transpose(1, 0, 2))
        b_rows.append(rights[g][:, :n_lat].transpose(1, 0, 2))
    a_rows = jnp.concatenate(a_rows, 1).astype(BF16)
    b_rows = jnp.concatenate(b_rows, 1).astype(BF16)
    n_left = a_rows.shape[1]
    packed = jnp.concatenate([a_rows.reshape(n_lat, n_left * 4, columns), b_rows], 1)
    packed = dp_rows(packed, n_data)
    a_rows = packed[:, : n_left * 4].reshape(n_all, n_left, width).transpose(1, 0, 2)
    b_rows = packed[:, n_left * 4 :].transpose(1, 0, 2)
    a_all = jnp.concatenate([cond_in[None], time_act[None], a_rows], 0)
    small_rows = jnp.where(
        jnp.arange(SMALL_ROWS)[:, None, None] == TIME_AT, d_second[None], d_small
    )
    b_all = jnp.concatenate([small_rows, b_rows], 0)
    kind = []
    for g, (low, high) in enumerate(GROUPS):
        split = low + 3 if g % 2 == 0 else low + 4
        kind += [2 + 2 * g + (b >= split) for b in range(low, high)]
    kind_of = np.where(BIG_OF >= 0, np.array(kind)[BIG_OF], np.where(SMALL_OF == TIME_AT, 1, 0))
    right_of = np.where(BIG_OF >= 0, SMALL_ROWS + BIG_OF, SMALL_OF)
    master_new, momentum_new = optimizer(
        big_slots,
        of_slot(kind_of),
        of_slot(right_of),
        a_all,
        b_all,
        master_bank,
        momentum_bank,
        [ring.held[g] for g in range(len(GROUPS))],
    )

    first_new = 0.5 * embed_first + 0.5 * grad_embed
    second_new = 0.5 * embed_second + 0.5 * grad_embed * grad_embed
    bias_fix = 1.0 - jnp.power(0.5, step_count[0].astype(F32))
    embed_new = embed_tables * (1.0 - LR_ADAM * WEIGHT_DECAY) - LR_ADAM * (first_new / bias_fix) / (
        jnp.sqrt(second_new / bias_fix) + 1e-08
    )
    return (loss, master_new, momentum_new, embed_new, first_new, second_new)


def solution(mesh):
    placed = (
        P("dp", None, None),
        P("dp", None, None),
        P("dp"),
        P("dp"),
        P(),
        P(),
        P("dp", None, "tensor"),
        P("dp", None, "tensor"),
        P(None, "tensor"),
        P(None, "tensor"),
        P(None, "tensor"),
    )
    return jax.shard_map(
        shards,
        mesh=mesh,
        in_specs=placed,
        out_specs=(
            P(),
            P("dp", None, "tensor"),
            P("dp", None, "tensor"),
            P(None, "tensor"),
            P(None, "tensor"),
            P(None, "tensor"),
        ),
        check_vma=False,
    )
```

```python
import functools
import math

import jax
import jax.numpy as jnp
import numpy as np
from jax import lax
from jax.experimental import pallas as pl
from jax.experimental.pallas import tpu as pltpu
from jax.sharding import PartitionSpec as P

D = 1024
HEAD_DIM = 64
FREQ = 256
CLASSES = 1000
GRID = 16
LAYERS = 2
BIG = 12
SMALL = 6
N_BIG = BIG * LAYERS
TIME_AT = SMALL * LAYERS
FINAL_AT = TIME_AT + 1
SMALL_ROWS = 16

NS_COEF = (3.4445, -4.775, 2.0315)
LR_MUON = 0.5
LR_ADAM = 0.02
WEIGHT_DECAY = 0.1
SCORE_SCALE = 1.0 / math.sqrt(HEAD_DIM)
HIGHEST_PREC = lax.Precision.HIGHEST

F32 = jnp.float32
BF16 = jnp.bfloat16
RING_VMEM = 8
RING_COST = pl.CostEstimate(flops=0, transcendentals=0, bytes_accessed=2**21)
GELU_C = math.sqrt(2.0 / math.pi)
GROUPS = ((0, 4), (4, 12), (12, 16), (16, 24))


def unit_tables():
    big, small = [], []
    for u in range(18 * LAYERS):
        layer, place = divmod(u, 18)
        big.append(layer * BIG + place if place < BIG else -1)
        small.append(-1 if place < BIG else layer * SMALL + place - BIG)
    return np.array(big + [-1] * 3), np.array(small + [TIME_AT, FINAL_AT, FINAL_AT + 1])


BIG_OF, SMALL_OF = unit_tables()


def params(limit, **more):
    return pltpu.CompilerParams(vmem_limit_bytes=limit * 1024 * 1024, **more)


def dot(a, b):
    return lax.dot_general(a, b, (((1,), (0,)), ((), ())), preferred_element_type=F32)


def dot_nt(a, b):
    return lax.dot_general(a, b, (((1,), (1,)), ((), ())), preferred_element_type=F32)


def dot_tn(a, b):
    return lax.dot_general(a, b, (((0,), (0,)), ((), ())), preferred_element_type=F32)


def shape(dims, kind):
    return jax.ShapeDtypeStruct(dims, kind)


def flip(values, axis, bit, size):
    return lax.ppermute(values, axis, [(i, i ^ bit) for i in range(size)])


def pick(values, axis, place):
    low, high = (lax.index_in_dim(values, i, axis, keepdims=False) for i in (0, 1))
    return jnp.where(place == 0, low, high)


def dp_sum(values, n_data):
    bit = 1
    while bit < n_data:
        values = values + flip(values, "dp", bit, n_data)
        bit *= 2
    return values


def dp_rows(values, n_data):
    bit = 1
    while bit < n_data:
        values = jnp.concatenate([values, flip(values, "dp", bit, n_data)], 0)
        bit *= 2
    return values


def core_flip(values):
    return flip(values, "tensor", 1, 4)


def x_flip(values):
    return flip(values, "tensor", 2, 4)


def gather_tokens(own):
    beside = core_flip(own)
    across = x_flip(own)
    return jnp.concatenate([own, beside, across, core_flip(across)], 0)


def scatter_tokens(keep, send):
    got = core_flip(send)
    near = keep[0] + got[0].astype(F32)
    far = (keep[1] + got[1].astype(F32)).astype(BF16)
    return near + x_flip(far).astype(F32)


def own_columns_sum(values, chip, core):
    split = values.reshape(values.shape[:-1] + (2, 2, values.shape[-1] // 4))
    axis = split.ndim - 2
    mine = pick(split, axis, core) + core_flip(pick(split, axis, 1 - core))
    axis = mine.ndim - 2
    return pick(mine, axis, chip) + x_flip(pick(mine, axis, 1 - chip))


def ring_order(n_data):
    return [0, 2, 4, 6, 7, 5, 3, 1] if n_data == 8 else list(range(n_data))


def sched_kernel(steps, depth, n_data, place_ref, own_ref, next_ref, out_ref):
    lane = lax.broadcasted_iota(jnp.int32, (n_data, 128), 1)
    row = lax.broadcasted_iota(jnp.int32, (n_data, 128), 0)
    far = jnp.int32(999)
    out_lane = lax.broadcasted_iota(jnp.int32, (1, 128), 1)

    def step(t, carry):
        line = jnp.full((1, 128), -1, jnp.int32)
        after = []
        for way in range(2):
            have, sent, *coming = carry[way]
            place = place_ref[way]
            before = jnp.where(place == 0, n_data - 1, place - 1)
            open_now = have * (1 - sent) * (1 - next_ref[way])
            first = jnp.min(jnp.where(open_now > 0, lane, far), axis=1, keepdims=True)
            chosen = (lane == first).astype(jnp.int32)
            first = jnp.broadcast_to(first, (n_data, 128))
            for k, who in enumerate((place, before)):
                index = jnp.min(jnp.where(row == who, first, far), axis=0, keepdims=True)
                index = jnp.where(index == far, -1, index)
                line = jnp.where(out_lane == 2 * way + k, index, line)
            coming = list(coming) + [pltpu.roll(chosen, 1, 0)]
            after.append((have + coming[0], sent + chosen, *coming[1:]))
        out_ref[pl.ds(t, 1), :] = line
        return tuple(after)

    none = jnp.zeros((n_data, 128), jnp.int32)
    lax.fori_loop(0, steps, step, tuple((own_ref[way], none) + (none,) * (depth - 1) for way in range(2)))


def ring_schedule(owners_big, n_data, steps, depth, my_data):
    order = np.array(ring_order(n_data))
    place_of = np.argsort(order)
    place = jnp.sum(jnp.where(jnp.arange(n_data) == my_data, place_of, 0)).astype(jnp.int32)
    at = jnp.arange(n_data)[:, None]
    owner_place = jnp.sum(jnp.where(owners_big[:, None] == jnp.arange(n_data)[None], place_of[None], 0), 1)
    owner_place = jnp.concatenate([owner_place, jnp.full((128 - N_BIG,), -9, owner_place.dtype)])[None]
    back_place = jnp.where(owner_place >= 0, n_data - 1 - owner_place, -9)
    own = jnp.stack([at == owner_place, at == back_place]).astype(jnp.int32)
    follow = (at + 1) % n_data
    nxt = jnp.stack([follow == owner_place, follow == back_place]).astype(jnp.int32)
    out = pl.pallas_call(
        functools.partial(sched_kernel, steps, depth, n_data),
        out_shape=shape((steps, 128), jnp.int32),
        in_specs=[
            pl.BlockSpec(memory_space=pltpu.SMEM),
            pl.BlockSpec(memory_space=pltpu.VMEM),
            pl.BlockSpec(memory_space=pltpu.VMEM),
        ],
        out_specs=pl.BlockSpec(memory_space=pltpu.VMEM),
        name="ring_schedule",
    )(jnp.stack([place, n_data - 1 - place]), own, nxt)
    return out[:, :4]


def spread_init_kernel(big_ref, bank_ref, *refs):
    outs, (wide, narrow, in_sem, out_sem) = refs[: len(GROUPS)], refs[len(GROUPS) :]
    n_slots = bank_ref.shape[0]

    def load(s):
        return pltpu.make_async_copy(bank_ref.at[s], wide.at[s % 2], in_sem.at[s % 2])

    def stores(s):
        unit = big_ref[s]
        for g, (low, high) in enumerate(GROUPS):
            inside = (unit >= low) & (unit < high)
            at = jnp.clip(unit - low, 0, high - low - 1)
            yield inside, pltpu.make_async_copy(narrow.at[s % 2], outs[g].at[at], out_sem.at[s % 2])

    def wait_stores(s):
        for inside, copy in stores(s):
            pl.when(inside)(copy.wait)

    load(0).start()
    for s in range(n_slots):
        if s + 1 < n_slots:
            load(s + 1).start()
        load(s).wait()
        if s >= 2:
            wait_stores(s - 2)
        narrow[s % 2] = wide[s % 2].astype(BF16)
        for inside, copy in stores(s):
            pl.when(inside)(copy.start)
    for s in range(max(n_slots - 2, 0), n_slots):
        wait_stores(s)


def spread_init(big_slots, master_bank):
    n_slots, rows, columns = master_bank.shape
    return pl.pallas_call(
        spread_init_kernel,
        out_shape=[pltpu.HBM((high - low, rows, columns), BF16) for low, high in GROUPS],
        in_specs=[pl.BlockSpec(memory_space=pltpu.SMEM), pl.BlockSpec(memory_space=pl.ANY)],
        out_specs=[pl.BlockSpec(memory_space=pltpu.HBM)] * len(GROUPS),
        scratch_shapes=[
            pltpu.VMEM((2, rows, columns), F32),
            pltpu.VMEM((2, rows, columns), BF16),
            pltpu.SemaphoreType.DMA((2,)),
            pltpu.SemaphoreType.DMA((2,)),
        ],
        compiler_params=params(16),
        name="own_weights",
    )(big_slots, master_bank)


def moves(index, groups, refs, way, half):
    for ref, (low, high) in zip(refs, groups):
        inside = (index >= low) & (index < high)
        at = jnp.clip(index - low, 0, high - low - 1)
        yield inside, ref.at[at, pl.ds(way * half, half)]


def spread_kernel(groups, half, place_at, fetch_at, tab_ref, *refs):
    n = len(groups)
    refs = list(refs)
    got = [refs.pop(0) for _ in range(2)] if place_at is not None else None
    refs = refs[n:]
    held = [refs.pop(0) for _ in range(n)]
    out = [refs.pop(0) for _ in range(2)] if fetch_at is not None else None
    sem = refs.pop(0)
    add = [tab_ref[place_at, 2 * way + 1] for way in range(2)] if place_at is not None else None
    take = [tab_ref[fetch_at, 2 * way] for way in range(2)] if fetch_at is not None else None
    copies = []
    for way in range(2):
        if take is not None:
            for inside, spot in moves(take[way], groups, held, way, half):
                if add is not None:
                    inside = inside & (take[way] != add[way])
                copies.append((inside, pltpu.make_async_copy(spot, out[way], sem.at[2 + way])))
        if add is not None:
            for inside, spot in moves(add[way], groups, held, way, half):
                copies.append((inside, pltpu.make_async_copy(got[way], spot, sem.at[way])))
    for inside, copy in copies:
        pl.when(inside)(copy.start)
    if add is not None and take is not None:
        for way in range(2):

            @pl.when(take[way] == add[way])
            def _():
                out[way][...] = got[way][...]

    for inside, copy in copies:
        pl.when(inside)(copy.wait)


def spread_step(tab, groups, held, got, place_at, fetch_at):
    n = len(groups)
    rows, columns = held[0].shape[1:]
    half = rows // 2
    any_spec = pl.BlockSpec(memory_space=pltpu.HBM)
    whole = pl.BlockSpec(memory_space=pltpu.VMEM)
    lead = list(got) if place_at is not None else []
    outs = [pltpu.HBM(h.shape, h.dtype) for h in held]
    sends = [pltpu.VMEM((half, columns), BF16)] * 2 if fetch_at is not None else []
    res = pl.pallas_call(
        functools.partial(spread_kernel, groups, half, place_at, fetch_at),
        out_shape=outs + sends,
        in_specs=[pl.BlockSpec(memory_space=pltpu.SMEM)] + [whole] * len(lead) + [any_spec] * n,
        out_specs=[any_spec] * n + [whole] * len(sends),
        scratch_shapes=[pltpu.SemaphoreType.DMA((4,))],
        input_output_aliases={1 + len(lead) + i: i for i in range(n)},
        compiler_params=params(RING_VMEM),
        cost_estimate=RING_COST,
        name="spread_step",
    )(tab, *lead, *held)
    return list(res[:n]), list(res[n:])


def ring_perms(n_data):
    order = ring_order(n_data)
    ahead = [(order[i], order[(i + 1) % n_data]) for i in range(n_data)]
    return ahead, [(b, a) for a, b in ahead]


def spread_weights(tab, held, n_data, steps, depth):
    perms = ring_perms(n_data)
    held = list(held)
    got = {}
    for t in range(steps + depth):
        place_at = t - depth if t >= depth else None
        fetch_at = t if t < steps else None
        live = [
            g
            for g, (low, high) in enumerate(GROUPS)
            if t - depth <= high - 1 + (n_data - 2) * depth
        ]
        new, sends = spread_step(
            tab, [GROUPS[g] for g in live], [held[g] for g in live], got.get(t - depth), place_at, fetch_at
        )
        for g, value in zip(live, new):
            held[g] = value
        if fetch_at is not None:
            got[t] = [lax.ppermute(sends[way], "dp", perms[way]) for way in range(2)]
    return held


def reduce_kernel(groups, half, place_at, fetch_at, tab_ref, *refs):
    n = len(groups)
    refs = list(refs)
    got = [refs.pop(0) for _ in range(2)] if place_at is not None else None
    refs = refs[n:]
    held = [refs.pop(0) for _ in range(n)]
    out = [refs.pop(0) for _ in range(2)] if fetch_at is not None else None
    total, other, sem = refs
    add = [tab_ref[place_at, 2 * way] for way in range(2)] if place_at is not None else None
    take = [tab_ref[fetch_at, 2 * way + 1] for way in range(2)] if fetch_at is not None else None
    first, second, back = [], [], []
    for way in range(2):
        if add is not None:
            for inside, spot in moves(add[way], groups, held, way, half):
                first.append((inside, pltpu.make_async_copy(spot, total.at[way], sem.at[way])))
                back.append((inside, pltpu.make_async_copy(total.at[way], spot, sem.at[4 + way])))
        if take is not None:
            for inside, spot in moves(take[way], groups, held, way, half):
                if add is not None:
                    inside = inside & (take[way] != add[way])
                second.append((inside, pltpu.make_async_copy(spot, other.at[way], sem.at[2 + way])))
    for inside, copy in first + second:
        pl.when(inside)(copy.start)
    if add is not None:
        for inside, copy in first:
            pl.when(inside)(copy.wait)
        for way in range(2):
            total[way] = total[way] + got[way][...].astype(F32)
        for inside, copy in back:
            pl.when(inside)(copy.start)
    if take is not None:
        for inside, copy in second:
            pl.when(inside)(copy.wait)
        for way in range(2):
            if add is None:
                out[way][...] = other[way].astype(BF16)
            else:
                same = take[way] == add[way]

                @pl.when(same)
                def _():
                    out[way][...] = total[way].astype(BF16)

                @pl.when(jnp.logical_not(same))
                def _():
                    out[way][...] = other[way].astype(BF16)

    if add is not None:
        for inside, copy in back:
            pl.when(inside)(copy.wait)


def reduce_step(tab, groups, held, got, place_at, fetch_at):
    n = len(groups)
    rows, columns = held[0].shape[1:]
    half = rows // 2
    any_spec = pl.BlockSpec(memory_space=pltpu.HBM)
    whole = pl.BlockSpec(memory_space=pltpu.VMEM)
    lead = list(got) if place_at is not None else []
    outs = [pltpu.HBM(h.shape, h.dtype) for h in held]
    sends = [pltpu.VMEM((half, columns), BF16)] * 2 if fetch_at is not None else []
    res = pl.pallas_call(
        functools.partial(reduce_kernel, groups, half, place_at, fetch_at),
        out_shape=outs + sends,
        in_specs=[pl.BlockSpec(memory_space=pltpu.SMEM)] + [whole] * len(lead) + [any_spec] * n,
        out_specs=[any_spec] * n + [whole] * len(sends),
        scratch_shapes=[
            pltpu.VMEM((2, half, columns), F32),
            pltpu.VMEM((2, half, columns), F32),
            pltpu.SemaphoreType.DMA((6,)),
        ],
        input_output_aliases={1 + len(lead) + i: i for i in range(n)},
        compiler_params=params(RING_VMEM),
        cost_estimate=RING_COST,
        name="reduce_step",
    )(tab, *lead, *held)
    return list(res[:n]), list(res[n:])


class Reducer:
    def __init__(self, tab, n_data, steps, depth):
        self.tab, self.n_data, self.steps, self.depth = tab, n_data, steps, depth
        self.perms = [p for p in reversed(ring_perms(n_data))]
        self.held = {}
        self.got = {}
        self.at = 0

    def lowest(self, k):
        return (self.steps - 1 - k) - (self.n_data - 2) * self.depth

    def run(self):
        ready = min(GROUPS[g][0] for g in self.held)
        while self.at < self.steps + self.depth:
            k = self.at
            if k < self.steps and max(self.lowest(k), 0) < ready:
                return
            live = sorted(self.held)
            place_at = self.steps - 1 - (k - self.depth) if k >= self.depth else None
            fetch_at = self.steps - 1 - k if k < self.steps else None
            new, sends = reduce_step(
                self.tab,
                [GROUPS[g] for g in live],
                [self.held[g] for g in live],
                self.got.get(k - self.depth),
                place_at,
                fetch_at,
            )
            for g, value in zip(live, new):
                self.held[g] = value
            if fetch_at is not None:
                self.got[k] = [lax.ppermute(sends[way], "dp", self.perms[way]) for way in range(2)]
            self.at += 1


def split_rows(total, keep_ref, send_ref):
    rows = total.shape[0] // 4
    for i in range(2):
        keep_ref[i] = total[2 * i * rows : (2 * i + 1) * rows]
        send_ref[i] = total[(2 * i + 1) * rows : (2 * i + 2) * rows].astype(BF16)


def part_shapes(rows, width):
    return [shape((2, rows // 4, width), F32), shape((2, rows // 4, width), BF16)]


def softmax_parts(q, k):
    scores = dot_nt(q, k) * SCORE_SCALE
    expo = jnp.exp(scores - jnp.max(scores, -1, keepdims=True))
    return expo / jnp.sum(expo, -1, keepdims=True)


def attention_kernel(n_lat, x_ref, w_ref, qkv_ref, mixed_ref, keep_ref, send_ref):
    x = x_ref[...]
    for j in range(3):
        qkv_ref[j] = dot(x, w_ref[j]).astype(BF16)
    toks = x.shape[0] // n_lat
    heads = w_ref.shape[2] // HEAD_DIM
    for l in range(n_lat):
        rows = slice(l * toks, (l + 1) * toks)
        outs = []
        for h in range(heads):
            cols = slice(h * HEAD_DIM, (h + 1) * HEAD_DIM)
            q, k, v = (qkv_ref[j, rows, cols] for j in range(3))
            outs.append(dot(softmax_parts(q, k).astype(BF16), v))
        mixed_ref[rows, :] = jnp.concatenate(outs, 1).astype(BF16)
    split_rows(dot_nt(mixed_ref[...], w_ref[3]), keep_ref, send_ref)


def attention(x, w, n_lat):
    rows, width = x.shape
    columns = w.shape[2]
    return pl.pallas_call(
        functools.partial(attention_kernel, n_lat),
        out_shape=[shape((3, rows, columns), BF16), shape((rows, columns), BF16)] + part_shapes(rows, width),
        compiler_params=params(32),
        name="attention",
    )(x, w)


def gelu(x):
    return 0.5 * x * (1.0 + jnp.tanh(GELU_C * (x + 0.044715 * x * x * x)))


def gelu_grad(x):
    t = jnp.tanh(GELU_C * (x + 0.044715 * x * x * x))
    return 0.5 * (1.0 + t) + 0.5 * x * (1.0 - t * t) * (GELU_C * (1.0 + 3 * 0.044715 * x * x))


def mlp_kernel(x_ref, w_ref, hidden_ref, active_ref, keep_ref, send_ref):
    x = x_ref[...]
    total = None
    for j in range(4):
        hidden = dot(x, w_ref[j])
        hidden_ref[j] = hidden
        active = gelu(hidden).astype(BF16)
        active_ref[j] = active
        part = dot_nt(active, w_ref[4 + j])
        total = part if total is None else total + part
    split_rows(total, keep_ref, send_ref)


def mlp(x, w):
    rows, width = x.shape
    columns = w.shape[2]
    return pl.pallas_call(
        mlp_kernel,
        out_shape=[shape((4, rows, columns), F32), shape((4, rows, columns), BF16)] + part_shapes(rows, width),
        compiler_params=params(40),
        name="mlp",
    )(x, w)


def mlp_back_kernel(d_ref, hidden_ref, w_ref, dh_ref, keep_ref, send_ref):
    d = d_ref[...]
    total = None
    for j in range(4):
        dh = (gelu_grad(hidden_ref[j]) * dot(d, w_ref[4 + j])).astype(BF16)
        dh_ref[j] = dh
        part = dot_nt(dh, w_ref[j])
        total = part if total is None else total + part
    split_rows(total, keep_ref, send_ref)


def mlp_back(d, hidden, w):
    rows, width = d.shape
    columns = w.shape[2]
    return pl.pallas_call(
        mlp_back_kernel,
        out_shape=[shape((4, rows, columns), BF16)] + part_shapes(rows, width),
        compiler_params=params(40),
        name="mlp_back",
    )(d, hidden, w)


def attention_back_kernel(n_lat, d_ref, qkv_ref, w_ref, dqkv_ref, keep_ref, send_ref):
    d_mixed = dot(d_ref[...], w_ref[3]).astype(BF16)
    toks = d_mixed.shape[0] // n_lat
    heads = w_ref.shape[2] // HEAD_DIM
    for l in range(n_lat):
        rows = slice(l * toks, (l + 1) * toks)
        outs = [[], [], []]
        for h in range(heads):
            cols = slice(h * HEAD_DIM, (h + 1) * HEAD_DIM)
            q, k, v = (qkv_ref[j, rows, cols] for j in range(3))
            do = d_mixed[rows, cols]
            probs = softmax_parts(q, k)
            d_probs = dot_nt(do, v)
            d_scores = probs * (d_probs - jnp.sum(probs * d_probs, -1, keepdims=True))
            d_scores = d_scores.astype(BF16)
            outs[0].append(dot(d_scores, k) * SCORE_SCALE)
            outs[1].append(dot_tn(d_scores, q) * SCORE_SCALE)
            outs[2].append(dot_tn(probs.astype(BF16), do))
        for j in range(3):
            dqkv_ref[j, rows, :] = jnp.concatenate(outs[j], 1).astype(BF16)
    total = dot_nt(dqkv_ref[0], w_ref[0]) + dot_nt(dqkv_ref[1], w_ref[1]) + dot_nt(dqkv_ref[2], w_ref[2])
    split_rows(total, keep_ref, send_ref)


def attention_back(d, qkv, w, n_lat):
    rows, width = d.shape
    columns = w.shape[2]
    return pl.pallas_call(
        functools.partial(attention_back_kernel, n_lat),
        out_shape=[shape((3, rows, columns), BF16)] + part_shapes(rows, width),
        compiler_params=params(40),
        name="attention_back",
    )(d, qkv, w)


def weight_grad_kernel(counts, n_lat, *refs):
    n = len(counts)
    lefts, rights, (out_ref, mean_ref, sum_ref) = refs[:n], refs[n : 2 * n], refs[2 * n :]
    step = pl.program_id(0)
    base = 0
    for k, count in enumerate(counts):

        @pl.when((step >= base) & (step < base + count))
        def _(left=lefts[k], right=rights[k], k=k):
            a, b = left[...], right[0]
            toks = a.shape[0] // n_lat
            means, sums = [], []
            for l in range(n_lat):
                rows = slice(l * toks, (l + 1) * toks)
                means.append(jnp.sum(a[rows].astype(F32), 0, keepdims=True) * (1.0 / toks))
                sums.append(jnp.sum(b[rows].astype(F32), 0, keepdims=True))
            mean = jnp.concatenate(means + [jnp.zeros((8 - n_lat, a.shape[1]), F32)], 0).astype(BF16)
            total = jnp.concatenate(sums + [jnp.zeros((8 - n_lat, b.shape[1]), F32)], 0).astype(BF16)
            mean_ref[k] = mean.astype(F32)
            sum_ref[0] = total.astype(F32)
            out_ref[0] = dot_tn(a, b) - dot_tn(mean, total)

        base += count


def weight_grads(pairs, n_lat):
    counts = [right.shape[0] for _, right in pairs]
    total = sum(counts)
    rows, width = pairs[0][0].shape
    columns = pairs[0][1].shape[2]
    bases = np.cumsum([0] + counts)

    def right_spec(k):
        base, count = int(bases[k]), counts[k]
        return pl.BlockSpec((1, rows, columns), lambda i: (jnp.clip(i - base, 0, count - 1), 0, 0))

    return pl.pallas_call(
        functools.partial(weight_grad_kernel, counts, n_lat),
        grid=(total,),
        in_specs=[pl.BlockSpec((rows, width), lambda i: (0, 0))] * len(pairs)
        + [right_spec(k) for k in range(len(pairs))],
        out_specs=[
            pl.BlockSpec((1, width, columns), lambda i: (i, 0, 0)),
            pl.BlockSpec((len(pairs), 8, width), lambda i: (0, 0, 0)),
            pl.BlockSpec((1, 8, columns), lambda i: (i, 0, 0)),
        ],
        out_shape=[
            shape((total, width, columns), F32),
            shape((len(pairs), 8, width), F32),
            shape((total, 8, columns), F32),
        ],
        compiler_params=params(24, dimension_semantics=("arbitrary",)),
        name="weight_grads",
    )(*[left for left, _ in pairs], *[right for _, right in pairs])


def modulation_kernel(small_ref, cond_ref, bank_ref, out_ref):
    s = pl.program_id(0)

    @pl.when(s == 0)
    def _():
        out_ref[...] = jnp.zeros_like(out_ref)

    unit = small_ref[s]

    @pl.when((unit >= 0) & (unit != TIME_AT))
    def _():
        out_ref[jnp.maximum(unit, 0)] = dot(cond_ref[...], bank_ref[0].astype(BF16))


def modulations(small_slots, cond_in, bank):
    n_slots, rows, columns = bank.shape
    n_all = cond_in.shape[0]
    return pl.pallas_call(
        modulation_kernel,
        grid_spec=pltpu.PrefetchScalarGridSpec(
            num_scalar_prefetch=1,
            grid=(n_slots,),
            in_specs=[
                pl.BlockSpec((n_all, rows), lambda s, t: (0, 0)),
                pl.BlockSpec((1, rows, columns), lambda s, t: (s, 0, 0)),
            ],
            out_specs=pl.BlockSpec((SMALL_ROWS, n_all, columns), lambda s, t: (0, 0, 0)),
        ),
        out_shape=shape((SMALL_ROWS, n_all, columns), F32),
        compiler_params=params(16, dimension_semantics=("arbitrary",)),
        name="modulations",
    )(small_slots, cond_in, bank)


def cond_back_kernel(small_ref, d_ref, bank_ref, out_ref):
    s = pl.program_id(0)

    @pl.when(s == 0)
    def _():
        out_ref[...] = jnp.zeros_like(out_ref)

    unit = small_ref[s]

    @pl.when((unit >= 0) & (unit != TIME_AT))
    def _():
        out_ref[...] += dot_nt(d_ref[jnp.maximum(unit, 0)], bank_ref[0].astype(BF16))


def cond_back(small_slots, d_small, bank):
    n_slots, rows, columns = bank.shape
    n_all = d_small.shape[1]
    return pl.pallas_call(
        cond_back_kernel,
        grid_spec=pltpu.PrefetchScalarGridSpec(
            num_scalar_prefetch=1,
            grid=(n_slots,),
            in_specs=[
                pl.BlockSpec(d_small.shape, lambda s, t: (0, 0, 0)),
                pl.BlockSpec((1, rows, columns), lambda s, t: (s, 0, 0)),
            ],
            out_specs=pl.BlockSpec((n_all, rows), lambda s, t: (0, 0)),
        ),
        out_shape=shape((n_all, rows), F32),
        compiler_params=params(16, dimension_semantics=("arbitrary",)),
        name="cond_back",
    )(small_slots, d_small, bank)


def halves(x):
    high = x.astype(BF16)
    return high, (x - high.astype(F32)).astype(BF16)


def newton_sweep(x):
    xh, xl = halves(x)
    cross = dot_tn(xh, xl)
    gram = dot_tn(xh, xh) + (cross + cross.T)
    gh, gl = halves(gram)
    cross = dot(gh, gl)
    square = dot(gh, gh) + (cross + cross.T)
    ph, pl_ = halves(NS_COEF[1] * gram + NS_COEF[2] * square)
    return NS_COEF[0] * x + (dot(xh, ph) + (dot(xl, ph) + dot(xh, pl_)))


def newton_kernel(
    big_ref, left_ref, right_ref, a_ref, b_ref, bank_ref, mom_ref, g0, g1, g2, g3, new_ref, mom_new_ref, grad, sem
):
    s = pl.program_id(0)
    unit, left, right = big_ref[s], left_ref[s], right_ref[s]

    @pl.when(right < 0)
    def _():
        new_ref[...] = bank_ref[...]
        mom_new_ref[...] = mom_ref[...]

    @pl.when(right >= 0)
    def _():
        copies = []
        for ref, (low, high) in zip((g0, g1, g2, g3), GROUPS):
            inside = (unit >= low) & (unit < high)
            at = jnp.clip(unit - low, 0, high - low - 1)
            copies.append((inside, pltpu.make_async_copy(ref.at[at], grad, sem.at[0])))
        for inside, copy in copies:
            pl.when(inside)(copy.start)
        some = dot_tn(a_ref[jnp.maximum(left, 0)], b_ref[jnp.maximum(right, 0)])
        for inside, copy in copies:
            pl.when(inside)(copy.wait)

        @pl.when(unit >= 0)
        def _():
            mom_new_ref[0] = 0.5 * mom_ref[0] + (some + grad[...])

        @pl.when(unit < 0)
        def _():
            mom_new_ref[0] = 0.5 * mom_ref[0] + some

        block = mom_new_ref[0]
        norm = jnp.sqrt(jnp.sum(block * block)) + 1e-07
        x = block / norm
        for _ in range(5):
            x = newton_sweep(x)
        new_ref[0] = bank_ref[0] - LR_MUON * x


def optimizer(big_slots, left_slots, right_slots, a_all, b_all, master, momentum, grads):
    n_slots, rows, columns = master.shape
    block = pl.BlockSpec((1, rows, columns), lambda s, *t: (s, 0, 0))
    any_spec = pl.BlockSpec(memory_space=pltpu.HBM)
    return pl.pallas_call(
        newton_kernel,
        grid_spec=pltpu.PrefetchScalarGridSpec(
            num_scalar_prefetch=3,
            grid=(n_slots,),
            in_specs=[
                pl.BlockSpec(a_all.shape, lambda s, *t: (0, 0, 0)),
                pl.BlockSpec(b_all.shape, lambda s, *t: (0, 0, 0)),
                block,
                block,
            ]
            + [any_spec] * 4,
            out_specs=[block, block],
            scratch_shapes=[pltpu.VMEM((rows, columns), F32), pltpu.SemaphoreType.DMA((1,))],
        ),
        out_shape=[shape(master.shape, F32), shape(momentum.shape, F32)],
        compiler_params=params(48, dimension_semantics=("arbitrary",)),
        name="optimizer",
    )(big_slots, left_slots, right_slots, a_all, b_all, master, momentum, *grads)


def layer_norm(values):
    centered = values - jnp.mean(values, -1, keepdims=True)
    inv_std = lax.rsqrt(jnp.mean(centered * centered, -1, keepdims=True) + 1e-06)
    return centered * inv_std, inv_std


def norm_back(grad_out, normed, inv_std):
    return inv_std * (
        grad_out
        - jnp.mean(grad_out, -1, keepdims=True)
        - normed * jnp.mean(grad_out * normed, -1, keepdims=True)
    )


def position_rows(first, rows):
    quarter = D // 4
    omega = jnp.exp(-math.log(10000.0) * jnp.arange(quarter, dtype=F32) / quarter)
    places = first + jnp.arange(rows, dtype=jnp.int32)
    rows_at = (places // GRID).astype(F32)[:, None] * omega[None]
    cols_at = (places % GRID).astype(F32)[:, None] * omega[None]
    return jnp.concatenate([jnp.sin(rows_at), jnp.cos(rows_at), jnp.sin(cols_at), jnp.cos(cols_at)], 1)


def time_features(timesteps):
    half_freq = FREQ // 2
    rates = jnp.exp(-math.log(10000.0) * jnp.arange(half_freq, dtype=F32) / half_freq)
    angles = timesteps.astype(F32)[:, None] * rates[None]
    return jnp.concatenate([jnp.cos(angles), jnp.sin(angles)], 1)


def shards(
    noisy_latents,
    noise_target,
    timesteps,
    labels,
    owners,
    step_count,
    master_bank,
    momentum_bank,
    embed_tables,
    embed_first,
    embed_second,
):
    n_lat, n_tok, n_patch = noisy_latents.shape
    n_slots, width, columns = master_bank.shape
    n_units = owners.shape[0]
    n_data = lax.axis_size("dp")
    my_data = lax.axis_index("dp")
    my_tensor = lax.axis_index("tensor")
    chip, core = my_tensor // 2, my_tensor % 2
    n_all = n_lat * n_data
    own_rows = n_lat * n_tok // 4
    count_all = float(n_all * n_tok * n_patch)
    depth = 2 if n_data <= 8 else 1
    steps = N_BIG + (n_data - 2) * depth

    unit_order = jnp.arange(n_units, dtype=jnp.int32)
    same_owner = owners[:, None] == owners[None, :]
    slot_of = jnp.sum((same_owner & (unit_order[None, :] < unit_order[:, None])).astype(jnp.int32), 1)
    mine = (owners[None, :] == my_data) & (
        slot_of[None, :] == jnp.arange(n_slots, dtype=jnp.int32)[:, None]
    )

    def of_slot(table):
        return jnp.sum(jnp.where(mine, jnp.asarray(table + 1, jnp.int32)[None], 0), 1) - 1

    big_slots, small_slots = of_slot(BIG_OF), of_slot(SMALL_OF)
    owners_big = jnp.concatenate([owners[18 * l : 18 * l + BIG] for l in range(LAYERS)])
    tab = ring_schedule(owners_big, n_data, steps, depth, my_data)
    held = spread_init(big_slots, master_bank)
    weights = spread_weights(tab, held, n_data, steps, depth)

    ids = jnp.stack([timesteps, labels], 1)[None]
    ids = jnp.where(jnp.arange(n_data)[:, None, None] == my_data, ids, 0)
    ids = dp_sum(ids, n_data).reshape(n_all, 2)
    narrow = embed_tables.astype(BF16)
    edge_rows = lax.all_gather(
        jnp.concatenate([narrow[:n_patch], narrow[n_patch + FREQ + CLASSES :]], 0), "tensor", axis=1, tiled=True
    )
    patch_w, head_w = edge_rows[:n_patch], edge_rows[n_patch:]
    features = time_features(ids[:, 0]).astype(BF16)
    time_one = jnp.dot(features, narrow[n_patch : n_patch + FREQ], preferred_element_type=F32)
    time_act = lax.all_gather(jax.nn.silu(time_one).astype(BF16), "tensor", axis=1, tiled=True)
    time_mine = owners[18 * LAYERS] == my_data
    time_w2 = lax.dynamic_index_in_dim(master_bank, slot_of[18 * LAYERS], 0, keepdims=False).astype(BF16)
    second = jnp.dot(time_act, time_w2, preferred_element_type=F32)
    second = dp_sum(jnp.where(time_mine, second, 0.0), n_data)
    onehot = ids[:, 1:2] == jnp.arange(CLASSES, dtype=jnp.int32)[None]
    class_w = narrow[n_patch + FREQ : n_patch + FREQ + CLASSES]
    condition = second + jnp.dot(onehot.astype(BF16), class_w, preferred_element_type=F32)
    cond_in = lax.all_gather(jax.nn.silu(condition).astype(BF16), "tensor", axis=1, tiled=True)
    mods = modulations(small_slots, cond_in, master_bank)
    mods = mods.transpose(1, 0, 2).reshape(n_data, n_lat, SMALL_ROWS, columns)
    bit = n_data // 2
    while bit:
        pairs = mods.reshape((2, mods.shape[0] // 2) + mods.shape[1:])
        side = (my_data // bit) % 2
        mods = pick(pairs, 0, side) + flip(pick(pairs, 0, 1 - side), "dp", bit, n_data)
        bit //= 2
    mods = lax.all_gather(mods[0], "tensor", axis=2, tiled=True)
    mods = pick(mods, 0, chip)

    first_row = my_tensor * own_rows
    noisy_own = lax.dynamic_slice_in_dim(noisy_latents.reshape(n_lat * n_tok, n_patch), first_row, own_rows, 0)
    target_own = lax.dynamic_slice_in_dim(noise_target.reshape(n_lat * n_tok, n_patch), first_row, own_rows, 0)
    stream = jnp.dot(noisy_own, patch_w, preferred_element_type=F32) + position_rows(
        first_row % n_tok, own_rows
    )

    def modulate(values, shift, scale):
        normed, inv_std = layer_norm(values)
        return (normed * (1.0 + scale) + shift).astype(BF16), normed, inv_std

    kept = []
    for layer in range(LAYERS):
        shift_a, scale_a, gate_a, shift_m, scale_m, gate_m = (mods[SMALL * layer + i][None] for i in range(SMALL))
        w_attn, w_mlp = weights[2 * layer], weights[2 * layer + 1]
        inner, normed, inv_std = modulate(stream, shift_a, scale_a)
        inner = gather_tokens(inner)
        qkv, mixed, keep, send = attention(inner, w_attn, n_lat)
        attended = scatter_tokens(keep, send)
        stream_mid = stream + gate_a * attended
        inner_mid, normed_mid, inv_mid = modulate(stream_mid, shift_m, scale_m)
        inner_mid = gather_tokens(inner_mid)
        hidden, active, keep, send = mlp(inner_mid, w_mlp)
        branch = scatter_tokens(keep, send)
        stream = stream_mid + gate_m * branch
        kept.append(
            (inner, normed, inv_std, qkv, mixed, attended, inner_mid, normed_mid, inv_mid, hidden, active, branch)
        )
    shift_f, scale_f = mods[FINAL_AT][None], mods[FINAL_AT + 1][None]
    inner_out, normed_out, inv_out = modulate(stream, shift_f, scale_f)
    output = lax.dot_general(inner_out, head_w, (((1,), (1,)), ((), ())), preferred_element_type=F32)
    error_out = output - target_own
    loss_own = jnp.sum(error_out * error_out) / count_all
    d_output = (2.0 * error_out / count_all).astype(BF16)
    grad_head = lax.dot_general(d_output, inner_out, (((0,), (0,)), ((), ())), preferred_element_type=F32)

    d_inner = jnp.dot(d_output, head_w, preferred_element_type=F32)
    d_mods = {FINAL_AT: jnp.sum(d_inner, 0), FINAL_AT + 1: jnp.sum(d_inner * normed_out, 0)}
    grad_flow = norm_back(d_inner * (1.0 + scale_f), normed_out, inv_out)
    ring = Reducer(tab, n_data, steps, depth)
    lefts, rights = {}, {}
    for layer in reversed(range(LAYERS)):
        (inner, normed, inv_std, qkv, mixed, attended, inner_mid, normed_mid, inv_mid, hidden, active, branch) = kept[
            layer
        ]
        shift_a, scale_a, gate_a, shift_m, scale_m, gate_m = (mods[SMALL * layer + i][None] for i in range(SMALL))
        w_attn, w_mlp = weights[2 * layer], weights[2 * layer + 1]
        d_branch = gather_tokens((gate_m * grad_flow).astype(BF16))
        d_gate_m = jnp.sum(grad_flow * branch, 0)
        d_hidden, keep, send = mlp_back(d_branch, hidden, w_mlp)
        d_inner_mid = scatter_tokens(keep, send)
        grads, left, right = weight_grads([(inner_mid, d_hidden), (d_branch, active)], n_lat)
        ring.held[2 * layer + 1] = grads
        lefts[2 * layer + 1], rights[2 * layer + 1] = left, right
        ring.run()
        d_shift_m = jnp.sum(d_inner_mid, 0)
        d_scale_m = jnp.sum(d_inner_mid * normed_mid, 0)
        grad_mid = grad_flow + norm_back(d_inner_mid * (1.0 + scale_m), normed_mid, inv_mid)
        d_attended = gather_tokens((gate_a * grad_mid).astype(BF16))
        d_gate_a = jnp.sum(grad_mid * attended, 0)
        d_qkv, keep, send = attention_back(d_attended, qkv, w_attn, n_lat)
        d_inner = scatter_tokens(keep, send)
        grads, left, right = weight_grads([(inner, d_qkv), (d_attended, mixed[None])], n_lat)
        ring.held[2 * layer] = grads
        lefts[2 * layer], rights[2 * layer] = left, right
        ring.run()
        d_shift_a = jnp.sum(d_inner, 0)
        d_scale_a = jnp.sum(d_inner * normed, 0)
        grad_flow = grad_mid + norm_back(d_inner * (1.0 + scale_a), normed, inv_std)
        for i, value in enumerate((d_shift_a, d_scale_a, d_gate_a, d_shift_m, d_scale_m, d_gate_m)):
            d_mods[SMALL * layer + i] = value

    d_mods[TIME_AT] = jnp.zeros((width,), F32)
    d_mods[SMALL_ROWS - 1] = jnp.zeros((width,), F32)
    d_small = jnp.stack([d_mods[i] for i in range(SMALL_ROWS)]).reshape(SMALL_ROWS, 2, 2, columns)
    d_small = pick(d_small, 2, core) + core_flip(pick(d_small, 2, 1 - core))
    near, far = pick(d_small, 1, chip), x_flip(pick(d_small, 1, 1 - chip))
    d_small = jnp.where(
        jnp.arange(2)[:, None, None] == chip, near[None], far[None]
    ).astype(BF16)
    d_small = jnp.where(jnp.arange(n_data)[:, None, None, None] == my_data, d_small[None], jnp.zeros((), BF16))
    d_small = dp_sum(d_small, n_data).reshape(n_all, SMALL_ROWS, columns).transpose(1, 0, 2)
    d_cond = cond_back(small_slots, d_small, master_bank)
    d_cond = dp_sum(own_columns_sum(d_cond, chip, core), n_data)
    unused, silu_pull = jax.vjp(jax.nn.silu, condition)
    d_condition = silu_pull(d_cond)[0]
    d_second = d_condition.astype(BF16)
    grad_class = lax.dot_general(
        onehot.astype(F32), d_condition, (((0,), (0,)), ((), ())), precision=HIGHEST_PREC
    )
    d_time_act = lax.dot_general(d_second, time_w2, (((1,), (1,)), ((), ())), preferred_element_type=F32)
    d_time_act = jnp.where(time_mine, d_time_act, 0.0)
    d_time_act = dp_sum(own_columns_sum(d_time_act, chip, core), n_data)
    unused, time_pull = jax.vjp(jax.nn.silu, time_one)
    d_time_one = time_pull(d_time_act)[0].astype(BF16)
    grad_time_one = lax.dot_general(features, d_time_one, (((0,), (0,)), ((), ())), preferred_element_type=F32)
    d_stream = grad_flow.astype(BF16)
    grad_patch = lax.dot_general(noisy_own, d_stream, (((0,), (0,)), ((), ())), preferred_element_type=F32)
    edges = jnp.concatenate([grad_patch, grad_head, jnp.full((1, width), loss_own)], 0)
    edges = dp_sum(own_columns_sum(edges, chip, core), n_data)
    loss = edges[2 * n_patch, 0]
    grad_embed = jnp.concatenate(
        [edges[:n_patch], grad_time_one, grad_class, edges[n_patch : 2 * n_patch]], 0
    )

    a_rows, b_rows = [], []
    for g in range(len(GROUPS)):
        a_rows.append(lefts[g][:, :n_lat].transpose(1, 0, 2))
        b_rows.append(rights[g][:, :n_lat].transpose(1, 0, 2))
    a_rows = jnp.concatenate(a_rows, 1).astype(BF16)
    b_rows = jnp.concatenate(b_rows, 1).astype(BF16)
    n_left = a_rows.shape[1]
    packed = jnp.concatenate([a_rows.reshape(n_lat, n_left * 4, columns), b_rows], 1)
    packed = dp_rows(packed, n_data)
    a_rows = packed[:, : n_left * 4].reshape(n_all, n_left, width).transpose(1, 0, 2)
    b_rows = packed[:, n_left * 4 :].transpose(1, 0, 2)
    a_all = jnp.concatenate([cond_in[None], time_act[None], a_rows], 0)
    small_rows = jnp.where(
        jnp.arange(SMALL_ROWS)[:, None, None] == TIME_AT, d_second[None], d_small
    )
    b_all = jnp.concatenate([small_rows, b_rows], 0)
    kind = []
    for g, (low, high) in enumerate(GROUPS):
        split = low + 3 if g % 2 == 0 else low + 4
        kind += [2 + 2 * g + (b >= split) for b in range(low, high)]
    kind_of = np.where(BIG_OF >= 0, np.array(kind)[BIG_OF], np.where(SMALL_OF == TIME_AT, 1, 0))
    right_of = np.where(BIG_OF >= 0, SMALL_ROWS + BIG_OF, SMALL_OF)
    master_new, momentum_new = optimizer(
        big_slots,
        of_slot(kind_of),
        of_slot(right_of),
        a_all,
        b_all,
        master_bank,
        momentum_bank,
        [ring.held[g] for g in range(len(GROUPS))],
    )

    first_new = 0.5 * embed_first + 0.5 * grad_embed
    second_new = 0.5 * embed_second + 0.5 * grad_embed * grad_embed
    bias_fix = 1.0 - jnp.power(0.5, step_count[0].astype(F32))
    embed_new = embed_tables * (1.0 - LR_ADAM * WEIGHT_DECAY) - LR_ADAM * (first_new / bias_fix) / (
        jnp.sqrt(second_new / bias_fix) + 1e-08
    )
    return (loss, master_new, momentum_new, embed_new, first_new, second_new)


def solution(mesh):
    placed = (
        P("dp", None, None),
        P("dp", None, None),
        P("dp"),
        P("dp"),
        P(),
        P(),
        P("dp", None, "tensor"),
        P("dp", None, "tensor"),
        P(None, "tensor"),
        P(None, "tensor"),
        P(None, "tensor"),
    )
    return jax.shard_map(
        shards,
        mesh=mesh,
        in_specs=placed,
        out_specs=(
            P(),
            P("dp", None, "tensor"),
            P("dp", None, "tensor"),
            P(None, "tensor"),
            P(None, "tensor"),
            P(None, "tensor"),
        ),
        check_vma=False,
    )
```

```python
import functools
import math

import jax
import jax.numpy as jnp
import numpy as np
from jax import lax
from jax.experimental import pallas as pl
from jax.experimental.pallas import tpu as pltpu
from jax.sharding import PartitionSpec as P

D = 1024
HEAD_DIM = 64
FREQ = 256
CLASSES = 1000
GRID = 16
LAYERS = 2
BIG = 12
SMALL = 6
N_BIG = BIG * LAYERS
TIME_AT = SMALL * LAYERS
FINAL_AT = TIME_AT + 1
SMALL_ROWS = 16

NS_COEF = (3.4445, -4.775, 2.0315)
LR_MUON = 0.5
LR_ADAM = 0.02
WEIGHT_DECAY = 0.1
SCORE_SCALE = 1.0 / math.sqrt(HEAD_DIM)
HIGHEST_PREC = lax.Precision.HIGHEST

F32 = jnp.float32
BF16 = jnp.bfloat16
RING_VMEM = 8
RING_COST = pl.CostEstimate(flops=0, transcendentals=0, bytes_accessed=2**21)
GELU_C = math.sqrt(2.0 / math.pi)
GROUPS = ((0, 4), (4, 12), (12, 16), (16, 24))


def unit_tables():
    big, small = [], []
    for u in range(18 * LAYERS):
        layer, place = divmod(u, 18)
        big.append(layer * BIG + place if place < BIG else -1)
        small.append(-1 if place < BIG else layer * SMALL + place - BIG)
    return np.array(big + [-1] * 3), np.array(small + [TIME_AT, FINAL_AT, FINAL_AT + 1])


BIG_OF, SMALL_OF = unit_tables()


def params(limit, **more):
    return pltpu.CompilerParams(vmem_limit_bytes=limit * 1024 * 1024, **more)


def dot(a, b):
    return lax.dot_general(a, b, (((1,), (0,)), ((), ())), preferred_element_type=F32)


def dot_nt(a, b):
    return lax.dot_general(a, b, (((1,), (1,)), ((), ())), preferred_element_type=F32)


def dot_tn(a, b):
    return lax.dot_general(a, b, (((0,), (0,)), ((), ())), preferred_element_type=F32)


def shape(dims, kind):
    return jax.ShapeDtypeStruct(dims, kind)


ISSUED = []


def order(values, after):
    if not after:
        return values
    flat, tree = jax.tree.flatten(values)
    tied = lax.optimization_barrier(tuple(flat) + tuple(after))
    return jax.tree.unflatten(tree, tied[: len(flat)])


def drive(work, line):
    ISSUED.clear()
    try:
        value = next(work)
        while True:
            after = tuple(ISSUED)
            ISSUED.clear()
            value = work.send(order(value, line(after)))
    except StopIteration as end:
        return end.value


def together(*works):
    ends, flying = [None] * len(works), {}

    def go(i, step):
        try:
            flying[i] = step()
        except StopIteration as end:
            flying.pop(i, None)
            ends[i] = end.value

    for i, work in enumerate(works):
        go(i, lambda: next(work))
    while flying:
        got = yield dict(flying)
        for i in list(got):
            go(i, lambda: works[i].send(got[i]))
    return ends


def resume(work, value):
    try:
        while True:
            value = work.send((yield value))
    except StopIteration as end:
        return end.value


def flip(values, axis, bit, size):
    ISSUED.append(values)
    return lax.ppermute(values, axis, [(i, i ^ bit) for i in range(size)])


def pick(values, axis, place):
    low, high = (lax.index_in_dim(values, i, axis, keepdims=False) for i in (0, 1))
    return jnp.where(place == 0, low, high)


def dp_sum(values, n_data):
    bit = 1
    while bit < n_data:
        values = values + (yield flip(values, "dp", bit, n_data))
        bit *= 2
    return values


def dp_rows(values, n_data):
    bit = 1
    while bit < n_data:
        values = jnp.concatenate([values, (yield flip(values, "dp", bit, n_data))], 0)
        bit *= 2
    return values


def core_flip(values):
    return flip(values, "tensor", 1, 4)


def x_flip(values):
    return flip(values, "tensor", 2, 4)


def gather_tokens(own):
    beside, across = yield (core_flip(own), x_flip(own))
    corner = yield core_flip(across)
    return jnp.concatenate([own, beside, across, corner], 0)


def gather_columns(own, chip, core):
    beside, across = yield (core_flip(own), x_flip(own))
    corner = yield core_flip(across)
    near = [jnp.where(core == i, own, beside) for i in range(2)]
    far = [jnp.where(core == i, across, corner) for i in range(2)]
    parts = [jnp.where(chip == i, near[j], far[j]) for i in range(2) for j in range(2)]
    return jnp.concatenate(parts, -1)


def scatter_tokens(keep, send):
    got = yield core_flip(send)
    near = keep[0] + got[0].astype(F32)
    far = (keep[1] + got[1].astype(F32)).astype(BF16)
    return near + (yield x_flip(far)).astype(F32)


def own_columns_sum(values, chip, core):
    split = values.reshape(values.shape[:-1] + (2, 2, values.shape[-1] // 4))
    axis = split.ndim - 2
    mine = pick(split, axis, core) + (yield core_flip(pick(split, axis, 1 - core)))
    axis = mine.ndim - 2
    return pick(mine, axis, chip) + (yield x_flip(pick(mine, axis, 1 - chip)))


def sum_of_columns(values, chip, core, n_data):
    return (yield from dp_sum((yield from own_columns_sum(values, chip, core)), n_data))


def ring_order(n_data):
    return [0, 2, 4, 6, 7, 5, 3, 1] if n_data == 8 else list(range(n_data))


def sched_kernel(steps, depth, n_data, place_ref, own_ref, next_ref, out_ref):
    lane = lax.broadcasted_iota(jnp.int32, (n_data, 128), 1)
    row = lax.broadcasted_iota(jnp.int32, (n_data, 128), 0)
    far = jnp.int32(999)
    out_lane = lax.broadcasted_iota(jnp.int32, (1, 128), 1)

    def step(t, carry):
        line = jnp.full((1, 128), -1, jnp.int32)
        after = []
        for way in range(2):
            have, sent, *coming = carry[way]
            place = place_ref[way]
            before = jnp.where(place == 0, n_data - 1, place - 1)
            open_now = have * (1 - sent) * (1 - next_ref[way])
            first = jnp.min(jnp.where(open_now > 0, lane, far), axis=1, keepdims=True)
            chosen = (lane == first).astype(jnp.int32)
            first = jnp.broadcast_to(first, (n_data, 128))
            for k, who in enumerate((place, before)):
                index = jnp.min(jnp.where(row == who, first, far), axis=0, keepdims=True)
                index = jnp.where(index == far, -1, index)
                line = jnp.where(out_lane == 2 * way + k, index, line)
            coming = list(coming) + [pltpu.roll(chosen, 1, 0)]
            after.append((have + coming[0], sent + chosen, *coming[1:]))
        out_ref[pl.ds(t, 1), :] = line
        return tuple(after)

    none = jnp.zeros((n_data, 128), jnp.int32)
    lax.fori_loop(0, steps, step, tuple((own_ref[way], none) + (none,) * (depth - 1) for way in range(2)))


def ring_schedule(owners_big, n_data, steps, depth, my_data):
    order = np.array(ring_order(n_data))
    place_of = np.argsort(order)
    place = jnp.sum(jnp.where(jnp.arange(n_data) == my_data, place_of, 0)).astype(jnp.int32)
    at = jnp.arange(n_data)[:, None]
    owner_place = jnp.sum(jnp.where(owners_big[:, None] == jnp.arange(n_data)[None], place_of[None], 0), 1)
    owner_place = jnp.concatenate([owner_place, jnp.full((128 - N_BIG,), -9, owner_place.dtype)])[None]
    back_place = jnp.where(owner_place >= 0, n_data - 1 - owner_place, -9)
    own = jnp.stack([at == owner_place, at == back_place]).astype(jnp.int32)
    follow = (at + 1) % n_data
    nxt = jnp.stack([follow == owner_place, follow == back_place]).astype(jnp.int32)
    out = pl.pallas_call(
        functools.partial(sched_kernel, steps, depth, n_data),
        out_shape=shape((steps, 128), jnp.int32),
        in_specs=[
            pl.BlockSpec(memory_space=pltpu.SMEM),
            pl.BlockSpec(memory_space=pltpu.VMEM),
            pl.BlockSpec(memory_space=pltpu.VMEM),
        ],
        out_specs=pl.BlockSpec(memory_space=pltpu.VMEM),
        name="ring_schedule",
    )(jnp.stack([place, n_data - 1 - place]), own, nxt)
    return out[:, :4]


def spread_init_kernel(big_ref, bank_ref, *refs):
    outs, (wide, narrow, in_sem, out_sem) = refs[: len(GROUPS)], refs[len(GROUPS) :]
    n_slots = bank_ref.shape[0]

    def load(s):
        return pltpu.make_async_copy(bank_ref.at[s], wide.at[s % 2], in_sem.at[s % 2])

    def stores(s):
        unit = big_ref[s]
        for g, (low, high) in enumerate(GROUPS):
            inside = (unit >= low) & (unit < high)
            at = jnp.clip(unit - low, 0, high - low - 1)
            yield inside, pltpu.make_async_copy(narrow.at[s % 2], outs[g].at[at], out_sem.at[s % 2])

    def wait_stores(s):
        for inside, copy in stores(s):
            pl.when(inside)(copy.wait)

    load(0).start()
    for s in range(n_slots):
        if s + 1 < n_slots:
            load(s + 1).start()
        load(s).wait()
        if s >= 2:
            wait_stores(s - 2)
        narrow[s % 2] = wide[s % 2].astype(BF16)
        for inside, copy in stores(s):
            pl.when(inside)(copy.start)
    for s in range(max(n_slots - 2, 0), n_slots):
        wait_stores(s)


def spread_init(big_slots, master_bank):
    n_slots, rows, columns = master_bank.shape
    return pl.pallas_call(
        spread_init_kernel,
        out_shape=[pltpu.HBM((high - low, rows, columns), BF16) for low, high in GROUPS],
        in_specs=[pl.BlockSpec(memory_space=pltpu.SMEM), pl.BlockSpec(memory_space=pl.ANY)],
        out_specs=[pl.BlockSpec(memory_space=pltpu.HBM)] * len(GROUPS),
        scratch_shapes=[
            pltpu.VMEM((2, rows, columns), F32),
            pltpu.VMEM((2, rows, columns), BF16),
            pltpu.SemaphoreType.DMA((2,)),
            pltpu.SemaphoreType.DMA((2,)),
        ],
        compiler_params=params(16),
        name="own_weights",
    )(big_slots, master_bank)


def moves(index, groups, refs, way, half):
    for ref, (low, high) in zip(refs, groups):
        inside = (index >= low) & (index < high)
        at = jnp.clip(index - low, 0, high - low - 1)
        yield inside, ref.at[at, pl.ds(way * half, half)]


def spread_kernel(groups, half, places, fetch_at, tab_ref, *refs):
    n = len(groups)
    refs = list(refs)
    got = [[refs.pop(0) for _ in range(2)] for _ in places]
    refs = refs[n:]
    held = [refs.pop(0) for _ in range(n)]
    out = [refs.pop(0) for _ in range(2)] if fetch_at is not None else None
    sem = refs.pop(0)
    copies = []
    for way in range(2):
        adds = [tab_ref[t, 2 * way + 1] for t in places]
        if fetch_at is not None:
            take = tab_ref[fetch_at, 2 * way]
            for inside, spot in moves(take, groups, held, way, half):
                for add in adds:
                    inside = inside & (take != add)
                copies.append((inside, pltpu.make_async_copy(spot, out[way], sem.at[way])))
        for k, add in enumerate(adds):
            for inside, spot in moves(add, groups, held, way, half):
                copies.append((inside, pltpu.make_async_copy(got[k][way], spot, sem.at[2 + 2 * k + way])))
    for inside, copy in copies:
        pl.when(inside)(copy.start)
    if fetch_at is not None:
        for way in range(2):
            for k, t in enumerate(places):

                @pl.when(tab_ref[fetch_at, 2 * way] == tab_ref[t, 2 * way + 1])
                def _(way=way, k=k):
                    out[way][...] = got[k][way][...]

    for inside, copy in copies:
        pl.when(inside)(copy.wait)


def spread_step(tab, groups, held, got, places, fetch_at):
    n = len(groups)
    rows, columns = held[0].shape[1:]
    half = rows // 2
    any_spec = pl.BlockSpec(memory_space=pltpu.HBM)
    whole = pl.BlockSpec(memory_space=pltpu.VMEM)
    outs = [pltpu.HBM(h.shape, h.dtype) for h in held]
    sends = [pltpu.VMEM((half, columns), BF16)] * 2 if fetch_at is not None else []
    res = pl.pallas_call(
        functools.partial(spread_kernel, groups, half, places, fetch_at),
        out_shape=outs + sends,
        in_specs=[pl.BlockSpec(memory_space=pltpu.SMEM)] + [whole] * len(got) + [any_spec] * n,
        out_specs=[any_spec] * n + [whole] * len(sends),
        scratch_shapes=[pltpu.SemaphoreType.DMA((2 + 2 * max(len(places), 1),))],
        input_output_aliases={1 + len(got) + i: i for i in range(n)},
        compiler_params=params(RING_VMEM),
        cost_estimate=RING_COST,
        name="spread_step",
    )(tab, *got, *held)
    return list(res[:n]), list(res[n:])


def ring_perms(n_data):
    order = ring_order(n_data)
    ahead = [(order[i], order[(i + 1) % n_data]) for i in range(n_data)]
    return ahead, [(b, a) for a, b in ahead]


class Spreader:
    def __init__(self, tab, held, n_data, steps, depth):
        self.tab, self.n_data, self.steps, self.depth = tab, n_data, steps, depth
        self.perms = ring_perms(n_data)
        self.held = list(held)
        self.got = {}
        self.at = 0

    def last(self, g):
        return GROUPS[g][1] - 1 + (self.n_data - 2) * self.depth

    def step(self, after=()):
        t = self.at
        if t > self.steps:
            return ()
        fetch_at = t if t < self.steps else None
        places = [t - self.depth] if fetch_at is not None else list(range(self.steps - self.depth, self.steps))
        places = [p for p in places if p >= 0]
        live = [g for g in range(len(GROUPS)) if t - self.depth <= self.last(g)]
        new, sends = spread_step(
            order(self.tab, after),
            [GROUPS[g] for g in live],
            [self.held[g] for g in live],
            [value for p in places for value in self.got.pop(p)],
            places,
            fetch_at,
        )
        for g, value in zip(live, new):
            self.held[g] = value
        if sends:
            self.got[t] = [lax.ppermute(sends[way], "dp", self.perms[way]) for way in range(2)]
        self.at += 1
        return tuple(sends)

    def weights(self, g, after=()):
        while self.at <= min(self.last(g) + self.depth, self.steps):
            self.step(after)
            after = ()
        return self.held[g]


def reduce_kernel(groups, half, place_at, fetch_at, tab_ref, *refs):
    n = len(groups)
    refs = list(refs)
    got = [refs.pop(0) for _ in range(2)] if place_at is not None else None
    refs = refs[n:]
    held = [refs.pop(0) for _ in range(n)]
    out = [refs.pop(0) for _ in range(2)] if fetch_at is not None else None
    total, other, sem = refs
    add = [tab_ref[place_at, 2 * way] for way in range(2)] if place_at is not None else None
    take = [tab_ref[fetch_at, 2 * way + 1] for way in range(2)] if fetch_at is not None else None
    first, second, back = [], [], []
    for way in range(2):
        if add is not None:
            for inside, spot in moves(add[way], groups, held, way, half):
                first.append((inside, pltpu.make_async_copy(spot, total.at[way], sem.at[way])))
                back.append((inside, pltpu.make_async_copy(total.at[way], spot, sem.at[4 + way])))
        if take is not None:
            for inside, spot in moves(take[way], groups, held, way, half):
                if add is not None:
                    inside = inside & (take[way] != add[way])
                second.append((inside, pltpu.make_async_copy(spot, other.at[way], sem.at[2 + way])))
    for inside, copy in first + second:
        pl.when(inside)(copy.start)
    if add is not None:
        for inside, copy in first:
            pl.when(inside)(copy.wait)
        for way in range(2):
            total[way] = total[way] + got[way][...].astype(F32)
        for inside, copy in back:
            pl.when(inside)(copy.start)
    if take is not None:
        for inside, copy in second:
            pl.when(inside)(copy.wait)
        for way in range(2):
            if add is None:
                out[way][...] = other[way].astype(BF16)
            else:
                same = take[way] == add[way]

                @pl.when(same)
                def _():
                    out[way][...] = total[way].astype(BF16)

                @pl.when(jnp.logical_not(same))
                def _():
                    out[way][...] = other[way].astype(BF16)

    if add is not None:
        for inside, copy in back:
            pl.when(inside)(copy.wait)


def reduce_step(tab, groups, held, got, place_at, fetch_at):
    n = len(groups)
    rows, columns = held[0].shape[1:]
    half = rows // 2
    any_spec = pl.BlockSpec(memory_space=pltpu.HBM)
    whole = pl.BlockSpec(memory_space=pltpu.VMEM)
    lead = list(got) if place_at is not None else []
    outs = [pltpu.HBM(h.shape, h.dtype) for h in held]
    sends = [pltpu.VMEM((half, columns), BF16)] * 2 if fetch_at is not None else []
    res = pl.pallas_call(
        functools.partial(reduce_kernel, groups, half, place_at, fetch_at),
        out_shape=outs + sends,
        in_specs=[pl.BlockSpec(memory_space=pltpu.SMEM)] + [whole] * len(lead) + [any_spec] * n,
        out_specs=[any_spec] * n + [whole] * len(sends),
        scratch_shapes=[
            pltpu.VMEM((2, half, columns), F32),
            pltpu.VMEM((2, half, columns), F32),
            pltpu.SemaphoreType.DMA((6,)),
        ],
        input_output_aliases={1 + len(lead) + i: i for i in range(n)},
        compiler_params=params(RING_VMEM),
        cost_estimate=RING_COST,
        name="reduce_step",
    )(tab, *lead, *held)
    return list(res[:n]), list(res[n:])


class Reducer:
    def __init__(self, tab, n_data, steps, depth):
        self.tab, self.n_data, self.steps, self.depth = tab, n_data, steps, depth
        self.perms = [p for p in reversed(ring_perms(n_data))]
        self.held = {}
        self.got = {}
        self.at = 0

    def lowest(self, k):
        return (self.steps - 1 - k) - (self.n_data - 2) * self.depth

    def step(self, after=()):
        k = self.at
        if k < self.steps and self.held and max(self.lowest(k), 0) >= min(GROUPS[g][0] for g in self.held):
            live = sorted(self.held)
            place_at = self.steps - 1 - (k - self.depth) if k >= self.depth else None
            fetch_at = self.steps - 1 - k
            new, sends = reduce_step(
                order(self.tab, after),
                [GROUPS[g] for g in live],
                [self.held[g] for g in live],
                self.got.get(k - self.depth),
                place_at,
                fetch_at,
            )
            for g, value in zip(live, new):
                self.held[g] = value
            self.got[k] = [lax.ppermute(sends[way], "dp", self.perms[way]) for way in range(2)]
            self.at += 1
            return tuple(sends)
        return ()

    def drain(self):
        while self.at < self.steps:
            self.step()

    def last(self):
        got, units = [], []
        for k in range(self.steps - self.depth, self.steps):
            for way in range(2):
                got.append(self.got[k][way])
                units.append(self.tab[self.steps - 1 - k, 2 * way])
        return got, jnp.stack(units)


def split_rows(total, keep_ref, send_ref):
    rows = total.shape[0] // 4
    for i in range(2):
        keep_ref[i] = total[2 * i * rows : (2 * i + 1) * rows]
        send_ref[i] = total[(2 * i + 1) * rows : (2 * i + 2) * rows].astype(BF16)


def part_shapes(rows, width):
    return [shape((2, rows // 4, width), F32), shape((2, rows // 4, width), BF16)]


def softmax_parts(q, k):
    scores = dot_nt(q, k) * SCORE_SCALE
    expo = jnp.exp(scores - jnp.max(scores, -1, keepdims=True))
    return expo / jnp.sum(expo, -1, keepdims=True)


def attention_kernel(n_lat, x_ref, w_ref, qkv_ref, mixed_ref, keep_ref, send_ref):
    x = x_ref[...]
    for j in range(3):
        qkv_ref[j] = dot(x, w_ref[j]).astype(BF16)
    toks = x.shape[0] // n_lat
    heads = w_ref.shape[2] // HEAD_DIM
    for l in range(n_lat):
        rows = slice(l * toks, (l + 1) * toks)
        outs = []
        for h in range(heads):
            cols = slice(h * HEAD_DIM, (h + 1) * HEAD_DIM)
            q, k, v = (qkv_ref[j, rows, cols] for j in range(3))
            outs.append(dot(softmax_parts(q, k).astype(BF16), v))
        mixed_ref[rows, :] = jnp.concatenate(outs, 1).astype(BF16)
    split_rows(dot_nt(mixed_ref[...], w_ref[3]), keep_ref, send_ref)


def attention(x, w, n_lat):
    rows, width = x.shape
    columns = w.shape[2]
    return pl.pallas_call(
        functools.partial(attention_kernel, n_lat),
        out_shape=[shape((3, rows, columns), BF16), shape((rows, columns), BF16)] + part_shapes(rows, width),
        compiler_params=params(32),
        name="attention",
    )(x, w)


def gelu(x):
    return 0.5 * x * (1.0 + jnp.tanh(GELU_C * (x + 0.044715 * x * x * x)))


def gelu_grad(x):
    t = jnp.tanh(GELU_C * (x + 0.044715 * x * x * x))
    return 0.5 * (1.0 + t) + 0.5 * x * (1.0 - t * t) * (GELU_C * (1.0 + 3 * 0.044715 * x * x))


def mlp_kernel(x_ref, w_ref, hidden_ref, active_ref, keep_ref, send_ref):
    x = x_ref[...]
    total = None
    for j in range(4):
        hidden = dot(x, w_ref[j])
        hidden_ref[j] = hidden
        active = gelu(hidden).astype(BF16)
        active_ref[j] = active
        part = dot_nt(active, w_ref[4 + j])
        total = part if total is None else total + part
    split_rows(total, keep_ref, send_ref)


def mlp(x, w):
    rows, width = x.shape
    columns = w.shape[2]
    return pl.pallas_call(
        mlp_kernel,
        out_shape=[shape((4, rows, columns), F32), shape((4, rows, columns), BF16)] + part_shapes(rows, width),
        compiler_params=params(40),
        name="mlp",
    )(x, w)


def mlp_back_kernel(d_ref, hidden_ref, w_ref, dh_ref, keep_ref, send_ref):
    d = d_ref[...]
    total = None
    for j in range(4):
        dh = (gelu_grad(hidden_ref[j]) * dot(d, w_ref[4 + j])).astype(BF16)
        dh_ref[j] = dh
        part = dot_nt(dh, w_ref[j])
        total = part if total is None else total + part
    split_rows(total, keep_ref, send_ref)


def mlp_back(d, hidden, w):
    rows, width = d.shape
    columns = w.shape[2]
    return pl.pallas_call(
        mlp_back_kernel,
        out_shape=[shape((4, rows, columns), BF16)] + part_shapes(rows, width),
        compiler_params=params(40),
        name="mlp_back",
    )(d, hidden, w)


def attention_back_kernel(n_lat, d_ref, qkv_ref, w_ref, dqkv_ref, keep_ref, send_ref):
    d_mixed = dot(d_ref[...], w_ref[3]).astype(BF16)
    toks = d_mixed.shape[0] // n_lat
    heads = w_ref.shape[2] // HEAD_DIM
    for l in range(n_lat):
        rows = slice(l * toks, (l + 1) * toks)
        outs = [[], [], []]
        for h in range(heads):
            cols = slice(h * HEAD_DIM, (h + 1) * HEAD_DIM)
            q, k, v = (qkv_ref[j, rows, cols] for j in range(3))
            do = d_mixed[rows, cols]
            probs = softmax_parts(q, k)
            d_probs = dot_nt(do, v)
            d_scores = probs * (d_probs - jnp.sum(probs * d_probs, -1, keepdims=True))
            d_scores = d_scores.astype(BF16)
            outs[0].append(dot(d_scores, k) * SCORE_SCALE)
            outs[1].append(dot_tn(d_scores, q) * SCORE_SCALE)
            outs[2].append(dot_tn(probs.astype(BF16), do))
        for j in range(3):
            dqkv_ref[j, rows, :] = jnp.concatenate(outs[j], 1).astype(BF16)
    total = dot_nt(dqkv_ref[0], w_ref[0]) + dot_nt(dqkv_ref[1], w_ref[1]) + dot_nt(dqkv_ref[2], w_ref[2])
    split_rows(total, keep_ref, send_ref)


def attention_back(d, qkv, w, n_lat):
    rows, width = d.shape
    columns = w.shape[2]
    return pl.pallas_call(
        functools.partial(attention_back_kernel, n_lat),
        out_shape=[shape((3, rows, columns), BF16)] + part_shapes(rows, width),
        compiler_params=params(40),
        name="attention_back",
    )(d, qkv, w)


def weight_grad_kernel(counts, n_lat, *refs):
    n = len(counts)
    lefts, rights, (out_ref, mean_ref, sum_ref) = refs[:n], refs[n : 2 * n], refs[2 * n :]
    step = pl.program_id(0)
    base = 0
    for k, count in enumerate(counts):

        @pl.when((step >= base) & (step < base + count))
        def _(left=lefts[k], right=rights[k], k=k):
            a, b = left[...], right[0]
            toks = a.shape[0] // n_lat
            means, sums = [], []
            for l in range(n_lat):
                rows = slice(l * toks, (l + 1) * toks)
                means.append(jnp.sum(a[rows].astype(F32), 0, keepdims=True) * (1.0 / toks))
                sums.append(jnp.sum(b[rows].astype(F32), 0, keepdims=True))
            mean = jnp.concatenate(means + [jnp.zeros((8 - n_lat, a.shape[1]), F32)], 0).astype(BF16)
            total = jnp.concatenate(sums + [jnp.zeros((8 - n_lat, b.shape[1]), F32)], 0).astype(BF16)
            mean_ref[k] = mean.astype(F32)
            sum_ref[0] = total.astype(F32)
            out_ref[0] = dot_tn(a, b) - dot_tn(mean, total)

        base += count


def weight_grads(pairs, n_lat):
    counts = [right.shape[0] for _, right in pairs]
    total = sum(counts)
    rows, width = pairs[0][0].shape
    columns = pairs[0][1].shape[2]
    bases = np.cumsum([0] + counts)

    def right_spec(k):
        base, count = int(bases[k]), counts[k]
        return pl.BlockSpec((1, rows, columns), lambda i: (jnp.clip(i - base, 0, count - 1), 0, 0))

    return pl.pallas_call(
        functools.partial(weight_grad_kernel, counts, n_lat),
        grid=(total,),
        in_specs=[pl.BlockSpec((rows, width), lambda i: (0, 0))] * len(pairs)
        + [right_spec(k) for k in range(len(pairs))],
        out_specs=[
            pl.BlockSpec((1, width, columns), lambda i: (i, 0, 0)),
            pl.BlockSpec((len(pairs), 8, width), lambda i: (0, 0, 0)),
            pl.BlockSpec((1, 8, columns), lambda i: (i, 0, 0)),
        ],
        out_shape=[
            shape((total, width, columns), F32),
            shape((len(pairs), 8, width), F32),
            shape((total, 8, columns), F32),
        ],
        compiler_params=params(24, dimension_semantics=("arbitrary",)),
        name="weight_grads",
    )(*[left for left, _ in pairs], *[right for _, right in pairs])


def modulation_kernel(small_ref, cond_ref, bank_ref, out_ref):
    s = pl.program_id(0)

    @pl.when(s == 0)
    def _():
        out_ref[...] = jnp.zeros_like(out_ref)

    unit = small_ref[s]

    @pl.when((unit >= 0) & (unit != TIME_AT))
    def _():
        out_ref[jnp.maximum(unit, 0)] = dot(cond_ref[...], bank_ref[0].astype(BF16))


def modulations(small_slots, cond_in, bank):
    n_slots, rows, columns = bank.shape
    n_all = cond_in.shape[0]
    return pl.pallas_call(
        modulation_kernel,
        grid_spec=pltpu.PrefetchScalarGridSpec(
            num_scalar_prefetch=1,
            grid=(n_slots,),
            in_specs=[
                pl.BlockSpec((n_all, rows), lambda s, t: (0, 0)),
                pl.BlockSpec((1, rows, columns), lambda s, t: (s, 0, 0)),
            ],
            out_specs=pl.BlockSpec((SMALL_ROWS, n_all, columns), lambda s, t: (0, 0, 0)),
        ),
        out_shape=shape((SMALL_ROWS, n_all, columns), F32),
        compiler_params=params(16, dimension_semantics=("arbitrary",)),
        name="modulations",
    )(small_slots, cond_in, bank)


def cond_back_kernel(small_ref, d_ref, bank_ref, out_ref):
    s = pl.program_id(0)

    @pl.when(s == 0)
    def _():
        out_ref[...] = jnp.zeros_like(out_ref)

    unit = small_ref[s]

    @pl.when((unit >= 0) & (unit != TIME_AT))
    def _():
        out_ref[...] += dot_nt(d_ref[jnp.maximum(unit, 0)], bank_ref[0].astype(BF16))


def cond_back(small_slots, d_small, bank):
    n_slots, rows, columns = bank.shape
    n_all = d_small.shape[1]
    return pl.pallas_call(
        cond_back_kernel,
        grid_spec=pltpu.PrefetchScalarGridSpec(
            num_scalar_prefetch=1,
            grid=(n_slots,),
            in_specs=[
                pl.BlockSpec(d_small.shape, lambda s, t: (0, 0, 0)),
                pl.BlockSpec((1, rows, columns), lambda s, t: (s, 0, 0)),
            ],
            out_specs=pl.BlockSpec((n_all, rows), lambda s, t: (0, 0)),
        ),
        out_shape=shape((n_all, rows), F32),
        compiler_params=params(16, dimension_semantics=("arbitrary",)),
        name="cond_back",
    )(small_slots, d_small, bank)


def halves(x):
    high = x.astype(BF16)
    return high, (x - high.astype(F32)).astype(BF16)


def newton_sweep(x):
    xh, xl = halves(x)
    cross = dot_tn(xh, xl)
    gram = dot_tn(xh, xh) + (cross + cross.T)
    gh, gl = halves(gram)
    cross = dot(gh, gl)
    square = dot(gh, gh) + (cross + cross.T)
    ph, pl_ = halves(NS_COEF[1] * gram + NS_COEF[2] * square)
    return NS_COEF[0] * x + (dot(xh, ph) + (dot(xl, ph) + dot(xh, pl_)))


def newton_kernel(n_last, big_ref, left_ref, right_ref, last_ref, a_ref, b_ref, bank_ref, mom_ref, *refs):
    held, got = refs[: len(GROUPS)], refs[len(GROUPS) : len(GROUPS) + n_last]
    new_ref, mom_new_ref, grad, sem = refs[len(GROUPS) + n_last :]
    s = pl.program_id(0)
    unit, left, right = big_ref[s], left_ref[s], right_ref[s]
    half = grad.shape[0] // 2

    @pl.when(right < 0)
    def _():
        new_ref[...] = bank_ref[...]
        mom_new_ref[...] = mom_ref[...]

    @pl.when(right >= 0)
    def _():
        copies = []
        for ref, (low, high) in zip(held, GROUPS):
            inside = (unit >= low) & (unit < high)
            at = jnp.clip(unit - low, 0, high - low - 1)
            copies.append((inside, pltpu.make_async_copy(ref.at[at], grad, sem.at[0])))
        for inside, copy in copies:
            pl.when(inside)(copy.start)
        some = dot_tn(a_ref[jnp.maximum(left, 0)], b_ref[jnp.maximum(right, 0)])
        for inside, copy in copies:
            pl.when(inside)(copy.wait)
        mom_new_ref[0] = 0.5 * mom_ref[0] + some

        @pl.when(unit >= 0)
        def _():
            mom_new_ref[0] += grad[...]
            for i in range(n_last):
                rows = slice((i % 2) * half, (i % 2 + 1) * half)

                @pl.when(last_ref[i] == unit)
                def _(i=i, rows=rows):
                    mom_new_ref[0, rows] += got[i][...].astype(F32)

        block = mom_new_ref[0]
        norm = jnp.sqrt(jnp.sum(block * block)) + 1e-07
        x = block / norm
        for _ in range(5):
            x = newton_sweep(x)
        new_ref[0] = bank_ref[0] - LR_MUON * x


def optimizer(big_slots, left_slots, right_slots, last_units, a_all, b_all, master, momentum, grads, got):
    n_slots, rows, columns = master.shape
    block = pl.BlockSpec((1, rows, columns), lambda s, *t: (s, 0, 0))
    any_spec = pl.BlockSpec(memory_space=pltpu.HBM)
    return pl.pallas_call(
        functools.partial(newton_kernel, len(got)),
        grid_spec=pltpu.PrefetchScalarGridSpec(
            num_scalar_prefetch=4,
            grid=(n_slots,),
            in_specs=[
                pl.BlockSpec(a_all.shape, lambda s, *t: (0, 0, 0)),
                pl.BlockSpec(b_all.shape, lambda s, *t: (0, 0, 0)),
                block,
                block,
            ]
            + [any_spec] * len(grads)
            + [pl.BlockSpec(g.shape, lambda s, *t: (0, 0)) for g in got],
            out_specs=[block, block],
            scratch_shapes=[pltpu.VMEM((rows, columns), F32), pltpu.SemaphoreType.DMA((1,))],
        ),
        out_shape=[shape(master.shape, F32), shape(momentum.shape, F32)],
        compiler_params=params(48, dimension_semantics=("arbitrary",)),
        name="optimizer",
    )(big_slots, left_slots, right_slots, last_units, a_all, b_all, master, momentum, *grads, *got)


def layer_norm(values):
    centered = values - jnp.mean(values, -1, keepdims=True)
    inv_std = lax.rsqrt(jnp.mean(centered * centered, -1, keepdims=True) + 1e-06)
    return centered * inv_std, inv_std


def norm_back(grad_out, normed, inv_std):
    return inv_std * (
        grad_out
        - jnp.mean(grad_out, -1, keepdims=True)
        - normed * jnp.mean(grad_out * normed, -1, keepdims=True)
    )


def position_rows(first, rows):
    quarter = D // 4
    omega = jnp.exp(-math.log(10000.0) * jnp.arange(quarter, dtype=F32) / quarter)
    places = first + jnp.arange(rows, dtype=jnp.int32)
    rows_at = (places // GRID).astype(F32)[:, None] * omega[None]
    cols_at = (places % GRID).astype(F32)[:, None] * omega[None]
    return jnp.concatenate([jnp.sin(rows_at), jnp.cos(rows_at), jnp.sin(cols_at), jnp.cos(cols_at)], 1)


def time_features(timesteps):
    half_freq = FREQ // 2
    rates = jnp.exp(-math.log(10000.0) * jnp.arange(half_freq, dtype=F32) / half_freq)
    angles = timesteps.astype(F32)[:, None] * rates[None]
    return jnp.concatenate([jnp.cos(angles), jnp.sin(angles)], 1)


def shards(
    noisy_latents,
    noise_target,
    timesteps,
    labels,
    owners,
    step_count,
    master_bank,
    momentum_bank,
    embed_tables,
    embed_first,
    embed_second,
):
    n_lat, n_tok, n_patch = noisy_latents.shape
    n_slots, width, columns = master_bank.shape
    n_units = owners.shape[0]
    n_data = lax.axis_size("dp")
    my_data = lax.axis_index("dp")
    my_tensor = lax.axis_index("tensor")
    chip, core = my_tensor // 2, my_tensor % 2
    n_all = n_lat * n_data
    own_rows = n_lat * n_tok // 4
    count_all = float(n_all * n_tok * n_patch)
    depth = 2 if n_data <= 8 else 1
    steps = N_BIG + (n_data - 2) * depth

    unit_order = jnp.arange(n_units, dtype=jnp.int32)
    same_owner = owners[:, None] == owners[None, :]
    slot_of = jnp.sum((same_owner & (unit_order[None, :] < unit_order[:, None])).astype(jnp.int32), 1)
    mine = (owners[None, :] == my_data) & (
        slot_of[None, :] == jnp.arange(n_slots, dtype=jnp.int32)[:, None]
    )

    def of_slot(table):
        return jnp.sum(jnp.where(mine, jnp.asarray(table + 1, jnp.int32)[None], 0), 1) - 1

    big_slots, small_slots = of_slot(BIG_OF), of_slot(SMALL_OF)
    owners_big = jnp.concatenate([owners[18 * l : 18 * l + BIG] for l in range(LAYERS)])
    tab = ring_schedule(owners_big, n_data, steps, depth, my_data)
    spread = Spreader(tab, spread_init(big_slots, master_bank), n_data, steps, depth)
    spread.step()
    ring = Reducer(tab, n_data, steps, depth)

    narrow = embed_tables.astype(BF16)
    first_row = my_tensor * own_rows
    noisy_own = lax.dynamic_slice_in_dim(noisy_latents.reshape(n_lat * n_tok, n_patch), first_row, own_rows, 0)
    target_own = lax.dynamic_slice_in_dim(noise_target.reshape(n_lat * n_tok, n_patch), first_row, own_rows, 0)
    time_mine = owners[18 * LAYERS] == my_data
    time_w2 = lax.dynamic_index_in_dim(master_bank, slot_of[18 * LAYERS], 0, keepdims=False).astype(BF16)

    def ids_of_all():
        ids = jnp.stack([timesteps, labels], 1)[None]
        ids = jnp.where(jnp.arange(n_data)[:, None, None] == my_data, ids, 0)
        return (yield from dp_sum(ids, n_data)).reshape(n_all, 2)

    def conditioning():
        ids, edge_rows = yield from together(
            ids_of_all(),
            gather_columns(
                jnp.concatenate([narrow[:n_patch], narrow[n_patch + FREQ + CLASSES :]], 0), chip, core
            ),
        )
        features = time_features(ids[:, 0]).astype(BF16)
        time_one = jnp.dot(features, narrow[n_patch : n_patch + FREQ], preferred_element_type=F32)
        time_act = yield from gather_columns(jax.nn.silu(time_one).astype(BF16), chip, core)
        second = jnp.dot(time_act, time_w2, preferred_element_type=F32)
        second = yield from dp_sum(jnp.where(time_mine, second, 0.0), n_data)
        onehot = ids[:, 1:2] == jnp.arange(CLASSES, dtype=jnp.int32)[None]
        class_w = narrow[n_patch + FREQ : n_patch + FREQ + CLASSES]
        condition = second + jnp.dot(onehot.astype(BF16), class_w, preferred_element_type=F32)
        cond_in = yield from gather_columns(jax.nn.silu(condition).astype(BF16), chip, core)
        mods = modulations(small_slots, cond_in, master_bank)
        mods = mods.transpose(1, 0, 2).reshape(n_data, n_lat, SMALL_ROWS, columns)
        bit = n_data // 2
        while bit:
            pairs = mods.reshape((2, mods.shape[0] // 2) + mods.shape[1:])
            side = (my_data // bit) % 2
            mods = pick(pairs, 0, side) + (yield flip(pick(pairs, 0, 1 - side), "dp", bit, n_data))
            bit //= 2
        mods = mods[0]
        across = yield x_flip(pick(mods, 0, 1 - chip))
        mine = pick(mods, 0, chip)
        halves_ = jnp.stack([jnp.where(chip == i, mine, across) for i in range(2)], 1)
        beside = yield core_flip(halves_)
        mods = jnp.stack([jnp.where(core == i, halves_, beside) for i in range(2)], 2)
        return edge_rows, features, time_one, time_act, onehot, condition, cond_in, mods.reshape(SMALL_ROWS, width)

    def modulate(values, shift, scale):
        normed, inv_std = layer_norm(values)
        return (normed * (1.0 + scale) + shift).astype(BF16), normed, inv_std

    def forward():
        cond = yield from conditioning()
        edge_rows, mods = cond[0], cond[-1]
        stream = jnp.dot(noisy_own, edge_rows[:n_patch], preferred_element_type=F32) + position_rows(
            first_row % n_tok, own_rows
        )
        kept = []
        for layer in range(LAYERS):
            shift_a, scale_a, gate_a, shift_m, scale_m, gate_m = (
                mods[SMALL * layer + i][None] for i in range(SMALL)
            )
            inner, normed, inv_std = modulate(stream, shift_a, scale_a)
            inner = yield from gather_tokens(inner)
            w_attn = spread.weights(2 * layer)
            qkv, mixed, keep, send = attention(inner, w_attn, n_lat)
            attended = yield from scatter_tokens(keep, send)
            stream_mid = stream + gate_a * attended
            inner_mid, normed_mid, inv_mid = modulate(stream_mid, shift_m, scale_m)
            inner_mid = yield from gather_tokens(inner_mid)
            w_mlp = spread.weights(2 * layer + 1)
            hidden, active, keep, send = mlp(inner_mid, w_mlp)
            branch = yield from scatter_tokens(keep, send)
            stream = stream_mid + gate_m * branch
            kept.append(
                (inner, normed, inv_std, qkv, mixed, attended, inner_mid, normed_mid, inv_mid, hidden, active, branch)
                + (w_attn, w_mlp)
            )
        return cond, kept, stream

    cond, kept, stream = drive(forward(), spread.step)
    edge_rows, features, time_one, time_act, onehot, condition, cond_in, mods = cond
    head_w = edge_rows[n_patch:]

    def backward():
        shift_f, scale_f = mods[FINAL_AT][None], mods[FINAL_AT + 1][None]
        inner_out, normed_out, inv_out = modulate(stream, shift_f, scale_f)
        output = lax.dot_general(inner_out, head_w, (((1,), (1,)), ((), ())), preferred_element_type=F32)
        error_out = output - target_own
        loss_own = jnp.sum(error_out * error_out) / count_all
        d_output = (2.0 * error_out / count_all).astype(BF16)
        d_inner = jnp.dot(d_output, head_w, preferred_element_type=F32)
        d_mods = {FINAL_AT: jnp.sum(d_inner, 0), FINAL_AT + 1: jnp.sum(d_inner * normed_out, 0)}
        grad_flow = norm_back(d_inner * (1.0 + scale_f), normed_out, inv_out)
        lefts, rights = {}, {}
        for layer in reversed(range(LAYERS)):
            (inner, normed, inv_std, qkv, mixed, attended, inner_mid, normed_mid, inv_mid, hidden, active, branch) = (
                kept[layer][:-2]
            )
            w_attn, w_mlp = kept[layer][-2:]
            shift_a, scale_a, gate_a, shift_m, scale_m, gate_m = (
                mods[SMALL * layer + i][None] for i in range(SMALL)
            )
            d_branch = yield from gather_tokens((gate_m * grad_flow).astype(BF16))
            d_gate_m = jnp.sum(grad_flow * branch, 0)
            d_hidden, keep, send = mlp_back(d_branch, hidden, w_mlp)
            back = scatter_tokens(keep, send)
            flying = next(back)
            grads, left, right = weight_grads([(inner_mid, d_hidden), (d_branch, active)], n_lat)
            ring.held[2 * layer + 1] = grads
            lefts[2 * layer + 1], rights[2 * layer + 1] = left, right
            d_inner_mid = yield from resume(back, flying)
            d_shift_m = jnp.sum(d_inner_mid, 0)
            d_scale_m = jnp.sum(d_inner_mid * normed_mid, 0)
            grad_mid = grad_flow + norm_back(d_inner_mid * (1.0 + scale_m), normed_mid, inv_mid)
            d_attended = yield from gather_tokens((gate_a * grad_mid).astype(BF16))
            d_gate_a = jnp.sum(grad_mid * attended, 0)
            d_qkv, keep, send = attention_back(d_attended, qkv, w_attn, n_lat)
            back = scatter_tokens(keep, send)
            flying = next(back)
            grads, left, right = weight_grads([(inner, d_qkv), (d_attended, mixed[None])], n_lat)
            ring.held[2 * layer] = grads
            lefts[2 * layer], rights[2 * layer] = left, right
            d_inner = yield from resume(back, flying)
            d_shift_a = jnp.sum(d_inner, 0)
            d_scale_a = jnp.sum(d_inner * normed, 0)
            grad_flow = grad_mid + norm_back(d_inner * (1.0 + scale_a), normed, inv_std)
            for i, value in enumerate((d_shift_a, d_scale_a, d_gate_a, d_shift_m, d_scale_m, d_gate_m)):
                d_mods[SMALL * layer + i] = value
        (d_small, d_second, grad_class, grad_time_one), edges, packed = yield from together(
            cond_backward(d_mods),
            edge_sums(grad_flow, d_output, inner_out, loss_own),
            factor_rows(lefts, rights),
        )
        return d_small, d_second, grad_class, grad_time_one, edges, packed

    def cond_backward(d_mods):
        d_mods[TIME_AT] = jnp.zeros((width,), F32)
        d_mods[SMALL_ROWS - 1] = jnp.zeros((width,), F32)
        d_small = jnp.stack([d_mods[i] for i in range(SMALL_ROWS)]).reshape(SMALL_ROWS, 2, 2, columns)
        d_small = pick(d_small, 2, core) + (yield core_flip(pick(d_small, 2, 1 - core)))
        near, far = pick(d_small, 1, chip), (yield x_flip(pick(d_small, 1, 1 - chip)))
        d_small = jnp.where(jnp.arange(2)[:, None, None] == chip, near[None], far[None]).astype(BF16)
        d_small = jnp.where(jnp.arange(n_data)[:, None, None, None] == my_data, d_small[None], jnp.zeros((), BF16))
        d_small = (yield from dp_sum(d_small, n_data)).reshape(n_all, SMALL_ROWS, columns).transpose(1, 0, 2)
        d_cond = cond_back(small_slots, d_small, master_bank)
        d_cond = yield from sum_of_columns(d_cond, chip, core, n_data)
        unused, silu_pull = jax.vjp(jax.nn.silu, condition)
        d_condition = silu_pull(d_cond)[0]
        d_second = d_condition.astype(BF16)
        grad_class = lax.dot_general(
            onehot.astype(F32), d_condition, (((0,), (0,)), ((), ())), precision=HIGHEST_PREC
        )
        d_time_act = lax.dot_general(d_second, time_w2, (((1,), (1,)), ((), ())), preferred_element_type=F32)
        d_time_act = jnp.where(time_mine, d_time_act, 0.0)
        d_time_act = yield from sum_of_columns(d_time_act, chip, core, n_data)
        unused, time_pull = jax.vjp(jax.nn.silu, time_one)
        d_time_one = time_pull(d_time_act)[0].astype(BF16)
        grad_time_one = lax.dot_general(
            features, d_time_one, (((0,), (0,)), ((), ())), preferred_element_type=F32
        )
        return d_small, d_second, grad_class, grad_time_one

    def edge_sums(grad_flow, d_output, inner_out, loss_own):
        grad_head = lax.dot_general(d_output, inner_out, (((0,), (0,)), ((), ())), preferred_element_type=F32)
        d_stream = grad_flow.astype(BF16)
        grad_patch = lax.dot_general(noisy_own, d_stream, (((0,), (0,)), ((), ())), preferred_element_type=F32)
        edges = jnp.concatenate([grad_patch, grad_head, jnp.full((1, width), loss_own)], 0)
        return (yield from sum_of_columns(edges, chip, core, n_data))

    def factor_rows(lefts, rights):
        a_rows = [lefts[g][:, :n_lat].transpose(1, 0, 2) for g in range(len(GROUPS))]
        b_rows = [rights[g][:, :n_lat].transpose(1, 0, 2) for g in range(len(GROUPS))]
        a_rows = jnp.concatenate(a_rows, 1).astype(BF16)
        b_rows = jnp.concatenate(b_rows, 1).astype(BF16)
        n_left = a_rows.shape[1]
        packed = jnp.concatenate([a_rows.reshape(n_lat, n_left * 4, columns), b_rows], 1)
        packed = yield from dp_rows(packed, n_data)
        a_rows = packed[:, : n_left * 4].reshape(n_all, n_left, width).transpose(1, 0, 2)
        return a_rows, packed[:, n_left * 4 :].transpose(1, 0, 2)

    d_small, d_second, grad_class, grad_time_one, edges, (a_rows, b_rows) = drive(backward(), ring.step)
    ring.drain()
    loss = edges[2 * n_patch, 0]
    grad_embed = jnp.concatenate(
        [edges[:n_patch], grad_time_one, grad_class, edges[n_patch : 2 * n_patch]], 0
    )
    a_all = jnp.concatenate([cond_in[None], time_act[None], a_rows], 0)
    small_rows = jnp.where(
        jnp.arange(SMALL_ROWS)[:, None, None] == TIME_AT, d_second[None], d_small
    )
    b_all = jnp.concatenate([small_rows, b_rows], 0)
    kind = []
    for g, (low, high) in enumerate(GROUPS):
        split = low + 3 if g % 2 == 0 else low + 4
        kind += [2 + 2 * g + (b >= split) for b in range(low, high)]
    kind_of = np.where(BIG_OF >= 0, np.array(kind)[BIG_OF], np.where(SMALL_OF == TIME_AT, 1, 0))
    right_of = np.where(BIG_OF >= 0, SMALL_ROWS + BIG_OF, SMALL_OF)
    got, last_units = ring.last()
    master_new, momentum_new = optimizer(
        big_slots,
        of_slot(kind_of),
        of_slot(right_of),
        last_units,
        a_all,
        b_all,
        master_bank,
        momentum_bank,
        [ring.held[g] for g in range(len(GROUPS))],
        got,
    )

    first_new = 0.5 * embed_first + 0.5 * grad_embed
    second_new = 0.5 * embed_second + 0.5 * grad_embed * grad_embed
    bias_fix = 1.0 - jnp.power(0.5, step_count[0].astype(F32))
    embed_new = embed_tables * (1.0 - LR_ADAM * WEIGHT_DECAY) - LR_ADAM * (first_new / bias_fix) / (
        jnp.sqrt(second_new / bias_fix) + 1e-08
    )
    return (loss, master_new, momentum_new, embed_new, first_new, second_new)


def solution(mesh):
    placed = (
        P("dp", None, None),
        P("dp", None, None),
        P("dp"),
        P("dp"),
        P(),
        P(),
        P("dp", None, "tensor"),
        P("dp", None, "tensor"),
        P(None, "tensor"),
        P(None, "tensor"),
        P(None, "tensor"),
    )
    return jax.shard_map(
        shards,
        mesh=mesh,
        in_specs=placed,
        out_specs=(
            P(),
            P("dp", None, "tensor"),
            P("dp", None, "tensor"),
            P(None, "tensor"),
            P(None, "tensor"),
            P(None, "tensor"),
        ),
        check_vma=False,
    )
```

```python
import functools
import math

import jax
import jax.numpy as jnp
import numpy as np
from jax import lax
from jax.experimental import pallas as pl
from jax.experimental.pallas import tpu as pltpu
from jax.sharding import PartitionSpec as P

D = 1024
HEAD_DIM = 64
FREQ = 256
CLASSES = 1000
GRID = 16
LAYERS = 2
BIG = 12
N_BIG = BIG * LAYERS
SMALL_ROWS = 16
SHIFT_F, SCALE_F, TIME_AT = 0, 1, 6 * LAYERS + 2


def small_at(layer, i):
    first = 2 + 6 * (LAYERS - 1 - layer)
    return first + (4, 5, 3, 1, 2, 0)[i]


NS_COEF = (3.4445, -4.775, 2.0315)
LR_MUON = 0.5
LR_ADAM = 0.02
WEIGHT_DECAY = 0.1
SCORE_SCALE = 1.0 / math.sqrt(HEAD_DIM)
HIGHEST_PREC = lax.Precision.HIGHEST

F32 = jnp.float32
BF16 = jnp.bfloat16
RING_VMEM = 16
RING_COST = pl.CostEstimate(flops=0, transcendentals=0, bytes_accessed=2**21)
GELU_C = math.sqrt(2.0 / math.pi)
GROUPS = ((0, 4), (4, 12), (12, 16), (16, 24))


def unit_tables():
    big, small = [], []
    for u in range(18 * LAYERS):
        layer, place = divmod(u, 18)
        big.append(layer * BIG + place if place < BIG else -1)
        small.append(-1 if place < BIG else small_at(layer, place - BIG))
    return np.array(big + [-1] * 3), np.array(small + [TIME_AT, SHIFT_F, SCALE_F])


BIG_OF, SMALL_OF = unit_tables()


def params(limit, **more):
    return pltpu.CompilerParams(vmem_limit_bytes=limit * 1024 * 1024, **more)


SMEM_SPEC = pl.BlockSpec(memory_space=pltpu.SMEM)
VMEM_SPEC = pl.BlockSpec(memory_space=pltpu.VMEM)


def in_hbm(values):
    return pltpu.with_memory_space_constraint(values, pltpu.HBM)


def dot(a, b):
    return lax.dot_general(a, b, (((1,), (0,)), ((), ())), preferred_element_type=F32)


def dot_nt(a, b):
    return lax.dot_general(a, b, (((1,), (1,)), ((), ())), preferred_element_type=F32)


def dot_tn(a, b):
    return lax.dot_general(a, b, (((0,), (0,)), ((), ())), preferred_element_type=F32)


def shape(dims, kind):
    return jax.ShapeDtypeStruct(dims, kind)


ISSUED = []


def order(values, after):
    if not after:
        return values
    flat, tree = jax.tree.flatten(values)
    tied = lax.optimization_barrier(tuple(flat) + tuple(after))
    return jax.tree.unflatten(tree, tied[: len(flat)])


def drive(work, line):
    ISSUED.clear()
    try:
        value = next(work)
        while True:
            after = tuple(ISSUED)
            ISSUED.clear()
            value = work.send(order(value, line(after)))
    except StopIteration as end:
        return end.value


def together(*works):
    ends, flying = [None] * len(works), {}

    def go(i, step):
        try:
            flying[i] = step()
        except StopIteration as end:
            flying.pop(i, None)
            ends[i] = end.value

    for i, work in enumerate(works):
        go(i, lambda: next(work))
    while flying:
        got = yield dict(flying)
        for i in list(got):
            go(i, lambda: works[i].send(got[i]))
    return ends


def resume(work, value):
    try:
        while True:
            value = work.send((yield value))
    except StopIteration as end:
        return end.value


def flip(values, axis, bit, size):
    ISSUED.append(values)
    return lax.ppermute(values, axis, [(i, i ^ bit) for i in range(size)])


def is_at(flag, value, ndim):
    return flag.reshape((1,) * ndim) == value


def pick(low, high, place, other=False):
    return jnp.where(is_at(place, 1 if other else 0, low.ndim), low, high)


def own_latents(values, axis, data, n_data):
    n_lat = values.shape[axis]
    dims = values.shape[:axis] + (n_lat * n_data,) + values.shape[axis + 1 :]
    at = lax.broadcasted_iota(jnp.int32, dims, axis)
    first = data.reshape((1,) * len(dims)) * n_lat
    placed = jnp.zeros(dims, values.dtype)
    for l in range(n_lat):
        placed = jnp.where(at == first + l, lax.slice_in_dim(values, l, l + 1, axis=axis), placed)
    return placed


def dp_sum(values, n_data):
    bit = 1
    while bit < n_data:
        values = values + (yield flip(values, "dp", bit, n_data))
        bit *= 2
    return values


def dp_rows(values, n_data):
    bit = 1
    while bit < n_data:
        values = jnp.concatenate([values, (yield flip(values, "dp", bit, n_data))], 0)
        bit *= 2
    return values


def core_flip(values):
    return flip(values, "tensor", 1, 4)


def x_flip(values):
    return flip(values, "tensor", 2, 4)


def gather_tokens(own):
    beside, across = yield (core_flip(own), x_flip(own))
    corner = yield core_flip(across)
    return own, beside, across, corner


def gather_columns(own, chip, core):
    beside, across = yield (core_flip(own), x_flip(own))
    corner = yield core_flip(across)
    at_core = [is_at(core, i, own.ndim) for i in range(2)]
    at_chip = [is_at(chip, i, own.ndim) for i in range(2)]
    near = [jnp.where(at_core[i], own, beside) for i in range(2)]
    far = [jnp.where(at_core[i], across, corner) for i in range(2)]
    parts = [jnp.where(at_chip[i], near[j], far[j]) for i in range(2) for j in range(2)]
    return jnp.concatenate(parts, -1)


def scatter_tokens(keep, send):
    got = yield core_flip(send)
    far = (keep[1] + got[1].astype(F32)).astype(BF16)
    return keep, got, (yield x_flip(far))


def core_columns(values, core, other=False):
    size = values.shape[-1] // 4
    block = [lax.slice_in_dim(values, j * size, (j + 1) * size, axis=values.ndim - 1) for j in range(4)]
    return [pick(block[2 * x], block[2 * x + 1], core, other) for x in range(2)]


def core_columns_sum(values, core):
    got = yield core_flip(jnp.concatenate(core_columns(values, core, True), -1))
    size = got.shape[-1] // 2
    return [
        mine + lax.slice_in_dim(got, x * size, (x + 1) * size, axis=got.ndim - 1)
        for x, mine in enumerate(core_columns(values, core))
    ]


def own_columns_sum(values, chip, core):
    mine = yield from core_columns_sum(values, core)
    return pick(*mine, chip) + (yield x_flip(pick(*mine, chip, True)))


def sum_of_columns(values, chip, core, n_data):
    return (yield from dp_sum((yield from own_columns_sum(values, chip, core)), n_data))


def ring_order(n_data):
    return [0, 2, 4, 6, 7, 5, 3, 1] if n_data == 8 else list(range(n_data))


def sched_kernel(steps, depth, n_data, place_ref, own_ref, next_ref, out_ref):
    lane = lax.broadcasted_iota(jnp.int32, (n_data, 128), 1)
    row = lax.broadcasted_iota(jnp.int32, (n_data, 128), 0)
    far = jnp.int32(999)
    out_lane = lax.broadcasted_iota(jnp.int32, (1, 128), 1)

    def step(t, carry):
        line = jnp.full((1, 128), -1, jnp.int32)
        after = []
        for way in range(2):
            have, sent, *coming = carry[way]
            place = place_ref[way]
            before = jnp.where(place == 0, n_data - 1, place - 1)
            open_now = have * (1 - sent) * (1 - next_ref[way])
            first = jnp.min(jnp.where(open_now > 0, lane, far), axis=1, keepdims=True)
            chosen = (lane == first).astype(jnp.int32)
            first = jnp.broadcast_to(first, (n_data, 128))
            for k, who in enumerate((place, before)):
                index = jnp.min(jnp.where(row == who, first, far), axis=0, keepdims=True)
                index = jnp.where(index == far, -1, index)
                line = jnp.where(out_lane == 2 * way + k, index, line)
            coming = list(coming) + [pltpu.roll(chosen, 1, 0)]
            after.append((have + coming[0], sent + chosen, *coming[1:]))
        out_ref[pl.ds(t, 1), :] = line
        return tuple(after)

    none = jnp.zeros((n_data, 128), jnp.int32)
    lax.fori_loop(0, steps, step, tuple((own_ref[way], none) + (none,) * (depth - 1) for way in range(2)))


def ring_schedule(owners_big, n_data, steps, depth, my_data):
    order = np.array(ring_order(n_data))
    place_of = np.argsort(order)
    place = jnp.sum(jnp.where(jnp.arange(n_data) == my_data, place_of, 0)).astype(jnp.int32)
    at = jnp.arange(n_data)[:, None]
    owner_place = jnp.sum(jnp.where(owners_big[:, None] == jnp.arange(n_data)[None], place_of[None], 0), 1)
    owner_place = jnp.concatenate([owner_place, jnp.full((128 - N_BIG,), -9, owner_place.dtype)])[None]
    back_place = jnp.where(owner_place >= 0, n_data - 1 - owner_place, -9)
    own = jnp.stack([at == owner_place, at == back_place]).astype(jnp.int32)
    follow = (at + 1) % n_data
    nxt = jnp.stack([follow == owner_place, follow == back_place]).astype(jnp.int32)
    out = pl.pallas_call(
        functools.partial(sched_kernel, steps, depth, n_data),
        out_shape=shape((steps, 128), jnp.int32),
        in_specs=[
            pl.BlockSpec(memory_space=pltpu.SMEM),
            pl.BlockSpec(memory_space=pltpu.VMEM),
            pl.BlockSpec(memory_space=pltpu.VMEM),
        ],
        out_specs=pl.BlockSpec(memory_space=pltpu.VMEM),
        name="ring_schedule",
    )(jnp.stack([place, n_data - 1 - place]), own, nxt)
    return out[:, :4]


def spread_init_kernel(slots_ref, bank_ref, out_ref, wide, sem):
    big_ref = [slots_ref[0, s] for s in range(bank_ref.shape[0])]
    n_slots = bank_ref.shape[0]
    for s in range(n_slots):
        copy = pltpu.make_async_copy(bank_ref.at[s], wide.at[s], sem.at[s])
        pl.when(big_ref[s] >= 0)(copy.start)
    for s in range(n_slots):
        copy = pltpu.make_async_copy(bank_ref.at[s], wide.at[s], sem.at[s])
        pl.when(big_ref[s] >= 0)(copy.wait)

        @pl.when(big_ref[s] >= 0)
        def _(s=s):
            out_ref[jnp.maximum(big_ref[s], 0)] = wide[s].astype(BF16)


def spread_init(big_slots, master_bank):
    n_slots, rows, columns = master_bank.shape
    return pl.pallas_call(
        spread_init_kernel,
        out_shape=pltpu.VMEM((N_BIG + BIG, rows, columns), BF16),
        in_specs=[SMEM_SPEC, pl.BlockSpec(memory_space=pltpu.HBM)],
        out_specs=VMEM_SPEC,
        scratch_shapes=[
            pltpu.VMEM((n_slots, rows, columns), F32),
            pltpu.SemaphoreType.DMA((n_slots,)),
        ],
        compiler_params=params(16),
        name="own_weights",
    )(big_slots, in_hbm(master_bank))


def spread_kernel(places, fetch_at, tab_ref, *refs):
    refs = list(refs)
    got = [[refs.pop(0) for _ in range(2)] for _ in places]
    held, out = refs[1], refs[2:]
    half = held.shape[1] // 2
    for way in range(2):
        rows = pl.ds(way * half, half)
        for k, t in enumerate(places):
            unit = tab_ref[t, 2 * way + 1]

            @pl.when(unit >= 0)
            def _():
                held[jnp.maximum(unit, 0), rows] = got[k][way][...]

        if fetch_at is not None:
            out[way][...] = held[jnp.maximum(tab_ref[fetch_at, 2 * way], 0), rows]


def spread_step(tab, held, got, places, fetch_at):
    rows, columns = held.shape[1:]
    sends = [pltpu.VMEM((rows // 2, columns), BF16)] * 2 if fetch_at is not None else []
    res = pl.pallas_call(
        functools.partial(spread_kernel, places, fetch_at),
        out_shape=[pltpu.VMEM(held.shape, held.dtype)] + sends,
        in_specs=[SMEM_SPEC] + [VMEM_SPEC] * (len(got) + 1),
        out_specs=[VMEM_SPEC] * (1 + len(sends)),
        input_output_aliases={1 + len(got): 0},
        compiler_params=params(RING_VMEM),
        cost_estimate=RING_COST,
        name="spread_step",
    )(tab, *got, held)
    return res[0], list(res[1:])


def ring_perms(n_data):
    order = ring_order(n_data)
    ahead = [(order[i], order[(i + 1) % n_data]) for i in range(n_data)]
    return ahead, [(b, a) for a, b in ahead]


class Spreader:
    def __init__(self, tab, held, n_data, steps, depth):
        self.tab, self.n_data, self.steps, self.depth = tab, n_data, steps, depth
        self.perms = ring_perms(n_data)
        self.held = held
        self.got = {}
        self.at = 0

    def last(self, g):
        return GROUPS[g][1] - 1 + (self.n_data - 2) * self.depth

    def step(self, after=()):
        t = self.at
        if t > self.steps:
            return ()
        fetch_at = t if t < self.steps else None
        places = [t - self.depth] if fetch_at is not None else list(range(self.steps - self.depth, self.steps))
        places = [p for p in places if p >= 0]
        self.held, sends = spread_step(
            order(self.tab, after), self.held, [value for p in places for value in self.got.pop(p)], places, fetch_at
        )
        if sends:
            self.got[t] = [lax.ppermute(sends[way], "dp", self.perms[way]) for way in range(2)]
        self.at += 1
        return tuple(sends)

    def weights(self, g, after=()):
        while self.at <= min(self.last(g) + self.depth, self.steps):
            self.step(after)
            after = ()
        return self.held


def reduce_kernel(place_at, fetch_at, tab_ref, *refs):
    got, (held, *out) = refs[:2], refs[-3:]
    half = held.shape[1] // 2
    for way in range(2):
        rows = pl.ds(way * half, half)
        if place_at is not None:
            unit = tab_ref[place_at, 2 * way]

            @pl.when(unit >= 0)
            def _():
                at = BIG + jnp.maximum(unit, 0)
                held[at, rows] = (held[at, rows].astype(F32) + got[way][...].astype(F32)).astype(BF16)

        out[way][...] = held[BIG + jnp.maximum(tab_ref[fetch_at, 2 * way + 1], 0), rows]


def reduce_step(tab, held, got, place_at, fetch_at):
    rows, columns = held.shape[1:]
    lead = list(got) if place_at is not None else []
    res = pl.pallas_call(
        functools.partial(reduce_kernel, place_at, fetch_at),
        out_shape=[pltpu.VMEM(held.shape, held.dtype)] + [pltpu.VMEM((rows // 2, columns), BF16)] * 2,
        in_specs=[SMEM_SPEC] + [VMEM_SPEC] * (len(lead) + 1),
        out_specs=[VMEM_SPEC] * 3,
        input_output_aliases={1 + len(lead): 0},
        compiler_params=params(RING_VMEM),
        cost_estimate=RING_COST,
        name="reduce_step",
    )(tab, *lead, held)
    return res[0], list(res[1:])


class Reducer:
    def __init__(self, tab, n_data, steps, depth):
        self.tab, self.n_data, self.steps, self.depth = tab, n_data, steps, depth
        self.perms = [p for p in reversed(ring_perms(n_data))]
        self.held = None
        self.ready = N_BIG
        self.got = {}
        self.at = 0

    def lowest(self, k):
        return (self.steps - 1 - k) - (self.n_data - 2) * self.depth

    def step(self, after=()):
        k = self.at
        if k < self.steps and max(self.lowest(k), 0) >= self.ready:
            place_at = self.steps - 1 - (k - self.depth) if k >= self.depth else None
            self.held, sends = reduce_step(
                order(self.tab, after), self.held, self.got.get(k - self.depth), place_at, self.steps - 1 - k
            )
            self.got[k] = [lax.ppermute(sends[way], "dp", self.perms[way]) for way in range(2)]
            self.at += 1
            return tuple(sends)
        return ()

    def drain(self):
        while self.at < self.steps:
            self.step()

    def last(self):
        return [self.got[self.steps - 1 - t][way] for t in range(self.depth) for way in range(2)]


def past(kernel, operands, beside):
    n, m = len(operands), len(beside)
    return lambda *refs: kernel(*refs[:n], *refs[n + m :])


def split_rows(total, keep_ref, send_ref):
    rows = total.shape[0] // 4
    for i in range(2):
        keep_ref[i] = total[2 * i * rows : (2 * i + 1) * rows]
        send_ref[i] = total[(2 * i + 1) * rows : (2 * i + 2) * rows].astype(BF16)


def part_shapes(rows, width):
    return [shape((2, rows // 4, width), F32), shape((2, rows // 4, width), BF16)]


def joined(refs):
    return jnp.concatenate([r[...] for r in refs], 0)


def softmax_parts(q, k):
    scores = dot_nt(q, k) * SCORE_SCALE
    expo = jnp.exp(scores - jnp.max(scores, -1, keepdims=True))
    return expo / jnp.sum(expo, -1, keepdims=True)


def attention_kernel(n_lat, base, x0, x1, x2, x3, w_ref, qkv_ref, mixed_ref, keep_ref, send_ref):
    x = joined((x0, x1, x2, x3))
    for j in range(3):
        qkv_ref[j] = dot(x, w_ref[base + j]).astype(BF16)
    toks = x.shape[0] // n_lat
    heads = w_ref.shape[2] // HEAD_DIM
    for l in range(n_lat):
        rows = slice(l * toks, (l + 1) * toks)
        outs = []
        for h in range(heads):
            cols = slice(h * HEAD_DIM, (h + 1) * HEAD_DIM)
            q, k, v = (qkv_ref[j, rows, cols] for j in range(3))
            outs.append(dot(softmax_parts(q, k).astype(BF16), v))
        mixed_ref[rows, :] = jnp.concatenate(outs, 1).astype(BF16)
    split_rows(dot_nt(mixed_ref[...], w_ref[base + 3]), keep_ref, send_ref)


def attention(x, w, base, n_lat):
    rows, width = 4 * x[0].shape[0], x[0].shape[1]
    columns = w.shape[2]
    return pl.pallas_call(
        functools.partial(attention_kernel, n_lat, base),
        out_shape=[shape((3, rows, columns), BF16), shape((rows, columns), BF16)] + part_shapes(rows, width),
        compiler_params=params(16),
        name="attention",
    )(*x, w)


def gelu(x):
    return 0.5 * x * (1.0 + jnp.tanh(GELU_C * (x + 0.044715 * x * x * x)))


def gelu_grad(x):
    t = jnp.tanh(GELU_C * (x + 0.044715 * x * x * x))
    return 0.5 * (1.0 + t) + 0.5 * x * (1.0 - t * t) * (GELU_C * (1.0 + 3 * 0.044715 * x * x))


def mlp_kernel(base, x0, x1, x2, x3, w_ref, hidden_ref, active_ref, keep_ref, send_ref):
    x = joined((x0, x1, x2, x3))
    total = None
    for j in range(4):
        hidden = dot(x, w_ref[base + j])
        hidden_ref[j] = hidden
        active = gelu(hidden).astype(BF16)
        active_ref[j] = active
        part = dot_nt(active, w_ref[base + 4 + j])
        total = part if total is None else total + part
    split_rows(total, keep_ref, send_ref)


def mlp(x, w, base):
    rows, width = 4 * x[0].shape[0], x[0].shape[1]
    columns = w.shape[2]
    return pl.pallas_call(
        functools.partial(mlp_kernel, base),
        out_shape=[shape((4, rows, columns), F32), shape((4, rows, columns), BF16)] + part_shapes(rows, width),
        compiler_params=params(16),
        name="mlp",
    )(*x, w)


def mlp_back_kernel(base, d0, d1, d2, d3, hidden_ref, w_ref, dh_ref, keep_ref, send_ref):
    d = joined((d0, d1, d2, d3))
    total = None
    for j in range(4):
        dh = (gelu_grad(hidden_ref[j]) * dot(d, w_ref[base + 4 + j])).astype(BF16)
        dh_ref[j] = dh
        part = dot_nt(dh, w_ref[base + j])
        total = part if total is None else total + part
    split_rows(total, keep_ref, send_ref)


def mlp_back(d, hidden, w, base):
    rows, width = 4 * d[0].shape[0], d[0].shape[1]
    columns = w.shape[2]
    operands = (*d, hidden, w)
    return pl.pallas_call(
        functools.partial(mlp_back_kernel, base),
        out_shape=[shape((4, rows, columns), BF16)] + part_shapes(rows, width),
        compiler_params=params(16),
        name="mlp_back",
    )(*operands)


def attention_back_kernel(n_lat, base, d0, d1, d2, d3, qkv_ref, w_ref, dqkv_ref, keep_ref, send_ref):
    d_mixed = dot(joined((d0, d1, d2, d3)), w_ref[base + 3]).astype(BF16)
    toks = d_mixed.shape[0] // n_lat
    heads = w_ref.shape[2] // HEAD_DIM
    for l in range(n_lat):
        rows = slice(l * toks, (l + 1) * toks)
        outs = [[], [], []]
        for h in range(heads):
            cols = slice(h * HEAD_DIM, (h + 1) * HEAD_DIM)
            q, k, v = (qkv_ref[j, rows, cols] for j in range(3))
            do = d_mixed[rows, cols]
            probs = softmax_parts(q, k)
            d_probs = dot_nt(do, v)
            d_scores = probs * (d_probs - jnp.sum(probs * d_probs, -1, keepdims=True))
            d_scores = d_scores.astype(BF16)
            outs[0].append(dot(d_scores, k) * SCORE_SCALE)
            outs[1].append(dot_tn(d_scores, q) * SCORE_SCALE)
            outs[2].append(dot_tn(probs.astype(BF16), do))
        for j in range(3):
            dqkv_ref[j, rows, :] = jnp.concatenate(outs[j], 1).astype(BF16)
    total = sum(dot_nt(dqkv_ref[j], w_ref[base + j]) for j in range(3))
    split_rows(total, keep_ref, send_ref)


def attention_back(d, qkv, w, base, n_lat):
    rows, width = 4 * d[0].shape[0], d[0].shape[1]
    columns = w.shape[2]
    operands = (*d, qkv, w)
    return pl.pallas_call(
        functools.partial(attention_back_kernel, n_lat, base),
        out_shape=[shape((3, rows, columns), BF16)] + part_shapes(rows, width),
        compiler_params=params(16),
        name="attention_back",
    )(*operands)


def weight_grad_kernel(counts, n_lat, base, *refs):
    n = len(counts)
    lefts, rights, (out_ref, mean_ref, sum_ref) = refs[: 4 * n], refs[4 * n : 5 * n], refs[-3:]
    at = 0
    for k, count in enumerate(counts):
        a = joined(lefts[4 * k : 4 * k + 4])
        toks = a.shape[0] // n_lat

        def rows_of(x, scale):
            parts = [
                jnp.sum(x[l * toks : (l + 1) * toks].astype(F32), 0, keepdims=True) * scale for l in range(n_lat)
            ]
            return jnp.concatenate(parts + [jnp.zeros((8 - n_lat, x.shape[1]), F32)], 0).astype(BF16)

        mean = rows_of(a, 1.0 / toks)
        mean_ref[k] = mean.astype(F32)
        for j in range(count):
            b = rights[k][j]
            total = rows_of(b, 1.0)
            sum_ref[at] = total.astype(F32)
            out_ref[BIG + base + at] = (dot_tn(a, b) - dot_tn(mean, total)).astype(BF16)
            at += 1


def weight_grads(held, base, pairs, n_lat):
    counts = [right.shape[0] for _, right in pairs]
    total = sum(counts)
    width = pairs[0][0][0].shape[1]
    columns = pairs[0][1].shape[2]
    operands = [part for left, _ in pairs for part in left] + [right for _, right in pairs]
    aliases = {len(operands): 0}
    operands.append(held)
    return pl.pallas_call(
        functools.partial(weight_grad_kernel, counts, n_lat, base),
        out_shape=[
            pltpu.VMEM(held.shape, BF16),
            shape((len(pairs), 8, width), F32),
            shape((total, 8, columns), F32),
        ],
        in_specs=[VMEM_SPEC] * len(operands),
        out_specs=[VMEM_SPEC] * 3,
        input_output_aliases=aliases,
        compiler_params=params(16),
        name="weight_grads",
    )(*operands)


def modulation_kernel(small_ref, cond_ref, bank_ref, out_ref):
    s = pl.program_id(0)

    @pl.when(s == 0)
    def _():
        out_ref[...] = jnp.zeros_like(out_ref)

    unit = small_ref[s]

    @pl.when((unit >= 0) & (unit != TIME_AT))
    def _():
        out_ref[jnp.maximum(unit, 0)] = dot(cond_ref[...], bank_ref[0].astype(BF16))


def modulations(small_slots, cond_in, bank):
    n_slots, rows, columns = bank.shape
    n_all = cond_in.shape[0]
    return pl.pallas_call(
        modulation_kernel,
        grid_spec=pltpu.PrefetchScalarGridSpec(
            num_scalar_prefetch=1,
            grid=(n_slots,),
            in_specs=[
                pl.BlockSpec((n_all, rows), lambda s, t: (0, 0)),
                pl.BlockSpec((1, rows, columns), lambda s, t: (s, 0, 0)),
            ],
            out_specs=pl.BlockSpec((SMALL_ROWS, n_all, columns), lambda s, t: (0, 0, 0)),
        ),
        out_shape=shape((SMALL_ROWS, n_all, columns), F32),
        compiler_params=params(16, dimension_semantics=("arbitrary",)),
        name="modulations",
    )(small_slots, cond_in, in_hbm(bank))


def cond_back_kernel(small_ref, d_ref, bank_ref, out_ref):
    s = pl.program_id(0)

    @pl.when(s == 0)
    def _():
        out_ref[...] = jnp.zeros_like(out_ref)

    unit = small_ref[s]

    @pl.when((unit >= 0) & (unit != TIME_AT))
    def _():
        out_ref[...] += dot_nt(d_ref[jnp.maximum(unit, 0)], bank_ref[0].astype(BF16))


def cond_back(small_slots, d_small, bank):
    n_slots, rows, columns = bank.shape
    n_all = d_small.shape[1]
    return pl.pallas_call(
        cond_back_kernel,
        grid_spec=pltpu.PrefetchScalarGridSpec(
            num_scalar_prefetch=1,
            grid=(n_slots,),
            in_specs=[
                pl.BlockSpec(d_small.shape, lambda s, t: (0, 0, 0)),
                pl.BlockSpec((1, rows, columns), lambda s, t: (s, 0, 0)),
            ],
            out_specs=pl.BlockSpec((n_all, rows), lambda s, t: (0, 0)),
        ),
        out_shape=shape((n_all, rows), F32),
        compiler_params=params(16, dimension_semantics=("arbitrary",)),
        name="cond_back",
    )(small_slots, d_small, in_hbm(bank))


def halves(x):
    high = x.astype(BF16)
    return high, (x - high.astype(F32)).astype(BF16)


def newton_sweep(x):
    xh, xl = halves(x)
    cross = dot_tn(xh, xl)
    gram = dot_tn(xh, xh) + (cross + cross.T)
    gh, gl = halves(gram)
    cross = dot(gh, gl)
    square = dot(gh, gh) + (cross + cross.T)
    ph, pl_ = halves(NS_COEF[1] * gram + NS_COEF[2] * square)
    return NS_COEF[0] * x + (dot(xh, ph) + (dot(xl, ph) + dot(xh, pl_)))


def newton_kernel(n_last, big_ref, left_ref, right_ref, tab_ref, a_ref, b_ref, bank_ref, mom_ref, *refs):
    held, got = refs[0], refs[1 : 1 + n_last]
    new_ref, mom_new_ref, grad, sem = refs[1 + n_last :]
    s = pl.program_id(0)
    unit, left, right = big_ref[s], left_ref[s], right_ref[s]
    half = got[0].shape[0]

    @pl.when(right < 0)
    def _():
        new_ref[...] = bank_ref[...]
        mom_new_ref[...] = mom_ref[...]

    @pl.when(right >= 0)
    def _():
        copy = pltpu.make_async_copy(held.at[BIG + jnp.maximum(unit, 0)], grad, sem.at[0])
        pl.when(unit >= 0)(copy.start)
        mom_new_ref[0] = 0.5 * mom_ref[0] + dot_tn(
            a_ref[jnp.maximum(left, 0)], b_ref[jnp.maximum(right, 0)]
        )
        pl.when(unit >= 0)(copy.wait)

        @pl.when(unit >= 0)
        def _():
            mom_new_ref[0] += grad[...].astype(F32)

        for i in range(n_last):
            rows = slice((i % 2) * half, (i % 2 + 1) * half)

            @pl.when((tab_ref[i // 2, 2 * (i % 2)] == unit) & (unit >= 0))
            def _(i=i, rows=rows):
                mom_new_ref[0, rows] += got[i][...].astype(F32)

        block = mom_new_ref[0]
        norm = jnp.sqrt(jnp.sum(block * block)) + 1e-07
        x = block / norm
        for _ in range(5):
            x = newton_sweep(x)
        new_ref[0] = bank_ref[0] - LR_MUON * x


def optimizer(big_slots, left_slots, right_slots, tab, a_all, b_all, master, momentum, held, got):
    n_slots, rows, columns = master.shape
    block = pl.BlockSpec((1, rows, columns), lambda s, *t: (s, 0, 0))
    return pl.pallas_call(
        functools.partial(newton_kernel, len(got)),
        grid_spec=pltpu.PrefetchScalarGridSpec(
            num_scalar_prefetch=4,
            grid=(n_slots,),
            in_specs=[
                pl.BlockSpec(a_all.shape, lambda s, *t: (0, 0, 0)),
                pl.BlockSpec(b_all.shape, lambda s, *t: (0, 0, 0)),
                block,
                block,
            ]
            + [pl.BlockSpec(memory_space=pl.ANY)]
            + [pl.BlockSpec(g.shape, lambda s, *t: (0, 0)) for g in got],
            out_specs=[block, block],
            scratch_shapes=[pltpu.VMEM((rows, columns), BF16), pltpu.SemaphoreType.DMA((1,))],
        ),
        out_shape=[shape(master.shape, F32), shape(momentum.shape, F32)],
        compiler_params=params(16, dimension_semantics=("arbitrary",)),
        name="optimizer",
    )(big_slots, left_slots, right_slots, tab, a_all, b_all, in_hbm(master), in_hbm(momentum), held, *got)


def layer_norm(values):
    centered = values - jnp.mean(values, -1, keepdims=True)
    inv_std = lax.rsqrt(jnp.mean(centered * centered, -1, keepdims=True) + 1e-06)
    return centered * inv_std, inv_std


def norm_back(grad_out, normed, inv_std):
    return inv_std * (
        grad_out
        - jnp.mean(grad_out, -1, keepdims=True)
        - normed * jnp.mean(grad_out * normed, -1, keepdims=True)
    )


def added(keep_ref, got_ref, far_ref):
    return keep_ref[0] + got_ref[0].astype(F32) + far_ref[...].astype(F32)


def row_of(mods_ref, at):
    return mods_ref[at : at + 1, :]


def enter_kernel(at, noisy_ref, patch_ref, place_ref, mods_ref, stream_ref, inner_ref, normed_ref, inv_ref):
    stream = dot(noisy_ref[...], patch_ref[...]) + place_ref[...]
    stream_ref[...] = stream
    normed, inv = layer_norm(stream)
    inner_ref[...] = (normed * (1.0 + row_of(mods_ref, at[1])) + row_of(mods_ref, at[0])).astype(BF16)
    normed_ref[...] = normed
    inv_ref[...] = jnp.broadcast_to(inv, inv_ref.shape)


def enter(noisy, patch, places, mods, at):
    rows, width = places.shape
    full = shape((rows, width), F32)
    return pl.pallas_call(
        functools.partial(enter_kernel, at),
        out_shape=[full, shape((rows, width), BF16), full, shape((rows, 128), F32)],
        compiler_params=params(16),
        name="enter",
    )(noisy, patch, places, mods)


def residual_kernel(
    at, keep_ref, got_ref, far_ref, stream_ref, mods_ref, part_ref, next_ref, inner_ref, normed_ref, inv_ref
):
    part = added(keep_ref, got_ref, far_ref)
    part_ref[...] = part
    stream = stream_ref[...] + row_of(mods_ref, at[0]) * part
    next_ref[...] = stream
    normed, inv = layer_norm(stream)
    inner_ref[...] = (normed * (1.0 + row_of(mods_ref, at[2])) + row_of(mods_ref, at[1])).astype(BF16)
    normed_ref[...] = normed
    inv_ref[...] = jnp.broadcast_to(inv, inv_ref.shape)


def residual(parts, stream, mods, at):
    rows, width = stream.shape
    full = shape((rows, width), F32)
    return pl.pallas_call(
        functools.partial(residual_kernel, at),
        out_shape=[full, full, shape((rows, width), BF16), full, shape((rows, 128), F32)],
        compiler_params=params(16),
        name="residual",
    )(*parts, stream, mods)


def leave_kernel(
    at,
    count_all,
    keep_ref,
    got_ref,
    far_ref,
    stream_ref,
    mods_ref,
    head_ref,
    target_ref,
    grad_ref,
    next_ref,
    rows_ref,
    edge_ref,
):
    branch = added(keep_ref, got_ref, far_ref)
    gate, shift, scale = (row_of(mods_ref, i) for i in at)
    normed, inv = layer_norm(stream_ref[...] + gate * branch)
    inner = (normed * (1.0 + scale) + shift).astype(BF16)
    head = head_ref[...]
    error = dot_nt(inner, head) - target_ref[...]
    d_output = (2.0 * error / count_all).astype(BF16)
    d_inner = dot(d_output, head)
    grad = norm_back(d_inner * (1.0 + scale), normed, inv)
    grad_ref[...] = grad
    next_ref[...] = (gate * grad).astype(BF16)
    rows_ref[...] = jnp.zeros_like(rows_ref)
    rows_ref[0:1, :] = jnp.sum(d_inner, 0, keepdims=True)
    rows_ref[1:2, :] = jnp.sum(d_inner * normed, 0, keepdims=True)
    rows_ref[2:3, :] = jnp.sum(grad * branch, 0, keepdims=True)
    n_patch = head.shape[0]
    loss = jnp.sum(jnp.sum(error * error, 1, keepdims=True), 0, keepdims=True) / count_all
    edge_ref[:n_patch, :] = dot_tn(d_output, inner)
    edge_ref[n_patch:, :] = jnp.broadcast_to(loss, (8, edge_ref.shape[1]))


def leave(parts, stream, mods, head, target, at, count_all):
    rows, width = stream.shape
    return pl.pallas_call(
        functools.partial(leave_kernel, at, count_all),
        out_shape=[
            shape((rows, width), F32),
            shape((rows, width), BF16),
            shape((SMALL_ROWS, width), F32),
            shape((head.shape[0] + 8, width), F32),
        ],
        compiler_params=params(16),
        name="leave",
    )(*parts, stream, mods, head, target)


def back_kernel(
    at,
    gate_at,
    first,
    keep_ref,
    got_ref,
    far_ref,
    normed_ref,
    inv_ref,
    grad_ref,
    part_ref,
    mods_ref,
    rows_in_ref,
    out_ref,
    next_ref,
    rows_ref,
):
    d_inner = added(keep_ref, got_ref, far_ref)
    normed = normed_ref[...]
    inv = inv_ref[:, 0:1]
    grad = grad_ref[...] + norm_back(d_inner * (1.0 + row_of(mods_ref, at)), normed, inv)
    out_ref[...] = grad
    rows_ref[...] = rows_in_ref[...]
    rows_ref[first : first + 1, :] = jnp.sum(d_inner, 0, keepdims=True)
    rows_ref[first + 1 : first + 2, :] = jnp.sum(d_inner * normed, 0, keepdims=True)
    if gate_at is None:
        next_ref[...] = grad.astype(BF16)
    else:
        next_ref[...] = (row_of(mods_ref, gate_at) * grad).astype(BF16)
        rows_ref[first + 2 : first + 3, :] = jnp.sum(grad * part_ref[...], 0, keepdims=True)


def back(parts, normed, inv, grad, part, mods, rows_in, at, gate_at, first, beside):
    rows, width = grad.shape
    operands = (*parts, normed, inv, grad, part, mods, rows_in)
    return pl.pallas_call(
        past(functools.partial(back_kernel, at, gate_at, first), operands, beside),
        out_shape=[shape((rows, width), F32), shape((rows, width), BF16), shape(rows_in.shape, F32)],
        compiler_params=params(16),
        name="back",
    )(*operands, *beside)


def tables_kernel(n_patch, fix_ref, edge_ref, time_ref, class_ref, table_ref, first_ref, second_ref, *outs):
    new_ref, first_new_ref, second_new_ref = outs
    at = 0
    for ref, low, count in (
        (edge_ref, 0, n_patch),
        (time_ref, 0, FREQ),
        (class_ref, 0, CLASSES),
        (edge_ref, n_patch, n_patch),
    ):
        rows = slice(at, at + count)
        grad = ref[low : low + count, :]
        first = 0.5 * first_ref[rows, :] + 0.5 * grad
        second = 0.5 * second_ref[rows, :] + 0.5 * grad * grad
        first_new_ref[rows, :] = first
        second_new_ref[rows, :] = second
        new_ref[rows, :] = table_ref[rows, :] * (1.0 - LR_ADAM * WEIGHT_DECAY) - LR_ADAM * (
            first / fix_ref[0]
        ) / (jnp.sqrt(second / fix_ref[0]) + 1e-08)
        at += count


def update_tables(n_patch, bias_fix, edges, grad_time, grad_class, table, first, second):
    return pl.pallas_call(
        functools.partial(tables_kernel, n_patch),
        out_shape=[shape(table.shape, F32)] * 3,
        in_specs=[SMEM_SPEC] + [VMEM_SPEC] * 6,
        compiler_params=params(16),
        name="update_tables",
    )(bias_fix, edges, grad_time, grad_class, table, first, second)


def position_rows(first, rows):
    quarter = D // 4
    omega = jnp.exp(-math.log(10000.0) * jnp.arange(quarter, dtype=F32) / quarter)
    places = first + jnp.arange(rows, dtype=jnp.int32)
    rows_at = (places // GRID).astype(F32)[:, None] * omega[None]
    cols_at = (places % GRID).astype(F32)[:, None] * omega[None]
    return jnp.concatenate([jnp.sin(rows_at), jnp.cos(rows_at), jnp.sin(cols_at), jnp.cos(cols_at)], 1)


def time_features(timesteps):
    half_freq = FREQ // 2
    rates = jnp.exp(-math.log(10000.0) * jnp.arange(half_freq, dtype=F32) / half_freq)
    angles = timesteps.astype(F32)[:, None] * rates[None]
    return jnp.concatenate([jnp.cos(angles), jnp.sin(angles)], 1)


def shards(
    noisy_latents,
    noise_target,
    timesteps,
    labels,
    owners,
    step_count,
    master_bank,
    momentum_bank,
    embed_tables,
    embed_first,
    embed_second,
):
    n_lat, n_tok, n_patch = noisy_latents.shape
    n_slots, width, columns = master_bank.shape
    n_units = owners.shape[0]
    n_data = lax.axis_size("dp")
    my_data = lax.axis_index("dp")
    my_tensor = lax.axis_index("tensor")
    n_all = n_lat * n_data
    own_rows = n_lat * n_tok // 4
    count_all = float(n_all * n_tok * n_patch)
    depth = 2 if n_data <= 8 else 1
    steps = N_BIG + (n_data - 2) * depth

    unit_order = jnp.arange(n_units, dtype=jnp.int32)
    same_owner = owners[:, None] == owners[None, :]
    slot_of = jnp.sum((same_owner & (unit_order[None, :] < unit_order[:, None])).astype(jnp.int32), 1)
    mine = (owners[None, :] == my_data) & (
        slot_of[None, :] == jnp.arange(n_slots, dtype=jnp.int32)[:, None]
    )
    kind = [2 + 2 * g + (b >= low + (3, 4)[g % 2]) for g, (low, high) in enumerate(GROUPS) for b in range(low, high)]
    slot_tables = np.stack(
        [
            BIG_OF,
            SMALL_OF,
            np.where(BIG_OF >= 0, np.array(kind)[BIG_OF], np.where(SMALL_OF == TIME_AT, 1, 0)),
            np.where(BIG_OF >= 0, SMALL_ROWS + BIG_OF, SMALL_OF),
        ]
    )
    slots = jnp.sum(jnp.where(mine[None], jnp.asarray(slot_tables + 1, jnp.int32)[:, None], 0), 2) - 1
    owners_big = jnp.concatenate([owners[18 * l : 18 * l + BIG] for l in range(LAYERS)])
    tab = ring_schedule(owners_big, n_data, steps, depth, my_data)

    def flag(value):
        return jnp.asarray(value, jnp.int32).reshape(1)

    first_row = my_tensor * own_rows
    early = dict(
        slots=slots,
        chip=flag(my_tensor // 2),
        core=flag(my_tensor % 2),
        data=flag(my_data),
        bits=[flag((my_data // (1 << i)) % 2) for i in range((n_data - 1).bit_length())],
        time_mine=flag(owners[18 * LAYERS] == my_data),
        time_w2=lax.dynamic_index_in_dim(master_bank, slot_of[18 * LAYERS], 0, keepdims=False).astype(BF16),
        noisy=lax.dynamic_slice_in_dim(noisy_latents.reshape(n_lat * n_tok, n_patch), first_row, own_rows, 0),
        target=lax.dynamic_slice_in_dim(noise_target.reshape(n_lat * n_tok, n_patch), first_row, own_rows, 0),
        places=position_rows(first_row % n_tok, own_rows),
        ids=jnp.stack([timesteps, labels], 1),
        bias_fix=1.0 - jnp.power(0.5, step_count.astype(F32)),
        tab=tab,
        edge_cols=jnp.concatenate(
            [embed_tables[:n_patch], embed_tables[n_patch + FREQ + CLASSES :]], 0
        ).astype(BF16),
        time_w1=embed_tables[n_patch : n_patch + FREQ].astype(BF16),
        class_w=embed_tables[n_patch + FREQ : n_patch + FREQ + CLASSES].astype(BF16),
    )
    flat, tree = jax.tree.flatten(early)
    early = jax.tree.unflatten(tree, lax.optimization_barrier(tuple(flat)))
    chip, core, data, time_w2, noisy_own = (early[k] for k in ("chip", "core", "data", "time_w2", "noisy"))
    tab = early["tab"]
    big_slots, small_slots, left_slots, right_slots = (early["slots"][i] for i in range(4))
    spread = Spreader(tab, spread_init(early["slots"], master_bank), n_data, steps, depth)
    spread.step()
    ring = Reducer(tab, n_data, steps, depth)

    def conditioning():
        ids, edge_rows = yield from together(
            dp_sum(own_latents(early["ids"], 0, data, n_data), n_data),
            gather_columns(early["edge_cols"], chip, core),
        )
        features = time_features(ids[:, 0]).astype(BF16)
        time_one = jnp.dot(features, early["time_w1"], preferred_element_type=F32)
        time_act = yield from gather_columns(jax.nn.silu(time_one).astype(BF16), chip, core)
        second = jnp.dot(time_act, time_w2, preferred_element_type=F32)
        second = yield from dp_sum(jnp.where(is_at(early["time_mine"], 1, 2), second, 0.0), n_data)
        onehot = ids[:, 1:2] == jnp.arange(CLASSES, dtype=jnp.int32)[None]
        condition = second + jnp.dot(onehot.astype(BF16), early["class_w"], preferred_element_type=F32)
        cond_in = yield from gather_columns(jax.nn.silu(condition).astype(BF16), chip, core)
        mods = modulations(small_slots, cond_in, master_bank)
        bit = n_data // 2
        while bit:
            half = mods.shape[1] // 2
            sides = mods[:, :half], mods[:, half:]
            side = early["bits"][bit.bit_length() - 1]
            mods = pick(*sides, side) + (yield flip(pick(*sides, side, True), "dp", bit, n_data))
            bit //= 2
        latents = mods[:, 0], mods[:, 1]
        across = yield x_flip(pick(*latents, chip, True))
        own = pick(*latents, chip)
        pair = [pick(own, across, chip), pick(across, own, chip)]
        beside = yield core_flip(jnp.concatenate(pair, 1))
        beside = [beside[:, x * columns : (x + 1) * columns] for x in range(2)]
        blocks = [pick(one, two, core) for x in range(2) for one, two in ((pair[x], beside[x]), (beside[x], pair[x]))]
        return edge_rows, features, time_one, time_act, onehot, condition, cond_in, jnp.concatenate(blocks, 1)

    def forward():
        cond = yield from conditioning()
        edge_rows, mods = cond[0], cond[-1]
        stream, inner, normed, inv = enter(
            noisy_own, edge_rows[:n_patch], early["places"], mods, (small_at(0, 0), small_at(0, 1))
        )
        kept = []
        for layer in range(LAYERS):
            inner = yield from gather_tokens(inner)
            qkv, mixed, keep, send = attention(inner, spread.weights(2 * layer), BIG * layer, n_lat)
            parts = yield from scatter_tokens(keep, send)
            attended, stream, inner_mid, normed_mid, inv_mid = residual(
                parts, stream, mods, tuple(small_at(layer, i) for i in (2, 3, 4))
            )
            inner_mid = yield from gather_tokens(inner_mid)
            hidden, active, keep, send = mlp(inner_mid, spread.weights(2 * layer + 1), BIG * layer + 4)
            parts = yield from scatter_tokens(keep, send)
            kept.append([inner, normed, inv, qkv, mixed, attended, inner_mid, normed_mid, inv_mid, hidden, active])
            if layer + 1 < LAYERS:
                branch, stream, inner, normed, inv = residual(
                    parts,
                    stream,
                    mods,
                    (small_at(layer, 5), small_at(layer + 1, 0), small_at(layer + 1, 1)),
                )
                kept[-1].append(branch)
        return cond, kept, parts, stream

    cond, kept, parts_last, stream_last = drive(forward(), spread.step)
    edge_rows, features, time_one, time_act, onehot, condition, cond_in, mods = cond
    ring.held = spread.held

    def backward():
        grad, d_branch, rows, edge_head = leave(
            parts_last,
            stream_last,
            mods,
            edge_rows[n_patch:],
            early["target"],
            (small_at(LAYERS - 1, 5), SHIFT_F, SCALE_F),
            count_all,
        )
        lefts, rights = {}, {}
        for layer in reversed(range(LAYERS)):
            inner, normed, inv, qkv, mixed, attended, inner_mid, normed_mid, inv_mid, hidden, active = kept[layer][:11]
            d_branch = yield from gather_tokens(d_branch)
            d_hidden, keep, send = mlp_back(d_branch, hidden, ring.held, BIG * layer + 4)
            work = scatter_tokens(keep, send)
            flying = next(work)
            ring.held, lefts[2 * layer + 1], rights[2 * layer + 1] = weight_grads(
                ring.held, BIG * layer + 4, [(inner_mid, d_hidden), (d_branch, active)], n_lat
            )
            ring.ready = BIG * layer + 4
            parts = yield from resume(work, flying)
            grad, d_attended, rows = back(
                parts,
                normed_mid,
                inv_mid,
                grad,
                attended,
                mods,
                rows,
                small_at(layer, 4),
                small_at(layer, 2),
                small_at(layer, 3),
                [ring.held],
            )
            d_attended = yield from gather_tokens(d_attended)
            d_qkv, keep, send = attention_back(d_attended, qkv, ring.held, BIG * layer, n_lat)
            work = scatter_tokens(keep, send)
            flying = next(work)
            ring.held, lefts[2 * layer], rights[2 * layer] = weight_grads(
                ring.held, BIG * layer, [(inner, d_qkv), (d_attended, mixed[None])], n_lat
            )
            ring.ready = BIG * layer
            parts = yield from resume(work, flying)
            below = kept[layer - 1][11] if layer else normed
            grad, d_branch, rows = back(
                parts,
                normed,
                inv,
                grad,
                below,
                mods,
                rows,
                small_at(layer, 1),
                small_at(layer - 1, 5) if layer else None,
                small_at(layer, 0),
                [ring.held],
            )
        (d_small, d_second, grad_class, grad_time_one), edges, packed = yield from together(
            cond_backward(rows),
            edge_sums(d_branch, edge_head),
            factor_rows(lefts, rights),
        )
        return d_small, d_second, grad_class, grad_time_one, edges, packed

    def cond_backward(rows):
        mine = yield from core_columns_sum(rows, core)
        near, far = pick(*mine, chip), (yield x_flip(pick(*mine, chip, True)))
        d_small = jnp.stack([pick(near, far, chip), pick(far, near, chip)], 1).astype(BF16)
        d_small = yield from dp_sum(own_latents(d_small, 1, data, n_data), n_data)
        d_cond = cond_back(small_slots, d_small, master_bank)
        d_cond = yield from sum_of_columns(d_cond, chip, core, n_data)
        unused, silu_pull = jax.vjp(jax.nn.silu, condition)
        d_condition = silu_pull(d_cond)[0]
        d_second = d_condition.astype(BF16)
        grad_class = lax.dot_general(
            onehot.astype(F32), d_condition, (((0,), (0,)), ((), ())), precision=HIGHEST_PREC
        )
        d_time_act = lax.dot_general(d_second, time_w2, (((1,), (1,)), ((), ())), preferred_element_type=F32)
        d_time_act = jnp.where(is_at(early["time_mine"], 1, 2), d_time_act, 0.0)
        d_time_act = yield from sum_of_columns(d_time_act, chip, core, n_data)
        unused, time_pull = jax.vjp(jax.nn.silu, time_one)
        d_time_one = time_pull(d_time_act)[0].astype(BF16)
        grad_time_one = lax.dot_general(
            features, d_time_one, (((0,), (0,)), ((), ())), preferred_element_type=F32
        )
        return d_small, d_second, grad_class, grad_time_one

    def edge_sums(d_stream, edge_head):
        grad_patch = lax.dot_general(noisy_own, d_stream, (((0,), (0,)), ((), ())), preferred_element_type=F32)
        edges = jnp.concatenate([grad_patch, edge_head], 0)
        return (yield from sum_of_columns(edges, chip, core, n_data))

    def factor_rows(lefts, rights):
        a_rows = jnp.concatenate([lefts[g][:, :n_lat] for g in range(len(GROUPS))], 0).transpose(1, 0, 2)
        b_rows = jnp.concatenate([rights[g][:, :n_lat] for g in range(len(GROUPS))], 0).transpose(1, 0, 2)
        a_rows, b_rows = yield from together(
            dp_rows(a_rows.astype(BF16), n_data), dp_rows(b_rows.astype(BF16), n_data)
        )
        return a_rows.transpose(1, 0, 2), b_rows.transpose(1, 0, 2)

    d_small, d_second, grad_class, grad_time_one, edges, (a_rows, b_rows) = drive(backward(), ring.step)
    ring.drain()
    loss = edges[2 * n_patch, 0]
    a_all = jnp.concatenate([cond_in[None], time_act[None], a_rows], 0)
    small_rows = jnp.where(jnp.arange(SMALL_ROWS)[:, None, None] == TIME_AT, d_second[None], d_small)
    b_all = jnp.concatenate([small_rows, b_rows], 0)
    master_new, momentum_new = optimizer(
        big_slots, left_slots, right_slots, tab, a_all, b_all, master_bank, momentum_bank, ring.held, ring.last()
    )
    embed_new, first_new, second_new = update_tables(
        n_patch, early["bias_fix"], edges, grad_time_one, grad_class, embed_tables, embed_first, embed_second
    )
    return (loss, master_new, momentum_new, embed_new, first_new, second_new)


def solution(mesh):
    placed = (
        P("dp", None, None),
        P("dp", None, None),
        P("dp"),
        P("dp"),
        P(),
        P(),
        P("dp", None, "tensor"),
        P("dp", None, "tensor"),
        P(None, "tensor"),
        P(None, "tensor"),
        P(None, "tensor"),
    )
    return jax.shard_map(
        shards,
        mesh=mesh,
        in_specs=placed,
        out_specs=(
            P(),
            P("dp", None, "tensor"),
            P("dp", None, "tensor"),
            P(None, "tensor"),
            P(None, "tensor"),
            P(None, "tensor"),
        ),
        check_vma=False,
    )
```

```python
import functools
import math

import jax
import jax.numpy as jnp
import numpy as np
from jax import lax
from jax.experimental import pallas as pl
from jax.experimental.pallas import tpu as pltpu
from jax.sharding import PartitionSpec as P

D = 1024
HEAD_DIM = 64
FREQ = 256
CLASSES = 1000
GRID = 16
LAYERS = 2
BIG = 12
N_BIG = BIG * LAYERS
SMALL_ROWS = 16
SHIFT_F, SCALE_F, TIME_AT = 0, 1, 6 * LAYERS + 2


def small_at(layer, i):
    first = 2 + 6 * (LAYERS - 1 - layer)
    return first + (4, 5, 3, 1, 2, 0)[i]


NS_COEF = (3.4445, -4.775, 2.0315)
LR_MUON = 0.5
LR_ADAM = 0.02
WEIGHT_DECAY = 0.1
SCORE_SCALE = 1.0 / math.sqrt(HEAD_DIM)
HIGHEST_PREC = lax.Precision.HIGHEST

F32 = jnp.float32
BF16 = jnp.bfloat16
SCOPE = 16
GELU_C = math.sqrt(2.0 / math.pi)
GROUPS = ((0, 4), (4, 12), (12, 16), (16, 24))


def unit_tables():
    big, small = [], []
    for u in range(18 * LAYERS):
        layer, place = divmod(u, 18)
        big.append(layer * BIG + place if place < BIG else -1)
        small.append(-1 if place < BIG else small_at(layer, place - BIG))
    return np.array(big + [-1] * 3), np.array(small + [TIME_AT, SHIFT_F, SCALE_F])


BIG_OF, SMALL_OF = unit_tables()


def params(limit, **more):
    return pltpu.CompilerParams(vmem_limit_bytes=limit * 1024 * 1024, **more)


SMEM_SPEC = pl.BlockSpec(memory_space=pltpu.SMEM)
VMEM_SPEC = pl.BlockSpec(memory_space=pltpu.VMEM)


def in_hbm(values):
    return pltpu.with_memory_space_constraint(values, pltpu.HBM)


def dot(a, b):
    return lax.dot_general(a, b, (((1,), (0,)), ((), ())), preferred_element_type=F32)


def dot_nt(a, b):
    return lax.dot_general(a, b, (((1,), (1,)), ((), ())), preferred_element_type=F32)


def dot_tn(a, b):
    return lax.dot_general(a, b, (((0,), (0,)), ((), ())), preferred_element_type=F32)


def shape(dims, kind):
    return jax.ShapeDtypeStruct(dims, kind)


ISSUED = []


def order(values, after):
    if not after:
        return values
    flat, tree = jax.tree.flatten(values)
    tied = lax.optimization_barrier(tuple(flat) + tuple(after))
    return jax.tree.unflatten(tree, tied[: len(flat)])


def drive(work, line):
    ISSUED.clear()
    try:
        value = next(work)
        while True:
            after = tuple(ISSUED)
            ISSUED.clear()
            value = work.send(order(value, line(after)))
    except StopIteration as end:
        return end.value


def together(*works):
    ends, flying = [None] * len(works), {}

    def go(i, step):
        try:
            flying[i] = step()
        except StopIteration as end:
            flying.pop(i, None)
            ends[i] = end.value

    for i, work in enumerate(works):
        go(i, lambda: next(work))
    while flying:
        got = yield dict(flying)
        for i in list(got):
            go(i, lambda: works[i].send(got[i]))
    return ends


def finish(work, value):
    try:
        work.send(value)
    except StopIteration as end:
        return end.value
    raise AssertionError


def flip(values, axis, bit, size):
    ISSUED.append(values)
    got = lax.ppermute(values, axis, [(i, i ^ bit) for i in range(size)])
    if axis == "tensor" and values.size < 2**16:
        ISSUED.append(got)
    return got


def is_at(flag, value, ndim):
    return flag.reshape((1,) * ndim) == value


def pick(low, high, place, other=False):
    return jnp.where(is_at(place, 1 if other else 0, low.ndim), low, high)


def own_latents(values, axis, data, n_data):
    n_lat = values.shape[axis]
    dims = values.shape[:axis] + (n_lat * n_data,) + values.shape[axis + 1 :]
    at = lax.broadcasted_iota(jnp.int32, dims, axis)
    first = data.reshape((1,) * len(dims)) * n_lat
    placed = jnp.zeros(dims, values.dtype)
    for l in range(n_lat):
        placed = jnp.where(at == first + l, lax.slice_in_dim(values, l, l + 1, axis=axis), placed)
    return placed


def dp_sum(values, n_data):
    bit = 1
    while bit < n_data:
        values = values + (yield flip(values, "dp", bit, n_data))
        bit *= 2
    return values


def dp_rows(values, n_data):
    bit = 1
    while bit < n_data:
        values = jnp.concatenate([values, (yield flip(values, "dp", bit, n_data))], 0)
        bit *= 2
    return values


def core_flip(values):
    return flip(values, "tensor", 1, 4)


def x_flip(values):
    return flip(values, "tensor", 2, 4)


def gather_tokens(own):
    beside, across = yield (core_flip(own), x_flip(own))
    return own, beside, across, core_flip(across)


def gather_columns(own, chip, core):
    beside, across = yield (core_flip(own), x_flip(own))
    corner = core_flip(across)
    at_core = [is_at(core, i, own.ndim) for i in range(2)]
    at_chip = [is_at(chip, i, own.ndim) for i in range(2)]
    near = [jnp.where(at_core[i], own, beside) for i in range(2)]
    far = [jnp.where(at_core[i], across, corner) for i in range(2)]
    parts = [jnp.where(at_chip[i], near[j], far[j]) for i in range(2) for j in range(2)]
    return jnp.concatenate(parts, -1)


def scatter_tokens(keep, send):
    got = core_flip(send)
    far = (keep[1] + got[1].astype(F32)).astype(BF16)
    return keep, got, (yield x_flip(far))


def core_columns(values, core, other=False):
    size = values.shape[-1] // 4
    block = [lax.slice_in_dim(values, j * size, (j + 1) * size, axis=values.ndim - 1) for j in range(4)]
    return [pick(block[2 * x], block[2 * x + 1], core, other) for x in range(2)]


def core_columns_sum(values, core):
    got = core_flip(jnp.concatenate(core_columns(values, core, True), -1))
    size = got.shape[-1] // 2
    return [
        mine + lax.slice_in_dim(got, x * size, (x + 1) * size, axis=got.ndim - 1)
        for x, mine in enumerate(core_columns(values, core))
    ]


def own_columns_sum(values, chip, core):
    mine = core_columns_sum(values, core)
    return pick(*mine, chip) + (yield x_flip(pick(*mine, chip, True)))


def sum_of_columns(values, chip, core, n_data):
    return (yield from dp_sum((yield from own_columns_sum(values, chip, core)), n_data))


def ring_order(n_data):
    return [0, 2, 4, 6, 7, 5, 3, 1] if n_data == 8 else list(range(n_data))


def sched_kernel(steps, depth, n_data, place_ref, own_ref, next_ref, out_ref):
    lane = lax.broadcasted_iota(jnp.int32, (n_data, 128), 1)
    row = lax.broadcasted_iota(jnp.int32, (n_data, 128), 0)
    far = jnp.int32(999)
    out_lane = lax.broadcasted_iota(jnp.int32, (1, 128), 1)

    def step(t, carry):
        line = jnp.full((1, 128), -1, jnp.int32)
        after = []
        for way in range(2):
            have, sent, *coming = carry[way]
            place = place_ref[way]
            before = jnp.where(place == 0, n_data - 1, place - 1)
            open_now = have * (1 - sent) * (1 - next_ref[way])
            first = jnp.min(jnp.where(open_now > 0, lane, far), axis=1, keepdims=True)
            chosen = (lane == first).astype(jnp.int32)
            first = jnp.broadcast_to(first, (n_data, 128))
            for k, who in enumerate((place, before)):
                index = jnp.min(jnp.where(row == who, first, far), axis=0, keepdims=True)
                index = jnp.where(index == far, -1, index)
                line = jnp.where(out_lane == 2 * way + k, index, line)
            coming = list(coming) + [pltpu.roll(chosen, 1, 0)]
            after.append((have + coming[0], sent + chosen, *coming[1:]))
        out_ref[pl.ds(t, 1), :] = line
        return tuple(after)

    none = jnp.zeros((n_data, 128), jnp.int32)
    lax.fori_loop(0, steps, step, tuple((own_ref[way], none) + (none,) * (depth - 1) for way in range(2)))


def ring_schedule(owners_big, n_data, steps, depth, my_data):
    order = np.array(ring_order(n_data))
    place_of = np.argsort(order)
    place = jnp.sum(jnp.where(jnp.arange(n_data) == my_data, place_of, 0)).astype(jnp.int32)
    at = jnp.arange(n_data)[:, None]
    owner_place = jnp.sum(jnp.where(owners_big[:, None] == jnp.arange(n_data)[None], place_of[None], 0), 1)
    owner_place = jnp.concatenate([owner_place, jnp.full((128 - N_BIG,), -9, owner_place.dtype)])[None]
    back_place = jnp.where(owner_place >= 0, n_data - 1 - owner_place, -9)
    own = jnp.stack([at == owner_place, at == back_place]).astype(jnp.int32)
    follow = (at + 1) % n_data
    nxt = jnp.stack([follow == owner_place, follow == back_place]).astype(jnp.int32)
    out = pl.pallas_call(
        functools.partial(sched_kernel, steps, depth, n_data),
        out_shape=shape((steps, 128), jnp.int32),
        in_specs=[
            pl.BlockSpec(memory_space=pltpu.SMEM),
            pl.BlockSpec(memory_space=pltpu.VMEM),
            pl.BlockSpec(memory_space=pltpu.VMEM),
        ],
        out_specs=pl.BlockSpec(memory_space=pltpu.VMEM),
        name="ring_schedule",
    )(jnp.stack([place, n_data - 1 - place]), own, nxt)
    return out[:, :4]


def spread_init_kernel(slots_ref, bank_ref, out_ref, wide, sem):
    big_ref = [slots_ref[0, s] for s in range(bank_ref.shape[0])]
    n_slots = bank_ref.shape[0]
    for s in range(n_slots):
        copy = pltpu.make_async_copy(bank_ref.at[s], wide.at[s], sem.at[s])
        pl.when(big_ref[s] >= 0)(copy.start)
    for s in range(n_slots):
        copy = pltpu.make_async_copy(bank_ref.at[s], wide.at[s], sem.at[s])
        pl.when(big_ref[s] >= 0)(copy.wait)

        @pl.when(big_ref[s] >= 0)
        def _(s=s):
            out_ref[jnp.maximum(big_ref[s], 0)] = wide[s].astype(BF16)


def spread_init(big_slots, master_bank):
    n_slots, rows, columns = master_bank.shape
    return pl.pallas_call(
        spread_init_kernel,
        out_shape=pltpu.VMEM((N_BIG + BIG, rows, columns), BF16),
        in_specs=[SMEM_SPEC, pl.BlockSpec(memory_space=pltpu.HBM)],
        out_specs=VMEM_SPEC,
        scratch_shapes=[
            pltpu.VMEM((n_slots, rows, columns), F32),
            pltpu.SemaphoreType.DMA((n_slots,)),
        ],
        compiler_params=params(SCOPE),
        name="own_weights",
    )(big_slots, in_hbm(master_bank))


def spread_kernel(places, fetch_at, tab_ref, got, held, out):
    half = held.shape[1] // 2
    for way in range(2):
        rows = pl.ds(way * half, half)
        for k, t in enumerate(places):
            unit = tab_ref[t, 2 * way + 1]

            @pl.when(unit >= 0)
            def _():
                held[jnp.maximum(unit, 0), rows] = got[2 * k + way][...]

        if fetch_at is not None:
            out[way][...] = held[jnp.maximum(tab_ref[fetch_at, 2 * way], 0), rows]


def ring_step(name, tab, held, got, sends, body, work=None, mail=(), mail_rows=0, keep_rows=0):
    rows, columns = held.shape[1:]
    extra, more, operands, shapes, scratch = (tuple(work) + ([],))[:5] if work else ("", None, [], [], [])
    specs = [value[1] if isinstance(value, tuple) else VMEM_SPEC for value in operands]
    operands = [value[0] if isinstance(value, tuple) else value for value in operands]
    operands, specs = list(mail) + list(operands), [VMEM_SPEC] * len(mail) + specs
    n, m, k = len(got), len(operands), len(mail)
    kept = 2 if keep_rows else 0
    shapes = [pltpu.VMEM((keep_rows, columns), BF16)] * kept + list(shapes)

    def kernel(tab_ref, *refs):
        out = refs[n + 1 + m :]
        if body is not None:
            body(tab_ref, refs[:n], out[0], out[1 : 1 + sends], *([refs[n + 1 : n + 1 + k]] if k else []))
        for way in range(kept):
            out[1 + sends + way][...] = refs[way][refs[way].shape[0] - keep_rows :]
        if more is not None:
            more(out[0], *refs[n + 1 + k : n + 1 + m], *out[1 + sends + kept :])

    res = pl.pallas_call(
        kernel,
        out_shape=[pltpu.VMEM(held.shape, held.dtype)] + [pltpu.VMEM((rows // 2 + mail_rows, columns), BF16)] * sends
        + list(shapes),
        in_specs=[SMEM_SPEC] + [VMEM_SPEC] * (n + 1) + specs,
        out_specs=[VMEM_SPEC] * (1 + sends + len(shapes)),
        scratch_shapes=scratch,
        input_output_aliases={1 + n: 0},
        compiler_params=params(SCOPE),
        name=name + extra,
    )(tab, *got, held, *operands)
    return res[0], list(res[1 : 1 + sends]), list(res[1 + sends :])


def ring_perms(n_data):
    order = ring_order(n_data)
    ahead = [(order[i], order[(i + 1) % n_data]) for i in range(n_data)]
    return ahead, [(b, a) for a, b in ahead]


class Spreader:
    def __init__(self, tab, held, n_data, steps, depth):
        self.tab, self.n_data, self.steps, self.depth = tab, n_data, steps, depth
        self.perms = ring_perms(n_data)
        self.held = held
        self.got = {}
        self.at = 0

    def last(self, g):
        return GROUPS[g][1] - 1 + (self.n_data - 2) * self.depth

    def step(self, after=()):
        self.work(None, after)
        return self.sent

    def work(self, work, after=()):
        t = self.at
        self.sent = ()
        if t > self.steps:
            return []
        fetch_at = t if t < self.steps else None
        places = [t - self.depth] if fetch_at is not None else list(range(self.steps - self.depth, self.steps))
        places = [p for p in places if p >= 0]
        self.held, sends, results = ring_step(
            "spread_step",
            order(self.tab, after),
            self.held,
            [value for p in places for value in self.got.pop(p)],
            0 if fetch_at is None else 2,
            functools.partial(spread_kernel, places, fetch_at),
            work,
        )
        if fetch_at is not None:
            self.got[t] = [lax.ppermute(sends[way], "dp", self.perms[way]) for way in range(2)]
        self.at += 1
        self.sent = tuple(sends) + tuple(self.got.get(t - 1, ()))
        return order(results, tuple(self.got.get(t - 1, ())))

    def prepare(self, g):
        while self.at < min(self.last(g) + self.depth, self.steps):
            self.step()


def reduce_kernel(place_at, fetch_at, mail, tab_ref, got, held, out, own=()):
    half = held.shape[1] // 2
    if mail:
        for way in range(2):
            out[way][half:] = own[0][...] if mail == "own" else got[way][half:]
    for way in range(2):
        rows = pl.ds(way * half, half)
        if place_at is not None:
            unit = tab_ref[place_at, 2 * way]

            @pl.when(unit >= 0)
            def _():
                at = BIG + jnp.maximum(unit, 0)
                held[at, rows] = (held[at, rows].astype(F32) + got[way][:half].astype(F32)).astype(BF16)

        out[way][:half] = held[BIG + jnp.maximum(tab_ref[fetch_at, 2 * way + 1], 0), rows]


class Reducer:
    def __init__(self, tab, n_data, steps, depth):
        self.tab, self.n_data, self.steps, self.depth = tab, n_data, steps, depth
        self.perms = [p for p in reversed(ring_perms(n_data))]
        self.held = None
        self.ready = N_BIG
        self.mail = {}
        self.come = {}
        self.got = {}
        self.at = 0

    def lowest(self, k):
        return (self.steps - 1 - k) - (self.n_data - 2) * self.depth

    def step(self, after=()):
        k = self.at
        self.sent = ()
        if k < self.steps and max(self.lowest(k), 0) >= self.ready:
            self.work(None, after)
        return self.sent

    def work(self, work, after=()):
        k = self.at
        self.sent = ()
        tab = order(self.tab, after)
        if k >= self.steps or max(self.lowest(k), 0) < self.ready:
            self.held, unused, results = ring_step("layer_", tab, self.held, [], 0, None, work)
            return results
        place_at = self.steps - 1 - (k - self.depth) if k >= self.depth else None
        payload, hops = self.mail.get(k, (None, 0))
        mail = None if payload is None else "own" if hops == 0 else "pass"
        keep_rows = self.mail[k - self.depth][0].shape[0] if k - self.depth in self.mail else 0
        self.held, sends, results = ring_step(
            "reduce_step",
            tab,
            self.held,
            self.got.get(k - self.depth, []),
            2,
            functools.partial(reduce_kernel, place_at, self.steps - 1 - k, mail),
            work,
            [payload] if mail == "own" else [],
            0 if payload is None else payload.shape[0],
            keep_rows,
        )
        if keep_rows:
            self.come[k - self.depth], results = results[:2], results[2:]
        self.got[k] = [lax.ppermute(sends[way], "dp", self.perms[way]) for way in range(2)]
        self.at += 1
        self.sent = tuple(sends) + tuple(self.got.get(k - 1, ()))
        return order(results, tuple(self.got.get(k - 1, ())))

    def gather(self, payload, place):
        far = self.n_data // 2
        start, last = self.at, self.at + (far - 1) * self.depth
        assert last + self.depth < self.steps
        for j in range(far):
            self.mail[start + j * self.depth] = (payload, j)
        while self.at <= last + self.depth:
            yield ()
        come = [[self.come[start + j * self.depth][way] for j in range(far)] for way in range(2)]
        come = order(come, self.sent)
        at = [payload] + come[0][: far - 1] + come[1][::-1]
        everyone = []
        for d in range(self.n_data):
            ahead = ring_order(self.n_data).index(d) - place.reshape((1, 1))
            ahead = jnp.where(ahead < 0, ahead + self.n_data, ahead)
            value = at[0]
            for i in range(1, self.n_data):
                value = jnp.where(ahead == i, at[i], value)
            everyone.append(value)
        return everyone

    def drain(self):
        while self.at < self.steps:
            self.step()

    def last(self):
        return [self.got[self.steps - 1 - t][way] for t in range(self.depth) for way in range(2)]


def past(kernel, operands, beside):
    n, m = len(operands), len(beside)
    return lambda *refs: kernel(*refs[:n], *refs[n + m :])


def split_rows(total, keep_ref, send_ref):
    rows = total.shape[0] // 4
    for i in range(2):
        keep_ref[i] = total[2 * i * rows : (2 * i + 1) * rows]
        send_ref[i] = total[(2 * i + 1) * rows : (2 * i + 2) * rows].astype(BF16)


def part_shapes(rows, width):
    return [shape((2, rows // 4, width), F32), shape((2, rows // 4, width), BF16)]


def joined(refs):
    return jnp.concatenate([r[...] for r in refs], 0)


def softmax_parts(q, k):
    scores = dot_nt(q, k) * SCORE_SCALE
    expo = jnp.exp(scores - jnp.max(scores, -1, keepdims=True))
    return expo / jnp.sum(expo, -1, keepdims=True)


def attention_kernel(n_lat, base, w_ref, x0, x1, x2, x3, qkv_ref, mixed_ref, keep_ref, send_ref):
    x = joined((x0, x1, x2, x3))
    for j in range(3):
        qkv_ref[j] = dot(x, w_ref[base + j]).astype(BF16)
    toks = x.shape[0] // n_lat
    heads = w_ref.shape[2] // HEAD_DIM
    for l in range(n_lat):
        rows = slice(l * toks, (l + 1) * toks)
        outs = []
        for h in range(heads):
            cols = slice(h * HEAD_DIM, (h + 1) * HEAD_DIM)
            q, k, v = (qkv_ref[j, rows, cols] for j in range(3))
            outs.append(dot(softmax_parts(q, k).astype(BF16), v))
        mixed_ref[rows, :] = jnp.concatenate(outs, 1).astype(BF16)
    split_rows(dot_nt(mixed_ref[...], w_ref[base + 3]), keep_ref, send_ref)


def attention(x, columns, base, n_lat):
    rows, width = 4 * x[0].shape[0], x[0].shape[1]
    shapes = [shape((3, rows, columns), BF16), shape((rows, columns), BF16)] + part_shapes(rows, width)
    return "_attention", functools.partial(attention_kernel, n_lat, base), x, shapes


def gelu(x):
    return 0.5 * x * (1.0 + jnp.tanh(GELU_C * (x + 0.044715 * x * x * x)))


def gelu_grad(x):
    t = jnp.tanh(GELU_C * (x + 0.044715 * x * x * x))
    return 0.5 * (1.0 + t) + 0.5 * x * (1.0 - t * t) * (GELU_C * (1.0 + 3 * 0.044715 * x * x))


def mlp_kernel(base, w_ref, x0, x1, x2, x3, hidden_ref, active_ref, keep_ref, send_ref):
    x = joined((x0, x1, x2, x3))
    total = None
    for j in range(4):
        hidden = dot(x, w_ref[base + j])
        hidden_ref[j] = hidden
        active = gelu(hidden).astype(BF16)
        active_ref[j] = active
        part = dot_nt(active, w_ref[base + 4 + j])
        total = part if total is None else total + part
    split_rows(total, keep_ref, send_ref)


def mlp(x, columns, base):
    rows, width = 4 * x[0].shape[0], x[0].shape[1]
    shapes = [shape((4, rows, columns), F32), shape((4, rows, columns), BF16)] + part_shapes(rows, width)
    return "_mlp", functools.partial(mlp_kernel, base), x, shapes


def mlp_back_kernel(base, w_ref, d0, d1, d2, d3, hidden_ref, dh_ref, keep_ref, send_ref):
    d = joined((d0, d1, d2, d3))
    total = None
    for j in range(4):
        dh = (gelu_grad(hidden_ref[j]) * dot(d, w_ref[base + 4 + j])).astype(BF16)
        dh_ref[j] = dh
        part = dot_nt(dh, w_ref[base + j])
        total = part if total is None else total + part
    split_rows(total, keep_ref, send_ref)


def mlp_back(d, hidden, base):
    rows, width = 4 * d[0].shape[0], d[0].shape[1]
    shapes = [shape(hidden.shape, BF16)] + part_shapes(rows, width)
    return "_mlp_back", functools.partial(mlp_back_kernel, base), [*d, hidden], shapes


def attention_back_kernel(n_lat, base, w_ref, d0, d1, d2, d3, qkv_ref, dqkv_ref, keep_ref, send_ref):
    d_mixed = dot(joined((d0, d1, d2, d3)), w_ref[base + 3]).astype(BF16)
    toks = d_mixed.shape[0] // n_lat
    heads = w_ref.shape[2] // HEAD_DIM
    for l in range(n_lat):
        rows = slice(l * toks, (l + 1) * toks)
        outs = [[], [], []]
        for h in range(heads):
            cols = slice(h * HEAD_DIM, (h + 1) * HEAD_DIM)
            q, k, v = (qkv_ref[j, rows, cols] for j in range(3))
            do = d_mixed[rows, cols]
            probs = softmax_parts(q, k)
            d_probs = dot_nt(do, v)
            d_scores = probs * (d_probs - jnp.sum(probs * d_probs, -1, keepdims=True))
            d_scores = d_scores.astype(BF16)
            outs[0].append(dot(d_scores, k) * SCORE_SCALE)
            outs[1].append(dot_tn(d_scores, q) * SCORE_SCALE)
            outs[2].append(dot_tn(probs.astype(BF16), do))
        for j in range(3):
            dqkv_ref[j, rows, :] = jnp.concatenate(outs[j], 1).astype(BF16)
    total = sum(dot_nt(dqkv_ref[j], w_ref[base + j]) for j in range(3))
    split_rows(total, keep_ref, send_ref)


def attention_back(d, qkv, base, n_lat):
    rows, width = 4 * d[0].shape[0], d[0].shape[1]
    shapes = [shape(qkv.shape, BF16)] + part_shapes(rows, width)
    return "_attention_back", functools.partial(attention_back_kernel, n_lat, base), [*d, qkv], shapes


def weight_grad_kernel(counts, n_lat, base, out_ref, *refs):
    n = len(counts)
    lefts, rights, (mean_ref, sum_ref) = refs[: 4 * n], refs[4 * n : 5 * n], refs[-2:]
    at = 0
    for k, count in enumerate(counts):
        a = joined(lefts[4 * k : 4 * k + 4])
        toks = a.shape[0] // n_lat

        def rows_of(x, scale):
            parts = [
                jnp.sum(x[l * toks : (l + 1) * toks].astype(F32), 0, keepdims=True) * scale for l in range(n_lat)
            ]
            return jnp.concatenate(parts + [jnp.zeros((8 - n_lat, x.shape[1]), F32)], 0).astype(BF16)

        mean = rows_of(a, 1.0 / toks)
        mean_ref[k] = mean.astype(F32)
        for j in range(count):
            b = rights[k][j]
            total = rows_of(b, 1.0)
            sum_ref[at] = total.astype(F32)
            out_ref[BIG + base + at] = (dot_tn(a, b) - dot_tn(mean, total)).astype(BF16)
            at += 1


def weight_grads(base, pairs, n_lat):
    counts = [right.shape[0] for _, right in pairs]
    width, columns = pairs[0][0][0].shape[1], pairs[0][1].shape[2]
    operands = [part for left, _ in pairs for part in left] + [right for _, right in pairs]
    shapes = [shape((len(pairs), 8, width), F32), shape((sum(counts), 8, columns), F32)]
    return "_weight_grads", functools.partial(weight_grad_kernel, counts, n_lat, base), operands, shapes


def small_weights(small_ref, bank_ref, wide, sem, use):
    units = [small_ref[s] for s in range(bank_ref.shape[0])]
    ours = [(unit >= 0) & (unit != TIME_AT) for unit in units]
    copies = [pltpu.make_async_copy(bank_ref.at[s], wide.at[s], sem.at[s]) for s in range(len(units))]
    for s, copy in enumerate(copies):
        pl.when(ours[s])(copy.start)
    for s, copy in enumerate(copies):

        @pl.when(ours[s])
        def _(s=s, copy=copy):
            copy.wait()
            use(jnp.maximum(units[s], 0), wide[s].astype(BF16))


def modulation_kernel(held_ref, small_ref, cond_ref, bank_ref, out_ref, wide, sem):
    out_ref[...] = jnp.zeros_like(out_ref)

    def use(unit, weight):
        out_ref[unit] = dot(cond_ref[...], weight)

    small_weights(small_ref, bank_ref, wide, sem, use)


def bank_scratch(bank):
    return [pltpu.VMEM(bank.shape, F32), pltpu.SemaphoreType.DMA((bank.shape[0],))]


def modulations(small_slots, cond_in, bank):
    operands = [(small_slots, SMEM_SPEC), cond_in, (in_hbm(bank), pl.BlockSpec(memory_space=pltpu.HBM))]
    shapes = [shape((SMALL_ROWS, cond_in.shape[0], bank.shape[2]), F32)]
    return "_modulations", modulation_kernel, operands, shapes, bank_scratch(bank)


def cond_back_kernel(held_ref, small_ref, d_ref, bank_ref, out_ref, wide, sem):
    out_ref[...] = jnp.zeros_like(out_ref)

    def use(unit, weight):
        out_ref[...] += dot_nt(d_ref[unit], weight)

    small_weights(small_ref, bank_ref, wide, sem, use)


def cond_back(small_slots, d_small, bank):
    operands = [(small_slots, SMEM_SPEC), d_small, (in_hbm(bank), pl.BlockSpec(memory_space=pltpu.HBM))]
    return "_cond_back", cond_back_kernel, operands, [shape((d_small.shape[1], bank.shape[1]), F32)], bank_scratch(bank)


def halves(x):
    high = x.astype(BF16)
    return high, (x - high.astype(F32)).astype(BF16)


def newton_sweep_coarse(x):
    xh = x.astype(BF16)
    gram = dot_tn(xh, xh)
    gh = gram.astype(BF16)
    poly = NS_COEF[1] * gram + NS_COEF[2] * dot(gh, gh)
    return NS_COEF[0] * x + dot(xh, poly.astype(BF16))


def newton_sweep(x):
    xh, xl = halves(x)
    cross = dot_tn(xh, xl)
    gram = dot_tn(xh, xh) + (cross + cross.T)
    gh, gl = halves(gram)
    cross = dot(gh, gl)
    square = dot(gh, gh) + (cross + cross.T)
    ph, pl_ = halves(NS_COEF[1] * gram + NS_COEF[2] * square)
    return NS_COEF[0] * x + (dot(xh, ph) + (dot(xl, ph) + dot(xh, pl_)))


def newton_kernel(n_last, big_ref, left_ref, right_ref, tab_ref, a_ref, b_ref, bank_ref, mom_ref, *refs):
    held, got = refs[0], refs[1 : 1 + n_last]
    new_ref, mom_new_ref, grad, sem = refs[1 + n_last :]
    s = pl.program_id(0)
    unit, left, right = big_ref[s], left_ref[s], right_ref[s]
    half = got[0].shape[0]

    @pl.when(right < 0)
    def _():
        new_ref[...] = bank_ref[...]
        mom_new_ref[...] = mom_ref[...]

    @pl.when(right >= 0)
    def _():
        copy = pltpu.make_async_copy(held.at[BIG + jnp.maximum(unit, 0)], grad, sem.at[0])
        pl.when(unit >= 0)(copy.start)
        mom_new_ref[0] = 0.5 * mom_ref[0] + dot_tn(
            a_ref[jnp.maximum(left, 0)], b_ref[jnp.maximum(right, 0)]
        )
        pl.when(unit >= 0)(copy.wait)

        @pl.when(unit >= 0)
        def _():
            mom_new_ref[0] += grad[...].astype(F32)

        for i in range(n_last):
            rows = slice((i % 2) * half, (i % 2 + 1) * half)

            @pl.when((tab_ref[i // 2, 2 * (i % 2)] == unit) & (unit >= 0))
            def _(i=i, rows=rows):
                mom_new_ref[0, rows] += got[i][...].astype(F32)

        block = mom_new_ref[0]
        norm = jnp.sqrt(jnp.sum(block * block)) + 1e-07
        x = block / norm
        for sweep in range(5):
            x = newton_sweep_coarse(x) if sweep < 3 else newton_sweep(x)
        new_ref[0] = bank_ref[0] - LR_MUON * x


def optimizer(big_slots, left_slots, right_slots, tab, a_all, b_all, master, momentum, held, got):
    n_slots, rows, columns = master.shape
    block = pl.BlockSpec((1, rows, columns), lambda s, *t: (s, 0, 0))
    return pl.pallas_call(
        functools.partial(newton_kernel, len(got)),
        grid_spec=pltpu.PrefetchScalarGridSpec(
            num_scalar_prefetch=4,
            grid=(n_slots,),
            in_specs=[
                pl.BlockSpec(a_all.shape, lambda s, *t: (0, 0, 0)),
                pl.BlockSpec(b_all.shape, lambda s, *t: (0, 0, 0)),
                block,
                block,
            ]
            + [pl.BlockSpec(memory_space=pl.ANY)]
            + [pl.BlockSpec(g.shape, lambda s, *t: (0, 0)) for g in got],
            out_specs=[block, block],
            scratch_shapes=[pltpu.VMEM((rows, columns), BF16), pltpu.SemaphoreType.DMA((1,))],
        ),
        out_shape=[shape(master.shape, F32), shape(momentum.shape, F32)],
        compiler_params=params(SCOPE, dimension_semantics=("arbitrary",)),
        name="optimizer",
    )(big_slots, left_slots, right_slots, tab, a_all, b_all, in_hbm(master), in_hbm(momentum), held, *got)


def layer_norm(values):
    centered = values - jnp.mean(values, -1, keepdims=True)
    inv_std = lax.rsqrt(jnp.mean(centered * centered, -1, keepdims=True) + 1e-06)
    return centered * inv_std, inv_std


def norm_back(grad_out, normed, inv_std):
    return inv_std * (
        grad_out
        - jnp.mean(grad_out, -1, keepdims=True)
        - normed * jnp.mean(grad_out * normed, -1, keepdims=True)
    )


def added(keep_ref, got_ref, far_ref):
    return keep_ref[0] + got_ref[0].astype(F32) + far_ref[...].astype(F32)


def row_of(mods_ref, at):
    return mods_ref[at : at + 1, :]


def enter_kernel(at, noisy_ref, patch_ref, place_ref, mods_ref, stream_ref, inner_ref, normed_ref, inv_ref):
    stream = dot(noisy_ref[...], patch_ref[...]) + place_ref[...]
    stream_ref[...] = stream
    normed, inv = layer_norm(stream)
    inner_ref[...] = (normed * (1.0 + row_of(mods_ref, at[1])) + row_of(mods_ref, at[0])).astype(BF16)
    normed_ref[...] = normed
    inv_ref[...] = jnp.broadcast_to(inv, inv_ref.shape)


def enter(noisy, patch, places, mods, at):
    rows, width = places.shape
    full = shape((rows, width), F32)
    return pl.pallas_call(
        functools.partial(enter_kernel, at),
        out_shape=[full, shape((rows, width), BF16), full, shape((rows, 128), F32)],
        compiler_params=params(SCOPE),
        name="enter",
    )(noisy, patch, places, mods)


def residual_kernel(
    at, keep_ref, got_ref, far_ref, stream_ref, mods_ref, part_ref, next_ref, inner_ref, normed_ref, inv_ref
):
    part = added(keep_ref, got_ref, far_ref)
    part_ref[...] = part
    stream = stream_ref[...] + row_of(mods_ref, at[0]) * part
    next_ref[...] = stream
    normed, inv = layer_norm(stream)
    inner_ref[...] = (normed * (1.0 + row_of(mods_ref, at[2])) + row_of(mods_ref, at[1])).astype(BF16)
    normed_ref[...] = normed
    inv_ref[...] = jnp.broadcast_to(inv, inv_ref.shape)


def residual(parts, stream, mods, at):
    rows, width = stream.shape
    full = shape((rows, width), F32)
    return pl.pallas_call(
        functools.partial(residual_kernel, at),
        out_shape=[full, full, shape((rows, width), BF16), full, shape((rows, 128), F32)],
        compiler_params=params(SCOPE),
        name="residual",
    )(*parts, stream, mods)


def leave_kernel(
    at,
    count_all,
    keep_ref,
    got_ref,
    far_ref,
    stream_ref,
    mods_ref,
    head_ref,
    target_ref,
    grad_ref,
    next_ref,
    rows_ref,
    edge_ref,
):
    branch = added(keep_ref, got_ref, far_ref)
    gate, shift, scale = (row_of(mods_ref, i) for i in at)
    normed, inv = layer_norm(stream_ref[...] + gate * branch)
    inner = (normed * (1.0 + scale) + shift).astype(BF16)
    head = head_ref[...]
    error = dot_nt(inner, head) - target_ref[...]
    d_output = (2.0 * error / count_all).astype(BF16)
    d_inner = dot(d_output, head)
    grad = norm_back(d_inner * (1.0 + scale), normed, inv)
    grad_ref[...] = grad
    next_ref[...] = (gate * grad).astype(BF16)
    rows_ref[...] = jnp.zeros_like(rows_ref)
    rows_ref[0:1, :] = jnp.sum(d_inner, 0, keepdims=True)
    rows_ref[1:2, :] = jnp.sum(d_inner * normed, 0, keepdims=True)
    rows_ref[2:3, :] = jnp.sum(grad * branch, 0, keepdims=True)
    n_patch = head.shape[0]
    loss = jnp.sum(jnp.sum(error * error, 1, keepdims=True), 0, keepdims=True) / count_all
    edge_ref[:n_patch, :] = dot_tn(d_output, inner)
    edge_ref[n_patch:, :] = jnp.broadcast_to(loss, (8, edge_ref.shape[1]))


def leave(parts, stream, mods, head, target, at, count_all):
    rows, width = stream.shape
    return pl.pallas_call(
        functools.partial(leave_kernel, at, count_all),
        out_shape=[
            shape((rows, width), F32),
            shape((rows, width), BF16),
            shape((SMALL_ROWS, width), F32),
            shape((head.shape[0] + 8, width), F32),
        ],
        compiler_params=params(SCOPE),
        name="leave",
    )(*parts, stream, mods, head, target)


def back_kernel(
    at,
    gate_at,
    first,
    keep_ref,
    got_ref,
    far_ref,
    normed_ref,
    inv_ref,
    grad_ref,
    part_ref,
    mods_ref,
    rows_in_ref,
    out_ref,
    next_ref,
    rows_ref,
):
    d_inner = added(keep_ref, got_ref, far_ref)
    normed = normed_ref[...]
    inv = inv_ref[:, 0:1]
    grad = grad_ref[...] + norm_back(d_inner * (1.0 + row_of(mods_ref, at)), normed, inv)
    out_ref[...] = grad
    rows_ref[...] = rows_in_ref[...]
    rows_ref[first : first + 1, :] = jnp.sum(d_inner, 0, keepdims=True)
    rows_ref[first + 1 : first + 2, :] = jnp.sum(d_inner * normed, 0, keepdims=True)
    if gate_at is None:
        next_ref[...] = grad.astype(BF16)
    else:
        next_ref[...] = (row_of(mods_ref, gate_at) * grad).astype(BF16)
        rows_ref[first + 2 : first + 3, :] = jnp.sum(grad * part_ref[...], 0, keepdims=True)


def back(parts, normed, inv, grad, part, mods, rows_in, at, gate_at, first, beside):
    rows, width = grad.shape
    operands = (*parts, normed, inv, grad, part, mods, rows_in)
    return pl.pallas_call(
        past(functools.partial(back_kernel, at, gate_at, first), operands, beside),
        out_shape=[shape((rows, width), F32), shape((rows, width), BF16), shape(rows_in.shape, F32)],
        compiler_params=params(SCOPE),
        name="back",
    )(*operands, *beside)


def tables_kernel(n_patch, fix_ref, edge_ref, time_ref, class_ref, table_ref, first_ref, second_ref, *outs):
    new_ref, first_new_ref, second_new_ref = outs
    at = 0
    for ref, low, count in (
        (edge_ref, 0, n_patch),
        (time_ref, 0, FREQ),
        (class_ref, 0, CLASSES),
        (edge_ref, n_patch, n_patch),
    ):
        rows = slice(at, at + count)
        grad = ref[low : low + count, :]
        first = 0.5 * first_ref[rows, :] + 0.5 * grad
        second = 0.5 * second_ref[rows, :] + 0.5 * grad * grad
        first_new_ref[rows, :] = first
        second_new_ref[rows, :] = second
        new_ref[rows, :] = table_ref[rows, :] * (1.0 - LR_ADAM * WEIGHT_DECAY) - LR_ADAM * (
            first / fix_ref[0]
        ) / (jnp.sqrt(second / fix_ref[0]) + 1e-08)
        at += count


def update_tables(n_patch, bias_fix, edges, grad_time, grad_class, table, first, second):
    return pl.pallas_call(
        functools.partial(tables_kernel, n_patch),
        out_shape=[shape(table.shape, F32)] * 3,
        in_specs=[SMEM_SPEC] + [VMEM_SPEC] * 6,
        compiler_params=params(SCOPE),
        name="update_tables",
    )(bias_fix, edges, grad_time, grad_class, table, first, second)


def position_rows(first, rows):
    quarter = D // 4
    omega = jnp.exp(-math.log(10000.0) * jnp.arange(quarter, dtype=F32) / quarter)
    places = first + jnp.arange(rows, dtype=jnp.int32)
    rows_at = (places // GRID).astype(F32)[:, None] * omega[None]
    cols_at = (places % GRID).astype(F32)[:, None] * omega[None]
    return jnp.concatenate([jnp.sin(rows_at), jnp.cos(rows_at), jnp.sin(cols_at), jnp.cos(cols_at)], 1)


def time_features(timesteps):
    half_freq = FREQ // 2
    rates = jnp.exp(-math.log(10000.0) * jnp.arange(half_freq, dtype=F32) / half_freq)
    angles = timesteps.astype(F32)[:, None] * rates[None]
    return jnp.concatenate([jnp.cos(angles), jnp.sin(angles)], 1)


def shards(
    noisy_latents,
    noise_target,
    timesteps,
    labels,
    owners,
    step_count,
    master_bank,
    momentum_bank,
    embed_tables,
    embed_first,
    embed_second,
):
    n_lat, n_tok, n_patch = noisy_latents.shape
    n_slots, width, columns = master_bank.shape
    n_units = owners.shape[0]
    n_data = lax.axis_size("dp")
    my_data = lax.axis_index("dp")
    my_tensor = lax.axis_index("tensor")
    n_all = n_lat * n_data
    own_rows = n_lat * n_tok // 4
    count_all = float(n_all * n_tok * n_patch)
    depth = 2 if n_data <= 8 else 1
    steps = N_BIG + (n_data - 2) * depth

    unit_order = jnp.arange(n_units, dtype=jnp.int32)
    same_owner = owners[:, None] == owners[None, :]
    slot_of = jnp.sum((same_owner & (unit_order[None, :] < unit_order[:, None])).astype(jnp.int32), 1)
    mine = (owners[None, :] == my_data) & (
        slot_of[None, :] == jnp.arange(n_slots, dtype=jnp.int32)[:, None]
    )
    kind = [2 + 2 * g + (b >= low + (3, 4)[g % 2]) for g, (low, high) in enumerate(GROUPS) for b in range(low, high)]
    slot_tables = np.stack(
        [
            BIG_OF,
            SMALL_OF,
            np.where(BIG_OF >= 0, np.array(kind)[BIG_OF], np.where(SMALL_OF == TIME_AT, 1, 0)),
            np.where(BIG_OF >= 0, SMALL_ROWS + BIG_OF, SMALL_OF),
        ]
    )
    slots = jnp.sum(jnp.where(mine[None], jnp.asarray(slot_tables + 1, jnp.int32)[:, None], 0), 2) - 1
    owners_big = jnp.concatenate([owners[18 * l : 18 * l + BIG] for l in range(LAYERS)])
    tab = ring_schedule(owners_big, n_data, steps, depth, my_data)

    def flag(value):
        return jnp.asarray(value, jnp.int32).reshape(1)

    first_row = my_tensor * own_rows
    early = dict(
        slots=slots,
        chip=flag(my_tensor // 2),
        core=flag(my_tensor % 2),
        data=flag(my_data),
        place=flag(jnp.sum(jnp.where(jnp.arange(n_data) == my_data, np.argsort(ring_order(n_data)), 0))),
        bits=[flag((my_data // (1 << i)) % 2) for i in range((n_data - 1).bit_length())],
        time_mine=flag(owners[18 * LAYERS] == my_data),
        time_w2=lax.dynamic_index_in_dim(master_bank, slot_of[18 * LAYERS], 0, keepdims=False).astype(BF16),
        noisy=lax.dynamic_slice_in_dim(noisy_latents.reshape(n_lat * n_tok, n_patch), first_row, own_rows, 0),
        target=lax.dynamic_slice_in_dim(noise_target.reshape(n_lat * n_tok, n_patch), first_row, own_rows, 0),
        places=position_rows(first_row % n_tok, own_rows),
        ids=jnp.stack([timesteps, labels], 1),
        bias_fix=1.0 - jnp.power(0.5, step_count.astype(F32)),
        tab=tab,
        edge_cols=jnp.concatenate(
            [embed_tables[:n_patch], embed_tables[n_patch + FREQ + CLASSES :]], 0
        ).astype(BF16),
        time_w1=embed_tables[n_patch : n_patch + FREQ].astype(BF16),
        class_w=embed_tables[n_patch + FREQ : n_patch + FREQ + CLASSES].astype(BF16),
    )
    flat, tree = jax.tree.flatten(early)
    early = jax.tree.unflatten(tree, lax.optimization_barrier(tuple(flat)))
    chip, core, data, time_w2, noisy_own = (early[k] for k in ("chip", "core", "data", "time_w2", "noisy"))
    tab = early["tab"]
    big_slots, small_slots, left_slots, right_slots = (early["slots"][i] for i in range(4))
    spread = Spreader(tab, spread_init(early["slots"], master_bank), n_data, steps, depth)
    spread.step()
    ring = Reducer(tab, n_data, steps, depth)

    def conditioning():
        ids, edge_rows = yield from together(
            dp_sum(own_latents(early["ids"], 0, data, n_data), n_data),
            gather_columns(early["edge_cols"], chip, core),
        )
        features = time_features(ids[:, 0]).astype(BF16)
        time_one = jnp.dot(features, early["time_w1"], preferred_element_type=F32)
        time_act = yield from gather_columns(jax.nn.silu(time_one).astype(BF16), chip, core)
        second = jnp.dot(time_act, time_w2, preferred_element_type=F32)
        second = yield from dp_sum(jnp.where(is_at(early["time_mine"], 1, 2), second, 0.0), n_data)
        onehot = ids[:, 1:2] == jnp.arange(CLASSES, dtype=jnp.int32)[None]
        condition = second + jnp.dot(onehot.astype(BF16), early["class_w"], preferred_element_type=F32)
        cond_in = yield from gather_columns(jax.nn.silu(condition).astype(BF16), chip, core)
        (mods,) = spread.work(modulations(small_slots, cond_in, master_bank), ISSUED)
        ISSUED.clear()
        bit = n_data // 2
        while bit:
            half = mods.shape[1] // 2
            sides = mods[:, :half], mods[:, half:]
            side = early["bits"][bit.bit_length() - 1]
            mods = pick(*sides, side) + (yield flip(pick(*sides, side, True), "dp", bit, n_data))
            bit //= 2
        latents = mods[:, 0], mods[:, 1]
        across = yield x_flip(pick(*latents, chip, True))
        own = pick(*latents, chip)
        pair = [pick(own, across, chip), pick(across, own, chip)]
        beside = core_flip(jnp.concatenate(pair, 1))
        beside = [beside[:, x * columns : (x + 1) * columns] for x in range(2)]
        blocks = [pick(one, two, core) for x in range(2) for one, two in ((pair[x], beside[x]), (beside[x], pair[x]))]
        return edge_rows, features, time_one, time_act, onehot, condition, cond_in, jnp.concatenate(blocks, 1)

    def forward():
        cond = yield from conditioning()
        edge_rows, mods = cond[0], cond[-1]
        stream, inner, normed, inv = enter(
            noisy_own, edge_rows[:n_patch], early["places"], mods, (small_at(0, 0), small_at(0, 1))
        )
        kept = []
        for layer in range(LAYERS):
            inner = yield from gather_tokens(inner)
            spread.prepare(2 * layer)
            qkv, mixed, keep, send = spread.work(attention(inner, columns, BIG * layer, n_lat))
            parts = yield from scatter_tokens(keep, send)
            attended, stream, inner_mid, normed_mid, inv_mid = residual(
                parts, stream, mods, tuple(small_at(layer, i) for i in (2, 3, 4))
            )
            inner_mid = yield from gather_tokens(inner_mid)
            spread.prepare(2 * layer + 1)
            hidden, active, keep, send = spread.work(mlp(inner_mid, columns, BIG * layer + 4))
            parts = yield from scatter_tokens(keep, send)
            kept.append([inner, normed, inv, qkv, mixed, attended, inner_mid, normed_mid, inv_mid, hidden, active])
            if layer + 1 < LAYERS:
                branch, stream, inner, normed, inv = residual(
                    parts,
                    stream,
                    mods,
                    (small_at(layer, 5), small_at(layer + 1, 0), small_at(layer + 1, 1)),
                )
                kept[-1].append(branch)
        return cond, kept, parts, stream

    cond, kept, parts_last, stream_last = drive(forward(), spread.step)
    edge_rows, features, time_one, time_act, onehot, condition, cond_in, mods = cond
    ring.held = spread.held

    def backward():
        grad, d_branch, rows, edge_head = leave(
            parts_last,
            stream_last,
            mods,
            edge_rows[n_patch:],
            early["target"],
            (small_at(LAYERS - 1, 5), SHIFT_F, SCALE_F),
            count_all,
        )
        lefts, rights = {}, {}
        for layer in reversed(range(LAYERS)):
            inner, normed, inv, qkv, mixed, attended, inner_mid, normed_mid, inv_mid, hidden, active = kept[layer][:11]
            d_branch = yield from gather_tokens(d_branch)
            d_hidden, keep, send = ring.work(mlp_back(d_branch, hidden, BIG * layer + 4))
            work = scatter_tokens(keep, send)
            flying = next(work)
            lefts[2 * layer + 1], rights[2 * layer + 1] = ring.work(
                weight_grads(BIG * layer + 4, [(inner_mid, d_hidden), (d_branch, active)], n_lat), ISSUED
            )
            ring.ready = BIG * layer + 4
            parts = finish(work, order(flying, (lefts[2 * layer + 1],) + ring.sent))
            grad, d_attended, rows = back(
                parts,
                normed_mid,
                inv_mid,
                grad,
                attended,
                mods,
                rows,
                small_at(layer, 4),
                small_at(layer, 2),
                small_at(layer, 3),
                [ring.held],
            )
            d_attended = yield from gather_tokens(d_attended)
            d_qkv, keep, send = ring.work(attention_back(d_attended, qkv, BIG * layer, n_lat))
            work = scatter_tokens(keep, send)
            flying = next(work)
            lefts[2 * layer], rights[2 * layer] = ring.work(
                weight_grads(BIG * layer, [(inner, d_qkv), (d_attended, mixed[None])], n_lat), ISSUED
            )
            ring.ready = BIG * layer
            parts = finish(work, order(flying, (lefts[2 * layer],) + ring.sent))
            below = kept[layer - 1][11] if layer else normed
            grad, d_branch, rows = back(
                parts,
                normed,
                inv,
                grad,
                below,
                mods,
                rows,
                small_at(layer, 1),
                small_at(layer - 1, 5) if layer else None,
                small_at(layer, 0),
                [ring.held],
            )
        return (yield from cond_backward(rows, d_branch, edge_head, lefts, rights))

    def cond_backward(rows, d_stream, edge_head, lefts, rights):
        mine = core_columns_sum(rows, core)
        near, far = pick(*mine, chip), (yield x_flip(pick(*mine, chip, True)))
        own = [pick(near, far, chip).astype(BF16), pick(far, near, chip).astype(BF16)]
        if n_data == 8:
            latents = yield from ring.gather(jnp.concatenate(own, 0), early["place"])
            d_small = jnp.stack([v[l * SMALL_ROWS : (l + 1) * SMALL_ROWS] for v in latents for l in range(n_lat)], 1)
        else:
            d_small = yield from dp_sum(own_latents(jnp.stack(own, 1), 1, data, n_data), n_data)
        (d_cond,) = ring.work(cond_back(small_slots, d_small, master_bank), ISSUED)
        ISSUED.clear()
        d_cond = yield from own_columns_sum(d_cond, chip, core)
        if n_data == 8:
            parts = yield from ring.gather(jnp.concatenate(halves(d_cond), 0), early["place"])
            d_cond = sum(p[:n_all].astype(F32) + p[n_all:].astype(F32) for p in parts)
        else:
            d_cond = yield from dp_sum(d_cond, n_data)
        unused, silu_pull = jax.vjp(jax.nn.silu, condition)
        d_condition = silu_pull(d_cond)[0]
        d_second = d_condition.astype(BF16)
        grad_class = lax.dot_general(
            onehot.astype(F32), d_condition, (((0,), (0,)), ((), ())), precision=HIGHEST_PREC
        )
        d_time_act = lax.dot_general(d_second, time_w2, (((1,), (1,)), ((), ())), preferred_element_type=F32)
        d_time_act = jnp.where(is_at(early["time_mine"], 1, 2), d_time_act, 0.0)
        grad_patch = lax.dot_general(noisy_own, d_stream, (((0,), (0,)), ((), ())), preferred_element_type=F32)
        sums = yield from own_columns_sum(jnp.concatenate([d_time_act, grad_patch, edge_head], 0), chip, core)
        ring.drain()
        sums, (a_rows, b_rows) = yield from together(
            dp_sum(order(sums, ring.last()), n_data), factor_rows(lefts, rights, ring.last())
        )
        d_time_act, edges = sums[:n_all], sums[n_all:]
        unused, time_pull = jax.vjp(jax.nn.silu, time_one)
        d_time_one = time_pull(d_time_act)[0].astype(BF16)
        grad_time_one = lax.dot_general(
            features, d_time_one, (((0,), (0,)), ((), ())), preferred_element_type=F32
        )
        return d_small, d_second, grad_class, grad_time_one, edges, (a_rows, b_rows)

    def factor_rows(lefts, rights, after):
        a_rows = jnp.concatenate([lefts[g][:, :n_lat] for g in range(len(GROUPS))], 0).transpose(1, 0, 2)
        b_rows = jnp.concatenate([rights[g][:, :n_lat] for g in range(len(GROUPS))], 0).transpose(1, 0, 2)
        n_left = a_rows.shape[1]
        packed = jnp.concatenate(
            [a_rows[:, :, j * columns : (j + 1) * columns] for j in range(4)] + [b_rows], 1
        ).astype(BF16)
        packed = yield from dp_rows(order(packed, after), n_data)
        a_rows = jnp.concatenate([packed[:, j * n_left : (j + 1) * n_left] for j in range(4)], 2)
        return a_rows.transpose(1, 0, 2), packed[:, 4 * n_left :].transpose(1, 0, 2)

    d_small, d_second, grad_class, grad_time_one, edges, (a_rows, b_rows) = drive(backward(), ring.step)
    loss = edges[2 * n_patch, 0]
    a_all = jnp.concatenate([cond_in[None], time_act[None], a_rows], 0)
    small_rows = jnp.where(jnp.arange(SMALL_ROWS)[:, None, None] == TIME_AT, d_second[None], d_small)
    b_all = jnp.concatenate([small_rows, b_rows], 0)
    master_new, momentum_new = optimizer(
        big_slots, left_slots, right_slots, tab, a_all, b_all, master_bank, momentum_bank, ring.held, ring.last()
    )
    embed_new, first_new, second_new = update_tables(
        n_patch, early["bias_fix"], edges, grad_time_one, grad_class, embed_tables, embed_first, embed_second
    )
    return (loss, master_new, momentum_new, embed_new, first_new, second_new)


def solution(mesh):
    placed = (
        P("dp", None, None),
        P("dp", None, None),
        P("dp"),
        P("dp"),
        P(),
        P(),
        P("dp", None, "tensor"),
        P("dp", None, "tensor"),
        P(None, "tensor"),
        P(None, "tensor"),
        P(None, "tensor"),
    )
    return jax.shard_map(
        shards,
        mesh=mesh,
        in_specs=placed,
        out_specs=(
            P(),
            P("dp", None, "tensor"),
            P("dp", None, "tensor"),
            P(None, "tensor"),
            P(None, "tensor"),
            P(None, "tensor"),
        ),
        check_vma=False,
    )
```

```python
import functools
import math

import jax
import jax.numpy as jnp
import numpy as np
from jax import lax
from jax.experimental import pallas as pl
from jax.experimental.pallas import tpu as pltpu
from jax.sharding import PartitionSpec as P

D = 1024
HEAD_DIM = 64
FREQ = 256
CLASSES = 1000
GRID = 16
LAYERS = 2
BIG = 12
N_BIG = BIG * LAYERS
SMALL_ROWS = 16
SHIFT_F, SCALE_F, TIME_AT = 0, 1, 6 * LAYERS + 2


def small_at(layer, i):
    first = 2 + 6 * (LAYERS - 1 - layer)
    return first + (4, 5, 3, 1, 2, 0)[i]


NS_COEF = (3.4445, -4.775, 2.0315)
LR_MUON = 0.5
LR_ADAM = 0.02
WEIGHT_DECAY = 0.1
SCORE_SCALE = 1.0 / math.sqrt(HEAD_DIM)
HIGHEST_PREC = lax.Precision.HIGHEST

F32 = jnp.float32
BF16 = jnp.bfloat16
SCOPE = 16
GELU_C = math.sqrt(2.0 / math.pi)
GROUPS = ((0, 4), (4, 12), (12, 16), (16, 24))


def unit_tables():
    big, small = [], []
    for u in range(18 * LAYERS):
        layer, place = divmod(u, 18)
        big.append(layer * BIG + place if place < BIG else -1)
        small.append(-1 if place < BIG else small_at(layer, place - BIG))
    return np.array(big + [-1] * 3), np.array(small + [TIME_AT, SHIFT_F, SCALE_F])


BIG_OF, SMALL_OF = unit_tables()


def params(limit, **more):
    return pltpu.CompilerParams(vmem_limit_bytes=limit * 1024 * 1024, **more)


SMEM_SPEC = pl.BlockSpec(memory_space=pltpu.SMEM)
VMEM_SPEC = pl.BlockSpec(memory_space=pltpu.VMEM)


def in_hbm(values):
    return pltpu.with_memory_space_constraint(values, pltpu.HBM)


def dot(a, b):
    return lax.dot_general(a, b, (((1,), (0,)), ((), ())), preferred_element_type=F32)


def dot_nt(a, b):
    return lax.dot_general(a, b, (((1,), (1,)), ((), ())), preferred_element_type=F32)


def dot_tn(a, b):
    return lax.dot_general(a, b, (((0,), (0,)), ((), ())), preferred_element_type=F32)


def shape(dims, kind):
    return jax.ShapeDtypeStruct(dims, kind)


ISSUED = []


def order(values, after):
    if not after:
        return values
    flat, tree = jax.tree.flatten(values)
    tied = lax.optimization_barrier(tuple(flat) + tuple(after))
    return jax.tree.unflatten(tree, tied[: len(flat)])


def drive(work, line):
    ISSUED.clear()
    try:
        value = next(work)
        while True:
            after = tuple(ISSUED)
            ISSUED.clear()
            value = work.send(order(value, line(after)))
    except StopIteration as end:
        return end.value


def together(*works):
    ends, flying = [None] * len(works), {}

    def go(i, step):
        try:
            flying[i] = step()
        except StopIteration as end:
            flying.pop(i, None)
            ends[i] = end.value

    for i, work in enumerate(works):
        go(i, lambda: next(work))
    while flying:
        got = yield dict(flying)
        for i in list(got):
            go(i, lambda: works[i].send(got[i]))
    return ends


def finish(work, value):
    try:
        work.send(value)
    except StopIteration as end:
        return end.value
    raise AssertionError


def flip(values, axis, bit, size):
    ISSUED.append(values)
    got = lax.ppermute(values, axis, [(i, i ^ bit) for i in range(size)])
    if axis == "tensor" and values.size < 2**16:
        ISSUED.append(got)
    return got


def is_at(flag, value, ndim):
    return flag.reshape((1,) * ndim) == value


def pick(low, high, place, other=False):
    return jnp.where(is_at(place, 1 if other else 0, low.ndim), low, high)


def own_latents(values, axis, data, n_data):
    n_lat = values.shape[axis]
    dims = values.shape[:axis] + (n_lat * n_data,) + values.shape[axis + 1 :]
    at = lax.broadcasted_iota(jnp.int32, dims, axis)
    first = data.reshape((1,) * len(dims)) * n_lat
    placed = jnp.zeros(dims, values.dtype)
    for l in range(n_lat):
        placed = jnp.where(at == first + l, lax.slice_in_dim(values, l, l + 1, axis=axis), placed)
    return placed


def dp_sum(values, n_data):
    bit = 1
    while bit < n_data:
        values = values + (yield flip(values, "dp", bit, n_data))
        bit *= 2
    return values


def dp_rows(values, n_data):
    bit = 1
    while bit < n_data:
        values = jnp.concatenate([values, (yield flip(values, "dp", bit, n_data))], 0)
        bit *= 2
    return values


def core_flip(values):
    return flip(values, "tensor", 1, 4)


def x_flip(values):
    return flip(values, "tensor", 2, 4)


def gather_tokens(own):
    beside, across = yield (core_flip(own), x_flip(own))
    return own, beside, across, core_flip(across)


def gather_columns(own, chip, core):
    beside, across = yield (core_flip(own), x_flip(own))
    corner = core_flip(across)
    at_core = [is_at(core, i, own.ndim) for i in range(2)]
    at_chip = [is_at(chip, i, own.ndim) for i in range(2)]
    near = [jnp.where(at_core[i], own, beside) for i in range(2)]
    far = [jnp.where(at_core[i], across, corner) for i in range(2)]
    parts = [jnp.where(at_chip[i], near[j], far[j]) for i in range(2) for j in range(2)]
    return jnp.concatenate(parts, -1)


def scatter_tokens(keep, send):
    got = core_flip(send)
    far = (keep[1] + got[1].astype(F32)).astype(BF16)
    return keep, got, (yield x_flip(far))


def core_columns(values, core, other=False):
    size = values.shape[-1] // 4
    block = [lax.slice_in_dim(values, j * size, (j + 1) * size, axis=values.ndim - 1) for j in range(4)]
    return [pick(block[2 * x], block[2 * x + 1], core, other) for x in range(2)]


def core_columns_sum(values, core):
    got = core_flip(jnp.concatenate(core_columns(values, core, True), -1))
    size = got.shape[-1] // 2
    return [
        mine + lax.slice_in_dim(got, x * size, (x + 1) * size, axis=got.ndim - 1)
        for x, mine in enumerate(core_columns(values, core))
    ]


def own_columns_sum(values, chip, core):
    mine = core_columns_sum(values, core)
    return pick(*mine, chip) + (yield x_flip(pick(*mine, chip, True)))


def sum_of_columns(values, chip, core, n_data):
    return (yield from dp_sum((yield from own_columns_sum(values, chip, core)), n_data))


def ring_order(n_data):
    return [0, 2, 4, 6, 7, 5, 3, 1] if n_data == 8 else list(range(n_data))


def plan_kernel(n_units, n_slots, steps, depth, n_data, me_ref, owner_ref, table_ref, tab_ref, slot_ref):
    me = me_ref[0]
    place_of = [int(v) for v in np.argsort(ring_order(n_data))]
    my_place = sum(jnp.where(me == d, place_of[d], 0) for d in range(n_data))
    owner = owner_ref[...]
    across = jnp.broadcast_to(owner, (128, 128))
    before = lax.broadcasted_iota(jnp.int32, (128, 128), 0) < lax.broadcasted_iota(jnp.int32, (128, 128), 1)
    slot = jnp.sum(jnp.where((across == across.T) & before, 1.0, 0.0), 0, keepdims=True)
    mine = owner == me.astype(F32)
    lane8 = lax.broadcasted_iota(jnp.int32, (8, 128), 1)
    row8 = lax.broadcasted_iota(jnp.int32, (8, 128), 0)
    result = jnp.full((8, 128), -1, jnp.int32)
    for s in range(n_slots):
        held = mine & (slot == s)
        value = jnp.sum(jnp.where(held, table_ref[...], 0), 1, keepdims=True) - 1
        result = jnp.where((lane8 == s) & (row8 < 4), value, result)
    lane1 = lax.broadcasted_iota(jnp.int32, (1, 128), 1)
    time = lane1 == 18 * LAYERS
    time_slot = jnp.sum(jnp.where(time, slot, 0.0), 1, keepdims=True).astype(jnp.int32)
    time_mine = jnp.sum(jnp.where(time & mine, 1.0, 0.0), 1, keepdims=True).astype(jnp.int32)
    result = jnp.where((row8 == 4) & (lane8 == 0), time_slot, result)
    result = jnp.where((row8 == 4) & (lane8 == 1), time_mine, result)
    peers = jnp.full((1, 128), -1, jnp.int32)
    place = jnp.full((1, 128), -9, jnp.int32)
    for d in range(n_data):
        ahead = place_of[d] - my_place
        peers = jnp.where(lane1 == jnp.where(ahead < 0, ahead + n_data, ahead), d, peers)
        place = jnp.where(owner == float(d), place_of[d], place)
    slot_ref[...] = jnp.where(row8 == 5, peers, result)

    big = jnp.where(lane1 < BIG, place, pltpu.roll(place, 128 - 6, 1))
    big = jnp.where(lane1 < N_BIG, big, -9)
    back = jnp.where(big >= 0, n_data - 1 - big, -9)
    lane = lax.broadcasted_iota(jnp.int32, (n_data, 128), 1)
    row = lax.broadcasted_iota(jnp.int32, (n_data, 128), 0)
    follow = jnp.where(row == n_data - 1, 0, row + 1)
    own = [(row == at).astype(jnp.int32) for at in (big, back)]
    open_to = [(follow != at).astype(jnp.int32) for at in (big, back)]
    spots = [my_place, n_data - 1 - my_place]
    far = jnp.int32(999)

    def step(t, carry):
        line = jnp.full((1, 128), -1, jnp.int32)
        after = []
        for way in range(2):
            have, sent, *coming = carry[way]
            here = spots[way]
            prior = jnp.where(here == 0, n_data - 1, here - 1)
            open_now = have * (1 - sent) * open_to[way]
            first = jnp.min(jnp.where(open_now > 0, lane, far), axis=1, keepdims=True)
            chosen = (lane == first).astype(jnp.int32)
            first = jnp.broadcast_to(first, (n_data, 128))
            for k, who in enumerate((here, prior)):
                index = jnp.min(jnp.where(row == who, first, far), axis=0, keepdims=True)
                index = jnp.where(index == far, -1, index)
                line = jnp.where(lane1 == 2 * way + k, index, line)
            coming = list(coming) + [pltpu.roll(chosen, 1, 0)]
            after.append((have + coming[0], sent + chosen, *coming[1:]))
        tab_ref[pl.ds(t, 1), :] = line
        return tuple(after)

    none = jnp.zeros((n_data, 128), jnp.int32)
    lax.fori_loop(0, steps, step, tuple((own[way], none) + (none,) * (depth - 1) for way in range(2)))


def plan(owners, tables, n_slots, n_data, steps, depth, my_data):
    n_units = owners.shape[0]
    padded = jnp.pad(owners.astype(F32), (0, 128 - n_units), constant_values=-1.0)[None]
    wide = np.zeros((8, 128), np.int32)
    wide[: len(tables), :n_units] = tables + 1
    tab, rows = pl.pallas_call(
        functools.partial(plan_kernel, n_units, n_slots, steps, depth, n_data),
        out_shape=[shape((steps, 128), jnp.int32), shape((8, 128), jnp.int32)],
        in_specs=[SMEM_SPEC, VMEM_SPEC, VMEM_SPEC],
        out_specs=[VMEM_SPEC, VMEM_SPEC],
        compiler_params=params(SCOPE),
        name="plan",
    )(my_data.reshape(1), padded, jnp.asarray(wide))
    return tab[:, :4], rows


def spread_init_kernel(slots_ref, bank_ref, out_ref, wide, sem):
    big_ref = [slots_ref[0, s] for s in range(bank_ref.shape[0])]
    n_slots = bank_ref.shape[0]
    for s in range(n_slots):
        copy = pltpu.make_async_copy(bank_ref.at[s], wide.at[s], sem.at[s])
        pl.when(big_ref[s] >= 0)(copy.start)
    for s in range(n_slots):
        copy = pltpu.make_async_copy(bank_ref.at[s], wide.at[s], sem.at[s])
        pl.when(big_ref[s] >= 0)(copy.wait)

        @pl.when(big_ref[s] >= 0)
        def _(s=s):
            out_ref[jnp.maximum(big_ref[s], 0)] = wide[s].astype(BF16)


def spread_init(big_slots, master_bank):
    n_slots, rows, columns = master_bank.shape
    return pl.pallas_call(
        spread_init_kernel,
        out_shape=pltpu.VMEM((N_BIG + BIG, rows, columns), BF16),
        in_specs=[SMEM_SPEC, pl.BlockSpec(memory_space=pltpu.HBM)],
        out_specs=VMEM_SPEC,
        scratch_shapes=[
            pltpu.VMEM((n_slots, rows, columns), F32),
            pltpu.SemaphoreType.DMA((n_slots,)),
        ],
        compiler_params=params(SCOPE),
        name="own_weights",
    )(big_slots, in_hbm(master_bank))


def spread_kernel(places, fetch_at, tab_ref, got, held, out):
    half = held.shape[1] // 2
    for way in range(2):
        rows = pl.ds(way * half, half)
        for k, t in enumerate(places):
            unit = tab_ref[t, 2 * way + 1]

            @pl.when(unit >= 0)
            def _():
                held[jnp.maximum(unit, 0), rows] = got[2 * k + way][...]

        if fetch_at is not None:
            out[way][...] = held[jnp.maximum(tab_ref[fetch_at, 2 * way], 0), rows]


def ring_step(name, tab, held, got, sends, body, work=None, mail=(), mail_rows=0, keep_rows=0):
    rows, columns = held.shape[1:]
    extra, more, operands, shapes, scratch = (tuple(work) + ([],))[:5] if work else ("", None, [], [], [])
    specs = [value[1] if isinstance(value, tuple) else VMEM_SPEC for value in operands]
    operands = [value[0] if isinstance(value, tuple) else value for value in operands]
    operands, specs = list(mail) + list(operands), [VMEM_SPEC] * len(mail) + specs
    n, m, k = len(got), len(operands), len(mail)
    kept = 2 if keep_rows else 0
    shapes = [pltpu.VMEM((keep_rows, columns), BF16)] * kept + list(shapes)

    def kernel(tab_ref, *refs):
        out = refs[n + 1 + m :]
        if body is not None:
            body(tab_ref, refs[:n], out[0], out[1 : 1 + sends], *([refs[n + 1 : n + 1 + k]] if k else []))
        for way in range(kept):
            out[1 + sends + way][...] = refs[way][refs[way].shape[0] - keep_rows :]
        if more is not None:
            more(out[0], *refs[n + 1 + k : n + 1 + m], *out[1 + sends + kept :])

    res = pl.pallas_call(
        kernel,
        out_shape=[pltpu.VMEM(held.shape, held.dtype)] + [pltpu.VMEM((rows // 2 + mail_rows, columns), BF16)] * sends
        + list(shapes),
        in_specs=[SMEM_SPEC] + [VMEM_SPEC] * (n + 1) + specs,
        out_specs=[VMEM_SPEC] * (1 + sends + len(shapes)),
        scratch_shapes=scratch,
        input_output_aliases={1 + n: 0},
        compiler_params=params(SCOPE),
        name=name + extra,
    )(tab, *got, held, *operands)
    return res[0], list(res[1 : 1 + sends]), list(res[1 + sends :])


def ring_perms(n_data):
    order = ring_order(n_data)
    ahead = [(order[i], order[(i + 1) % n_data]) for i in range(n_data)]
    return ahead, [(b, a) for a, b in ahead]


class Spreader:
    def __init__(self, tab, held, n_data, steps, depth):
        self.tab, self.n_data, self.steps, self.depth = tab, n_data, steps, depth
        self.perms = ring_perms(n_data)
        self.held = held
        self.got = {}
        self.at = 0

    def last(self, g):
        return GROUPS[g][1] - 1 + (self.n_data - 2) * self.depth

    def step(self, after=()):
        self.work(None, after)
        return self.sent

    def work(self, work, after=()):
        t = self.at
        self.sent = ()
        if t > self.steps:
            return []
        fetch_at = t if t < self.steps else None
        places = [t - self.depth] if fetch_at is not None else list(range(self.steps - self.depth, self.steps))
        places = [p for p in places if p >= 0]
        self.held, sends, results = ring_step(
            "spread_step",
            order(self.tab, after),
            self.held,
            [value for p in places for value in self.got.pop(p)],
            0 if fetch_at is None else 2,
            functools.partial(spread_kernel, places, fetch_at),
            work,
        )
        if fetch_at is not None:
            self.got[t] = [lax.ppermute(sends[way], "dp", self.perms[way]) for way in range(2)]
        self.at += 1
        self.sent = tuple(sends) + tuple(self.got.get(t - 1, ()))
        return order(results, tuple(self.got.get(t - 1, ())))

    def prepare(self, g):
        while self.at < min(self.last(g) + self.depth, self.steps):
            self.step()


def reduce_kernel(place_at, fetch_at, mail, tab_ref, got, held, out, own=()):
    half = held.shape[1] // 2
    if mail:
        for way in range(2):
            out[way][half:] = own[0][...] if mail == "own" else got[way][half:]
    for way in range(2):
        rows = pl.ds(way * half, half)
        if place_at is not None:
            unit = tab_ref[place_at, 2 * way]

            @pl.when(unit >= 0)
            def _():
                at = BIG + jnp.maximum(unit, 0)
                held[at, rows] = (held[at, rows].astype(F32) + got[way][:half].astype(F32)).astype(BF16)

        out[way][:half] = held[BIG + jnp.maximum(tab_ref[fetch_at, 2 * way + 1], 0), rows]


class Reducer:
    def __init__(self, tab, n_data, steps, depth):
        self.tab, self.n_data, self.steps, self.depth = tab, n_data, steps, depth
        self.perms = [p for p in reversed(ring_perms(n_data))]
        self.held = None
        self.ready = N_BIG
        self.mail = {}
        self.come = {}
        self.got = {}
        self.at = 0

    def lowest(self, k):
        return (self.steps - 1 - k) - (self.n_data - 2) * self.depth

    def step(self, after=()):
        k = self.at
        self.sent = ()
        if k < self.steps and max(self.lowest(k), 0) >= self.ready:
            self.work(None, after)
        return self.sent

    def work(self, work, after=()):
        k = self.at
        self.sent = ()
        tab = order(self.tab, after)
        if k >= self.steps or max(self.lowest(k), 0) < self.ready:
            self.held, unused, results = ring_step("layer_", tab, self.held, [], 0, None, work)
            return results
        place_at = self.steps - 1 - (k - self.depth) if k >= self.depth else None
        payload, hops = self.mail.get(k, (None, 0))
        mail = None if payload is None else "own" if hops == 0 else "pass"
        keep_rows = self.mail[k - self.depth][0].shape[0] if k - self.depth in self.mail else 0
        self.held, sends, results = ring_step(
            "reduce_step",
            tab,
            self.held,
            self.got.get(k - self.depth, []),
            2,
            functools.partial(reduce_kernel, place_at, self.steps - 1 - k, mail),
            work,
            [payload] if mail == "own" else [],
            0 if payload is None else payload.shape[0],
            keep_rows,
        )
        if keep_rows:
            self.come[k - self.depth], results = results[:2], results[2:]
        self.got[k] = [lax.ppermute(sends[way], "dp", self.perms[way]) for way in range(2)]
        self.at += 1
        self.sent = tuple(sends) + tuple(self.got.get(k - 1, ()))
        return order(results, tuple(self.got.get(k - 1, ())))

    def gather(self, *payloads):
        far = self.n_data // 2
        starts = [self.at + i for i in range(len(payloads))]
        for start, payload in zip(starts, payloads):
            for j in range(far):
                self.mail[start + j * self.depth] = (payload, j)
        last = starts[-1] + far * self.depth
        assert len(payloads) <= self.depth and last < self.steps
        while self.at <= last:
            yield ()
        everyone = []
        for start, payload in zip(starts, payloads):
            come = [[self.come[start + j * self.depth][way] for j in range(far)] for way in range(2)]
            everyone.append(order([payload] + come[0][: far - 1] + come[1][::-1], self.sent))
        return everyone

    def drain(self):
        while self.at < self.steps:
            self.step()

    def last(self):
        return [self.got[self.steps - 1 - t][way] for t in range(self.depth) for way in range(2)]


def past(kernel, operands, beside):
    n, m = len(operands), len(beside)
    return lambda *refs: kernel(*refs[:n], *refs[n + m :])


def split_rows(total, keep_ref, send_ref):
    rows = total.shape[0] // 4
    for i in range(2):
        keep_ref[i] = total[2 * i * rows : (2 * i + 1) * rows]
        send_ref[i] = total[(2 * i + 1) * rows : (2 * i + 2) * rows].astype(BF16)


def part_shapes(rows, width):
    return [shape((2, rows // 4, width), F32), shape((2, rows // 4, width), BF16)]


def joined(refs):
    return jnp.concatenate([r[...] for r in refs], 0)


def softmax_parts(q, k):
    scores = dot_nt(q, k) * SCORE_SCALE
    expo = jnp.exp(scores - jnp.max(scores, -1, keepdims=True))
    return expo / jnp.sum(expo, -1, keepdims=True)


def attention_kernel(n_lat, base, w_ref, x0, x1, x2, x3, qkv_ref, mixed_ref, keep_ref, send_ref):
    x = joined((x0, x1, x2, x3))
    for j in range(3):
        qkv_ref[j] = dot(x, w_ref[base + j]).astype(BF16)
    toks = x.shape[0] // n_lat
    heads = w_ref.shape[2] // HEAD_DIM
    for l in range(n_lat):
        rows = slice(l * toks, (l + 1) * toks)
        outs = []
        for h in range(heads):
            cols = slice(h * HEAD_DIM, (h + 1) * HEAD_DIM)
            q, k, v = (qkv_ref[j, rows, cols] for j in range(3))
            outs.append(dot(softmax_parts(q, k).astype(BF16), v))
        mixed_ref[rows, :] = jnp.concatenate(outs, 1).astype(BF16)
    split_rows(dot_nt(mixed_ref[...], w_ref[base + 3]), keep_ref, send_ref)


def attention(x, columns, base, n_lat):
    rows, width = 4 * x[0].shape[0], x[0].shape[1]
    shapes = [shape((3, rows, columns), BF16), shape((rows, columns), BF16)] + part_shapes(rows, width)
    return "_attention", functools.partial(attention_kernel, n_lat, base), x, shapes


def gelu(x):
    return 0.5 * x * (1.0 + jnp.tanh(GELU_C * (x + 0.044715 * x * x * x)))


def gelu_grad(x):
    t = jnp.tanh(GELU_C * (x + 0.044715 * x * x * x))
    return 0.5 * (1.0 + t) + 0.5 * x * (1.0 - t * t) * (GELU_C * (1.0 + 3 * 0.044715 * x * x))


def mlp_kernel(base, w_ref, x0, x1, x2, x3, hidden_ref, active_ref, keep_ref, send_ref):
    x = joined((x0, x1, x2, x3))
    total = None
    for j in range(4):
        hidden = dot(x, w_ref[base + j])
        hidden_ref[j] = hidden
        active = gelu(hidden).astype(BF16)
        active_ref[j] = active
        part = dot_nt(active, w_ref[base + 4 + j])
        total = part if total is None else total + part
    split_rows(total, keep_ref, send_ref)


def mlp(x, columns, base):
    rows, width = 4 * x[0].shape[0], x[0].shape[1]
    shapes = [shape((4, rows, columns), F32), shape((4, rows, columns), BF16)] + part_shapes(rows, width)
    return "_mlp", functools.partial(mlp_kernel, base), x, shapes


def mlp_back_kernel(base, w_ref, d0, d1, d2, d3, hidden_ref, dh_ref, keep_ref, send_ref):
    d = joined((d0, d1, d2, d3))
    total = None
    for j in range(4):
        dh = (gelu_grad(hidden_ref[j]) * dot(d, w_ref[base + 4 + j])).astype(BF16)
        dh_ref[j] = dh
        part = dot_nt(dh, w_ref[base + j])
        total = part if total is None else total + part
    split_rows(total, keep_ref, send_ref)


def mlp_back(d, hidden, base):
    rows, width = 4 * d[0].shape[0], d[0].shape[1]
    shapes = [shape(hidden.shape, BF16)] + part_shapes(rows, width)
    return "_mlp_back", functools.partial(mlp_back_kernel, base), [*d, hidden], shapes


def attention_back_kernel(n_lat, base, w_ref, d0, d1, d2, d3, qkv_ref, dqkv_ref, keep_ref, send_ref):
    d_mixed = dot(joined((d0, d1, d2, d3)), w_ref[base + 3]).astype(BF16)
    toks = d_mixed.shape[0] // n_lat
    heads = w_ref.shape[2] // HEAD_DIM
    for l in range(n_lat):
        rows = slice(l * toks, (l + 1) * toks)
        outs = [[], [], []]
        for h in range(heads):
            cols = slice(h * HEAD_DIM, (h + 1) * HEAD_DIM)
            q, k, v = (qkv_ref[j, rows, cols] for j in range(3))
            do = d_mixed[rows, cols]
            probs = softmax_parts(q, k)
            d_probs = dot_nt(do, v)
            d_scores = probs * (d_probs - jnp.sum(probs * d_probs, -1, keepdims=True))
            d_scores = d_scores.astype(BF16)
            outs[0].append(dot(d_scores, k) * SCORE_SCALE)
            outs[1].append(dot_tn(d_scores, q) * SCORE_SCALE)
            outs[2].append(dot_tn(probs.astype(BF16), do))
        for j in range(3):
            dqkv_ref[j, rows, :] = jnp.concatenate(outs[j], 1).astype(BF16)
    total = sum(dot_nt(dqkv_ref[j], w_ref[base + j]) for j in range(3))
    split_rows(total, keep_ref, send_ref)


def attention_back(d, qkv, base, n_lat):
    rows, width = 4 * d[0].shape[0], d[0].shape[1]
    shapes = [shape(qkv.shape, BF16)] + part_shapes(rows, width)
    return "_attention_back", functools.partial(attention_back_kernel, n_lat, base), [*d, qkv], shapes


def weight_grad_kernel(counts, n_lat, base, out_ref, *refs):
    n = len(counts)
    lefts, rights, (mean_ref, sum_ref) = refs[: 4 * n], refs[4 * n : 5 * n], refs[-2:]
    at = 0
    for k, count in enumerate(counts):
        a = joined(lefts[4 * k : 4 * k + 4])
        toks = a.shape[0] // n_lat

        def rows_of(x, scale):
            parts = [
                jnp.sum(x[l * toks : (l + 1) * toks].astype(F32), 0, keepdims=True) * scale for l in range(n_lat)
            ]
            return jnp.concatenate(parts + [jnp.zeros((8 - n_lat, x.shape[1]), F32)], 0).astype(BF16)

        mean = rows_of(a, 1.0 / toks)
        mean_ref[k] = mean.astype(F32)
        for j in range(count):
            b = rights[k][j]
            total = rows_of(b, 1.0)
            sum_ref[at] = total.astype(F32)
            out_ref[BIG + base + at] = (dot_tn(a, b) - dot_tn(mean, total)).astype(BF16)
            at += 1


def weight_grads(base, pairs, n_lat):
    counts = [right.shape[0] for _, right in pairs]
    width, columns = pairs[0][0][0].shape[1], pairs[0][1].shape[2]
    operands = [part for left, _ in pairs for part in left] + [right for _, right in pairs]
    shapes = [shape((len(pairs), 8, width), F32), shape((sum(counts), 8, columns), F32)]
    return "_weight_grads", functools.partial(weight_grad_kernel, counts, n_lat, base), operands, shapes


def small_weights(small_ref, bank_ref, wide, sem, use):
    units = [small_ref[s] for s in range(bank_ref.shape[0])]
    ours = [(unit >= 0) & (unit != TIME_AT) for unit in units]
    copies = [pltpu.make_async_copy(bank_ref.at[s], wide.at[s], sem.at[s]) for s in range(len(units))]
    for s, copy in enumerate(copies):
        pl.when(ours[s])(copy.start)
    for s, copy in enumerate(copies):

        @pl.when(ours[s])
        def _(s=s, copy=copy):
            copy.wait()
            use(jnp.maximum(units[s], 0), wide[s].astype(BF16))


def modulation_kernel(held_ref, small_ref, cond_ref, bank_ref, out_ref, wide, sem):
    out_ref[...] = jnp.zeros_like(out_ref)

    def use(unit, weight):
        out_ref[unit] = dot(cond_ref[...], weight)

    small_weights(small_ref, bank_ref, wide, sem, use)


def bank_scratch(bank):
    return [pltpu.VMEM(bank.shape, F32), pltpu.SemaphoreType.DMA((bank.shape[0],))]


def modulations(small_slots, cond_in, bank):
    operands = [(small_slots, SMEM_SPEC), cond_in, (in_hbm(bank), pl.BlockSpec(memory_space=pltpu.HBM))]
    shapes = [shape((SMALL_ROWS, cond_in.shape[0], bank.shape[2]), F32)]
    return "_modulations", modulation_kernel, operands, shapes, bank_scratch(bank)


def cond_back_kernel(n_mail, held_ref, small_ref, peer_ref, *refs):
    mail, (bank_ref, d_ref, out_ref, wide, sem) = refs[:n_mail], refs[n_mail:]
    if n_mail == 1:
        d_ref[...] = mail[0][...]
    else:
        n_lat = d_ref.shape[0] // n_mail
        for i in range(n_mail):
            for l in range(n_lat):
                d_ref[peer_ref[i] * n_lat + l] = mail[i][l * SMALL_ROWS : (l + 1) * SMALL_ROWS]
    out_ref[...] = jnp.zeros_like(out_ref)

    def use(unit, weight):
        d = d_ref[...].astype(F32)
        d = jnp.sum(jnp.where(lax.broadcasted_iota(jnp.int32, d.shape, 1) == unit, d, 0.0), 1)
        out_ref[...] += dot_nt(d.astype(BF16), weight)

    small_weights(small_ref, bank_ref, wide, sem, use)


def cond_back(small_slots, peers, mail, n_all, bank):
    columns = bank.shape[2]
    operands = [(small_slots, SMEM_SPEC), (peers, SMEM_SPEC)] + list(mail)
    operands += [(in_hbm(bank), pl.BlockSpec(memory_space=pltpu.HBM))]
    shapes = [shape((n_all, SMALL_ROWS, columns), BF16), shape((n_all, bank.shape[1]), F32)]
    return "_cond_back", functools.partial(cond_back_kernel, len(mail)), operands, shapes, bank_scratch(bank)


def mail_sum_kernel(n_mail, held_ref, peer_ref, *refs):
    mail, (out_ref, whole) = refs[:n_mail], refs[n_mail:]
    rows = out_ref.shape[0]
    for i in range(n_mail):
        whole[peer_ref[i]] = mail[i][:rows].astype(F32) + mail[i][rows:].astype(F32)
    total = whole[0]
    for i in range(1, n_mail):
        total = total + whole[i]
    out_ref[...] = total


def mail_sum(peers, mail):
    rows, columns = mail[0].shape[0] // 2, mail[0].shape[1]
    scratch = [pltpu.VMEM((len(mail), rows, columns), F32)]
    operands = [(peers, SMEM_SPEC)] + list(mail)
    return "_mail_sum", functools.partial(mail_sum_kernel, len(mail)), operands, [shape((rows, columns), F32)], scratch


def halves(x):
    high = x.astype(BF16)
    return high, (x - high.astype(F32)).astype(BF16)


def newton_sweep_coarse(x):
    xh = x.astype(BF16)
    gram = dot_tn(xh, xh)
    gh = gram.astype(BF16)
    poly = NS_COEF[1] * gram + NS_COEF[2] * dot(gh, gh)
    return NS_COEF[0] * x + dot(xh, poly.astype(BF16))


def newton_sweep(x):
    xh, xl = halves(x)
    cross = dot_tn(xh, xl)
    gram = dot_tn(xh, xh) + (cross + cross.T)
    gh, gl = halves(gram)
    cross = dot(gh, gl)
    square = dot(gh, gh) + (cross + cross.T)
    ph, pl_ = halves(NS_COEF[1] * gram + NS_COEF[2] * square)
    return NS_COEF[0] * x + (dot(xh, ph) + (dot(xl, ph) + dot(xh, pl_)))


def newton_kernel(n_last, big_ref, left_ref, right_ref, tab_ref, a_ref, b_ref, bank_ref, mom_ref, *refs):
    held, got = refs[0], refs[1 : 1 + n_last]
    new_ref, mom_new_ref, grad, sem = refs[1 + n_last :]
    s = pl.program_id(0)
    unit, left, right = big_ref[s], left_ref[s], right_ref[s]
    half = got[0].shape[0]

    @pl.when(right < 0)
    def _():
        new_ref[...] = bank_ref[...]
        mom_new_ref[...] = mom_ref[...]

    @pl.when(right >= 0)
    def _():
        copy = pltpu.make_async_copy(held.at[BIG + jnp.maximum(unit, 0)], grad, sem.at[0])
        pl.when(unit >= 0)(copy.start)
        mom_new_ref[0] = 0.5 * mom_ref[0] + dot_tn(
            a_ref[jnp.maximum(left, 0)], b_ref[jnp.maximum(right, 0)]
        )
        pl.when(unit >= 0)(copy.wait)

        @pl.when(unit >= 0)
        def _():
            mom_new_ref[0] += grad[...].astype(F32)

        for i in range(n_last):
            rows = slice((i % 2) * half, (i % 2 + 1) * half)

            @pl.when((tab_ref[i // 2, 2 * (i % 2)] == unit) & (unit >= 0))
            def _(i=i, rows=rows):
                mom_new_ref[0, rows] += got[i][...].astype(F32)

        block = mom_new_ref[0]
        norm = jnp.sqrt(jnp.sum(block * block)) + 1e-07
        x = block / norm
        for sweep in range(5):
            x = newton_sweep_coarse(x) if sweep < 3 else newton_sweep(x)
        new_ref[0] = bank_ref[0] - LR_MUON * x


def optimizer(big_slots, left_slots, right_slots, tab, a_all, b_all, master, momentum, held, got):
    n_slots, rows, columns = master.shape
    block = pl.BlockSpec((1, rows, columns), lambda s, *t: (s, 0, 0))
    return pl.pallas_call(
        functools.partial(newton_kernel, len(got)),
        grid_spec=pltpu.PrefetchScalarGridSpec(
            num_scalar_prefetch=4,
            grid=(n_slots,),
            in_specs=[
                pl.BlockSpec(a_all.shape, lambda s, *t: (0, 0, 0)),
                pl.BlockSpec(b_all.shape, lambda s, *t: (0, 0, 0)),
                block,
                block,
            ]
            + [pl.BlockSpec(memory_space=pl.ANY)]
            + [pl.BlockSpec(g.shape, lambda s, *t: (0, 0)) for g in got],
            out_specs=[block, block],
            scratch_shapes=[pltpu.VMEM((rows, columns), BF16), pltpu.SemaphoreType.DMA((1,))],
        ),
        out_shape=[shape(master.shape, F32), shape(momentum.shape, F32)],
        compiler_params=params(SCOPE, dimension_semantics=("arbitrary",)),
        name="optimizer",
    )(big_slots, left_slots, right_slots, tab, a_all, b_all, in_hbm(master), in_hbm(momentum), held, *got)


def layer_norm(values):
    centered = values - jnp.mean(values, -1, keepdims=True)
    inv_std = lax.rsqrt(jnp.mean(centered * centered, -1, keepdims=True) + 1e-06)
    return centered * inv_std, inv_std


def norm_back(grad_out, normed, inv_std):
    return inv_std * (
        grad_out
        - jnp.mean(grad_out, -1, keepdims=True)
        - normed * jnp.mean(grad_out * normed, -1, keepdims=True)
    )


def added(keep_ref, got_ref, far_ref):
    return keep_ref[0] + got_ref[0].astype(F32) + far_ref[...].astype(F32)


def row_of(mods_ref, at):
    return mods_ref[at : at + 1, :]


def enter_kernel(at, noisy_ref, patch_ref, place_ref, mods_ref, stream_ref, inner_ref, normed_ref, inv_ref):
    stream = dot(noisy_ref[...], patch_ref[...]) + place_ref[...]
    stream_ref[...] = stream
    normed, inv = layer_norm(stream)
    inner_ref[...] = (normed * (1.0 + row_of(mods_ref, at[1])) + row_of(mods_ref, at[0])).astype(BF16)
    normed_ref[...] = normed
    inv_ref[...] = jnp.broadcast_to(inv, inv_ref.shape)


def enter(noisy, patch, places, mods, at):
    rows, width = places.shape
    full = shape((rows, width), F32)
    return pl.pallas_call(
        functools.partial(enter_kernel, at),
        out_shape=[full, shape((rows, width), BF16), full, shape((rows, 128), F32)],
        compiler_params=params(SCOPE),
        name="enter",
    )(noisy, patch, places, mods)


def residual_kernel(
    at, keep_ref, got_ref, far_ref, stream_ref, mods_ref, part_ref, next_ref, inner_ref, normed_ref, inv_ref
):
    part = added(keep_ref, got_ref, far_ref)
    part_ref[...] = part
    stream = stream_ref[...] + row_of(mods_ref, at[0]) * part
    next_ref[...] = stream
    normed, inv = layer_norm(stream)
    inner_ref[...] = (normed * (1.0 + row_of(mods_ref, at[2])) + row_of(mods_ref, at[1])).astype(BF16)
    normed_ref[...] = normed
    inv_ref[...] = jnp.broadcast_to(inv, inv_ref.shape)


def residual(parts, stream, mods, at):
    rows, width = stream.shape
    full = shape((rows, width), F32)
    return pl.pallas_call(
        functools.partial(residual_kernel, at),
        out_shape=[full, full, shape((rows, width), BF16), full, shape((rows, 128), F32)],
        compiler_params=params(SCOPE),
        name="residual",
    )(*parts, stream, mods)


def leave_kernel(
    at,
    count_all,
    keep_ref,
    got_ref,
    far_ref,
    stream_ref,
    mods_ref,
    head_ref,
    target_ref,
    grad_ref,
    next_ref,
    rows_ref,
    edge_ref,
):
    branch = added(keep_ref, got_ref, far_ref)
    gate, shift, scale = (row_of(mods_ref, i) for i in at)
    normed, inv = layer_norm(stream_ref[...] + gate * branch)
    inner = (normed * (1.0 + scale) + shift).astype(BF16)
    head = head_ref[...]
    error = dot_nt(inner, head) - target_ref[...]
    d_output = (2.0 * error / count_all).astype(BF16)
    d_inner = dot(d_output, head)
    grad = norm_back(d_inner * (1.0 + scale), normed, inv)
    grad_ref[...] = grad
    next_ref[...] = (gate * grad).astype(BF16)
    rows_ref[...] = jnp.zeros_like(rows_ref)
    rows_ref[0:1, :] = jnp.sum(d_inner, 0, keepdims=True)
    rows_ref[1:2, :] = jnp.sum(d_inner * normed, 0, keepdims=True)
    rows_ref[2:3, :] = jnp.sum(grad * branch, 0, keepdims=True)
    n_patch = head.shape[0]
    loss = jnp.sum(jnp.sum(error * error, 1, keepdims=True), 0, keepdims=True) / count_all
    edge_ref[:n_patch, :] = dot_tn(d_output, inner)
    edge_ref[n_patch:, :] = jnp.broadcast_to(loss, (8, edge_ref.shape[1]))


def leave(parts, stream, mods, head, target, at, count_all):
    rows, width = stream.shape
    return pl.pallas_call(
        functools.partial(leave_kernel, at, count_all),
        out_shape=[
            shape((rows, width), F32),
            shape((rows, width), BF16),
            shape((SMALL_ROWS, width), F32),
            shape((head.shape[0] + 8, width), F32),
        ],
        compiler_params=params(SCOPE),
        name="leave",
    )(*parts, stream, mods, head, target)


def back_kernel(
    at,
    gate_at,
    first,
    keep_ref,
    got_ref,
    far_ref,
    normed_ref,
    inv_ref,
    grad_ref,
    part_ref,
    mods_ref,
    rows_in_ref,
    out_ref,
    next_ref,
    rows_ref,
):
    d_inner = added(keep_ref, got_ref, far_ref)
    normed = normed_ref[...]
    inv = inv_ref[:, 0:1]
    grad = grad_ref[...] + norm_back(d_inner * (1.0 + row_of(mods_ref, at)), normed, inv)
    out_ref[...] = grad
    rows_ref[...] = rows_in_ref[...]
    rows_ref[first : first + 1, :] = jnp.sum(d_inner, 0, keepdims=True)
    rows_ref[first + 1 : first + 2, :] = jnp.sum(d_inner * normed, 0, keepdims=True)
    if gate_at is None:
        next_ref[...] = grad.astype(BF16)
    else:
        next_ref[...] = (row_of(mods_ref, gate_at) * grad).astype(BF16)
        rows_ref[first + 2 : first + 3, :] = jnp.sum(grad * part_ref[...], 0, keepdims=True)


def back(parts, normed, inv, grad, part, mods, rows_in, at, gate_at, first, beside):
    rows, width = grad.shape
    operands = (*parts, normed, inv, grad, part, mods, rows_in)
    return pl.pallas_call(
        past(functools.partial(back_kernel, at, gate_at, first), operands, beside),
        out_shape=[shape((rows, width), F32), shape((rows, width), BF16), shape(rows_in.shape, F32)],
        compiler_params=params(SCOPE),
        name="back",
    )(*operands, *beside)


def tables_kernel(n_patch, fix_ref, edge_ref, time_ref, class_ref, table_ref, first_ref, second_ref, *outs):
    new_ref, first_new_ref, second_new_ref = outs
    at = 0
    for ref, low, count in (
        (edge_ref, 0, n_patch),
        (time_ref, 0, FREQ),
        (class_ref, 0, CLASSES),
        (edge_ref, n_patch, n_patch),
    ):
        rows = slice(at, at + count)
        grad = ref[low : low + count, :]
        first = 0.5 * first_ref[rows, :] + 0.5 * grad
        second = 0.5 * second_ref[rows, :] + 0.5 * grad * grad
        first_new_ref[rows, :] = first
        second_new_ref[rows, :] = second
        new_ref[rows, :] = table_ref[rows, :] * (1.0 - LR_ADAM * WEIGHT_DECAY) - LR_ADAM * (
            first / fix_ref[0]
        ) / (jnp.sqrt(second / fix_ref[0]) + 1e-08)
        at += count


def update_tables(n_patch, bias_fix, edges, grad_time, grad_class, table, first, second):
    return pl.pallas_call(
        functools.partial(tables_kernel, n_patch),
        out_shape=[shape(table.shape, F32)] * 3,
        in_specs=[SMEM_SPEC] + [VMEM_SPEC] * 6,
        compiler_params=params(SCOPE),
        name="update_tables",
    )(bias_fix, edges, grad_time, grad_class, table, first, second)


def position_rows(first, rows):
    quarter = D // 4
    omega = jnp.exp(-math.log(10000.0) * jnp.arange(quarter, dtype=F32) / quarter)
    places = first + jnp.arange(rows, dtype=jnp.int32)
    rows_at = (places // GRID).astype(F32)[:, None] * omega[None]
    cols_at = (places % GRID).astype(F32)[:, None] * omega[None]
    return jnp.concatenate([jnp.sin(rows_at), jnp.cos(rows_at), jnp.sin(cols_at), jnp.cos(cols_at)], 1)


def time_features(timesteps):
    half_freq = FREQ // 2
    rates = jnp.exp(-math.log(10000.0) * jnp.arange(half_freq, dtype=F32) / half_freq)
    angles = timesteps.astype(F32)[:, None] * rates[None]
    return jnp.concatenate([jnp.cos(angles), jnp.sin(angles)], 1)


def shards(
    noisy_latents,
    noise_target,
    timesteps,
    labels,
    owners,
    step_count,
    master_bank,
    momentum_bank,
    embed_tables,
    embed_first,
    embed_second,
):
    n_lat, n_tok, n_patch = noisy_latents.shape
    n_slots, width, columns = master_bank.shape
    n_data = lax.axis_size("dp")
    my_data = lax.axis_index("dp")
    my_tensor = lax.axis_index("tensor")
    n_all = n_lat * n_data
    own_rows = n_lat * n_tok // 4
    count_all = float(n_all * n_tok * n_patch)
    depth = 2 if n_data <= 8 else 1
    steps = N_BIG + (n_data - 2) * depth

    kind = [2 + 2 * g + (b >= low + (3, 4)[g % 2]) for g, (low, high) in enumerate(GROUPS) for b in range(low, high)]
    slot_tables = np.stack(
        [
            BIG_OF,
            SMALL_OF,
            np.where(BIG_OF >= 0, np.array(kind)[BIG_OF], np.where(SMALL_OF == TIME_AT, 1, 0)),
            np.where(BIG_OF >= 0, SMALL_ROWS + BIG_OF, SMALL_OF),
        ]
    )
    tab, planned = plan(owners, slot_tables, n_slots, n_data, steps, depth, my_data)

    def flag(value):
        return jnp.asarray(value, jnp.int32).reshape(1)

    first_row = my_tensor * own_rows
    early = dict(
        slots=planned[:4, :n_slots],
        peers=planned[5, :n_data],
        chip=flag(my_tensor // 2),
        core=flag(my_tensor % 2),
        data=flag(my_data),
        bits=[flag((my_data // (1 << i)) % 2) for i in range((n_data - 1).bit_length())],
        time_mine=planned[4, 1:2],
        time_w2=lax.dynamic_index_in_dim(master_bank, planned[4, 0], 0, keepdims=False).astype(BF16),
        noisy=lax.dynamic_slice_in_dim(noisy_latents.reshape(n_lat * n_tok, n_patch), first_row, own_rows, 0),
        target=lax.dynamic_slice_in_dim(noise_target.reshape(n_lat * n_tok, n_patch), first_row, own_rows, 0),
        places=position_rows(first_row % n_tok, own_rows),
        ids=jnp.stack([timesteps, labels], 1),
        bias_fix=1.0 - jnp.power(0.5, step_count.astype(F32)),
        tab=tab,
        edge_cols=jnp.concatenate(
            [embed_tables[:n_patch], embed_tables[n_patch + FREQ + CLASSES :]], 0
        ).astype(BF16),
        time_w1=embed_tables[n_patch : n_patch + FREQ].astype(BF16),
        class_w=embed_tables[n_patch + FREQ : n_patch + FREQ + CLASSES].astype(BF16),
    )
    flat, tree = jax.tree.flatten(early)
    early = jax.tree.unflatten(tree, lax.optimization_barrier(tuple(flat)))
    chip, core, data, time_w2, noisy_own = (early[k] for k in ("chip", "core", "data", "time_w2", "noisy"))
    tab, peers = early["tab"], early["peers"]
    big_slots, small_slots, left_slots, right_slots = (early["slots"][i] for i in range(4))
    spread = Spreader(tab, spread_init(early["slots"], master_bank), n_data, steps, depth)
    spread.step()
    ring = Reducer(tab, n_data, steps, depth)

    def conditioning():
        ids, edge_rows = yield from together(
            dp_sum(own_latents(early["ids"], 0, data, n_data), n_data),
            gather_columns(early["edge_cols"], chip, core),
        )
        features = time_features(ids[:, 0]).astype(BF16)
        time_one = jnp.dot(features, early["time_w1"], preferred_element_type=F32)
        time_act = yield from gather_columns(jax.nn.silu(time_one).astype(BF16), chip, core)
        second = jnp.dot(time_act, time_w2, preferred_element_type=F32)
        second = yield from dp_sum(jnp.where(is_at(early["time_mine"], 1, 2), second, 0.0), n_data)
        onehot = ids[:, 1:2] == jnp.arange(CLASSES, dtype=jnp.int32)[None]
        condition = second + jnp.dot(onehot.astype(BF16), early["class_w"], preferred_element_type=F32)
        cond_in = yield from gather_columns(jax.nn.silu(condition).astype(BF16), chip, core)
        (mods,) = spread.work(modulations(small_slots, cond_in, master_bank), ISSUED)
        ISSUED.clear()
        bit = n_data // 2
        while bit:
            half = mods.shape[1] // 2
            sides = mods[:, :half], mods[:, half:]
            side = early["bits"][bit.bit_length() - 1]
            mods = pick(*sides, side) + (yield flip(pick(*sides, side, True), "dp", bit, n_data))
            bit //= 2
        latents = mods[:, 0], mods[:, 1]
        across = yield x_flip(pick(*latents, chip, True))
        own = pick(*latents, chip)
        pair = [pick(own, across, chip), pick(across, own, chip)]
        beside = core_flip(jnp.concatenate(pair, 1))
        beside = [beside[:, x * columns : (x + 1) * columns] for x in range(2)]
        blocks = [pick(one, two, core) for x in range(2) for one, two in ((pair[x], beside[x]), (beside[x], pair[x]))]
        return edge_rows, features, time_one, time_act, onehot, condition, cond_in, jnp.concatenate(blocks, 1)

    def forward():
        cond = yield from conditioning()
        edge_rows, mods = cond[0], cond[-1]
        stream, inner, normed, inv = enter(
            noisy_own, edge_rows[:n_patch], early["places"], mods, (small_at(0, 0), small_at(0, 1))
        )
        kept = []
        for layer in range(LAYERS):
            inner = yield from gather_tokens(inner)
            spread.prepare(2 * layer)
            qkv, mixed, keep, send = spread.work(attention(inner, columns, BIG * layer, n_lat))
            parts = yield from scatter_tokens(keep, send)
            attended, stream, inner_mid, normed_mid, inv_mid = residual(
                parts, stream, mods, tuple(small_at(layer, i) for i in (2, 3, 4))
            )
            inner_mid = yield from gather_tokens(inner_mid)
            spread.prepare(2 * layer + 1)
            hidden, active, keep, send = spread.work(mlp(inner_mid, columns, BIG * layer + 4))
            parts = yield from scatter_tokens(keep, send)
            kept.append([inner, normed, inv, qkv, mixed, attended, inner_mid, normed_mid, inv_mid, hidden, active])
            if layer + 1 < LAYERS:
                branch, stream, inner, normed, inv = residual(
                    parts,
                    stream,
                    mods,
                    (small_at(layer, 5), small_at(layer + 1, 0), small_at(layer + 1, 1)),
                )
                kept[-1].append(branch)
        return cond, kept, parts, stream

    cond, kept, parts_last, stream_last = drive(forward(), spread.step)
    edge_rows, features, time_one, time_act, onehot, condition, cond_in, mods = cond
    ring.held = spread.held

    def backward():
        grad, d_branch, rows, edge_head = leave(
            parts_last,
            stream_last,
            mods,
            edge_rows[n_patch:],
            early["target"],
            (small_at(LAYERS - 1, 5), SHIFT_F, SCALE_F),
            count_all,
        )
        lefts, rights = {}, {}
        for layer in reversed(range(LAYERS)):
            inner, normed, inv, qkv, mixed, attended, inner_mid, normed_mid, inv_mid, hidden, active = kept[layer][:11]
            d_branch = yield from gather_tokens(d_branch)
            d_hidden, keep, send = ring.work(mlp_back(d_branch, hidden, BIG * layer + 4))
            work = scatter_tokens(keep, send)
            flying = next(work)
            lefts[2 * layer + 1], rights[2 * layer + 1] = ring.work(
                weight_grads(BIG * layer + 4, [(inner_mid, d_hidden), (d_branch, active)], n_lat), ISSUED
            )
            ring.ready = BIG * layer + 4
            parts = finish(work, order(flying, (lefts[2 * layer + 1],) + ring.sent))
            grad, d_attended, rows = back(
                parts,
                normed_mid,
                inv_mid,
                grad,
                attended,
                mods,
                rows,
                small_at(layer, 4),
                small_at(layer, 2),
                small_at(layer, 3),
                [ring.held],
            )
            d_attended = yield from gather_tokens(d_attended)
            d_qkv, keep, send = ring.work(attention_back(d_attended, qkv, BIG * layer, n_lat))
            work = scatter_tokens(keep, send)
            flying = next(work)
            lefts[2 * layer], rights[2 * layer] = ring.work(
                weight_grads(BIG * layer, [(inner, d_qkv), (d_attended, mixed[None])], n_lat), ISSUED
            )
            ring.ready = BIG * layer
            parts = finish(work, order(flying, (lefts[2 * layer],) + ring.sent))
            below = kept[layer - 1][11] if layer else normed
            grad, d_branch, rows = back(
                parts,
                normed,
                inv,
                grad,
                below,
                mods,
                rows,
                small_at(layer, 1),
                small_at(layer - 1, 5) if layer else None,
                small_at(layer, 0),
                [ring.held],
            )
        return (yield from cond_backward(rows, d_branch, edge_head, lefts, rights))

    def cond_backward(rows, d_stream, edge_head, lefts, rights):
        mine = core_columns_sum(rows, core)
        near, far = pick(*mine, chip), (yield x_flip(pick(*mine, chip, True)))
        own = [pick(near, far, chip).astype(BF16), pick(far, near, chip).astype(BF16)]
        if n_data == 8:
            first, *others = factor_rows(lefts, rights)
            one, two = jnp.concatenate(own + [first], 0), jnp.concatenate(others, 0)
            one, two = (jnp.pad(v, ((0, -len(v) % 96), (0, 0))) for v in (one, two))
            latents, others = yield from ring.gather(one, two)
            n_own, n_rows = n_lat * SMALL_ROWS, first.shape[0]
            factors = [v[n_own : n_own + n_rows] for v in latents] + [v[:n_rows] for v in others]
            factors = jnp.concatenate(factors, 0).reshape(n_all, n_rows, columns)
        else:
            latents = [(yield from dp_sum(own_latents(jnp.stack(own, 0), 0, data, n_data), n_data))]
        d_small, d_cond = ring.work(cond_back(small_slots, peers, latents, n_all, master_bank), ISSUED)
        ISSUED.clear()
        d_cond = yield from own_columns_sum(d_cond, chip, core)
        if n_data == 8:
            (parts,) = yield from ring.gather(jnp.concatenate(halves(d_cond), 0))
            (d_cond,) = ring.work(mail_sum(peers, parts))
        else:
            d_cond = yield from dp_sum(d_cond, n_data)
        unused, silu_pull = jax.vjp(jax.nn.silu, condition)
        d_condition = silu_pull(d_cond)[0]
        d_second = d_condition.astype(BF16)
        grad_class = lax.dot_general(
            onehot.astype(F32), d_condition, (((0,), (0,)), ((), ())), precision=HIGHEST_PREC
        )
        d_time_act = lax.dot_general(d_second, time_w2, (((1,), (1,)), ((), ())), preferred_element_type=F32)
        d_time_act = jnp.where(is_at(early["time_mine"], 1, 2), d_time_act, 0.0)
        grad_patch = lax.dot_general(noisy_own, d_stream, (((0,), (0,)), ((), ())), preferred_element_type=F32)
        sums = yield from own_columns_sum(jnp.concatenate([d_time_act, grad_patch, edge_head], 0), chip, core)
        ring.drain()
        sums = yield from dp_sum(order(sums, ring.last()), n_data)
        if n_data != 8:
            factors = yield from dp_rows(jnp.stack(factor_rows(lefts, rights)), n_data)
        n_left = sum(v.shape[0] for v in lefts.values())
        a_rows = jnp.concatenate([factors[:, j * n_left : (j + 1) * n_left] for j in range(4)], 2).transpose(1, 0, 2)
        b_rows = factors[:, 4 * n_left : 4 * n_left + N_BIG].transpose(1, 0, 2)
        d_time_act, edges = sums[:n_all], sums[n_all:]
        unused, time_pull = jax.vjp(jax.nn.silu, time_one)
        d_time_one = time_pull(d_time_act)[0].astype(BF16)
        grad_time_one = lax.dot_general(
            features, d_time_one, (((0,), (0,)), ((), ())), preferred_element_type=F32
        )
        return d_small, d_second, grad_class, grad_time_one, edges, (a_rows, b_rows)

    def factor_rows(lefts, rights):
        a_rows = jnp.concatenate([lefts[g] for g in range(len(GROUPS))], 0)
        b_rows = jnp.concatenate([rights[g] for g in range(len(GROUPS))], 0)
        parts = []
        for l in range(n_lat):
            part = [a_rows[:, l, j * columns : (j + 1) * columns] for j in range(4)] + [b_rows[:, l]]
            part = jnp.concatenate(part, 0).astype(BF16)
            parts.append(jnp.pad(part, ((0, -len(part) % 32), (0, 0))))
        return parts

    d_small, d_second, grad_class, grad_time_one, edges, (a_rows, b_rows) = drive(backward(), ring.step)
    loss = edges[2 * n_patch, 0]
    a_all = jnp.concatenate([cond_in[None], time_act[None], a_rows], 0)
    small_rows = jnp.where(jnp.arange(SMALL_ROWS)[:, None, None] == TIME_AT, d_second[None], d_small.transpose(1, 0, 2))
    b_all = jnp.concatenate([small_rows, b_rows], 0)
    master_new, momentum_new = optimizer(
        big_slots, left_slots, right_slots, tab, a_all, b_all, master_bank, momentum_bank, ring.held, ring.last()
    )
    embed_new, first_new, second_new = update_tables(
        n_patch, early["bias_fix"], edges, grad_time_one, grad_class, embed_tables, embed_first, embed_second
    )
    return (loss, master_new, momentum_new, embed_new, first_new, second_new)


def solution(mesh):
    placed = (
        P("dp", None, None),
        P("dp", None, None),
        P("dp"),
        P("dp"),
        P(),
        P(),
        P("dp", None, "tensor"),
        P("dp", None, "tensor"),
        P(None, "tensor"),
        P(None, "tensor"),
        P(None, "tensor"),
    )
    return jax.shard_map(
        shards,
        mesh=mesh,
        in_specs=placed,
        out_specs=(
            P(),
            P("dp", None, "tensor"),
            P("dp", None, "tensor"),
            P(None, "tensor"),
            P(None, "tensor"),
            P(None, "tensor"),
        ),
        check_vma=False,
    )
```

```python
import functools
import math

import jax
import jax.numpy as jnp
import numpy as np
from jax import lax
from jax.experimental import pallas as pl
from jax.experimental.pallas import tpu as pltpu
from jax.sharding import PartitionSpec as P

D = 1024
HEAD_DIM = 64
FREQ = 256
CLASSES = 1000
GRID = 16
LAYERS = 2
BIG = 12
N_BIG = BIG * LAYERS
SMALL_ROWS = 16
SHIFT_F, SCALE_F, TIME_AT = 0, 1, 6 * LAYERS + 2


def small_at(layer, i):
    first = 2 + 6 * (LAYERS - 1 - layer)
    return first + (4, 5, 3, 1, 2, 0)[i]


NS_COEF = (3.4445, -4.775, 2.0315)
LR_MUON = 0.5
LR_ADAM = 0.02
WEIGHT_DECAY = 0.1
SCORE_SCALE = 1.0 / math.sqrt(HEAD_DIM)
HIGHEST_PREC = lax.Precision.HIGHEST

F32 = jnp.float32
BF16 = jnp.bfloat16
SCOPE = 16
GELU_C = math.sqrt(2.0 / math.pi)
GROUPS = ((0, 4), (4, 12), (12, 16), (16, 24))


def unit_tables():
    big, small = [], []
    for u in range(18 * LAYERS):
        layer, place = divmod(u, 18)
        big.append(layer * BIG + place if place < BIG else -1)
        small.append(-1 if place < BIG else small_at(layer, place - BIG))
    return np.array(big + [-1] * 3), np.array(small + [TIME_AT, SHIFT_F, SCALE_F])


BIG_OF, SMALL_OF = unit_tables()


def params(limit, **more):
    return pltpu.CompilerParams(vmem_limit_bytes=limit * 1024 * 1024, **more)


SMEM_SPEC = pl.BlockSpec(memory_space=pltpu.SMEM)
VMEM_SPEC = pl.BlockSpec(memory_space=pltpu.VMEM)


def in_hbm(values):
    return pltpu.with_memory_space_constraint(values, pltpu.HBM)


def dot(a, b):
    return lax.dot_general(a, b, (((1,), (0,)), ((), ())), preferred_element_type=F32)


def dot_nt(a, b):
    return lax.dot_general(a, b, (((1,), (1,)), ((), ())), preferred_element_type=F32)


def dot_tn(a, b):
    return lax.dot_general(a, b, (((0,), (0,)), ((), ())), preferred_element_type=F32)


def shape(dims, kind):
    return jax.ShapeDtypeStruct(dims, kind)


ISSUED = []


def order(values, after):
    if not after:
        return values
    flat, tree = jax.tree.flatten(values)
    tied = lax.optimization_barrier(tuple(flat) + tuple(after))
    return jax.tree.unflatten(tree, tied[: len(flat)])


def drive(work, line):
    ISSUED.clear()
    try:
        value = next(work)
        while True:
            after = tuple(ISSUED)
            ISSUED.clear()
            value = work.send(order(value, line(after)))
    except StopIteration as end:
        return end.value


def together(*works):
    ends, flying = [None] * len(works), {}

    def go(i, step):
        try:
            flying[i] = step()
        except StopIteration as end:
            flying.pop(i, None)
            ends[i] = end.value

    for i, work in enumerate(works):
        go(i, lambda: next(work))
    while flying:
        got = yield dict(flying)
        for i in list(got):
            go(i, lambda: works[i].send(got[i]))
    return ends


def finish(work, value):
    try:
        work.send(value)
    except StopIteration as end:
        return end.value
    raise AssertionError


def flip(values, axis, bit, size):
    ISSUED.append(values)
    got = lax.ppermute(values, axis, [(i, i ^ bit) for i in range(size)])
    if axis == "tensor" and values.size < 2**16:
        ISSUED.append(got)
    return got


def is_at(flag, value, ndim):
    return flag.reshape((1,) * ndim) == value


def pick(low, high, place, other=False):
    return jnp.where(is_at(place, 1 if other else 0, low.ndim), low, high)


def own_latents(values, axis, data, n_data):
    n_lat = values.shape[axis]
    dims = values.shape[:axis] + (n_lat * n_data,) + values.shape[axis + 1 :]
    at = lax.broadcasted_iota(jnp.int32, dims, axis)
    first = data.reshape((1,) * len(dims)) * n_lat
    placed = jnp.zeros(dims, values.dtype)
    for l in range(n_lat):
        placed = jnp.where(at == first + l, lax.slice_in_dim(values, l, l + 1, axis=axis), placed)
    return placed


def dp_sum(values, n_data):
    bit = 1
    while bit < n_data:
        values = values + (yield flip(values, "dp", bit, n_data))
        bit *= 2
    return values


def dp_rows(values, n_data):
    bit = 1
    while bit < n_data:
        values = jnp.concatenate([values, (yield flip(values, "dp", bit, n_data))], 0)
        bit *= 2
    return values


def core_flip(values):
    return flip(values, "tensor", 1, 4)


def x_flip(values):
    return flip(values, "tensor", 2, 4)


def gather_tokens(own, waits=1):
    flying = core_flip(own), x_flip(own)
    for _ in range(waits):
        flying = yield flying
    beside, across = flying
    return own, beside, across, core_flip(across)


def gather_columns(own, chip, core):
    beside, across = yield (core_flip(own), x_flip(own))
    corner = core_flip(across)
    at_core = [is_at(core, i, own.ndim) for i in range(2)]
    at_chip = [is_at(chip, i, own.ndim) for i in range(2)]
    near = [jnp.where(at_core[i], own, beside) for i in range(2)]
    far = [jnp.where(at_core[i], across, corner) for i in range(2)]
    parts = [jnp.where(at_chip[i], near[j], far[j]) for i in range(2) for j in range(2)]
    return jnp.concatenate(parts, -1)


def scatter_tokens(keep, send):
    got = core_flip(send)
    far = (keep[1] + got[1].astype(F32)).astype(BF16)
    return keep, got, (yield x_flip(far))


def core_columns(values, core, other=False):
    size = values.shape[-1] // 4
    block = [lax.slice_in_dim(values, j * size, (j + 1) * size, axis=values.ndim - 1) for j in range(4)]
    return [pick(block[2 * x], block[2 * x + 1], core, other) for x in range(2)]


def core_columns_sum(values, core):
    got = core_flip(jnp.concatenate(core_columns(values, core, True), -1))
    size = got.shape[-1] // 2
    return [
        mine + lax.slice_in_dim(got, x * size, (x + 1) * size, axis=got.ndim - 1)
        for x, mine in enumerate(core_columns(values, core))
    ]


def own_columns_sum(values, chip, core):
    mine = core_columns_sum(values, core)
    return pick(*mine, chip) + (yield x_flip(pick(*mine, chip, True)))


def sum_of_columns(values, chip, core, n_data):
    return (yield from dp_sum((yield from own_columns_sum(values, chip, core)), n_data))


def ring_order(n_data):
    return [0, 2, 4, 6, 7, 5, 3, 1] if n_data == 8 else list(range(n_data))


def plan_kernel(n_units, n_slots, steps, depth, n_data, me_ref, owner_ref, table_ref, tab_ref, slot_ref):
    me = me_ref[0]
    place_of = [int(v) for v in np.argsort(ring_order(n_data))]
    my_place = sum(jnp.where(me == d, place_of[d], 0) for d in range(n_data))
    owner = owner_ref[...]
    across = jnp.broadcast_to(owner, (128, 128))
    before = lax.broadcasted_iota(jnp.int32, (128, 128), 0) < lax.broadcasted_iota(jnp.int32, (128, 128), 1)
    slot = jnp.sum(jnp.where((across == across.T) & before, 1.0, 0.0), 0, keepdims=True)
    mine = owner == me.astype(F32)
    lane8 = lax.broadcasted_iota(jnp.int32, (8, 128), 1)
    row8 = lax.broadcasted_iota(jnp.int32, (8, 128), 0)
    result = jnp.full((8, 128), -1, jnp.int32)
    for s in range(n_slots):
        held = mine & (slot == s)
        value = jnp.sum(jnp.where(held, table_ref[...], 0), 1, keepdims=True) - 1
        result = jnp.where((lane8 == s) & (row8 < 4), value, result)
    lane1 = lax.broadcasted_iota(jnp.int32, (1, 128), 1)
    time = lane1 == 18 * LAYERS
    time_slot = jnp.sum(jnp.where(time, slot, 0.0), 1, keepdims=True).astype(jnp.int32)
    time_mine = jnp.sum(jnp.where(time & mine, 1.0, 0.0), 1, keepdims=True).astype(jnp.int32)
    result = jnp.where((row8 == 4) & (lane8 == 0), time_slot, result)
    result = jnp.where((row8 == 4) & (lane8 == 1), time_mine, result)
    peers = jnp.full((1, 128), -1, jnp.int32)
    place = jnp.full((1, 128), -9, jnp.int32)
    for d in range(n_data):
        ahead = place_of[d] - my_place
        peers = jnp.where(lane1 == jnp.where(ahead < 0, ahead + n_data, ahead), d, peers)
        place = jnp.where(owner == float(d), place_of[d], place)
    slot_ref[...] = jnp.where(row8 == 5, peers, result)

    big = jnp.where(lane1 < BIG, place, pltpu.roll(place, 128 - 6, 1))
    big = jnp.where(lane1 < N_BIG, big, -9)
    back = jnp.where(big >= 0, n_data - 1 - big, -9)
    lane = lax.broadcasted_iota(jnp.int32, (n_data, 128), 1)
    row = lax.broadcasted_iota(jnp.int32, (n_data, 128), 0)
    follow = jnp.where(row == n_data - 1, 0, row + 1)
    own = [(row == at).astype(jnp.int32) for at in (big, back)]
    open_to = [(follow != at).astype(jnp.int32) for at in (big, back)]
    spots = [my_place, n_data - 1 - my_place]
    far = jnp.int32(999)

    def step(t, carry):
        line = jnp.full((1, 128), -1, jnp.int32)
        after = []
        for way in range(2):
            have, sent, *coming = carry[way]
            here = spots[way]
            prior = jnp.where(here == 0, n_data - 1, here - 1)
            open_now = have * (1 - sent) * open_to[way]
            first = jnp.min(jnp.where(open_now > 0, lane, far), axis=1, keepdims=True)
            chosen = (lane == first).astype(jnp.int32)
            first = jnp.broadcast_to(first, (n_data, 128))
            for k, who in enumerate((here, prior)):
                index = jnp.min(jnp.where(row == who, first, far), axis=0, keepdims=True)
                index = jnp.where(index == far, -1, index)
                line = jnp.where(lane1 == 2 * way + k, index, line)
            coming = list(coming) + [pltpu.roll(chosen, 1, 0)]
            after.append((have + coming[0], sent + chosen, *coming[1:]))
        tab_ref[pl.ds(t, 1), :] = line
        return tuple(after)

    none = jnp.zeros((n_data, 128), jnp.int32)
    lax.fori_loop(0, steps, step, tuple((own[way], none) + (none,) * (depth - 1) for way in range(2)))


def plan(owners, tables, n_slots, n_data, steps, depth, my_data):
    n_units = owners.shape[0]
    padded = jnp.pad(owners.astype(F32), (0, 128 - n_units), constant_values=-1.0)[None]
    wide = np.zeros((8, 128), np.int32)
    wide[: len(tables), :n_units] = tables + 1
    tab, rows = pl.pallas_call(
        functools.partial(plan_kernel, n_units, n_slots, steps, depth, n_data),
        out_shape=[shape((steps, 128), jnp.int32), shape((8, 128), jnp.int32)],
        in_specs=[SMEM_SPEC, VMEM_SPEC, VMEM_SPEC],
        out_specs=[VMEM_SPEC, VMEM_SPEC],
        compiler_params=params(SCOPE),
        name="plan",
    )(my_data.reshape(1), padded, jnp.asarray(wide))
    return tab[:, :4], rows


def spread_init_kernel(slots_ref, bank_ref, out_ref, wide, sem):
    big_ref = [slots_ref[0, s] for s in range(bank_ref.shape[0])]
    n_slots = bank_ref.shape[0]
    for s in range(n_slots):
        copy = pltpu.make_async_copy(bank_ref.at[s], wide.at[s], sem.at[s])
        pl.when(big_ref[s] >= 0)(copy.start)
    for s in range(n_slots):
        copy = pltpu.make_async_copy(bank_ref.at[s], wide.at[s], sem.at[s])
        pl.when(big_ref[s] >= 0)(copy.wait)

        @pl.when(big_ref[s] >= 0)
        def _(s=s):
            out_ref[jnp.maximum(big_ref[s], 0)] = wide[s].astype(BF16)


def spread_init(big_slots, master_bank):
    n_slots, rows, columns = master_bank.shape
    return pl.pallas_call(
        spread_init_kernel,
        out_shape=pltpu.VMEM((N_BIG + BIG, rows, columns), BF16),
        in_specs=[SMEM_SPEC, pl.BlockSpec(memory_space=pltpu.HBM)],
        out_specs=VMEM_SPEC,
        scratch_shapes=[
            pltpu.VMEM((n_slots, rows, columns), F32),
            pltpu.SemaphoreType.DMA((n_slots,)),
        ],
        compiler_params=params(SCOPE),
        name="own_weights",
    )(big_slots, in_hbm(master_bank))


def spread_kernel(places, fetch_at, tab_ref, got, held, out):
    half = held.shape[1] // 2
    for way in range(2):
        rows = pl.ds(way * half, half)
        for k, t in enumerate(places):
            unit = tab_ref[t, 2 * way + 1]

            @pl.when(unit >= 0)
            def _():
                held[jnp.maximum(unit, 0), rows] = got[2 * k + way][...]

        if fetch_at is not None:
            out[way][...] = held[jnp.maximum(tab_ref[fetch_at, 2 * way], 0), rows]


def ring_step(name, tab, held, got, sends, body, work=None, mail=(), mail_rows=0, keep_rows=0):
    rows, columns = held.shape[1:]
    extra, more, operands, shapes, scratch = (tuple(work) + ([],))[:5] if work else ("", None, [], [], [])
    specs = [value[1] if isinstance(value, tuple) else VMEM_SPEC for value in operands]
    operands = [value[0] if isinstance(value, tuple) else value for value in operands]
    operands, specs = list(mail) + list(operands), [VMEM_SPEC] * len(mail) + specs
    n, m, k = len(got), len(operands), len(mail)
    kept = 2 if keep_rows else 0
    shapes = [pltpu.VMEM((keep_rows, columns), BF16)] * kept + list(shapes)

    def kernel(tab_ref, *refs):
        out = refs[n + 1 + m :]
        if body is not None:
            body(tab_ref, refs[:n], out[0], out[1 : 1 + sends], *([refs[n + 1 : n + 1 + k]] if k else []))
        for way in range(kept):
            out[1 + sends + way][...] = refs[way][refs[way].shape[0] - keep_rows :]
        if more is not None:
            more(out[0], *refs[n + 1 + k : n + 1 + m], *out[1 + sends + kept :])

    res = pl.pallas_call(
        kernel,
        out_shape=[pltpu.VMEM(held.shape, held.dtype)] + [pltpu.VMEM((rows // 2 + mail_rows, columns), BF16)] * sends
        + list(shapes),
        in_specs=[SMEM_SPEC] + [VMEM_SPEC] * (n + 1) + specs,
        out_specs=[VMEM_SPEC] * (1 + sends + len(shapes)),
        scratch_shapes=scratch,
        input_output_aliases={1 + n: 0},
        compiler_params=params(SCOPE),
        name=name + extra,
    )(tab, *got, held, *operands)
    return res[0], list(res[1 : 1 + sends]), list(res[1 + sends :])


def ring_perms(n_data):
    order = ring_order(n_data)
    ahead = [(order[i], order[(i + 1) % n_data]) for i in range(n_data)]
    return ahead, [(b, a) for a, b in ahead]


class Spreader:
    def __init__(self, tab, held, n_data, steps, depth):
        self.tab, self.n_data, self.steps, self.depth = tab, n_data, steps, depth
        self.perms = ring_perms(n_data)
        self.held = held
        self.got = {}
        self.at = 0

    def last(self, g):
        return GROUPS[g][1] - 1 + (self.n_data - 2) * self.depth

    def step(self, after=()):
        self.work(None, after)
        return self.sent

    def work(self, work, after=()):
        t = self.at
        self.sent = ()
        if t > self.steps:
            return []
        fetch_at = t if t < self.steps else None
        places = [t - self.depth] if fetch_at is not None else list(range(self.steps - self.depth, self.steps))
        places = [p for p in places if p >= 0]
        self.held, sends, results = ring_step(
            "spread_step",
            order(self.tab, after),
            self.held,
            [value for p in places for value in self.got.pop(p)],
            0 if fetch_at is None else 2,
            functools.partial(spread_kernel, places, fetch_at),
            work,
        )
        if fetch_at is not None:
            self.got[t] = [lax.ppermute(sends[way], "dp", self.perms[way]) for way in range(2)]
        self.at += 1
        self.sent = tuple(sends) + tuple(self.got.get(t - 1, ()))
        return order(results, tuple(self.got.get(t - 1, ())))

    def prepare(self, g):
        while self.at < min(self.last(g) + self.depth, self.steps):
            self.step()


def reduce_kernel(place_at, fetch_at, mail, tab_ref, got, held, out, own=()):
    half = held.shape[1] // 2
    if mail:
        for way in range(2):
            out[way][half:] = own[0][...] if mail == "own" else got[way][half:]
    for way in range(2):
        rows = pl.ds(way * half, half)
        if place_at is not None:
            unit = tab_ref[place_at, 2 * way]

            @pl.when(unit >= 0)
            def _():
                at = BIG + jnp.maximum(unit, 0)
                held[at, rows] = (held[at, rows].astype(F32) + got[way][:half].astype(F32)).astype(BF16)

        out[way][:half] = held[BIG + jnp.maximum(tab_ref[fetch_at, 2 * way + 1], 0), rows]


class Reducer:
    def __init__(self, tab, n_data, steps, depth):
        self.tab, self.n_data, self.steps, self.depth = tab, n_data, steps, depth
        self.perms = [p for p in reversed(ring_perms(n_data))]
        self.held = None
        self.ready = N_BIG
        self.mail = {}
        self.come = {}
        self.got = {}
        self.at = 0

    def lowest(self, k):
        return (self.steps - 1 - k) - (self.n_data - 2) * self.depth

    def step(self, after=()):
        k = self.at
        self.sent = ()
        if k < self.steps and max(self.lowest(k), 0) >= self.ready:
            self.work(None, after)
        return self.sent

    def work(self, work, after=()):
        k = self.at
        self.sent = ()
        tab = order(self.tab, after)
        if k >= self.steps or max(self.lowest(k), 0) < self.ready:
            self.held, unused, results = ring_step("layer_", tab, self.held, [], 0, None, work)
            return results
        place_at = self.steps - 1 - (k - self.depth) if k >= self.depth else None
        payload, hops = self.mail.get(k, (None, 0))
        mail = None if payload is None else "own" if hops == 0 else "pass"
        keep_rows = self.mail[k - self.depth][0].shape[0] if k - self.depth in self.mail else 0
        self.held, sends, results = ring_step(
            "reduce_step",
            tab,
            self.held,
            self.got.get(k - self.depth, []),
            2,
            functools.partial(reduce_kernel, place_at, self.steps - 1 - k, mail),
            work,
            [payload] if mail == "own" else [],
            0 if payload is None else payload.shape[0],
            keep_rows,
        )
        if keep_rows:
            self.come[k - self.depth], results = results[:2], results[2:]
        self.got[k] = [lax.ppermute(sends[way], "dp", self.perms[way]) for way in range(2)]
        self.at += 1
        self.sent = tuple(sends) + tuple(self.got.get(k - 1, ()))
        return order(results, tuple(self.got.get(k - 1, ())))

    def gather(self, *payloads):
        far = self.n_data // 2
        starts = [self.at + i for i in range(len(payloads))]
        for start, payload in zip(starts, payloads):
            for j in range(far):
                self.mail[start + j * self.depth] = (payload, j)
        ISSUED.extend(payloads[1:])
        last = starts[-1] + far * self.depth
        assert len(payloads) <= self.depth and last < self.steps
        while self.at <= last:
            yield ()
        everyone = []
        for start, payload in zip(starts, payloads):
            come = [[self.come[start + j * self.depth][way] for j in range(far)] for way in range(2)]
            everyone.append(order([payload] + come[0][: far - 1] + come[1][::-1], self.sent))
        return everyone

    def drain(self):
        while self.at < self.steps:
            self.step()

    def last(self):
        return [self.got[self.steps - 1 - t][way] for t in range(self.depth) for way in range(2)]


def past(kernel, operands, beside):
    n, m = len(operands), len(beside)
    return lambda *refs: kernel(*refs[:n], *refs[n + m :])


def split_rows(total, keep_ref, send_ref):
    rows = total.shape[0] // 4
    for i in range(2):
        keep_ref[i] = total[2 * i * rows : (2 * i + 1) * rows]
        send_ref[i] = total[(2 * i + 1) * rows : (2 * i + 2) * rows].astype(BF16)


def part_shapes(rows, width):
    return [shape((2, rows // 4, width), F32), shape((2, rows // 4, width), BF16)]


def joined(refs):
    return jnp.concatenate([r[...] for r in refs], 0)


def softmax_parts(q, k):
    scores = dot_nt(q, k) * SCORE_SCALE
    expo = jnp.exp(scores - jnp.max(scores, -1, keepdims=True))
    return expo / jnp.sum(expo, -1, keepdims=True)


def attention_kernel(n_lat, base, w_ref, x0, x1, x2, x3, qkv_ref, mixed_ref, keep_ref, send_ref):
    x = joined((x0, x1, x2, x3))
    for j in range(3):
        qkv_ref[j] = dot(x, w_ref[base + j]).astype(BF16)
    toks = x.shape[0] // n_lat
    heads = w_ref.shape[2] // HEAD_DIM
    for l in range(n_lat):
        rows = slice(l * toks, (l + 1) * toks)
        outs = []
        for h in range(heads):
            cols = slice(h * HEAD_DIM, (h + 1) * HEAD_DIM)
            q, k, v = (qkv_ref[j, rows, cols] for j in range(3))
            outs.append(dot(softmax_parts(q, k).astype(BF16), v))
        mixed_ref[rows, :] = jnp.concatenate(outs, 1).astype(BF16)
    split_rows(dot_nt(mixed_ref[...], w_ref[base + 3]), keep_ref, send_ref)


def attention(x, columns, base, n_lat):
    rows, width = 4 * x[0].shape[0], x[0].shape[1]
    shapes = [shape((3, rows, columns), BF16), shape((rows, columns), BF16)] + part_shapes(rows, width)
    return "_attention", functools.partial(attention_kernel, n_lat, base), x, shapes


def gelu(x):
    return 0.5 * x * (1.0 + jnp.tanh(GELU_C * (x + 0.044715 * x * x * x)))


def gelu_grad(x):
    t = jnp.tanh(GELU_C * (x + 0.044715 * x * x * x))
    return 0.5 * (1.0 + t) + 0.5 * x * (1.0 - t * t) * (GELU_C * (1.0 + 3 * 0.044715 * x * x))


def mlp_kernel(base, w_ref, x0, x1, x2, x3, hidden_ref, active_ref, keep_ref, send_ref):
    x = joined((x0, x1, x2, x3))
    total = None
    for j in range(4):
        hidden = dot(x, w_ref[base + j])
        hidden_ref[j] = hidden
        active = gelu(hidden).astype(BF16)
        active_ref[j] = active
        part = dot_nt(active, w_ref[base + 4 + j])
        total = part if total is None else total + part
    split_rows(total, keep_ref, send_ref)


def mlp(x, columns, base):
    rows, width = 4 * x[0].shape[0], x[0].shape[1]
    shapes = [shape((4, rows, columns), F32), shape((4, rows, columns), BF16)] + part_shapes(rows, width)
    return "_mlp", functools.partial(mlp_kernel, base), x, shapes


def mlp_back_kernel(base, w_ref, d0, d1, d2, d3, hidden_ref, dh_ref, keep_ref, send_ref):
    d = joined((d0, d1, d2, d3))
    total = None
    for j in range(4):
        dh = (gelu_grad(hidden_ref[j]) * dot(d, w_ref[base + 4 + j])).astype(BF16)
        dh_ref[j] = dh
        part = dot_nt(dh, w_ref[base + j])
        total = part if total is None else total + part
    split_rows(total, keep_ref, send_ref)


def mlp_back(d, hidden, base):
    rows, width = 4 * d[0].shape[0], d[0].shape[1]
    shapes = [shape(hidden.shape, BF16)] + part_shapes(rows, width)
    return "_mlp_back", functools.partial(mlp_back_kernel, base), [*d, hidden], shapes


def attention_back_kernel(n_lat, base, w_ref, d0, d1, d2, d3, qkv_ref, dqkv_ref, keep_ref, send_ref):
    d_mixed = dot(joined((d0, d1, d2, d3)), w_ref[base + 3]).astype(BF16)
    toks = d_mixed.shape[0] // n_lat
    heads = w_ref.shape[2] // HEAD_DIM
    for l in range(n_lat):
        rows = slice(l * toks, (l + 1) * toks)
        outs = [[], [], []]
        for h in range(heads):
            cols = slice(h * HEAD_DIM, (h + 1) * HEAD_DIM)
            q, k, v = (qkv_ref[j, rows, cols] for j in range(3))
            do = d_mixed[rows, cols]
            probs = softmax_parts(q, k)
            d_probs = dot_nt(do, v)
            d_scores = probs * (d_probs - jnp.sum(probs * d_probs, -1, keepdims=True))
            d_scores = d_scores.astype(BF16)
            outs[0].append(dot(d_scores, k) * SCORE_SCALE)
            outs[1].append(dot_tn(d_scores, q) * SCORE_SCALE)
            outs[2].append(dot_tn(probs.astype(BF16), do))
        for j in range(3):
            dqkv_ref[j, rows, :] = jnp.concatenate(outs[j], 1).astype(BF16)
    total = sum(dot_nt(dqkv_ref[j], w_ref[base + j]) for j in range(3))
    split_rows(total, keep_ref, send_ref)


def attention_back(d, qkv, base, n_lat):
    rows, width = 4 * d[0].shape[0], d[0].shape[1]
    shapes = [shape(qkv.shape, BF16)] + part_shapes(rows, width)
    return "_attention_back", functools.partial(attention_back_kernel, n_lat, base), [*d, qkv], shapes


def weight_grad_kernel(counts, n_lat, base, out_ref, *refs):
    n = len(counts)
    lefts, rights, (mean_ref, sum_ref) = refs[: 4 * n], refs[4 * n : 5 * n], refs[-2:]
    at = 0
    for k, count in enumerate(counts):
        a = joined(lefts[4 * k : 4 * k + 4])
        toks = a.shape[0] // n_lat

        def rows_of(x, scale):
            parts = [
                jnp.sum(x[l * toks : (l + 1) * toks].astype(F32), 0, keepdims=True) * scale for l in range(n_lat)
            ]
            return jnp.concatenate(parts + [jnp.zeros((8 - n_lat, x.shape[1]), F32)], 0).astype(BF16)

        mean = rows_of(a, 1.0 / toks)
        mean_ref[k] = mean.astype(F32)
        for j in range(count):
            b = rights[k][j]
            total = rows_of(b, 1.0)
            sum_ref[at] = total.astype(F32)
            out_ref[BIG + base + at] = (dot_tn(a, b) - dot_tn(mean, total)).astype(BF16)
            at += 1


def weight_grads(base, pairs, n_lat):
    counts = [right.shape[0] for _, right in pairs]
    width, columns = pairs[0][0][0].shape[1], pairs[0][1].shape[2]
    operands = [part for left, _ in pairs for part in left] + [right for _, right in pairs]
    shapes = [shape((len(pairs), 8, width), F32), shape((sum(counts), 8, columns), F32)]
    return "_weight_grads", functools.partial(weight_grad_kernel, counts, n_lat, base), operands, shapes


def small_weights(small_ref, bank_ref, wide, sem, use):
    units = [small_ref[s] for s in range(bank_ref.shape[0])]
    ours = [(unit >= 0) & (unit != TIME_AT) for unit in units]
    copies = [pltpu.make_async_copy(bank_ref.at[s], wide.at[s], sem.at[s]) for s in range(len(units))]
    for s, copy in enumerate(copies):
        pl.when(ours[s])(copy.start)
    for s, copy in enumerate(copies):

        @pl.when(ours[s])
        def _(s=s, copy=copy):
            copy.wait()
            use(jnp.maximum(units[s], 0), wide[s].astype(BF16))


def modulation_kernel(held_ref, small_ref, cond_ref, bank_ref, out_ref, wide, sem):
    out_ref[...] = jnp.zeros_like(out_ref)

    def use(unit, weight):
        out_ref[unit] = dot(cond_ref[...], weight)

    small_weights(small_ref, bank_ref, wide, sem, use)


def bank_scratch(bank):
    return [pltpu.VMEM(bank.shape, F32), pltpu.SemaphoreType.DMA((bank.shape[0],))]


def modulations(small_slots, cond_in, bank):
    operands = [(small_slots, SMEM_SPEC), cond_in, (in_hbm(bank), pl.BlockSpec(memory_space=pltpu.HBM))]
    shapes = [shape((SMALL_ROWS, cond_in.shape[0], bank.shape[2]), F32)]
    return "_modulations", modulation_kernel, operands, shapes, bank_scratch(bank)


def cond_back_kernel(n_mail, held_ref, small_ref, peer_ref, *refs):
    mail, (bank_ref, d_ref, out_ref, wide, sem) = refs[:n_mail], refs[n_mail:]
    if n_mail == 1:
        d_ref[...] = mail[0][...]
    else:
        n_lat = d_ref.shape[0] // n_mail
        for i in range(n_mail):
            for l in range(n_lat):
                d_ref[peer_ref[i] * n_lat + l] = mail[i][l * SMALL_ROWS : (l + 1) * SMALL_ROWS]
    out_ref[...] = jnp.zeros_like(out_ref)

    def use(unit, weight):
        d = d_ref[...].astype(F32)
        d = jnp.sum(jnp.where(lax.broadcasted_iota(jnp.int32, d.shape, 1) == unit, d, 0.0), 1)
        out_ref[...] += dot_nt(d.astype(BF16), weight)

    small_weights(small_ref, bank_ref, wide, sem, use)


def cond_back(small_slots, peers, mail, n_all, bank):
    columns = bank.shape[2]
    operands = [(small_slots, SMEM_SPEC), (peers, SMEM_SPEC)] + list(mail)
    operands += [(in_hbm(bank), pl.BlockSpec(memory_space=pltpu.HBM))]
    shapes = [shape((n_all, SMALL_ROWS, columns), BF16), shape((n_all, bank.shape[1]), F32)]
    return "_cond_back", functools.partial(cond_back_kernel, len(mail)), operands, shapes, bank_scratch(bank)


def mail_sum_kernel(n_mail, held_ref, peer_ref, *refs):
    mail, (out_ref, whole) = refs[:n_mail], refs[n_mail:]
    rows = out_ref.shape[0]
    for i in range(n_mail):
        whole[peer_ref[i]] = mail[i][:rows].astype(F32) + mail[i][rows:].astype(F32)
    total = whole[0]
    for i in range(1, n_mail):
        total = total + whole[i]
    out_ref[...] = total


def mail_sum(peers, mail):
    rows, columns = mail[0].shape[0] // 2, mail[0].shape[1]
    scratch = [pltpu.VMEM((len(mail), rows, columns), F32)]
    operands = [(peers, SMEM_SPEC)] + list(mail)
    return "_mail_sum", functools.partial(mail_sum_kernel, len(mail)), operands, [shape((rows, columns), F32)], scratch


def halves(x):
    high = x.astype(BF16)
    return high, (x - high.astype(F32)).astype(BF16)


def newton_sweep_coarse(x):
    xh = x.astype(BF16)
    gram = dot_tn(xh, xh)
    gh = gram.astype(BF16)
    poly = NS_COEF[1] * gram + NS_COEF[2] * dot(gh, gh)
    return NS_COEF[0] * x + dot(xh, poly.astype(BF16))


def newton_sweep(x):
    xh, xl = halves(x)
    cross = dot_tn(xh, xl)
    gram = dot_tn(xh, xh) + (cross + cross.T)
    gh, gl = halves(gram)
    cross = dot(gh, gl)
    square = dot(gh, gh) + (cross + cross.T)
    ph, pl_ = halves(NS_COEF[1] * gram + NS_COEF[2] * square)
    return NS_COEF[0] * x + (dot(xh, ph) + (dot(xl, ph) + dot(xh, pl_)))


def newton_kernel(n_last, base, big_ref, left_ref, right_ref, tab_ref, a_ref, b_ref, bank_ref, mom_ref, *refs):
    held, got = refs[0], refs[1 : 1 + n_last]
    new_ref, mom_new_ref, mark_ref, grad, sem = refs[-5:]
    s = base + pl.program_id(0)
    mark_ref[...] = jnp.zeros_like(mark_ref)
    unit, left, right = big_ref[s], left_ref[s], right_ref[s]
    half = got[0].shape[0]

    @pl.when(right < 0)
    def _():
        new_ref[...] = bank_ref[...]
        mom_new_ref[...] = mom_ref[...]

    @pl.when(right >= 0)
    def _():
        copy = pltpu.make_async_copy(held.at[BIG + jnp.maximum(unit, 0)], grad, sem.at[0])
        pl.when(unit >= 0)(copy.start)
        mom_new_ref[0] = 0.5 * mom_ref[0] + dot_tn(
            a_ref[jnp.maximum(left, 0)], b_ref[jnp.maximum(right, 0)]
        )
        pl.when(unit >= 0)(copy.wait)

        @pl.when(unit >= 0)
        def _():
            mom_new_ref[0] += grad[...].astype(F32)

        for i in range(n_last):
            rows = slice((i % 2) * half, (i % 2 + 1) * half)

            @pl.when((tab_ref[i // 2, 2 * (i % 2)] == unit) & (unit >= 0))
            def _(i=i, rows=rows):
                mom_new_ref[0, rows] += got[i][...].astype(F32)

        block = mom_new_ref[0]
        norm = jnp.sqrt(jnp.sum(block * block)) + 1e-07
        x = block / norm
        for sweep in range(5):
            x = newton_sweep_coarse(x) if sweep < 3 else newton_sweep(x)
        new_ref[0] = bank_ref[0] - LR_MUON * x


class Optimizer:
    def __init__(self, slots, tab, a_all, b_all, master, momentum, held, got):
        self.scalars = [*slots, tab]
        self.arrays = [a_all, b_all, in_hbm(master), in_hbm(momentum), held, *got]
        self.news = []
        self.at = 0

    def step(self, after=(), count=3):
        a_all, b_all, master, momentum, held, *got = self.arrays
        n_slots, rows, columns = master.shape
        base, count = self.at, min(count, n_slots - self.at)
        if count == 0:
            return ()
        self.at += count
        block = pl.BlockSpec((1, rows, columns), lambda s, *t: (base + s, 0, 0))
        any_spec = pl.BlockSpec(memory_space=pl.ANY)
        scalars = [order(self.scalars[0], after)] + self.scalars[1:]
        first = len(scalars) + len(self.arrays)
        *self.news, mark = pl.pallas_call(
            functools.partial(newton_kernel, len(got), base),
            grid_spec=pltpu.PrefetchScalarGridSpec(
                num_scalar_prefetch=len(scalars),
                grid=(count,),
                in_specs=[
                    pl.BlockSpec(a_all.shape, lambda s, *t: (0, 0, 0)),
                    pl.BlockSpec(b_all.shape, lambda s, *t: (0, 0, 0)),
                    block,
                    block,
                    any_spec,
                ]
                + [pl.BlockSpec(g.shape, lambda s, *t: (0, 0)) for g in got]
                + [any_spec] * len(self.news),
                out_specs=[block, block, pl.BlockSpec((8, 128), lambda s, *t: (0, 0))],
                scratch_shapes=[pltpu.VMEM((rows, columns), BF16), pltpu.SemaphoreType.DMA((1,))],
            ),
            out_shape=[shape(master.shape, F32), shape(momentum.shape, F32), shape((8, 128), F32)],
            input_output_aliases={first + i: i for i in range(len(self.news))},
            compiler_params=params(SCOPE, dimension_semantics=("arbitrary",)),
            name="optimizer",
        )(*scalars, *self.arrays, *self.news)
        return (mark,)

    def all(self):
        while self.at < self.arrays[2].shape[0]:
            self.step()
        return self.news


def layer_norm(values):
    centered = values - jnp.mean(values, -1, keepdims=True)
    inv_std = lax.rsqrt(jnp.mean(centered * centered, -1, keepdims=True) + 1e-06)
    return centered * inv_std, inv_std


def norm_back(grad_out, normed, inv_std):
    return inv_std * (
        grad_out
        - jnp.mean(grad_out, -1, keepdims=True)
        - normed * jnp.mean(grad_out * normed, -1, keepdims=True)
    )


def added(keep_ref, got_ref, far_ref):
    return keep_ref[0] + got_ref[0].astype(F32) + far_ref[...].astype(F32)


def row_of(mods_ref, at):
    return mods_ref[at : at + 1, :]


def enter_kernel(at, noisy_ref, patch_ref, place_ref, mods_ref, stream_ref, inner_ref, normed_ref, inv_ref):
    stream = dot(noisy_ref[...], patch_ref[...]) + place_ref[...]
    stream_ref[...] = stream
    normed, inv = layer_norm(stream)
    inner_ref[...] = (normed * (1.0 + row_of(mods_ref, at[1])) + row_of(mods_ref, at[0])).astype(BF16)
    normed_ref[...] = normed
    inv_ref[...] = jnp.broadcast_to(inv, inv_ref.shape)


def enter(noisy, patch, places, mods, at):
    rows, width = places.shape
    full = shape((rows, width), F32)
    return pl.pallas_call(
        functools.partial(enter_kernel, at),
        out_shape=[full, shape((rows, width), BF16), full, shape((rows, 128), F32)],
        compiler_params=params(SCOPE),
        name="enter",
    )(noisy, patch, places, mods)


def residual_kernel(
    at, keep_ref, got_ref, far_ref, stream_ref, mods_ref, part_ref, next_ref, inner_ref, normed_ref, inv_ref
):
    part = added(keep_ref, got_ref, far_ref)
    part_ref[...] = part
    stream = stream_ref[...] + row_of(mods_ref, at[0]) * part
    next_ref[...] = stream
    normed, inv = layer_norm(stream)
    inner_ref[...] = (normed * (1.0 + row_of(mods_ref, at[2])) + row_of(mods_ref, at[1])).astype(BF16)
    normed_ref[...] = normed
    inv_ref[...] = jnp.broadcast_to(inv, inv_ref.shape)


def residual(parts, stream, mods, at):
    rows, width = stream.shape
    full = shape((rows, width), F32)
    return pl.pallas_call(
        functools.partial(residual_kernel, at),
        out_shape=[full, full, shape((rows, width), BF16), full, shape((rows, 128), F32)],
        compiler_params=params(SCOPE),
        name="residual",
    )(*parts, stream, mods)


def leave_kernel(
    at,
    count_all,
    keep_ref,
    got_ref,
    far_ref,
    stream_ref,
    mods_ref,
    head_ref,
    target_ref,
    grad_ref,
    next_ref,
    rows_ref,
    edge_ref,
):
    branch = added(keep_ref, got_ref, far_ref)
    gate, shift, scale = (row_of(mods_ref, i) for i in at)
    normed, inv = layer_norm(stream_ref[...] + gate * branch)
    inner = (normed * (1.0 + scale) + shift).astype(BF16)
    head = head_ref[...]
    error = dot_nt(inner, head) - target_ref[...]
    d_output = (2.0 * error / count_all).astype(BF16)
    d_inner = dot(d_output, head)
    grad = norm_back(d_inner * (1.0 + scale), normed, inv)
    grad_ref[...] = grad
    next_ref[...] = (gate * grad).astype(BF16)
    rows_ref[...] = jnp.zeros_like(rows_ref)
    rows_ref[0:1, :] = jnp.sum(d_inner, 0, keepdims=True)
    rows_ref[1:2, :] = jnp.sum(d_inner * normed, 0, keepdims=True)
    rows_ref[2:3, :] = jnp.sum(grad * branch, 0, keepdims=True)
    n_patch = head.shape[0]
    loss = jnp.sum(jnp.sum(error * error, 1, keepdims=True), 0, keepdims=True) / count_all
    edge_ref[:n_patch, :] = dot_tn(d_output, inner)
    edge_ref[n_patch:, :] = jnp.broadcast_to(loss, (8, edge_ref.shape[1]))


def leave(parts, stream, mods, head, target, at, count_all):
    rows, width = stream.shape
    return pl.pallas_call(
        functools.partial(leave_kernel, at, count_all),
        out_shape=[
            shape((rows, width), F32),
            shape((rows, width), BF16),
            shape((SMALL_ROWS, width), F32),
            shape((head.shape[0] + 8, width), F32),
        ],
        compiler_params=params(SCOPE),
        name="leave",
    )(*parts, stream, mods, head, target)


def back_kernel(
    at,
    gate_at,
    first,
    keep_ref,
    got_ref,
    far_ref,
    normed_ref,
    inv_ref,
    grad_ref,
    part_ref,
    mods_ref,
    rows_in_ref,
    out_ref,
    next_ref,
    rows_ref,
):
    d_inner = added(keep_ref, got_ref, far_ref)
    normed = normed_ref[...]
    inv = inv_ref[:, 0:1]
    grad = grad_ref[...] + norm_back(d_inner * (1.0 + row_of(mods_ref, at)), normed, inv)
    out_ref[...] = grad
    rows_ref[...] = rows_in_ref[...]
    rows_ref[first : first + 1, :] = jnp.sum(d_inner, 0, keepdims=True)
    rows_ref[first + 1 : first + 2, :] = jnp.sum(d_inner * normed, 0, keepdims=True)
    if gate_at is None:
        next_ref[...] = grad.astype(BF16)
    else:
        next_ref[...] = (row_of(mods_ref, gate_at) * grad).astype(BF16)
        rows_ref[first + 2 : first + 3, :] = jnp.sum(grad * part_ref[...], 0, keepdims=True)


def back(parts, normed, inv, grad, part, mods, rows_in, at, gate_at, first, beside):
    rows, width = grad.shape
    operands = (*parts, normed, inv, grad, part, mods, rows_in)
    return pl.pallas_call(
        past(functools.partial(back_kernel, at, gate_at, first), operands, beside),
        out_shape=[shape((rows, width), F32), shape((rows, width), BF16), shape(rows_in.shape, F32)],
        compiler_params=params(SCOPE),
        name="back",
    )(*operands, *beside)


def tables_kernel(n_patch, fix_ref, edge_ref, time_ref, class_ref, table_ref, first_ref, second_ref, *outs):
    new_ref, first_new_ref, second_new_ref = outs
    at = 0
    for ref, low, count in (
        (edge_ref, 0, n_patch),
        (time_ref, 0, FREQ),
        (class_ref, 0, CLASSES),
        (edge_ref, n_patch, n_patch),
    ):
        rows = slice(at, at + count)
        grad = ref[low : low + count, :]
        first = 0.5 * first_ref[rows, :] + 0.5 * grad
        second = 0.5 * second_ref[rows, :] + 0.5 * grad * grad
        first_new_ref[rows, :] = first
        second_new_ref[rows, :] = second
        new_ref[rows, :] = table_ref[rows, :] * (1.0 - LR_ADAM * WEIGHT_DECAY) - LR_ADAM * (
            first / fix_ref[0]
        ) / (jnp.sqrt(second / fix_ref[0]) + 1e-08)
        at += count


def update_tables(n_patch, bias_fix, edges, grad_time, grad_class, table, first, second):
    return pl.pallas_call(
        functools.partial(tables_kernel, n_patch),
        out_shape=[shape(table.shape, F32)] * 3,
        in_specs=[SMEM_SPEC] + [VMEM_SPEC] * 6,
        compiler_params=params(SCOPE),
        name="update_tables",
    )(bias_fix, edges, grad_time, grad_class, table, first, second)


def position_rows(first, rows):
    quarter = D // 4
    omega = jnp.exp(-math.log(10000.0) * jnp.arange(quarter, dtype=F32) / quarter)
    places = first + jnp.arange(rows, dtype=jnp.int32)
    rows_at = (places // GRID).astype(F32)[:, None] * omega[None]
    cols_at = (places % GRID).astype(F32)[:, None] * omega[None]
    return jnp.concatenate([jnp.sin(rows_at), jnp.cos(rows_at), jnp.sin(cols_at), jnp.cos(cols_at)], 1)


def time_features(timesteps):
    half_freq = FREQ // 2
    rates = jnp.exp(-math.log(10000.0) * jnp.arange(half_freq, dtype=F32) / half_freq)
    angles = timesteps.astype(F32)[:, None] * rates[None]
    return jnp.concatenate([jnp.cos(angles), jnp.sin(angles)], 1)


def shards(
    noisy_latents,
    noise_target,
    timesteps,
    labels,
    owners,
    step_count,
    master_bank,
    momentum_bank,
    embed_tables,
    embed_first,
    embed_second,
):
    n_lat, n_tok, n_patch = noisy_latents.shape
    n_slots, width, columns = master_bank.shape
    n_data = lax.axis_size("dp")
    my_data = lax.axis_index("dp")
    my_tensor = lax.axis_index("tensor")
    n_all = n_lat * n_data
    own_rows = n_lat * n_tok // 4
    count_all = float(n_all * n_tok * n_patch)
    depth = 2 if n_data <= 8 else 1
    steps = N_BIG + (n_data - 2) * depth

    kind = [2 + 2 * g + (b >= low + (3, 4)[g % 2]) for g, (low, high) in enumerate(GROUPS) for b in range(low, high)]
    slot_tables = np.stack(
        [
            BIG_OF,
            SMALL_OF,
            np.where(BIG_OF >= 0, np.array(kind)[BIG_OF], np.where(SMALL_OF == TIME_AT, 1, 0)),
            np.where(BIG_OF >= 0, SMALL_ROWS + BIG_OF, SMALL_OF),
        ]
    )
    tab, planned = plan(owners, slot_tables, n_slots, n_data, steps, depth, my_data)

    def flag(value):
        return jnp.asarray(value, jnp.int32).reshape(1)

    first_row = my_tensor * own_rows
    early = dict(
        slots=planned[:4, :n_slots],
        peers=planned[5, :n_data],
        chip=flag(my_tensor // 2),
        core=flag(my_tensor % 2),
        data=flag(my_data),
        bits=[flag((my_data // (1 << i)) % 2) for i in range((n_data - 1).bit_length())],
        time_mine=planned[4, 1:2],
        time_w2=lax.dynamic_index_in_dim(master_bank, planned[4, 0], 0, keepdims=False).astype(BF16),
        noisy=lax.dynamic_slice_in_dim(noisy_latents.reshape(n_lat * n_tok, n_patch), first_row, own_rows, 0),
        target=lax.dynamic_slice_in_dim(noise_target.reshape(n_lat * n_tok, n_patch), first_row, own_rows, 0),
        places=position_rows(first_row % n_tok, own_rows),
        ids=jnp.stack([timesteps, labels], 1),
        bias_fix=1.0 - jnp.power(0.5, step_count.astype(F32)),
        tab=tab,
        edge_cols=jnp.concatenate(
            [embed_tables[:n_patch], embed_tables[n_patch + FREQ + CLASSES :]], 0
        ).astype(BF16),
        time_w1=embed_tables[n_patch : n_patch + FREQ].astype(BF16),
        class_w=embed_tables[n_patch + FREQ : n_patch + FREQ + CLASSES].astype(BF16),
    )
    flat, tree = jax.tree.flatten(early)
    early = jax.tree.unflatten(tree, lax.optimization_barrier(tuple(flat)))
    chip, core, data, time_w2, noisy_own = (early[k] for k in ("chip", "core", "data", "time_w2", "noisy"))
    tab, peers = early["tab"], early["peers"]
    big_slots, small_slots, left_slots, right_slots = (early["slots"][i] for i in range(4))
    spread = Spreader(tab, spread_init(early["slots"], master_bank), n_data, steps, depth)
    spread.step()
    ring = Reducer(tab, n_data, steps, depth)

    def conditioning():
        ids, edge_rows = yield from together(
            dp_sum(own_latents(early["ids"], 0, data, n_data), n_data),
            gather_columns(early["edge_cols"], chip, core),
        )
        features = time_features(ids[:, 0]).astype(BF16)
        time_one = jnp.dot(features, early["time_w1"], preferred_element_type=F32)
        time_act = yield from gather_columns(jax.nn.silu(time_one).astype(BF16), chip, core)
        second = jnp.dot(time_act, time_w2, preferred_element_type=F32)
        second = yield from dp_sum(jnp.where(is_at(early["time_mine"], 1, 2), second, 0.0), n_data)
        onehot = ids[:, 1:2] == jnp.arange(CLASSES, dtype=jnp.int32)[None]
        condition = second + jnp.dot(onehot.astype(BF16), early["class_w"], preferred_element_type=F32)
        cond_in = yield from gather_columns(jax.nn.silu(condition).astype(BF16), chip, core)
        (mods,) = spread.work(modulations(small_slots, cond_in, master_bank), ISSUED)
        ISSUED.clear()
        bit = n_data // 2
        while bit:
            half = mods.shape[1] // 2
            sides = mods[:, :half], mods[:, half:]
            side = early["bits"][bit.bit_length() - 1]
            mods = pick(*sides, side) + (yield flip(pick(*sides, side, True), "dp", bit, n_data))
            bit //= 2
        latents = mods[:, 0], mods[:, 1]
        across = yield x_flip(pick(*latents, chip, True))
        own = pick(*latents, chip)
        pair = [pick(own, across, chip), pick(across, own, chip)]
        beside = core_flip(jnp.concatenate(pair, 1))
        beside = [beside[:, x * columns : (x + 1) * columns] for x in range(2)]
        blocks = [pick(one, two, core) for x in range(2) for one, two in ((pair[x], beside[x]), (beside[x], pair[x]))]
        return edge_rows, features, time_one, time_act, onehot, condition, cond_in, jnp.concatenate(blocks, 1)

    def forward():
        cond = yield from conditioning()
        edge_rows, mods = cond[0], cond[-1]
        stream, inner, normed, inv = enter(
            noisy_own, edge_rows[:n_patch], early["places"], mods, (small_at(0, 0), small_at(0, 1))
        )
        kept = []
        for layer in range(LAYERS):
            inner = yield from gather_tokens(inner)
            spread.prepare(2 * layer)
            qkv, mixed, keep, send = spread.work(attention(inner, columns, BIG * layer, n_lat))
            parts = yield from scatter_tokens(keep, send)
            attended, stream, inner_mid, normed_mid, inv_mid = residual(
                parts, stream, mods, tuple(small_at(layer, i) for i in (2, 3, 4))
            )
            inner_mid = yield from gather_tokens(inner_mid)
            spread.prepare(2 * layer + 1)
            hidden, active, keep, send = spread.work(mlp(inner_mid, columns, BIG * layer + 4))
            parts = yield from scatter_tokens(keep, send)
            kept.append([inner, normed, inv, qkv, mixed, attended, inner_mid, normed_mid, inv_mid, hidden, active])
            if layer + 1 < LAYERS:
                branch, stream, inner, normed, inv = residual(
                    parts,
                    stream,
                    mods,
                    (small_at(layer, 5), small_at(layer + 1, 0), small_at(layer + 1, 1)),
                )
                kept[-1].append(branch)
        return cond, kept, parts, stream

    cond, kept, parts_last, stream_last = drive(forward(), spread.step)
    edge_rows, features, time_one, time_act, onehot, condition, cond_in, mods = cond
    ring.held = spread.held

    def backward():
        grad, d_branch, rows, edge_head = leave(
            parts_last,
            stream_last,
            mods,
            edge_rows[n_patch:],
            early["target"],
            (small_at(LAYERS - 1, 5), SHIFT_F, SCALE_F),
            count_all,
        )
        lefts, rights = {}, {}
        for layer in reversed(range(LAYERS)):
            inner, normed, inv, qkv, mixed, attended, inner_mid, normed_mid, inv_mid, hidden, active = kept[layer][:11]
            d_branch = yield from gather_tokens(d_branch, 1 if layer == LAYERS - 1 else 2)
            d_hidden, keep, send = ring.work(mlp_back(d_branch, hidden, BIG * layer + 4))
            work = scatter_tokens(keep, send)
            flying = next(work)
            lefts[2 * layer + 1], rights[2 * layer + 1] = ring.work(
                weight_grads(BIG * layer + 4, [(inner_mid, d_hidden), (d_branch, active)], n_lat), ISSUED
            )
            ring.ready = BIG * layer + 4
            if layer == LAYERS - 1:
                ring.step((lefts[2 * layer + 1],))
            parts = finish(work, order(flying, (lefts[2 * layer + 1],) + ring.sent))
            grad, d_attended, rows = back(
                parts,
                normed_mid,
                inv_mid,
                grad,
                attended,
                mods,
                rows,
                small_at(layer, 4),
                small_at(layer, 2),
                small_at(layer, 3),
                [ring.held],
            )
            d_attended = yield from gather_tokens(d_attended, 2)
            d_qkv, keep, send = ring.work(attention_back(d_attended, qkv, BIG * layer, n_lat))
            work = scatter_tokens(keep, send)
            flying = next(work)
            lefts[2 * layer], rights[2 * layer] = ring.work(
                weight_grads(BIG * layer, [(inner, d_qkv), (d_attended, mixed[None])], n_lat), ISSUED
            )
            ring.ready = BIG * layer
            parts = finish(work, order(flying, (lefts[2 * layer],) + ring.sent))
            below = kept[layer - 1][11] if layer else normed
            grad, d_branch, rows = back(
                parts,
                normed,
                inv,
                grad,
                below,
                mods,
                rows,
                small_at(layer, 1),
                small_at(layer - 1, 5) if layer else None,
                small_at(layer, 0),
                [ring.held],
            )
        return (yield from cond_backward(rows, d_branch, edge_head, lefts, rights))

    def cond_backward(rows, d_stream, edge_head, lefts, rights):
        mine = core_columns_sum(rows, core)
        near, far = pick(*mine, chip), x_flip(pick(*mine, chip, True))
        own = [pick(near, far, chip).astype(BF16), pick(far, near, chip).astype(BF16)]
        if n_data == 8:
            first, *others = factor_rows(lefts, rights)
            one, two = jnp.concatenate(own + [first], 0), jnp.concatenate(others, 0)
            one, two = (jnp.pad(v, ((0, -len(v) % 96), (0, 0))) for v in (one, two))
            latents, others = yield from ring.gather(one, two)
            n_own, n_rows = n_lat * SMALL_ROWS, first.shape[0]
            factors = [v[n_own : n_own + n_rows] for v in latents] + [v[:n_rows] for v in others]
            factors = jnp.concatenate(factors, 0).reshape(n_all, n_rows, columns)
        else:
            latents = [(yield from dp_sum(own_latents(jnp.stack(own, 0), 0, data, n_data), n_data))]
        d_small, d_cond = ring.work(cond_back(small_slots, peers, latents, n_all, master_bank), ISSUED)
        ISSUED.clear()
        d_cond = yield from own_columns_sum(d_cond, chip, core)
        if n_data == 8:
            (parts,) = yield from ring.gather(jnp.concatenate(halves(d_cond), 0))
            (d_cond,) = ring.work(mail_sum(peers, parts))
        else:
            d_cond = yield from dp_sum(d_cond, n_data)
        unused, silu_pull = jax.vjp(jax.nn.silu, condition)
        d_condition = silu_pull(d_cond)[0]
        d_second = d_condition.astype(BF16)
        grad_class = lax.dot_general(
            onehot.astype(F32), d_condition, (((0,), (0,)), ((), ())), precision=HIGHEST_PREC
        )
        d_time_act = lax.dot_general(d_second, time_w2, (((1,), (1,)), ((), ())), preferred_element_type=F32)
        d_time_act = jnp.where(is_at(early["time_mine"], 1, 2), d_time_act, 0.0)
        grad_patch = lax.dot_general(noisy_own, d_stream, (((0,), (0,)), ((), ())), preferred_element_type=F32)
        sums = yield from own_columns_sum(jnp.concatenate([d_time_act, grad_patch, edge_head], 0), chip, core)
        ring.drain()
        if n_data != 8:
            factors = yield from dp_rows(jnp.stack(factor_rows(lefts, rights)), n_data)
        n_left = sum(v.shape[0] for v in lefts.values())
        a_rows = jnp.concatenate([factors[:, j * n_left : (j + 1) * n_left] for j in range(4)], 2).transpose(1, 0, 2)
        b_rows = factors[:, 4 * n_left : 4 * n_left + N_BIG].transpose(1, 0, 2)
        return d_small, d_second, grad_class, sums, a_rows, b_rows

    def factor_rows(lefts, rights):
        a_rows = jnp.concatenate([lefts[g] for g in range(len(GROUPS))], 0)
        b_rows = jnp.concatenate([rights[g] for g in range(len(GROUPS))], 0)
        parts = []
        for l in range(n_lat):
            part = [a_rows[:, l, j * columns : (j + 1) * columns] for j in range(4)] + [b_rows[:, l]]
            part = jnp.concatenate(part, 0).astype(BF16)
            parts.append(jnp.pad(part, ((0, -len(part) % 32), (0, 0))))
        return parts

    d_small, d_second, grad_class, sums, a_rows, b_rows = drive(backward(), ring.step)
    a_all = jnp.concatenate([cond_in[None], time_act[None], a_rows], 0)
    small_rows = jnp.where(
        jnp.arange(SMALL_ROWS)[:, None, None] == TIME_AT, d_second[None], d_small.transpose(1, 0, 2)
    )
    b_all = jnp.concatenate([small_rows, b_rows], 0)
    optimizer = Optimizer(
        (big_slots, left_slots, right_slots), tab, a_all, b_all, master_bank, momentum_bank, ring.held, ring.last()
    )
    adding = dp_sum(order(sums, ring.last()), n_data)
    flying = next(adding)
    try:
        while True:
            (mark,) = optimizer.step(ISSUED[-2:-1]) or (jnp.zeros((8, 128), F32),)
            flying = adding.send(flying + mark[:1, :1])
    except StopIteration as end:
        sums = end.value
    master_new, momentum_new = optimizer.all()
    d_time_act, edges = sums[:n_all], sums[n_all:]
    unused, time_pull = jax.vjp(jax.nn.silu, time_one)
    d_time_one = time_pull(d_time_act)[0].astype(BF16)
    grad_time_one = lax.dot_general(
        features, d_time_one, (((0,), (0,)), ((), ())), preferred_element_type=F32
    )
    loss = edges[2 * n_patch, 0]
    embed_new, first_new, second_new = update_tables(
        n_patch, early["bias_fix"], edges, grad_time_one, grad_class, embed_tables, embed_first, embed_second
    )
    return (loss, master_new, momentum_new, embed_new, first_new, second_new)


def solution(mesh):
    placed = (
        P("dp", None, None),
        P("dp", None, None),
        P("dp"),
        P("dp"),
        P(),
        P(),
        P("dp", None, "tensor"),
        P("dp", None, "tensor"),
        P(None, "tensor"),
        P(None, "tensor"),
        P(None, "tensor"),
    )
    return jax.shard_map(
        shards,
        mesh=mesh,
        in_specs=placed,
        out_specs=(
            P(),
            P("dp", None, "tensor"),
            P("dp", None, "tensor"),
            P(None, "tensor"),
            P(None, "tensor"),
            P(None, "tensor"),
        ),
        check_vma=False,
    )
```

```python
import functools
import math

import jax
import jax.numpy as jnp
import numpy as np
from jax import lax
from jax.experimental import pallas as pl
from jax.experimental.pallas import tpu as pltpu
from jax.sharding import PartitionSpec as P

D = 1024
HEAD_DIM = 64
FREQ = 256
CLASSES = 1000
GRID = 16
LAYERS = 2
BIG = 12
N_BIG = BIG * LAYERS
SMALL_ROWS = 16
SHIFT_F, SCALE_F, TIME_AT = 0, 1, 6 * LAYERS + 2


def small_at(layer, i):
    first = 2 + 6 * (LAYERS - 1 - layer)
    return first + (4, 5, 3, 1, 2, 0)[i]


NS_COEF = (3.4445, -4.775, 2.0315)
LR_MUON = 0.5
LR_ADAM = 0.02
WEIGHT_DECAY = 0.1
SCORE_SCALE = 1.0 / math.sqrt(HEAD_DIM)
HIGHEST_PREC = lax.Precision.HIGHEST

F32 = jnp.float32
BF16 = jnp.bfloat16
SCOPE = 16
GELU_C = math.sqrt(2.0 / math.pi)
GROUPS = ((0, 4), (4, 12), (12, 16), (16, 24))


def unit_tables():
    big, small = [], []
    for u in range(18 * LAYERS):
        layer, place = divmod(u, 18)
        big.append(layer * BIG + place if place < BIG else -1)
        small.append(-1 if place < BIG else small_at(layer, place - BIG))
    return np.array(big + [-1] * 3), np.array(small + [TIME_AT, SHIFT_F, SCALE_F])


BIG_OF, SMALL_OF = unit_tables()


def params(limit, **more):
    return pltpu.CompilerParams(vmem_limit_bytes=limit * 1024 * 1024, **more)


SMEM_SPEC = pl.BlockSpec(memory_space=pltpu.SMEM)
VMEM_SPEC = pl.BlockSpec(memory_space=pltpu.VMEM)


def in_hbm(values):
    return pltpu.with_memory_space_constraint(values, pltpu.HBM)


def dot(a, b):
    return lax.dot_general(a, b, (((1,), (0,)), ((), ())), preferred_element_type=F32)


def dot_nt(a, b):
    return lax.dot_general(a, b, (((1,), (1,)), ((), ())), preferred_element_type=F32)


def dot_tn(a, b):
    return lax.dot_general(a, b, (((0,), (0,)), ((), ())), preferred_element_type=F32)


def shape(dims, kind):
    return jax.ShapeDtypeStruct(dims, kind)


ISSUED = []


def order(values, after):
    if not after:
        return values
    flat, tree = jax.tree.flatten(values)
    tied = lax.optimization_barrier(tuple(flat) + tuple(after))
    return jax.tree.unflatten(tree, tied[: len(flat)])


def drive(work, line):
    ISSUED.clear()
    try:
        value = next(work)
        while True:
            after = tuple(ISSUED)
            ISSUED.clear()
            value = work.send(order(value, line(after)))
    except StopIteration as end:
        return end.value


def together(*works):
    ends, flying = [None] * len(works), {}

    def go(i, step):
        try:
            flying[i] = step()
        except StopIteration as end:
            flying.pop(i, None)
            ends[i] = end.value

    for i, work in enumerate(works):
        go(i, lambda: next(work))
    while flying:
        got = yield dict(flying)
        for i in list(got):
            go(i, lambda: works[i].send(got[i]))
    return ends


def finish(work, value):
    try:
        work.send(value)
    except StopIteration as end:
        return end.value
    raise AssertionError


def flip(values, axis, bit, size):
    ISSUED.append(values)
    got = lax.ppermute(values, axis, [(i, i ^ bit) for i in range(size)])
    if axis == "tensor" and values.size < 2**16:
        ISSUED.append(got)
    return got


def is_at(flag, value, ndim):
    return flag.reshape((1,) * ndim) == value


def pick(low, high, place, other=False):
    return jnp.where(is_at(place, 1 if other else 0, low.ndim), low, high)


def own_latents(values, axis, data, n_data):
    n_lat = values.shape[axis]
    dims = values.shape[:axis] + (n_lat * n_data,) + values.shape[axis + 1 :]
    at = lax.broadcasted_iota(jnp.int32, dims, axis)
    first = data.reshape((1,) * len(dims)) * n_lat
    placed = jnp.zeros(dims, values.dtype)
    for l in range(n_lat):
        placed = jnp.where(at == first + l, lax.slice_in_dim(values, l, l + 1, axis=axis), placed)
    return placed


def dp_sum(values, n_data):
    bit = 1
    while bit < n_data:
        values = values + (yield flip(values, "dp", bit, n_data))
        bit *= 2
    return values


def dp_rows(values, n_data):
    bit = 1
    while bit < n_data:
        values = jnp.concatenate([values, (yield flip(values, "dp", bit, n_data))], 0)
        bit *= 2
    return values


def core_flip(values):
    return flip(values, "tensor", 1, 4)


def x_flip(values):
    return flip(values, "tensor", 2, 4)


def gather_tokens(own, waits=1):
    flying = core_flip(own), x_flip(own)
    for _ in range(waits):
        flying = yield flying
    beside, across = flying
    return own, beside, across, core_flip(across)


def gather_columns(own, chip, core):
    beside, across = yield (core_flip(own), x_flip(own))
    corner = core_flip(across)
    at_core = [is_at(core, i, own.ndim) for i in range(2)]
    at_chip = [is_at(chip, i, own.ndim) for i in range(2)]
    near = [jnp.where(at_core[i], own, beside) for i in range(2)]
    far = [jnp.where(at_core[i], across, corner) for i in range(2)]
    parts = [jnp.where(at_chip[i], near[j], far[j]) for i in range(2) for j in range(2)]
    return jnp.concatenate(parts, -1)


def scatter_tokens(keep, send):
    got = core_flip(send)
    far = (keep[1] + got[1].astype(F32)).astype(BF16)
    return keep, got, (yield x_flip(far))


def core_columns(values, core, other=False):
    size = values.shape[-1] // 4
    block = [lax.slice_in_dim(values, j * size, (j + 1) * size, axis=values.ndim - 1) for j in range(4)]
    return [pick(block[2 * x], block[2 * x + 1], core, other) for x in range(2)]


def core_columns_sum(values, core):
    got = core_flip(jnp.concatenate(core_columns(values, core, True), -1))
    size = got.shape[-1] // 2
    return [
        mine + lax.slice_in_dim(got, x * size, (x + 1) * size, axis=got.ndim - 1)
        for x, mine in enumerate(core_columns(values, core))
    ]


def own_columns_sum(values, chip, core):
    mine = core_columns_sum(values, core)
    return pick(*mine, chip) + (yield x_flip(pick(*mine, chip, True)))


def sum_of_columns(values, chip, core, n_data):
    return (yield from dp_sum((yield from own_columns_sum(values, chip, core)), n_data))


def ring_order(n_data):
    return [0, 2, 4, 6, 7, 5, 3, 1] if n_data == 8 else list(range(n_data))


def plan_kernel(n_units, n_slots, steps, depth, n_data, me_ref, owner_ref, table_ref, tab_ref, slot_ref):
    me = me_ref[0]
    place_of = [int(v) for v in np.argsort(ring_order(n_data))]
    my_place = sum(jnp.where(me == d, place_of[d], 0) for d in range(n_data))
    owner = owner_ref[...]
    across = jnp.broadcast_to(owner, (128, 128))
    before = lax.broadcasted_iota(jnp.int32, (128, 128), 0) < lax.broadcasted_iota(jnp.int32, (128, 128), 1)
    slot = jnp.sum(jnp.where((across == across.T) & before, 1.0, 0.0), 0, keepdims=True)
    mine = owner == me.astype(F32)
    lane8 = lax.broadcasted_iota(jnp.int32, (8, 128), 1)
    row8 = lax.broadcasted_iota(jnp.int32, (8, 128), 0)
    result = jnp.full((8, 128), -1, jnp.int32)
    for s in range(n_slots):
        held = mine & (slot == s)
        value = jnp.sum(jnp.where(held, table_ref[...], 0), 1, keepdims=True) - 1
        result = jnp.where((lane8 == s) & (row8 < 4), value, result)
    lane1 = lax.broadcasted_iota(jnp.int32, (1, 128), 1)
    time = lane1 == 18 * LAYERS
    time_slot = jnp.sum(jnp.where(time, slot, 0.0), 1, keepdims=True).astype(jnp.int32)
    time_mine = jnp.sum(jnp.where(time & mine, 1.0, 0.0), 1, keepdims=True).astype(jnp.int32)
    result = jnp.where((row8 == 4) & (lane8 == 0), time_slot, result)
    result = jnp.where((row8 == 4) & (lane8 == 1), time_mine, result)
    peers = jnp.full((1, 128), -1, jnp.int32)
    place = jnp.full((1, 128), -9, jnp.int32)
    for d in range(n_data):
        ahead = place_of[d] - my_place
        peers = jnp.where(lane1 == jnp.where(ahead < 0, ahead + n_data, ahead), d, peers)
        place = jnp.where(owner == float(d), place_of[d], place)
    slot_ref[...] = jnp.where(row8 == 5, peers, result)

    big = jnp.where(lane1 < BIG, place, pltpu.roll(place, 128 - 6, 1))
    big = jnp.where(lane1 < N_BIG, big, -9)
    back = jnp.where(big >= 0, n_data - 1 - big, -9)
    lane = lax.broadcasted_iota(jnp.int32, (n_data, 128), 1)
    row = lax.broadcasted_iota(jnp.int32, (n_data, 128), 0)
    follow = jnp.where(row == n_data - 1, 0, row + 1)
    own = [(row == at).astype(jnp.int32) for at in (big, back)]
    open_to = [(follow != at).astype(jnp.int32) for at in (big, back)]
    spots = [my_place, n_data - 1 - my_place]
    far = jnp.int32(999)

    def step(t, carry):
        line = jnp.full((1, 128), -1, jnp.int32)
        after = []
        for way in range(2):
            have, sent, *coming = carry[way]
            here = spots[way]
            prior = jnp.where(here == 0, n_data - 1, here - 1)
            open_now = have * (1 - sent) * open_to[way]
            first = jnp.min(jnp.where(open_now > 0, lane, far), axis=1, keepdims=True)
            chosen = (lane == first).astype(jnp.int32)
            first = jnp.broadcast_to(first, (n_data, 128))
            for k, who in enumerate((here, prior)):
                index = jnp.min(jnp.where(row == who, first, far), axis=0, keepdims=True)
                index = jnp.where(index == far, -1, index)
                line = jnp.where(lane1 == 2 * way + k, index, line)
            coming = list(coming) + [pltpu.roll(chosen, 1, 0)]
            after.append((have + coming[0], sent + chosen, *coming[1:]))
        tab_ref[pl.ds(t, 1), :] = line
        return tuple(after)

    none = jnp.zeros((n_data, 128), jnp.int32)
    lax.fori_loop(0, steps, step, tuple((own[way], none) + (none,) * (depth - 1) for way in range(2)))


def plan(owners, tables, n_slots, n_data, steps, depth, my_data):
    n_units = owners.shape[0]
    padded = jnp.pad(owners.astype(F32), (0, 128 - n_units), constant_values=-1.0)[None]
    wide = np.zeros((8, 128), np.int32)
    wide[: len(tables), :n_units] = tables + 1
    tab, rows = pl.pallas_call(
        functools.partial(plan_kernel, n_units, n_slots, steps, depth, n_data),
        out_shape=[shape((steps, 128), jnp.int32), shape((8, 128), jnp.int32)],
        in_specs=[SMEM_SPEC, VMEM_SPEC, VMEM_SPEC],
        out_specs=[VMEM_SPEC, VMEM_SPEC],
        compiler_params=params(SCOPE),
        name="plan",
    )(my_data.reshape(1), padded, jnp.asarray(wide))
    return tab[:, :4], rows


def spread_init_kernel(slots_ref, bank_ref, out_ref, wide, sem):
    big_ref = [slots_ref[0, s] for s in range(bank_ref.shape[0])]
    n_slots = bank_ref.shape[0]
    for s in range(n_slots):
        copy = pltpu.make_async_copy(bank_ref.at[s], wide.at[s], sem.at[s])
        pl.when(big_ref[s] >= 0)(copy.start)
    for s in range(n_slots):
        copy = pltpu.make_async_copy(bank_ref.at[s], wide.at[s], sem.at[s])
        pl.when(big_ref[s] >= 0)(copy.wait)

        @pl.when(big_ref[s] >= 0)
        def _(s=s):
            out_ref[jnp.maximum(big_ref[s], 0)] = wide[s].astype(BF16)


def spread_init(big_slots, master_bank):
    n_slots, rows, columns = master_bank.shape
    return pl.pallas_call(
        spread_init_kernel,
        out_shape=pltpu.VMEM((N_BIG + BIG, rows, columns), BF16),
        in_specs=[SMEM_SPEC, pl.BlockSpec(memory_space=pltpu.HBM)],
        out_specs=VMEM_SPEC,
        scratch_shapes=[
            pltpu.VMEM((n_slots, rows, columns), F32),
            pltpu.SemaphoreType.DMA((n_slots,)),
        ],
        compiler_params=params(SCOPE),
        name="own_weights",
    )(big_slots, in_hbm(master_bank))


def spread_kernel(places, fetch_at, tab_ref, got, held, out):
    half = held.shape[1] // 2
    for way in range(2):
        rows = pl.ds(way * half, half)
        for k, t in enumerate(places):
            unit = tab_ref[t, 2 * way + 1]

            @pl.when(unit >= 0)
            def _():
                held[jnp.maximum(unit, 0), rows] = got[2 * k + way][...]

        if fetch_at is not None:
            out[way][...] = held[jnp.maximum(tab_ref[fetch_at, 2 * way], 0), rows]


def ring_step(name, tab, held, got, sends, body, work=None, mail=(), mail_rows=0, keep_rows=0):
    rows, columns = held.shape[1:]
    extra, more, operands, shapes, scratch = (tuple(work) + ([],))[:5] if work else ("", None, [], [], [])
    specs = [value[1] if isinstance(value, tuple) else VMEM_SPEC for value in operands]
    operands = [value[0] if isinstance(value, tuple) else value for value in operands]
    operands, specs = list(mail) + list(operands), [VMEM_SPEC] * len(mail) + specs
    n, m, k = len(got), len(operands), len(mail)
    kept = 2 if keep_rows else 0
    shapes = [pltpu.VMEM((keep_rows, columns), BF16)] * kept + list(shapes)

    def kernel(tab_ref, *refs):
        out = refs[n + 1 + m :]
        if body is not None:
            body(tab_ref, refs[:n], out[0], out[1 : 1 + sends], *([refs[n + 1 : n + 1 + k]] if k else []))
        for way in range(kept):
            out[1 + sends + way][...] = refs[way][refs[way].shape[0] - keep_rows :]
        if more is not None:
            more(out[0], *refs[n + 1 + k : n + 1 + m], *out[1 + sends + kept :])

    res = pl.pallas_call(
        kernel,
        out_shape=[pltpu.VMEM(held.shape, held.dtype)] + [pltpu.VMEM((rows // 2 + mail_rows, columns), BF16)] * sends
        + list(shapes),
        in_specs=[SMEM_SPEC] + [VMEM_SPEC] * (n + 1) + specs,
        out_specs=[VMEM_SPEC] * (1 + sends + len(shapes)),
        scratch_shapes=scratch,
        input_output_aliases={1 + n: 0},
        compiler_params=params(SCOPE),
        name=name + extra,
    )(tab, *got, held, *operands)
    return res[0], list(res[1 : 1 + sends]), list(res[1 + sends :])


def ring_perms(n_data):
    order = ring_order(n_data)
    ahead = [(order[i], order[(i + 1) % n_data]) for i in range(n_data)]
    return ahead, [(b, a) for a, b in ahead]


class Spreader:
    def __init__(self, tab, held, n_data, steps, depth):
        self.tab, self.n_data, self.steps, self.depth = tab, n_data, steps, depth
        self.perms = ring_perms(n_data)
        self.held = held
        self.got = {}
        self.at = 0

    def last(self, g):
        return GROUPS[g][1] - 1 + (self.n_data - 2) * self.depth

    def step(self, after=()):
        self.work(None, after)
        return self.sent

    def work(self, work, after=()):
        t = self.at
        self.sent = ()
        if t > self.steps:
            return []
        fetch_at = t if t < self.steps else None
        places = [t - self.depth] if fetch_at is not None else list(range(self.steps - self.depth, self.steps))
        places = [p for p in places if p >= 0]
        self.held, sends, results = ring_step(
            "spread_step",
            order(self.tab, after),
            self.held,
            [value for p in places for value in self.got.pop(p)],
            0 if fetch_at is None else 2,
            functools.partial(spread_kernel, places, fetch_at),
            work,
        )
        if fetch_at is not None:
            self.got[t] = [lax.ppermute(sends[way], "dp", self.perms[way]) for way in range(2)]
        self.at += 1
        self.sent = tuple(sends) + tuple(self.got.get(t - 1, ()))
        return order(results, tuple(self.got.get(t - 1, ())))

    def prepare(self, g):
        while self.at < min(self.last(g) + self.depth, self.steps):
            self.step()


def reduce_kernel(place_at, fetch_at, mail, tab_ref, got, held, out, own=()):
    half = held.shape[1] // 2
    if mail:
        for way in range(2):
            out[way][half:] = own[0][...] if mail == "own" else got[way][half:]
    for way in range(2):
        rows = pl.ds(way * half, half)
        if place_at is not None:
            unit = tab_ref[place_at, 2 * way]

            @pl.when(unit >= 0)
            def _():
                at = BIG + jnp.maximum(unit, 0)
                held[at, rows] = (held[at, rows].astype(F32) + got[way][:half].astype(F32)).astype(BF16)

        out[way][:half] = held[BIG + jnp.maximum(tab_ref[fetch_at, 2 * way + 1], 0), rows]


class Reducer:
    def __init__(self, tab, n_data, steps, depth):
        self.tab, self.n_data, self.steps, self.depth = tab, n_data, steps, depth
        self.perms = [p for p in reversed(ring_perms(n_data))]
        self.held = None
        self.ready = N_BIG
        self.mail = {}
        self.come = {}
        self.got = {}
        self.at = 0

    def lowest(self, k):
        return (self.steps - 1 - k) - (self.n_data - 2) * self.depth

    def step(self, after=()):
        k = self.at
        self.sent = ()
        if k < self.steps and max(self.lowest(k), 0) >= self.ready:
            self.work(None, after)
        return self.sent

    def work(self, work, after=()):
        k = self.at
        self.sent = ()
        tab = order(self.tab, after)
        if k >= self.steps or max(self.lowest(k), 0) < self.ready:
            self.held, unused, results = ring_step("layer_", tab, self.held, [], 0, None, work)
            return results
        place_at = self.steps - 1 - (k - self.depth) if k >= self.depth else None
        payload, hops = self.mail.get(k, (None, 0))
        mail = None if payload is None else "own" if hops == 0 else "pass"
        keep_rows = self.mail[k - self.depth][0].shape[0] if k - self.depth in self.mail else 0
        self.held, sends, results = ring_step(
            "reduce_step",
            tab,
            self.held,
            self.got.get(k - self.depth, []),
            2,
            functools.partial(reduce_kernel, place_at, self.steps - 1 - k, mail),
            work,
            [payload] if mail == "own" else [],
            0 if payload is None else payload.shape[0],
            keep_rows,
        )
        if keep_rows:
            self.come[k - self.depth], results = results[:2], results[2:]
        self.got[k] = [lax.ppermute(sends[way], "dp", self.perms[way]) for way in range(2)]
        self.at += 1
        self.sent = tuple(sends) + tuple(self.got.get(k - 1, ()))
        return order(results, tuple(self.got.get(k - 1, ())))

    def gather(self, *payloads):
        far = self.n_data // 2
        starts = [self.at + i for i in range(len(payloads))]
        for start, payload in zip(starts, payloads):
            for j in range(far):
                self.mail[start + j * self.depth] = (payload, j)
        ISSUED.extend(payloads[1:])
        last = starts[-1] + far * self.depth
        assert len(payloads) <= self.depth and last < self.steps
        while self.at <= last:
            yield ()
        everyone = []
        for start, payload in zip(starts, payloads):
            come = [[self.come[start + j * self.depth][way] for j in range(far)] for way in range(2)]
            everyone.append(order([payload] + come[0][: far - 1] + come[1][::-1], self.sent))
        return everyone

    def drain(self):
        while self.at < self.steps:
            self.step()

    def last(self):
        return [self.got[self.steps - 1 - t][way] for t in range(self.depth) for way in range(2)]


def past(kernel, operands, beside):
    n, m = len(operands), len(beside)
    return lambda *refs: kernel(*refs[:n], *refs[n + m :])


def split_rows(total, keep_ref, send_ref):
    rows = total.shape[0] // 4
    for i in range(2):
        keep_ref[i] = total[2 * i * rows : (2 * i + 1) * rows]
        send_ref[i] = total[(2 * i + 1) * rows : (2 * i + 2) * rows].astype(BF16)


def part_shapes(rows, width):
    return [shape((2, rows // 4, width), F32), shape((2, rows // 4, width), BF16)]


def joined(refs):
    return jnp.concatenate([r[...] for r in refs], 0)


def softmax_parts(q, k):
    scores = dot_nt(q, k) * SCORE_SCALE
    expo = jnp.exp(scores - jnp.max(scores, -1, keepdims=True))
    return expo / jnp.sum(expo, -1, keepdims=True)


def attention_kernel(n_lat, base, w_ref, x0, x1, x2, x3, qkv_ref, mixed_ref, keep_ref, send_ref):
    x = joined((x0, x1, x2, x3))
    for j in range(3):
        qkv_ref[j] = dot(x, w_ref[base + j]).astype(BF16)
    toks = x.shape[0] // n_lat
    heads = w_ref.shape[2] // HEAD_DIM
    for l in range(n_lat):
        rows = slice(l * toks, (l + 1) * toks)
        outs = []
        for h in range(heads):
            cols = slice(h * HEAD_DIM, (h + 1) * HEAD_DIM)
            q, k, v = (qkv_ref[j, rows, cols] for j in range(3))
            outs.append(dot(softmax_parts(q, k).astype(BF16), v))
        mixed_ref[rows, :] = jnp.concatenate(outs, 1).astype(BF16)
    split_rows(dot_nt(mixed_ref[...], w_ref[base + 3]), keep_ref, send_ref)


def attention(x, columns, base, n_lat):
    rows, width = 4 * x[0].shape[0], x[0].shape[1]
    shapes = [shape((3, rows, columns), BF16), shape((rows, columns), BF16)] + part_shapes(rows, width)
    return "_attention", functools.partial(attention_kernel, n_lat, base), x, shapes


def gelu(x):
    return 0.5 * x * (1.0 + jnp.tanh(GELU_C * (x + 0.044715 * x * x * x)))


def gelu_grad(x):
    t = jnp.tanh(GELU_C * (x + 0.044715 * x * x * x))
    return 0.5 * (1.0 + t) + 0.5 * x * (1.0 - t * t) * (GELU_C * (1.0 + 3 * 0.044715 * x * x))


def mlp_kernel(base, w_ref, x0, x1, x2, x3, hidden_ref, active_ref, keep_ref, send_ref):
    x = joined((x0, x1, x2, x3))
    total = None
    for j in range(4):
        hidden = dot(x, w_ref[base + j])
        hidden_ref[j] = hidden
        active = gelu(hidden).astype(BF16)
        active_ref[j] = active
        part = dot_nt(active, w_ref[base + 4 + j])
        total = part if total is None else total + part
    split_rows(total, keep_ref, send_ref)


def mlp(x, columns, base):
    rows, width = 4 * x[0].shape[0], x[0].shape[1]
    shapes = [shape((4, rows, columns), F32), shape((4, rows, columns), BF16)] + part_shapes(rows, width)
    return "_mlp", functools.partial(mlp_kernel, base), x, shapes


def mlp_back_kernel(base, w_ref, d0, d1, d2, d3, hidden_ref, dh_ref, keep_ref, send_ref):
    d = joined((d0, d1, d2, d3))
    total = None
    for j in range(4):
        dh = (gelu_grad(hidden_ref[j]) * dot(d, w_ref[base + 4 + j])).astype(BF16)
        dh_ref[j] = dh
        part = dot_nt(dh, w_ref[base + j])
        total = part if total is None else total + part
    split_rows(total, keep_ref, send_ref)


def mlp_back(d, hidden, base):
    rows, width = 4 * d[0].shape[0], d[0].shape[1]
    shapes = [shape(hidden.shape, BF16)] + part_shapes(rows, width)
    return "_mlp_back", functools.partial(mlp_back_kernel, base), [*d, hidden], shapes


def attention_back_kernel(n_lat, base, w_ref, d0, d1, d2, d3, qkv_ref, dqkv_ref, keep_ref, send_ref):
    d_mixed = dot(joined((d0, d1, d2, d3)), w_ref[base + 3]).astype(BF16)
    toks = d_mixed.shape[0] // n_lat
    heads = w_ref.shape[2] // HEAD_DIM
    for l in range(n_lat):
        rows = slice(l * toks, (l + 1) * toks)
        outs = [[], [], []]
        for h in range(heads):
            cols = slice(h * HEAD_DIM, (h + 1) * HEAD_DIM)
            q, k, v = (qkv_ref[j, rows, cols] for j in range(3))
            do = d_mixed[rows, cols]
            probs = softmax_parts(q, k)
            d_probs = dot_nt(do, v)
            d_scores = probs * (d_probs - jnp.sum(probs * d_probs, -1, keepdims=True))
            d_scores = d_scores.astype(BF16)
            outs[0].append(dot(d_scores, k) * SCORE_SCALE)
            outs[1].append(dot_tn(d_scores, q) * SCORE_SCALE)
            outs[2].append(dot_tn(probs.astype(BF16), do))
        for j in range(3):
            dqkv_ref[j, rows, :] = jnp.concatenate(outs[j], 1).astype(BF16)
    total = sum(dot_nt(dqkv_ref[j], w_ref[base + j]) for j in range(3))
    split_rows(total, keep_ref, send_ref)


def attention_back(d, qkv, base, n_lat):
    rows, width = 4 * d[0].shape[0], d[0].shape[1]
    shapes = [shape(qkv.shape, BF16)] + part_shapes(rows, width)
    return "_attention_back", functools.partial(attention_back_kernel, n_lat, base), [*d, qkv], shapes


def weight_grad_kernel(counts, n_lat, base, out_ref, *refs):
    n = len(counts)
    lefts, rights, (mean_ref, sum_ref) = refs[: 4 * n], refs[4 * n : 5 * n], refs[-2:]
    at = 0
    for k, count in enumerate(counts):
        a = joined(lefts[4 * k : 4 * k + 4])
        toks = a.shape[0] // n_lat

        def rows_of(x, scale):
            parts = [
                jnp.sum(x[l * toks : (l + 1) * toks].astype(F32), 0, keepdims=True) * scale for l in range(n_lat)
            ]
            return jnp.concatenate(parts + [jnp.zeros((8 - n_lat, x.shape[1]), F32)], 0).astype(BF16)

        mean = rows_of(a, 1.0 / toks)
        mean_ref[k] = mean.astype(F32)
        for j in range(count):
            b = rights[k][j]
            total = rows_of(b, 1.0)
            sum_ref[at] = total.astype(F32)
            out_ref[BIG + base + at] = (dot_tn(a, b) - dot_tn(mean, total)).astype(BF16)
            at += 1


def weight_grads(base, pairs, n_lat):
    counts = [right.shape[0] for _, right in pairs]
    width, columns = pairs[0][0][0].shape[1], pairs[0][1].shape[2]
    operands = [part for left, _ in pairs for part in left] + [right for _, right in pairs]
    shapes = [shape((len(pairs), 8, width), F32), shape((sum(counts), 8, columns), F32)]
    return "_weight_grads", functools.partial(weight_grad_kernel, counts, n_lat, base), operands, shapes


def small_weights(small_ref, bank_ref, wide, sem, use):
    units = [small_ref[s] for s in range(bank_ref.shape[0])]
    ours = [(unit >= 0) & (unit != TIME_AT) for unit in units]
    copies = [pltpu.make_async_copy(bank_ref.at[s], wide.at[s], sem.at[s]) for s in range(len(units))]
    for s, copy in enumerate(copies):
        pl.when(ours[s])(copy.start)
    for s, copy in enumerate(copies):

        @pl.when(ours[s])
        def _(s=s, copy=copy):
            copy.wait()
            use(jnp.maximum(units[s], 0), wide[s].astype(BF16))


def modulation_kernel(held_ref, small_ref, cond_ref, bank_ref, out_ref, wide, sem):
    out_ref[...] = jnp.zeros_like(out_ref)

    def use(unit, weight):
        out_ref[unit] = dot(cond_ref[...], weight)

    small_weights(small_ref, bank_ref, wide, sem, use)


def bank_scratch(bank):
    return [pltpu.VMEM(bank.shape, F32), pltpu.SemaphoreType.DMA((bank.shape[0],))]


def modulations(small_slots, cond_in, bank):
    operands = [(small_slots, SMEM_SPEC), cond_in, (in_hbm(bank), pl.BlockSpec(memory_space=pltpu.HBM))]
    shapes = [shape((SMALL_ROWS, cond_in.shape[0], bank.shape[2]), F32)]
    return "_modulations", modulation_kernel, operands, shapes, bank_scratch(bank)


def cond_back_kernel(n_mail, held_ref, small_ref, peer_ref, *refs):
    mail, (bank_ref, d_ref, out_ref, wide, sem) = refs[:n_mail], refs[n_mail:]
    if n_mail == 1:
        d_ref[...] = mail[0][...]
    else:
        n_lat = d_ref.shape[0] // n_mail
        for i in range(n_mail):
            for l in range(n_lat):
                d_ref[peer_ref[i] * n_lat + l] = mail[i][l * SMALL_ROWS : (l + 1) * SMALL_ROWS]
    out_ref[...] = jnp.zeros_like(out_ref)

    def use(unit, weight):
        d = d_ref[...].astype(F32)
        d = jnp.sum(jnp.where(lax.broadcasted_iota(jnp.int32, d.shape, 1) == unit, d, 0.0), 1)
        out_ref[...] += dot_nt(d.astype(BF16), weight)

    small_weights(small_ref, bank_ref, wide, sem, use)


def cond_back(small_slots, peers, mail, n_all, bank):
    columns = bank.shape[2]
    operands = [(small_slots, SMEM_SPEC), (peers, SMEM_SPEC)] + list(mail)
    operands += [(in_hbm(bank), pl.BlockSpec(memory_space=pltpu.HBM))]
    shapes = [shape((n_all, SMALL_ROWS, columns), BF16), shape((n_all, bank.shape[1]), F32)]
    return "_cond_back", functools.partial(cond_back_kernel, len(mail)), operands, shapes, bank_scratch(bank)


def mail_sum_kernel(n_mail, held_ref, peer_ref, *refs):
    mail, (out_ref, whole) = refs[:n_mail], refs[n_mail:]
    rows = out_ref.shape[0]
    for i in range(n_mail):
        whole[peer_ref[i]] = mail[i][:rows].astype(F32) + mail[i][rows:].astype(F32)
    total = whole[0]
    for i in range(1, n_mail):
        total = total + whole[i]
    out_ref[...] = total


def mail_sum(peers, mail):
    rows, columns = mail[0].shape[0] // 2, mail[0].shape[1]
    scratch = [pltpu.VMEM((len(mail), rows, columns), F32)]
    operands = [(peers, SMEM_SPEC)] + list(mail)
    return "_mail_sum", functools.partial(mail_sum_kernel, len(mail)), operands, [shape((rows, columns), F32)], scratch


def halves(x):
    high = x.astype(BF16)
    return high, (x - high.astype(F32)).astype(BF16)


def newton_sweep_coarse(x):
    xh = x.astype(BF16)
    gram = dot_tn(xh, xh)
    gh = gram.astype(BF16)
    poly = NS_COEF[1] * gram + NS_COEF[2] * dot(gh, gh)
    return NS_COEF[0] * x + dot(xh, poly.astype(BF16))


def newton_sweep(x):
    xh, xl = halves(x)
    cross = dot_tn(xh, xl)
    gram = dot_tn(xh, xh) + (cross + cross.T)
    gh, gl = halves(gram)
    cross = dot(gh, gl)
    square = dot(gh, gh) + (cross + cross.T)
    ph, pl_ = halves(NS_COEF[1] * gram + NS_COEF[2] * square)
    return NS_COEF[0] * x + (dot(xh, ph) + (dot(xl, ph) + dot(xh, pl_)))


def newton_kernel(n_last, base, big_ref, left_ref, right_ref, tab_ref, a_ref, b_ref, bank_ref, mom_ref, *refs):
    held, got = refs[0], refs[1 : 1 + n_last]
    new_ref, mom_new_ref, mark_ref, grad, sem = refs[-5:]
    s = base + pl.program_id(0)
    mark_ref[...] = jnp.zeros_like(mark_ref)
    unit, left, right = big_ref[s], left_ref[s], right_ref[s]
    half = got[0].shape[0]

    @pl.when(right < 0)
    def _():
        new_ref[...] = bank_ref[...]
        mom_new_ref[...] = mom_ref[...]

    @pl.when(right >= 0)
    def _():
        copy = pltpu.make_async_copy(held.at[BIG + jnp.maximum(unit, 0)], grad, sem.at[0])
        pl.when(unit >= 0)(copy.start)
        mom_new_ref[0] = 0.5 * mom_ref[0] + dot_tn(
            a_ref[jnp.maximum(left, 0)], b_ref[jnp.maximum(right, 0)]
        )
        pl.when(unit >= 0)(copy.wait)

        @pl.when(unit >= 0)
        def _():
            mom_new_ref[0] += grad[...].astype(F32)

        for i in range(n_last):
            rows = slice((i % 2) * half, (i % 2 + 1) * half)

            @pl.when((tab_ref[i // 2, 2 * (i % 2)] == unit) & (unit >= 0))
            def _(i=i, rows=rows):
                mom_new_ref[0, rows] += got[i][...].astype(F32)

        block = mom_new_ref[0]
        norm = jnp.sqrt(jnp.sum(block * block)) + 1e-07
        x = block / norm
        for sweep in range(5):
            x = newton_sweep_coarse(x) if sweep < 4 else newton_sweep(x)
        new_ref[0] = bank_ref[0] - LR_MUON * x


class Optimizer:
    def __init__(self, slots, tab, a_all, b_all, master, momentum, held, got):
        self.scalars = [*slots, tab]
        self.arrays = [a_all, b_all, in_hbm(master), in_hbm(momentum), held, *got]
        self.news = []
        self.at = 0

    def step(self, after=(), count=3):
        a_all, b_all, master, momentum, held, *got = self.arrays
        n_slots, rows, columns = master.shape
        base, count = self.at, min(count, n_slots - self.at)
        if count == 0:
            return ()
        self.at += count
        block = pl.BlockSpec((1, rows, columns), lambda s, *t: (base + s, 0, 0))
        any_spec = pl.BlockSpec(memory_space=pl.ANY)
        scalars = [order(self.scalars[0], after)] + self.scalars[1:]
        first = len(scalars) + len(self.arrays)
        *self.news, mark = pl.pallas_call(
            functools.partial(newton_kernel, len(got), base),
            grid_spec=pltpu.PrefetchScalarGridSpec(
                num_scalar_prefetch=len(scalars),
                grid=(count,),
                in_specs=[
                    pl.BlockSpec(a_all.shape, lambda s, *t: (0, 0, 0)),
                    pl.BlockSpec(b_all.shape, lambda s, *t: (0, 0, 0)),
                    block,
                    block,
                    any_spec,
                ]
                + [pl.BlockSpec(g.shape, lambda s, *t: (0, 0)) for g in got]
                + [any_spec] * len(self.news),
                out_specs=[block, block, pl.BlockSpec((8, 128), lambda s, *t: (0, 0))],
                scratch_shapes=[pltpu.VMEM((rows, columns), BF16), pltpu.SemaphoreType.DMA((1,))],
            ),
            out_shape=[shape(master.shape, F32), shape(momentum.shape, F32), shape((8, 128), F32)],
            input_output_aliases={first + i: i for i in range(len(self.news))},
            compiler_params=params(SCOPE, dimension_semantics=("arbitrary",)),
            name="optimizer",
        )(*scalars, *self.arrays, *self.news)
        return (mark,)

    def all(self):
        while self.at < self.arrays[2].shape[0]:
            self.step()
        return self.news


def layer_norm(values):
    centered = values - jnp.mean(values, -1, keepdims=True)
    inv_std = lax.rsqrt(jnp.mean(centered * centered, -1, keepdims=True) + 1e-06)
    return centered * inv_std, inv_std


def norm_back(grad_out, normed, inv_std):
    return inv_std * (
        grad_out
        - jnp.mean(grad_out, -1, keepdims=True)
        - normed * jnp.mean(grad_out * normed, -1, keepdims=True)
    )


def added(keep_ref, got_ref, far_ref):
    return keep_ref[0] + got_ref[0].astype(F32) + far_ref[...].astype(F32)


def row_of(mods_ref, at):
    return mods_ref[at : at + 1, :]


def enter_kernel(at, noisy_ref, patch_ref, place_ref, mods_ref, stream_ref, inner_ref, normed_ref, inv_ref):
    stream = dot(noisy_ref[...], patch_ref[...]) + place_ref[...]
    stream_ref[...] = stream
    normed, inv = layer_norm(stream)
    inner_ref[...] = (normed * (1.0 + row_of(mods_ref, at[1])) + row_of(mods_ref, at[0])).astype(BF16)
    normed_ref[...] = normed
    inv_ref[...] = jnp.broadcast_to(inv, inv_ref.shape)


def enter(noisy, patch, places, mods, at):
    rows, width = places.shape
    full = shape((rows, width), F32)
    return pl.pallas_call(
        functools.partial(enter_kernel, at),
        out_shape=[full, shape((rows, width), BF16), full, shape((rows, 128), F32)],
        compiler_params=params(SCOPE),
        name="enter",
    )(noisy, patch, places, mods)


def residual_kernel(
    at, keep_ref, got_ref, far_ref, stream_ref, mods_ref, part_ref, next_ref, inner_ref, normed_ref, inv_ref
):
    part = added(keep_ref, got_ref, far_ref)
    part_ref[...] = part
    stream = stream_ref[...] + row_of(mods_ref, at[0]) * part
    next_ref[...] = stream
    normed, inv = layer_norm(stream)
    inner_ref[...] = (normed * (1.0 + row_of(mods_ref, at[2])) + row_of(mods_ref, at[1])).astype(BF16)
    normed_ref[...] = normed
    inv_ref[...] = jnp.broadcast_to(inv, inv_ref.shape)


def residual(parts, stream, mods, at):
    rows, width = stream.shape
    full = shape((rows, width), F32)
    return pl.pallas_call(
        functools.partial(residual_kernel, at),
        out_shape=[full, full, shape((rows, width), BF16), full, shape((rows, 128), F32)],
        compiler_params=params(SCOPE),
        name="residual",
    )(*parts, stream, mods)


def leave_kernel(
    at,
    count_all,
    keep_ref,
    got_ref,
    far_ref,
    stream_ref,
    mods_ref,
    head_ref,
    target_ref,
    grad_ref,
    next_ref,
    rows_ref,
    edge_ref,
):
    branch = added(keep_ref, got_ref, far_ref)
    gate, shift, scale = (row_of(mods_ref, i) for i in at)
    normed, inv = layer_norm(stream_ref[...] + gate * branch)
    inner = (normed * (1.0 + scale) + shift).astype(BF16)
    head = head_ref[...]
    error = dot_nt(inner, head) - target_ref[...]
    d_output = (2.0 * error / count_all).astype(BF16)
    d_inner = dot(d_output, head)
    grad = norm_back(d_inner * (1.0 + scale), normed, inv)
    grad_ref[...] = grad
    next_ref[...] = (gate * grad).astype(BF16)
    rows_ref[...] = jnp.zeros_like(rows_ref)
    rows_ref[0:1, :] = jnp.sum(d_inner, 0, keepdims=True)
    rows_ref[1:2, :] = jnp.sum(d_inner * normed, 0, keepdims=True)
    rows_ref[2:3, :] = jnp.sum(grad * branch, 0, keepdims=True)
    n_patch = head.shape[0]
    loss = jnp.sum(jnp.sum(error * error, 1, keepdims=True), 0, keepdims=True) / count_all
    edge_ref[:n_patch, :] = dot_tn(d_output, inner)
    edge_ref[n_patch:, :] = jnp.broadcast_to(loss, (8, edge_ref.shape[1]))


def leave(parts, stream, mods, head, target, at, count_all):
    rows, width = stream.shape
    return pl.pallas_call(
        functools.partial(leave_kernel, at, count_all),
        out_shape=[
            shape((rows, width), F32),
            shape((rows, width), BF16),
            shape((SMALL_ROWS, width), F32),
            shape((head.shape[0] + 8, width), F32),
        ],
        compiler_params=params(SCOPE),
        name="leave",
    )(*parts, stream, mods, head, target)


def back_kernel(
    at,
    gate_at,
    first,
    keep_ref,
    got_ref,
    far_ref,
    normed_ref,
    inv_ref,
    grad_ref,
    part_ref,
    mods_ref,
    rows_in_ref,
    out_ref,
    next_ref,
    rows_ref,
):
    d_inner = added(keep_ref, got_ref, far_ref)
    normed = normed_ref[...]
    inv = inv_ref[:, 0:1]
    grad = grad_ref[...] + norm_back(d_inner * (1.0 + row_of(mods_ref, at)), normed, inv)
    out_ref[...] = grad
    rows_ref[...] = rows_in_ref[...]
    rows_ref[first : first + 1, :] = jnp.sum(d_inner, 0, keepdims=True)
    rows_ref[first + 1 : first + 2, :] = jnp.sum(d_inner * normed, 0, keepdims=True)
    if gate_at is None:
        next_ref[...] = grad.astype(BF16)
    else:
        next_ref[...] = (row_of(mods_ref, gate_at) * grad).astype(BF16)
        rows_ref[first + 2 : first + 3, :] = jnp.sum(grad * part_ref[...], 0, keepdims=True)


def back(parts, normed, inv, grad, part, mods, rows_in, at, gate_at, first, beside):
    rows, width = grad.shape
    operands = (*parts, normed, inv, grad, part, mods, rows_in)
    return pl.pallas_call(
        past(functools.partial(back_kernel, at, gate_at, first), operands, beside),
        out_shape=[shape((rows, width), F32), shape((rows, width), BF16), shape(rows_in.shape, F32)],
        compiler_params=params(SCOPE),
        name="back",
    )(*operands, *beside)


def tables_kernel(n_patch, fix_ref, edge_ref, time_ref, class_ref, table_ref, first_ref, second_ref, *outs):
    new_ref, first_new_ref, second_new_ref = outs
    at = 0
    for ref, low, count in (
        (edge_ref, 0, n_patch),
        (time_ref, 0, FREQ),
        (class_ref, 0, CLASSES),
        (edge_ref, n_patch, n_patch),
    ):
        rows = slice(at, at + count)
        grad = ref[low : low + count, :]
        first = 0.5 * first_ref[rows, :] + 0.5 * grad
        second = 0.5 * second_ref[rows, :] + 0.5 * grad * grad
        first_new_ref[rows, :] = first
        second_new_ref[rows, :] = second
        new_ref[rows, :] = table_ref[rows, :] * (1.0 - LR_ADAM * WEIGHT_DECAY) - LR_ADAM * (
            first / fix_ref[0]
        ) / (jnp.sqrt(second / fix_ref[0]) + 1e-08)
        at += count


def update_tables(n_patch, bias_fix, edges, grad_time, grad_class, table, first, second):
    return pl.pallas_call(
        functools.partial(tables_kernel, n_patch),
        out_shape=[shape(table.shape, F32)] * 3,
        in_specs=[SMEM_SPEC] + [VMEM_SPEC] * 6,
        compiler_params=params(SCOPE),
        name="update_tables",
    )(bias_fix, edges, grad_time, grad_class, table, first, second)


def position_rows(first, rows):
    quarter = D // 4
    omega = jnp.exp(-math.log(10000.0) * jnp.arange(quarter, dtype=F32) / quarter)
    places = first + jnp.arange(rows, dtype=jnp.int32)
    rows_at = (places // GRID).astype(F32)[:, None] * omega[None]
    cols_at = (places % GRID).astype(F32)[:, None] * omega[None]
    return jnp.concatenate([jnp.sin(rows_at), jnp.cos(rows_at), jnp.sin(cols_at), jnp.cos(cols_at)], 1)


def time_features(timesteps):
    half_freq = FREQ // 2
    rates = jnp.exp(-math.log(10000.0) * jnp.arange(half_freq, dtype=F32) / half_freq)
    angles = timesteps.astype(F32)[:, None] * rates[None]
    return jnp.concatenate([jnp.cos(angles), jnp.sin(angles)], 1)


def shards(
    noisy_latents,
    noise_target,
    timesteps,
    labels,
    owners,
    step_count,
    master_bank,
    momentum_bank,
    embed_tables,
    embed_first,
    embed_second,
):
    n_lat, n_tok, n_patch = noisy_latents.shape
    n_slots, width, columns = master_bank.shape
    n_data = lax.axis_size("dp")
    my_data = lax.axis_index("dp")
    my_tensor = lax.axis_index("tensor")
    n_all = n_lat * n_data
    own_rows = n_lat * n_tok // 4
    count_all = float(n_all * n_tok * n_patch)
    depth = 2 if n_data <= 8 else 1
    steps = N_BIG + (n_data - 2) * depth

    kind = [2 + 2 * g + (b >= low + (3, 4)[g % 2]) for g, (low, high) in enumerate(GROUPS) for b in range(low, high)]
    slot_tables = np.stack(
        [
            BIG_OF,
            SMALL_OF,
            np.where(BIG_OF >= 0, np.array(kind)[BIG_OF], np.where(SMALL_OF == TIME_AT, 1, 0)),
            np.where(BIG_OF >= 0, SMALL_ROWS + BIG_OF, SMALL_OF),
        ]
    )
    tab, planned = plan(owners, slot_tables, n_slots, n_data, steps, depth, my_data)

    def flag(value):
        return jnp.asarray(value, jnp.int32).reshape(1)

    first_row = my_tensor * own_rows
    early = dict(
        slots=planned[:4, :n_slots],
        peers=planned[5, :n_data],
        chip=flag(my_tensor // 2),
        core=flag(my_tensor % 2),
        data=flag(my_data),
        bits=[flag((my_data // (1 << i)) % 2) for i in range((n_data - 1).bit_length())],
        time_mine=planned[4, 1:2],
        time_w2=lax.dynamic_index_in_dim(master_bank, planned[4, 0], 0, keepdims=False).astype(BF16),
        noisy=lax.dynamic_slice_in_dim(noisy_latents.reshape(n_lat * n_tok, n_patch), first_row, own_rows, 0),
        target=lax.dynamic_slice_in_dim(noise_target.reshape(n_lat * n_tok, n_patch), first_row, own_rows, 0),
        places=position_rows(first_row % n_tok, own_rows),
        ids=jnp.stack([timesteps, labels], 1),
        bias_fix=1.0 - jnp.power(0.5, step_count.astype(F32)),
        tab=tab,
        edge_cols=jnp.concatenate(
            [embed_tables[:n_patch], embed_tables[n_patch + FREQ + CLASSES :]], 0
        ).astype(BF16),
        time_w1=embed_tables[n_patch : n_patch + FREQ].astype(BF16),
        class_w=embed_tables[n_patch + FREQ : n_patch + FREQ + CLASSES].astype(BF16),
    )
    flat, tree = jax.tree.flatten(early)
    early = jax.tree.unflatten(tree, lax.optimization_barrier(tuple(flat)))
    chip, core, data, time_w2, noisy_own = (early[k] for k in ("chip", "core", "data", "time_w2", "noisy"))
    tab, peers = early["tab"], early["peers"]
    big_slots, small_slots, left_slots, right_slots = (early["slots"][i] for i in range(4))
    spread = Spreader(tab, spread_init(early["slots"], master_bank), n_data, steps, depth)
    spread.step()
    ring = Reducer(tab, n_data, steps, depth)

    def conditioning():
        ids, edge_rows = yield from together(
            dp_sum(own_latents(early["ids"], 0, data, n_data), n_data),
            gather_columns(early["edge_cols"], chip, core),
        )
        features = time_features(ids[:, 0]).astype(BF16)
        time_one = jnp.dot(features, early["time_w1"], preferred_element_type=F32)
        time_act = yield from gather_columns(jax.nn.silu(time_one).astype(BF16), chip, core)
        second = jnp.dot(time_act, time_w2, preferred_element_type=F32)
        second = yield from dp_sum(jnp.where(is_at(early["time_mine"], 1, 2), second, 0.0), n_data)
        onehot = ids[:, 1:2] == jnp.arange(CLASSES, dtype=jnp.int32)[None]
        condition = second + jnp.dot(onehot.astype(BF16), early["class_w"], preferred_element_type=F32)
        cond_in = yield from gather_columns(jax.nn.silu(condition).astype(BF16), chip, core)
        (mods,) = spread.work(modulations(small_slots, cond_in, master_bank), ISSUED)
        ISSUED.clear()
        bit = n_data // 2
        while bit:
            half = mods.shape[1] // 2
            sides = mods[:, :half], mods[:, half:]
            side = early["bits"][bit.bit_length() - 1]
            mods = pick(*sides, side) + (yield flip(pick(*sides, side, True), "dp", bit, n_data))
            bit //= 2
        latents = mods[:, 0], mods[:, 1]
        across = yield x_flip(pick(*latents, chip, True))
        own = pick(*latents, chip)
        pair = [pick(own, across, chip), pick(across, own, chip)]
        beside = core_flip(jnp.concatenate(pair, 1))
        beside = [beside[:, x * columns : (x + 1) * columns] for x in range(2)]
        blocks = [pick(one, two, core) for x in range(2) for one, two in ((pair[x], beside[x]), (beside[x], pair[x]))]
        return edge_rows, features, time_one, time_act, onehot, condition, cond_in, jnp.concatenate(blocks, 1)

    def forward():
        cond = yield from conditioning()
        edge_rows, mods = cond[0], cond[-1]
        stream, inner, normed, inv = enter(
            noisy_own, edge_rows[:n_patch], early["places"], mods, (small_at(0, 0), small_at(0, 1))
        )
        kept = []
        for layer in range(LAYERS):
            inner = yield from gather_tokens(inner)
            spread.prepare(2 * layer)
            qkv, mixed, keep, send = spread.work(attention(inner, columns, BIG * layer, n_lat))
            parts = yield from scatter_tokens(keep, send)
            attended, stream, inner_mid, normed_mid, inv_mid = residual(
                parts, stream, mods, tuple(small_at(layer, i) for i in (2, 3, 4))
            )
            inner_mid = yield from gather_tokens(inner_mid)
            spread.prepare(2 * layer + 1)
            hidden, active, keep, send = spread.work(mlp(inner_mid, columns, BIG * layer + 4))
            parts = yield from scatter_tokens(keep, send)
            kept.append([inner, normed, inv, qkv, mixed, attended, inner_mid, normed_mid, inv_mid, hidden, active])
            if layer + 1 < LAYERS:
                branch, stream, inner, normed, inv = residual(
                    parts,
                    stream,
                    mods,
                    (small_at(layer, 5), small_at(layer + 1, 0), small_at(layer + 1, 1)),
                )
                kept[-1].append(branch)
        return cond, kept, parts, stream

    cond, kept, parts_last, stream_last = drive(forward(), spread.step)
    edge_rows, features, time_one, time_act, onehot, condition, cond_in, mods = cond
    ring.held = spread.held

    def backward():
        grad, d_branch, rows, edge_head = leave(
            parts_last,
            stream_last,
            mods,
            edge_rows[n_patch:],
            early["target"],
            (small_at(LAYERS - 1, 5), SHIFT_F, SCALE_F),
            count_all,
        )
        lefts, rights = {}, {}
        for layer in reversed(range(LAYERS)):
            inner, normed, inv, qkv, mixed, attended, inner_mid, normed_mid, inv_mid, hidden, active = kept[layer][:11]
            d_branch = yield from gather_tokens(d_branch, 1 if layer == LAYERS - 1 else 2)
            d_hidden, keep, send = ring.work(mlp_back(d_branch, hidden, BIG * layer + 4))
            work = scatter_tokens(keep, send)
            flying = next(work)
            lefts[2 * layer + 1], rights[2 * layer + 1] = ring.work(
                weight_grads(BIG * layer + 4, [(inner_mid, d_hidden), (d_branch, active)], n_lat), ISSUED
            )
            ring.ready = BIG * layer + 4
            if layer == LAYERS - 1:
                ring.step((lefts[2 * layer + 1],))
            parts = finish(work, order(flying, (lefts[2 * layer + 1],) + ring.sent))
            grad, d_attended, rows = back(
                parts,
                normed_mid,
                inv_mid,
                grad,
                attended,
                mods,
                rows,
                small_at(layer, 4),
                small_at(layer, 2),
                small_at(layer, 3),
                [ring.held],
            )
            d_attended = yield from gather_tokens(d_attended, 2)
            d_qkv, keep, send = ring.work(attention_back(d_attended, qkv, BIG * layer, n_lat))
            work = scatter_tokens(keep, send)
            flying = next(work)
            lefts[2 * layer], rights[2 * layer] = ring.work(
                weight_grads(BIG * layer, [(inner, d_qkv), (d_attended, mixed[None])], n_lat), ISSUED
            )
            ring.ready = BIG * layer
            parts = finish(work, order(flying, (lefts[2 * layer],) + ring.sent))
            below = kept[layer - 1][11] if layer else normed
            grad, d_branch, rows = back(
                parts,
                normed,
                inv,
                grad,
                below,
                mods,
                rows,
                small_at(layer, 1),
                small_at(layer - 1, 5) if layer else None,
                small_at(layer, 0),
                [ring.held],
            )
        return (yield from cond_backward(rows, d_branch, edge_head, lefts, rights))

    def cond_backward(rows, d_stream, edge_head, lefts, rights):
        mine = core_columns_sum(rows, core)
        near, far = pick(*mine, chip), x_flip(pick(*mine, chip, True))
        own = [pick(near, far, chip).astype(BF16), pick(far, near, chip).astype(BF16)]
        if n_data == 8:
            first, *others = factor_rows(lefts, rights)
            one, two = jnp.concatenate(own + [first], 0), jnp.concatenate(others, 0)
            one, two = (jnp.pad(v, ((0, -len(v) % 96), (0, 0))) for v in (one, two))
            latents, others = yield from ring.gather(one, two)
            n_own, n_rows = n_lat * SMALL_ROWS, first.shape[0]
            factors = [v[n_own : n_own + n_rows] for v in latents] + [v[:n_rows] for v in others]
            factors = jnp.concatenate(factors, 0).reshape(n_all, n_rows, columns)
        else:
            latents = [(yield from dp_sum(own_latents(jnp.stack(own, 0), 0, data, n_data), n_data))]
        d_small, d_cond = ring.work(cond_back(small_slots, peers, latents, n_all, master_bank), ISSUED)
        ISSUED.clear()
        d_cond = yield from own_columns_sum(d_cond, chip, core)
        if n_data == 8:
            (parts,) = yield from ring.gather(jnp.concatenate(halves(d_cond), 0))
            (d_cond,) = ring.work(mail_sum(peers, parts))
        else:
            d_cond = yield from dp_sum(d_cond, n_data)
        unused, silu_pull = jax.vjp(jax.nn.silu, condition)
        d_condition = silu_pull(d_cond)[0]
        d_second = d_condition.astype(BF16)
        grad_class = lax.dot_general(
            onehot.astype(F32), d_condition, (((0,), (0,)), ((), ())), precision=HIGHEST_PREC
        )
        d_time_act = lax.dot_general(d_second, time_w2, (((1,), (1,)), ((), ())), preferred_element_type=F32)
        d_time_act = jnp.where(is_at(early["time_mine"], 1, 2), d_time_act, 0.0)
        grad_patch = lax.dot_general(noisy_own, d_stream, (((0,), (0,)), ((), ())), preferred_element_type=F32)
        sums = yield from own_columns_sum(jnp.concatenate([d_time_act, grad_patch, edge_head], 0), chip, core)
        ring.drain()
        if n_data != 8:
            factors = yield from dp_rows(jnp.stack(factor_rows(lefts, rights)), n_data)
        n_left = sum(v.shape[0] for v in lefts.values())
        a_rows = jnp.concatenate([factors[:, j * n_left : (j + 1) * n_left] for j in range(4)], 2).transpose(1, 0, 2)
        b_rows = factors[:, 4 * n_left : 4 * n_left + N_BIG].transpose(1, 0, 2)
        return d_small, d_second, grad_class, sums, a_rows, b_rows

    def factor_rows(lefts, rights):
        a_rows = jnp.concatenate([lefts[g] for g in range(len(GROUPS))], 0)
        b_rows = jnp.concatenate([rights[g] for g in range(len(GROUPS))], 0)
        parts = []
        for l in range(n_lat):
            part = [a_rows[:, l, j * columns : (j + 1) * columns] for j in range(4)] + [b_rows[:, l]]
            part = jnp.concatenate(part, 0).astype(BF16)
            parts.append(jnp.pad(part, ((0, -len(part) % 32), (0, 0))))
        return parts

    d_small, d_second, grad_class, sums, a_rows, b_rows = drive(backward(), ring.step)
    a_all = jnp.concatenate([cond_in[None], time_act[None], a_rows], 0)
    small_rows = jnp.where(
        jnp.arange(SMALL_ROWS)[:, None, None] == TIME_AT, d_second[None], d_small.transpose(1, 0, 2)
    )
    b_all = jnp.concatenate([small_rows, b_rows], 0)
    optimizer = Optimizer(
        (big_slots, left_slots, right_slots), tab, a_all, b_all, master_bank, momentum_bank, ring.held, ring.last()
    )
    adding = dp_sum(order(sums, ring.last()), n_data)
    flying = next(adding)
    try:
        while True:
            (mark,) = optimizer.step(ISSUED[-2:-1]) or (jnp.zeros((8, 128), F32),)
            flying = adding.send(flying + mark[:1, :1])
    except StopIteration as end:
        sums = end.value
    master_new, momentum_new = optimizer.all()
    d_time_act, edges = sums[:n_all], sums[n_all:]
    unused, time_pull = jax.vjp(jax.nn.silu, time_one)
    d_time_one = time_pull(d_time_act)[0].astype(BF16)
    grad_time_one = lax.dot_general(
        features, d_time_one, (((0,), (0,)), ((), ())), preferred_element_type=F32
    )
    loss = edges[2 * n_patch, 0]
    embed_new, first_new, second_new = update_tables(
        n_patch, early["bias_fix"], edges, grad_time_one, grad_class, embed_tables, embed_first, embed_second
    )
    return (loss, master_new, momentum_new, embed_new, first_new, second_new)


def solution(mesh):
    placed = (
        P("dp", None, None),
        P("dp", None, None),
        P("dp"),
        P("dp"),
        P(),
        P(),
        P("dp", None, "tensor"),
        P("dp", None, "tensor"),
        P(None, "tensor"),
        P(None, "tensor"),
        P(None, "tensor"),
    )
    return jax.shard_map(
        shards,
        mesh=mesh,
        in_specs=placed,
        out_specs=(
            P(),
            P("dp", None, "tensor"),
            P("dp", None, "tensor"),
            P(None, "tensor"),
            P(None, "tensor"),
            P(None, "tensor"),
        ),
        check_vma=False,
    )
```

```python
import functools
import math

import jax
import jax.numpy as jnp
import numpy as np
from jax import lax
from jax.experimental import pallas as pl
from jax.experimental.pallas import tpu as pltpu
from jax.sharding import PartitionSpec as P

D = 1024
HEAD_DIM = 64
FREQ = 256
CLASSES = 1000
GRID = 16
LAYERS = 2
BIG = 12
N_BIG = BIG * LAYERS
SMALL_ROWS = 16
SHIFT_F, SCALE_F, TIME_AT = 0, 1, 6 * LAYERS + 2


def small_at(layer, i):
    first = 2 + 6 * (LAYERS - 1 - layer)
    return first + (4, 5, 3, 1, 2, 0)[i]


NS_COEF = (3.4445, -4.775, 2.0315)
LR_MUON = 0.5
LR_ADAM = 0.02
WEIGHT_DECAY = 0.1
SCORE_SCALE = 1.0 / math.sqrt(HEAD_DIM)
HIGHEST_PREC = lax.Precision.HIGHEST

F32 = jnp.float32
BF16 = jnp.bfloat16
SCOPE = 16
GELU_C = math.sqrt(2.0 / math.pi)
GROUPS = ((0, 4), (4, 12), (12, 16), (16, 24))


def unit_tables():
    big, small = [], []
    for u in range(18 * LAYERS):
        layer, place = divmod(u, 18)
        big.append(layer * BIG + place if place < BIG else -1)
        small.append(-1 if place < BIG else small_at(layer, place - BIG))
    return np.array(big + [-1] * 3), np.array(small + [TIME_AT, SHIFT_F, SCALE_F])


BIG_OF, SMALL_OF = unit_tables()


def params(limit, **more):
    return pltpu.CompilerParams(vmem_limit_bytes=limit * 1024 * 1024, **more)


SMEM_SPEC = pl.BlockSpec(memory_space=pltpu.SMEM)
VMEM_SPEC = pl.BlockSpec(memory_space=pltpu.VMEM)


def in_hbm(values):
    return pltpu.with_memory_space_constraint(values, pltpu.HBM)


def dot(a, b):
    return lax.dot_general(a, b, (((1,), (0,)), ((), ())), preferred_element_type=F32)


def dot_nt(a, b):
    return lax.dot_general(a, b, (((1,), (1,)), ((), ())), preferred_element_type=F32)


def dot_tn(a, b):
    return lax.dot_general(a, b, (((0,), (0,)), ((), ())), preferred_element_type=F32)


def shape(dims, kind):
    return jax.ShapeDtypeStruct(dims, kind)


ISSUED = []


def order(values, after):
    if not after:
        return values
    flat, tree = jax.tree.flatten(values)
    tied = lax.optimization_barrier(tuple(flat) + tuple(after))
    return jax.tree.unflatten(tree, tied[: len(flat)])


def drive(work, line):
    ISSUED.clear()
    try:
        value = next(work)
        while True:
            after = tuple(ISSUED)
            ISSUED.clear()
            value = work.send(order(value, line(after)))
    except StopIteration as end:
        return end.value


def together(*works):
    ends, flying = [None] * len(works), {}

    def go(i, step):
        try:
            flying[i] = step()
        except StopIteration as end:
            flying.pop(i, None)
            ends[i] = end.value

    for i, work in enumerate(works):
        go(i, lambda: next(work))
    while flying:
        got = yield dict(flying)
        for i in list(got):
            go(i, lambda: works[i].send(got[i]))
    return ends


def finish(work, value):
    try:
        work.send(value)
    except StopIteration as end:
        return end.value
    raise AssertionError


def flip(values, axis, bit, size):
    ISSUED.append(values)
    got = lax.ppermute(values, axis, [(i, i ^ bit) for i in range(size)])
    if axis == "tensor" and values.size < 2**16:
        ISSUED.append(got)
    return got


def is_at(flag, value, ndim):
    return flag.reshape((1,) * ndim) == value


def pick(low, high, place, other=False):
    return jnp.where(is_at(place, 1 if other else 0, low.ndim), low, high)


def own_latents(values, axis, data, n_data):
    n_lat = values.shape[axis]
    dims = values.shape[:axis] + (n_lat * n_data,) + values.shape[axis + 1 :]
    at = lax.broadcasted_iota(jnp.int32, dims, axis)
    first = data.reshape((1,) * len(dims)) * n_lat
    placed = jnp.zeros(dims, values.dtype)
    for l in range(n_lat):
        placed = jnp.where(at == first + l, lax.slice_in_dim(values, l, l + 1, axis=axis), placed)
    return placed


def dp_sum(values, n_data):
    bit = 1
    while bit < n_data:
        values = values + (yield flip(values, "dp", bit, n_data))
        bit *= 2
    return values


def dp_rows(values, n_data):
    bit = 1
    while bit < n_data:
        values = jnp.concatenate([values, (yield flip(values, "dp", bit, n_data))], 0)
        bit *= 2
    return values


def core_flip(values):
    return flip(values, "tensor", 1, 4)


def x_flip(values):
    return flip(values, "tensor", 2, 4)


def gather_tokens(own, waits=1):
    flying = core_flip(own), x_flip(own)
    for _ in range(waits):
        flying = yield flying
    beside, across = flying
    return own, beside, across, core_flip(across)


def gather_columns(own, chip, core):
    beside, across = yield (core_flip(own), x_flip(own))
    corner = core_flip(across)
    at_core = [is_at(core, i, own.ndim) for i in range(2)]
    at_chip = [is_at(chip, i, own.ndim) for i in range(2)]
    near = [jnp.where(at_core[i], own, beside) for i in range(2)]
    far = [jnp.where(at_core[i], across, corner) for i in range(2)]
    parts = [jnp.where(at_chip[i], near[j], far[j]) for i in range(2) for j in range(2)]
    return jnp.concatenate(parts, -1)


def scatter_tokens(keep, send):
    got = core_flip(send)
    far = (keep[1] + got[1].astype(F32)).astype(BF16)
    return keep, got, (yield x_flip(far))


def core_columns(values, core, other=False):
    size = values.shape[-1] // 4
    block = [lax.slice_in_dim(values, j * size, (j + 1) * size, axis=values.ndim - 1) for j in range(4)]
    return [pick(block[2 * x], block[2 * x + 1], core, other) for x in range(2)]


def core_columns_sum(values, core):
    got = core_flip(jnp.concatenate(core_columns(values, core, True), -1))
    size = got.shape[-1] // 2
    return [
        mine + lax.slice_in_dim(got, x * size, (x + 1) * size, axis=got.ndim - 1)
        for x, mine in enumerate(core_columns(values, core))
    ]


def own_columns_sum(values, chip, core):
    mine = core_columns_sum(values, core)
    return pick(*mine, chip) + (yield x_flip(pick(*mine, chip, True)))


def sum_of_columns(values, chip, core, n_data):
    return (yield from dp_sum((yield from own_columns_sum(values, chip, core)), n_data))


def ring_order(n_data):
    return [0, 2, 4, 6, 7, 5, 3, 1] if n_data == 8 else list(range(n_data))


def plan_kernel(n_units, n_slots, steps, depth, n_data, me_ref, owner_ref, table_ref, tab_ref, slot_ref):
    me = me_ref[0]
    place_of = [int(v) for v in np.argsort(ring_order(n_data))]
    my_place = sum(jnp.where(me == d, place_of[d], 0) for d in range(n_data))
    owner = owner_ref[...]
    across = jnp.broadcast_to(owner, (128, 128))
    before = lax.broadcasted_iota(jnp.int32, (128, 128), 0) < lax.broadcasted_iota(jnp.int32, (128, 128), 1)
    slot = jnp.sum(jnp.where((across == across.T) & before, 1.0, 0.0), 0, keepdims=True)
    mine = owner == me.astype(F32)
    lane8 = lax.broadcasted_iota(jnp.int32, (8, 128), 1)
    row8 = lax.broadcasted_iota(jnp.int32, (8, 128), 0)
    result = jnp.full((8, 128), -1, jnp.int32)
    for s in range(n_slots):
        held = mine & (slot == s)
        value = jnp.sum(jnp.where(held, table_ref[...], 0), 1, keepdims=True) - 1
        result = jnp.where((lane8 == s) & (row8 < 4), value, result)
    lane1 = lax.broadcasted_iota(jnp.int32, (1, 128), 1)
    time = lane1 == 18 * LAYERS
    time_slot = jnp.sum(jnp.where(time, slot, 0.0), 1, keepdims=True).astype(jnp.int32)
    time_mine = jnp.sum(jnp.where(time & mine, 1.0, 0.0), 1, keepdims=True).astype(jnp.int32)
    result = jnp.where((row8 == 4) & (lane8 == 0), time_slot, result)
    result = jnp.where((row8 == 4) & (lane8 == 1), time_mine, result)
    peers = jnp.full((1, 128), -1, jnp.int32)
    place = jnp.full((1, 128), -9, jnp.int32)
    for d in range(n_data):
        ahead = place_of[d] - my_place
        peers = jnp.where(lane1 == jnp.where(ahead < 0, ahead + n_data, ahead), d, peers)
        place = jnp.where(owner == float(d), place_of[d], place)
    slot_ref[...] = jnp.where(row8 == 5, peers, result)

    big = jnp.where(lane1 < BIG, place, pltpu.roll(place, 128 - 6, 1))
    big = jnp.where(lane1 < N_BIG, big, -9)
    back = jnp.where(big >= 0, n_data - 1 - big, -9)
    lane = lax.broadcasted_iota(jnp.int32, (n_data, 128), 1)
    row = lax.broadcasted_iota(jnp.int32, (n_data, 128), 0)
    follow = jnp.where(row == n_data - 1, 0, row + 1)
    own = [(row == at).astype(jnp.int32) for at in (big, back)]
    open_to = [(follow != at).astype(jnp.int32) for at in (big, back)]
    spots = [my_place, n_data - 1 - my_place]
    far = jnp.int32(999)

    def step(t, carry):
        line = jnp.full((1, 128), -1, jnp.int32)
        after = []
        for way in range(2):
            have, sent, *coming = carry[way]
            here = spots[way]
            prior = jnp.where(here == 0, n_data - 1, here - 1)
            open_now = have * (1 - sent) * open_to[way]
            first = jnp.min(jnp.where(open_now > 0, lane, far), axis=1, keepdims=True)
            chosen = (lane == first).astype(jnp.int32)
            first = jnp.broadcast_to(first, (n_data, 128))
            for k, who in enumerate((here, prior)):
                index = jnp.min(jnp.where(row == who, first, far), axis=0, keepdims=True)
                index = jnp.where(index == far, -1, index)
                line = jnp.where(lane1 == 2 * way + k, index, line)
            coming = list(coming) + [pltpu.roll(chosen, 1, 0)]
            after.append((have + coming[0], sent + chosen, *coming[1:]))
        tab_ref[pl.ds(t, 1), :] = line
        return tuple(after)

    none = jnp.zeros((n_data, 128), jnp.int32)
    lax.fori_loop(0, steps, step, tuple((own[way], none) + (none,) * (depth - 1) for way in range(2)))


def plan(owners, tables, n_slots, n_data, steps, depth, my_data):
    n_units = owners.shape[0]
    padded = jnp.pad(owners.astype(F32), (0, 128 - n_units), constant_values=-1.0)[None]
    wide = np.zeros((8, 128), np.int32)
    wide[: len(tables), :n_units] = tables + 1
    tab, rows = pl.pallas_call(
        functools.partial(plan_kernel, n_units, n_slots, steps, depth, n_data),
        out_shape=[shape((steps, 128), jnp.int32), shape((8, 128), jnp.int32)],
        in_specs=[SMEM_SPEC, VMEM_SPEC, VMEM_SPEC],
        out_specs=[VMEM_SPEC, VMEM_SPEC],
        compiler_params=params(SCOPE),
        name="plan",
    )(my_data.reshape(1), padded, jnp.asarray(wide))
    return tab[:, :4], rows


def spread_init_kernel(slots_ref, bank_ref, out_ref, wide, sem):
    big_ref = [slots_ref[0, s] for s in range(bank_ref.shape[0])]
    n_slots = bank_ref.shape[0]
    for s in range(n_slots):
        copy = pltpu.make_async_copy(bank_ref.at[s], wide.at[s], sem.at[s])
        pl.when(big_ref[s] >= 0)(copy.start)
    for s in range(n_slots):
        copy = pltpu.make_async_copy(bank_ref.at[s], wide.at[s], sem.at[s])
        pl.when(big_ref[s] >= 0)(copy.wait)

        @pl.when(big_ref[s] >= 0)
        def _(s=s):
            out_ref[jnp.maximum(big_ref[s], 0)] = wide[s].astype(BF16)


def spread_init(big_slots, master_bank):
    n_slots, rows, columns = master_bank.shape
    return pl.pallas_call(
        spread_init_kernel,
        out_shape=pltpu.VMEM((N_BIG + BIG, rows, columns), BF16),
        in_specs=[SMEM_SPEC, pl.BlockSpec(memory_space=pltpu.HBM)],
        out_specs=VMEM_SPEC,
        scratch_shapes=[
            pltpu.VMEM((n_slots, rows, columns), F32),
            pltpu.SemaphoreType.DMA((n_slots,)),
        ],
        compiler_params=params(SCOPE),
        name="own_weights",
    )(big_slots, in_hbm(master_bank))


def spread_kernel(places, fetch_at, tab_ref, got, held, out):
    half = held.shape[1] // 2
    for way in range(2):
        rows = pl.ds(way * half, half)
        for k, t in enumerate(places):
            unit = tab_ref[t, 2 * way + 1]

            @pl.when(unit >= 0)
            def _():
                held[jnp.maximum(unit, 0), rows] = got[2 * k + way][...]

        if fetch_at is not None:
            out[way][...] = held[jnp.maximum(tab_ref[fetch_at, 2 * way], 0), rows]


def ring_step(name, tab, held, got, sends, body, work=None, mail=(), mail_rows=0, keep_rows=0):
    rows, columns = held.shape[1:]
    extra, more, operands, shapes, scratch = (tuple(work) + ([],))[:5] if work else ("", None, [], [], [])
    specs = [value[1] if isinstance(value, tuple) else VMEM_SPEC for value in operands]
    operands = [value[0] if isinstance(value, tuple) else value for value in operands]
    operands, specs = list(mail) + list(operands), [VMEM_SPEC] * len(mail) + specs
    n, m, k = len(got), len(operands), len(mail)
    kept = 2 if keep_rows else 0
    shapes = [pltpu.VMEM((keep_rows, columns), BF16)] * kept + list(shapes)

    def kernel(tab_ref, *refs):
        out = refs[n + 1 + m :]
        if body is not None:
            body(tab_ref, refs[:n], out[0], out[1 : 1 + sends], *([refs[n + 1 : n + 1 + k]] if k else []))
        for way in range(kept):
            out[1 + sends + way][...] = refs[way][refs[way].shape[0] - keep_rows :]
        if more is not None:
            more(out[0], *refs[n + 1 + k : n + 1 + m], *out[1 + sends + kept :])

    res = pl.pallas_call(
        kernel,
        out_shape=[pltpu.VMEM(held.shape, held.dtype)] + [pltpu.VMEM((rows // 2 + mail_rows, columns), BF16)] * sends
        + list(shapes),
        in_specs=[SMEM_SPEC] + [VMEM_SPEC] * (n + 1) + specs,
        out_specs=[VMEM_SPEC] * (1 + sends + len(shapes)),
        scratch_shapes=scratch,
        input_output_aliases={1 + n: 0},
        compiler_params=params(SCOPE),
        name=name + extra,
    )(tab, *got, held, *operands)
    return res[0], list(res[1 : 1 + sends]), list(res[1 + sends :])


def ring_perms(n_data):
    order = ring_order(n_data)
    ahead = [(order[i], order[(i + 1) % n_data]) for i in range(n_data)]
    return ahead, [(b, a) for a, b in ahead]


class Spreader:
    def __init__(self, tab, held, n_data, steps, depth):
        self.tab, self.n_data, self.steps, self.depth = tab, n_data, steps, depth
        self.perms = ring_perms(n_data)
        self.held = held
        self.got = {}
        self.at = 0

    def last(self, g):
        return GROUPS[g][1] - 1 + (self.n_data - 2) * self.depth

    def step(self, after=()):
        self.work(None, after)
        return self.sent

    def work(self, work, after=()):
        t = self.at
        self.sent = ()
        if t > self.steps:
            return []
        fetch_at = t if t < self.steps else None
        places = [t - self.depth] if fetch_at is not None else list(range(self.steps - self.depth, self.steps))
        places = [p for p in places if p >= 0]
        self.held, sends, results = ring_step(
            "spread_step",
            order(self.tab, after),
            self.held,
            [value for p in places for value in self.got.pop(p)],
            0 if fetch_at is None else 2,
            functools.partial(spread_kernel, places, fetch_at),
            work,
        )
        if fetch_at is not None:
            self.got[t] = [lax.ppermute(sends[way], "dp", self.perms[way]) for way in range(2)]
        self.at += 1
        self.sent = tuple(sends) + tuple(self.got.get(t - 1, ()))
        return order(results, tuple(self.got.get(t - 1, ())))

    def prepare(self, g):
        while self.at < min(self.last(g) + self.depth, self.steps):
            self.step()


def reduce_kernel(place_at, fetch_at, mail, tab_ref, got, held, out, own=()):
    half = held.shape[1] // 2
    if mail:
        for way in range(2):
            out[way][half:] = own[0][...] if mail == "own" else got[way][half:]
    for way in range(2):
        rows = pl.ds(way * half, half)
        if place_at is not None:
            unit = tab_ref[place_at, 2 * way]

            @pl.when(unit >= 0)
            def _():
                at = BIG + jnp.maximum(unit, 0)
                held[at, rows] = (held[at, rows].astype(F32) + got[way][:half].astype(F32)).astype(BF16)

        out[way][:half] = held[BIG + jnp.maximum(tab_ref[fetch_at, 2 * way + 1], 0), rows]


class Reducer:
    def __init__(self, tab, n_data, steps, depth):
        self.tab, self.n_data, self.steps, self.depth = tab, n_data, steps, depth
        self.perms = [p for p in reversed(ring_perms(n_data))]
        self.held = None
        self.ready = N_BIG
        self.mail = {}
        self.come = {}
        self.got = {}
        self.at = 0

    def lowest(self, k):
        return (self.steps - 1 - k) - (self.n_data - 2) * self.depth

    def step(self, after=()):
        k = self.at
        self.sent = ()
        if k < self.steps and max(self.lowest(k), 0) >= self.ready:
            self.work(None, after)
        return self.sent

    def work(self, work, after=()):
        k = self.at
        self.sent = ()
        tab = order(self.tab, after)
        if k >= self.steps or max(self.lowest(k), 0) < self.ready:
            self.held, unused, results = ring_step("layer_", tab, self.held, [], 0, None, work)
            return results
        place_at = self.steps - 1 - (k - self.depth) if k >= self.depth else None
        payload, hops = self.mail.get(k, (None, 0))
        mail = None if payload is None else "own" if hops == 0 else "pass"
        keep_rows = self.mail[k - self.depth][0].shape[0] if k - self.depth in self.mail else 0
        self.held, sends, results = ring_step(
            "reduce_step",
            tab,
            self.held,
            self.got.get(k - self.depth, []),
            2,
            functools.partial(reduce_kernel, place_at, self.steps - 1 - k, mail),
            work,
            [payload] if mail == "own" else [],
            0 if payload is None else payload.shape[0],
            keep_rows,
        )
        if keep_rows:
            self.come[k - self.depth], results = results[:2], results[2:]
        self.got[k] = [lax.ppermute(sends[way], "dp", self.perms[way]) for way in range(2)]
        self.at += 1
        self.sent = tuple(sends) + tuple(self.got.get(k - 1, ()))
        return order(results, tuple(self.got.get(k - 1, ())))

    def gather(self, *payloads):
        far = self.n_data // 2
        starts = [self.at + i for i in range(len(payloads))]
        for start, payload in zip(starts, payloads):
            for j in range(far):
                self.mail[start + j * self.depth] = (payload, j)
        ISSUED.extend(payloads[1:])
        last = starts[-1] + far * self.depth
        assert len(payloads) <= self.depth and last < self.steps
        while self.at <= last:
            yield ()
        everyone = []
        for start, payload in zip(starts, payloads):
            come = [[self.come[start + j * self.depth][way] for j in range(far)] for way in range(2)]
            everyone.append(order([payload] + come[0][: far - 1] + come[1][::-1], self.sent))
        return everyone

    def drain(self):
        while self.at < self.steps:
            self.step()

    def last(self):
        return [self.got[self.steps - 1 - t][way] for t in range(self.depth) for way in range(2)]


def past(kernel, operands, beside):
    n, m = len(operands), len(beside)
    return lambda *refs: kernel(*refs[:n], *refs[n + m :])


def split_rows(total, keep_ref, send_ref):
    rows = total.shape[0] // 4
    for i in range(2):
        keep_ref[i] = total[2 * i * rows : (2 * i + 1) * rows]
        send_ref[i] = total[(2 * i + 1) * rows : (2 * i + 2) * rows].astype(BF16)


def part_shapes(rows, width):
    return [shape((2, rows // 4, width), F32), shape((2, rows // 4, width), BF16)]


def joined(refs):
    return jnp.concatenate([r[...] for r in refs], 0)


def softmax_parts(q, k):
    scores = dot_nt(q, k) * SCORE_SCALE
    expo = jnp.exp(scores - jnp.max(scores, -1, keepdims=True))
    return expo / jnp.sum(expo, -1, keepdims=True)


def attention_kernel(n_lat, base, w_ref, x0, x1, x2, x3, qkv_ref, mixed_ref, keep_ref, send_ref):
    x = joined((x0, x1, x2, x3))
    for j in range(3):
        qkv_ref[j] = dot(x, w_ref[base + j]).astype(BF16)
    toks = x.shape[0] // n_lat
    heads = w_ref.shape[2] // HEAD_DIM
    for l in range(n_lat):
        rows = slice(l * toks, (l + 1) * toks)
        outs = []
        for h in range(heads):
            cols = slice(h * HEAD_DIM, (h + 1) * HEAD_DIM)
            q, k, v = (qkv_ref[j, rows, cols] for j in range(3))
            outs.append(dot(softmax_parts(q, k).astype(BF16), v))
        mixed_ref[rows, :] = jnp.concatenate(outs, 1).astype(BF16)
    split_rows(dot_nt(mixed_ref[...], w_ref[base + 3]), keep_ref, send_ref)


def attention(x, columns, base, n_lat):
    rows, width = 4 * x[0].shape[0], x[0].shape[1]
    shapes = [shape((3, rows, columns), BF16), shape((rows, columns), BF16)] + part_shapes(rows, width)
    return "_attention", functools.partial(attention_kernel, n_lat, base), x, shapes


def gelu(x):
    return 0.5 * x * (1.0 + jnp.tanh(GELU_C * (x + 0.044715 * x * x * x)))


def gelu_grad(x):
    t = jnp.tanh(GELU_C * (x + 0.044715 * x * x * x))
    return 0.5 * (1.0 + t) + 0.5 * x * (1.0 - t * t) * (GELU_C * (1.0 + 3 * 0.044715 * x * x))


def mlp_kernel(base, w_ref, x0, x1, x2, x3, hidden_ref, active_ref, keep_ref, send_ref):
    x = joined((x0, x1, x2, x3))
    total = None
    for j in range(4):
        hidden = dot(x, w_ref[base + j])
        hidden_ref[j] = hidden
        active = gelu(hidden).astype(BF16)
        active_ref[j] = active
        part = dot_nt(active, w_ref[base + 4 + j])
        total = part if total is None else total + part
    split_rows(total, keep_ref, send_ref)


def mlp(x, columns, base):
    rows, width = 4 * x[0].shape[0], x[0].shape[1]
    shapes = [shape((4, rows, columns), F32), shape((4, rows, columns), BF16)] + part_shapes(rows, width)
    return "_mlp", functools.partial(mlp_kernel, base), x, shapes


def mlp_back_kernel(base, w_ref, d0, d1, d2, d3, hidden_ref, dh_ref, keep_ref, send_ref):
    d = joined((d0, d1, d2, d3))
    total = None
    for j in range(4):
        dh = (gelu_grad(hidden_ref[j]) * dot(d, w_ref[base + 4 + j])).astype(BF16)
        dh_ref[j] = dh
        part = dot_nt(dh, w_ref[base + j])
        total = part if total is None else total + part
    split_rows(total, keep_ref, send_ref)


def mlp_back(d, hidden, base):
    rows, width = 4 * d[0].shape[0], d[0].shape[1]
    shapes = [shape(hidden.shape, BF16)] + part_shapes(rows, width)
    return "_mlp_back", functools.partial(mlp_back_kernel, base), [*d, hidden], shapes


def attention_back_kernel(n_lat, base, w_ref, d0, d1, d2, d3, qkv_ref, dqkv_ref, keep_ref, send_ref):
    d_mixed = dot(joined((d0, d1, d2, d3)), w_ref[base + 3]).astype(BF16)
    toks = d_mixed.shape[0] // n_lat
    heads = w_ref.shape[2] // HEAD_DIM
    for l in range(n_lat):
        rows = slice(l * toks, (l + 1) * toks)
        outs = [[], [], []]
        for h in range(heads):
            cols = slice(h * HEAD_DIM, (h + 1) * HEAD_DIM)
            q, k, v = (qkv_ref[j, rows, cols] for j in range(3))
            do = d_mixed[rows, cols]
            probs = softmax_parts(q, k)
            d_probs = dot_nt(do, v)
            d_scores = probs * (d_probs - jnp.sum(probs * d_probs, -1, keepdims=True))
            d_scores = d_scores.astype(BF16)
            outs[0].append(dot(d_scores, k) * SCORE_SCALE)
            outs[1].append(dot_tn(d_scores, q) * SCORE_SCALE)
            outs[2].append(dot_tn(probs.astype(BF16), do))
        for j in range(3):
            dqkv_ref[j, rows, :] = jnp.concatenate(outs[j], 1).astype(BF16)
    total = sum(dot_nt(dqkv_ref[j], w_ref[base + j]) for j in range(3))
    split_rows(total, keep_ref, send_ref)


def attention_back(d, qkv, base, n_lat):
    rows, width = 4 * d[0].shape[0], d[0].shape[1]
    shapes = [shape(qkv.shape, BF16)] + part_shapes(rows, width)
    return "_attention_back", functools.partial(attention_back_kernel, n_lat, base), [*d, qkv], shapes


def weight_grad_kernel(counts, n_lat, base, out_ref, *refs):
    n = len(counts)
    lefts, rights, (mean_ref, sum_ref) = refs[: 4 * n], refs[4 * n : 5 * n], refs[-2:]
    at = 0
    for k, count in enumerate(counts):
        a = joined(lefts[4 * k : 4 * k + 4])
        toks = a.shape[0] // n_lat

        def rows_of(x, scale):
            parts = [
                jnp.sum(x[l * toks : (l + 1) * toks].astype(F32), 0, keepdims=True) * scale for l in range(n_lat)
            ]
            return jnp.concatenate(parts + [jnp.zeros((8 - n_lat, x.shape[1]), F32)], 0).astype(BF16)

        mean = rows_of(a, 1.0 / toks)
        mean_ref[k] = mean.astype(F32)
        for j in range(count):
            b = rights[k][j]
            total = rows_of(b, 1.0)
            sum_ref[at] = total.astype(F32)
            out_ref[BIG + base + at] = (dot_tn(a, b) - dot_tn(mean, total)).astype(BF16)
            at += 1


def weight_grads(base, pairs, n_lat):
    counts = [right.shape[0] for _, right in pairs]
    width, columns = pairs[0][0][0].shape[1], pairs[0][1].shape[2]
    operands = [part for left, _ in pairs for part in left] + [right for _, right in pairs]
    shapes = [shape((len(pairs), 8, width), F32), shape((sum(counts), 8, columns), F32)]
    return "_weight_grads", functools.partial(weight_grad_kernel, counts, n_lat, base), operands, shapes


def small_weights(small_ref, bank_ref, wide, sem, use):
    units = [small_ref[s] for s in range(bank_ref.shape[0])]
    ours = [(unit >= 0) & (unit != TIME_AT) for unit in units]
    copies = [pltpu.make_async_copy(bank_ref.at[s], wide.at[s], sem.at[s]) for s in range(len(units))]
    for s, copy in enumerate(copies):
        pl.when(ours[s])(copy.start)
    for s, copy in enumerate(copies):

        @pl.when(ours[s])
        def _(s=s, copy=copy):
            copy.wait()
            use(jnp.maximum(units[s], 0), wide[s].astype(BF16))


def modulation_kernel(held_ref, small_ref, cond_ref, bank_ref, out_ref, wide, sem):
    out_ref[...] = jnp.zeros_like(out_ref)

    def use(unit, weight):
        out_ref[unit] = dot(cond_ref[...], weight)

    small_weights(small_ref, bank_ref, wide, sem, use)


def bank_scratch(bank):
    return [pltpu.VMEM(bank.shape, F32), pltpu.SemaphoreType.DMA((bank.shape[0],))]


def modulations(small_slots, cond_in, bank):
    operands = [(small_slots, SMEM_SPEC), cond_in, (in_hbm(bank), pl.BlockSpec(memory_space=pltpu.HBM))]
    shapes = [shape((SMALL_ROWS, cond_in.shape[0], bank.shape[2]), F32)]
    return "_modulations", modulation_kernel, operands, shapes, bank_scratch(bank)


def cond_back_kernel(n_mail, held_ref, small_ref, peer_ref, *refs):
    mail, (bank_ref, d_ref, out_ref, wide, sem) = refs[:n_mail], refs[n_mail:]
    if n_mail == 1:
        d_ref[...] = mail[0][...]
    else:
        n_lat = d_ref.shape[0] // n_mail
        for i in range(n_mail):
            for l in range(n_lat):
                d_ref[peer_ref[i] * n_lat + l] = mail[i][l * SMALL_ROWS : (l + 1) * SMALL_ROWS]
    out_ref[...] = jnp.zeros_like(out_ref)

    def use(unit, weight):
        d = d_ref[...].astype(F32)
        d = jnp.sum(jnp.where(lax.broadcasted_iota(jnp.int32, d.shape, 1) == unit, d, 0.0), 1)
        out_ref[...] += dot_nt(d.astype(BF16), weight)

    small_weights(small_ref, bank_ref, wide, sem, use)


def cond_back(small_slots, peers, mail, n_all, bank):
    columns = bank.shape[2]
    operands = [(small_slots, SMEM_SPEC), (peers, SMEM_SPEC)] + list(mail)
    operands += [(in_hbm(bank), pl.BlockSpec(memory_space=pltpu.HBM))]
    shapes = [shape((n_all, SMALL_ROWS, columns), BF16), shape((n_all, bank.shape[1]), F32)]
    return "_cond_back", functools.partial(cond_back_kernel, len(mail)), operands, shapes, bank_scratch(bank)


def mail_sum_kernel(n_mail, held_ref, peer_ref, *refs):
    mail, (out_ref, whole) = refs[:n_mail], refs[n_mail:]
    rows = out_ref.shape[0]
    for i in range(n_mail):
        whole[peer_ref[i]] = mail[i][:rows].astype(F32) + mail[i][rows:].astype(F32)
    total = whole[0]
    for i in range(1, n_mail):
        total = total + whole[i]
    out_ref[...] = total


def mail_sum(peers, mail):
    rows, columns = mail[0].shape[0] // 2, mail[0].shape[1]
    scratch = [pltpu.VMEM((len(mail), rows, columns), F32)]
    operands = [(peers, SMEM_SPEC)] + list(mail)
    return "_mail_sum", functools.partial(mail_sum_kernel, len(mail)), operands, [shape((rows, columns), F32)], scratch


def halves(x):
    high = x.astype(BF16)
    return high, (x - high.astype(F32)).astype(BF16)


def newton_sweep_coarse(x):
    xh = x.astype(BF16)
    gram = dot_tn(xh, xh)
    gh = gram.astype(BF16)
    poly = NS_COEF[1] * gram + NS_COEF[2] * dot(gh, gh)
    return NS_COEF[0] * x + dot(xh, poly.astype(BF16))


def newton_sweep(x):
    xh, xl = halves(x)
    cross = dot_tn(xh, xl)
    gram = dot_tn(xh, xh) + (cross + cross.T)
    gh, gl = halves(gram)
    cross = dot(gh, gl)
    square = dot(gh, gh) + (cross + cross.T)
    ph, pl_ = halves(NS_COEF[1] * gram + NS_COEF[2] * square)
    return NS_COEF[0] * x + (dot(xh, ph) + (dot(xl, ph) + dot(xh, pl_)))


def newton_kernel(n_last, base, big_ref, left_ref, right_ref, tab_ref, a_ref, b_ref, bank_ref, mom_ref, *refs):
    held, got = refs[0], refs[1 : 1 + n_last]
    new_ref, mom_new_ref, mark_ref, grad, sem = refs[-5:]
    s = base + pl.program_id(0)
    mark_ref[...] = jnp.zeros_like(mark_ref)
    unit, left, right = big_ref[s], left_ref[s], right_ref[s]
    half = got[0].shape[0]

    @pl.when(right < 0)
    def _():
        new_ref[...] = bank_ref[...]
        mom_new_ref[...] = mom_ref[...]

    @pl.when(right >= 0)
    def _():
        copy = pltpu.make_async_copy(held.at[BIG + jnp.maximum(unit, 0)], grad, sem.at[0])
        pl.when(unit >= 0)(copy.start)
        mom_new_ref[0] = 0.5 * mom_ref[0] + dot_tn(
            a_ref[jnp.maximum(left, 0)], b_ref[jnp.maximum(right, 0)]
        )
        pl.when(unit >= 0)(copy.wait)

        @pl.when(unit >= 0)
        def _():
            mom_new_ref[0] += grad[...].astype(F32)

        for i in range(n_last):
            rows = slice((i % 2) * half, (i % 2 + 1) * half)

            @pl.when((tab_ref[i // 2, 2 * (i % 2)] == unit) & (unit >= 0))
            def _(i=i, rows=rows):
                mom_new_ref[0, rows] += got[i][...].astype(F32)

        block = mom_new_ref[0]
        norm = jnp.sqrt(jnp.sum(block * block)) + 1e-07
        x = block / norm
        for sweep in range(5):
            x = newton_sweep_coarse(x) if sweep < 3 else newton_sweep(x)
        new_ref[0] = bank_ref[0] - LR_MUON * x


class Optimizer:
    def __init__(self, slots, tab, a_all, b_all, master, momentum, held, got):
        self.scalars = [*slots, tab]
        self.arrays = [a_all, b_all, in_hbm(master), in_hbm(momentum), held, *got]
        self.news = []
        self.at = 0

    def step(self, after=(), count=4):
        a_all, b_all, master, momentum, held, *got = self.arrays
        n_slots, rows, columns = master.shape
        base, count = self.at, min(count, n_slots - self.at)
        if count == 0:
            return ()
        self.at += count
        block = pl.BlockSpec((1, rows, columns), lambda s, *t: (base + s, 0, 0))
        any_spec = pl.BlockSpec(memory_space=pl.ANY)
        scalars = [order(self.scalars[0], after)] + self.scalars[1:]
        first = len(scalars) + len(self.arrays)
        *self.news, mark = pl.pallas_call(
            functools.partial(newton_kernel, len(got), base),
            grid_spec=pltpu.PrefetchScalarGridSpec(
                num_scalar_prefetch=len(scalars),
                grid=(count,),
                in_specs=[
                    pl.BlockSpec(a_all.shape, lambda s, *t: (0, 0, 0)),
                    pl.BlockSpec(b_all.shape, lambda s, *t: (0, 0, 0)),
                    block,
                    block,
                    any_spec,
                ]
                + [pl.BlockSpec(g.shape, lambda s, *t: (0, 0)) for g in got]
                + [any_spec] * len(self.news),
                out_specs=[block, block, pl.BlockSpec((8, 128), lambda s, *t: (0, 0))],
                scratch_shapes=[pltpu.VMEM((rows, columns), BF16), pltpu.SemaphoreType.DMA((1,))],
            ),
            out_shape=[shape(master.shape, F32), shape(momentum.shape, F32), shape((8, 128), F32)],
            input_output_aliases={first + i: i for i in range(len(self.news))},
            compiler_params=params(SCOPE, dimension_semantics=("arbitrary",)),
            name="optimizer",
        )(*scalars, *self.arrays, *self.news)
        return (mark,)

    def all(self):
        while self.at < self.arrays[2].shape[0]:
            self.step()
        return self.news


def layer_norm(values):
    centered = values - jnp.mean(values, -1, keepdims=True)
    inv_std = lax.rsqrt(jnp.mean(centered * centered, -1, keepdims=True) + 1e-06)
    return centered * inv_std, inv_std


def norm_back(grad_out, normed, inv_std):
    return inv_std * (
        grad_out
        - jnp.mean(grad_out, -1, keepdims=True)
        - normed * jnp.mean(grad_out * normed, -1, keepdims=True)
    )


def added(keep_ref, got_ref, far_ref):
    return keep_ref[0] + got_ref[0].astype(F32) + far_ref[...].astype(F32)


def row_of(mods_ref, at):
    return mods_ref[at : at + 1, :]


def enter_kernel(at, noisy_ref, patch_ref, place_ref, mods_ref, stream_ref, inner_ref, normed_ref, inv_ref):
    stream = dot(noisy_ref[...], patch_ref[...]) + place_ref[...]
    stream_ref[...] = stream
    normed, inv = layer_norm(stream)
    inner_ref[...] = (normed * (1.0 + row_of(mods_ref, at[1])) + row_of(mods_ref, at[0])).astype(BF16)
    normed_ref[...] = normed
    inv_ref[...] = jnp.broadcast_to(inv, inv_ref.shape)


def enter(noisy, patch, places, mods, at):
    rows, width = places.shape
    full = shape((rows, width), F32)
    return pl.pallas_call(
        functools.partial(enter_kernel, at),
        out_shape=[full, shape((rows, width), BF16), full, shape((rows, 128), F32)],
        compiler_params=params(SCOPE),
        name="enter",
    )(noisy, patch, places, mods)


def residual_kernel(
    at, keep_ref, got_ref, far_ref, stream_ref, mods_ref, part_ref, next_ref, inner_ref, normed_ref, inv_ref
):
    part = added(keep_ref, got_ref, far_ref)
    part_ref[...] = part
    stream = stream_ref[...] + row_of(mods_ref, at[0]) * part
    next_ref[...] = stream
    normed, inv = layer_norm(stream)
    inner_ref[...] = (normed * (1.0 + row_of(mods_ref, at[2])) + row_of(mods_ref, at[1])).astype(BF16)
    normed_ref[...] = normed
    inv_ref[...] = jnp.broadcast_to(inv, inv_ref.shape)


def residual(parts, stream, mods, at):
    rows, width = stream.shape
    full = shape((rows, width), F32)
    return pl.pallas_call(
        functools.partial(residual_kernel, at),
        out_shape=[full, full, shape((rows, width), BF16), full, shape((rows, 128), F32)],
        compiler_params=params(SCOPE),
        name="residual",
    )(*parts, stream, mods)


def leave_kernel(
    at,
    count_all,
    keep_ref,
    got_ref,
    far_ref,
    stream_ref,
    mods_ref,
    head_ref,
    target_ref,
    grad_ref,
    next_ref,
    rows_ref,
    edge_ref,
):
    branch = added(keep_ref, got_ref, far_ref)
    gate, shift, scale = (row_of(mods_ref, i) for i in at)
    normed, inv = layer_norm(stream_ref[...] + gate * branch)
    inner = (normed * (1.0 + scale) + shift).astype(BF16)
    head = head_ref[...]
    error = dot_nt(inner, head) - target_ref[...]
    d_output = (2.0 * error / count_all).astype(BF16)
    d_inner = dot(d_output, head)
    grad = norm_back(d_inner * (1.0 + scale), normed, inv)
    grad_ref[...] = grad
    next_ref[...] = (gate * grad).astype(BF16)
    rows_ref[...] = jnp.zeros_like(rows_ref)
    rows_ref[0:1, :] = jnp.sum(d_inner, 0, keepdims=True)
    rows_ref[1:2, :] = jnp.sum(d_inner * normed, 0, keepdims=True)
    rows_ref[2:3, :] = jnp.sum(grad * branch, 0, keepdims=True)
    n_patch = head.shape[0]
    loss = jnp.sum(jnp.sum(error * error, 1, keepdims=True), 0, keepdims=True) / count_all
    edge_ref[:n_patch, :] = dot_tn(d_output, inner)
    edge_ref[n_patch:, :] = jnp.broadcast_to(loss, (8, edge_ref.shape[1]))


def leave(parts, stream, mods, head, target, at, count_all):
    rows, width = stream.shape
    return pl.pallas_call(
        functools.partial(leave_kernel, at, count_all),
        out_shape=[
            shape((rows, width), F32),
            shape((rows, width), BF16),
            shape((SMALL_ROWS, width), F32),
            shape((head.shape[0] + 8, width), F32),
        ],
        compiler_params=params(SCOPE),
        name="leave",
    )(*parts, stream, mods, head, target)


def back_kernel(
    at,
    gate_at,
    first,
    keep_ref,
    got_ref,
    far_ref,
    normed_ref,
    inv_ref,
    grad_ref,
    part_ref,
    mods_ref,
    rows_in_ref,
    out_ref,
    next_ref,
    rows_ref,
):
    d_inner = added(keep_ref, got_ref, far_ref)
    normed = normed_ref[...]
    inv = inv_ref[:, 0:1]
    grad = grad_ref[...] + norm_back(d_inner * (1.0 + row_of(mods_ref, at)), normed, inv)
    out_ref[...] = grad
    rows_ref[...] = rows_in_ref[...]
    rows_ref[first : first + 1, :] = jnp.sum(d_inner, 0, keepdims=True)
    rows_ref[first + 1 : first + 2, :] = jnp.sum(d_inner * normed, 0, keepdims=True)
    if gate_at is None:
        next_ref[...] = grad.astype(BF16)
    else:
        next_ref[...] = (row_of(mods_ref, gate_at) * grad).astype(BF16)
        rows_ref[first + 2 : first + 3, :] = jnp.sum(grad * part_ref[...], 0, keepdims=True)


def back(parts, normed, inv, grad, part, mods, rows_in, at, gate_at, first, beside):
    rows, width = grad.shape
    operands = (*parts, normed, inv, grad, part, mods, rows_in)
    return pl.pallas_call(
        past(functools.partial(back_kernel, at, gate_at, first), operands, beside),
        out_shape=[shape((rows, width), F32), shape((rows, width), BF16), shape(rows_in.shape, F32)],
        compiler_params=params(SCOPE),
        name="back",
    )(*operands, *beside)


def tables_kernel(n_patch, fix_ref, edge_ref, time_ref, class_ref, table_ref, first_ref, second_ref, *outs):
    new_ref, first_new_ref, second_new_ref = outs
    at = 0
    for ref, low, count in (
        (edge_ref, 0, n_patch),
        (time_ref, 0, FREQ),
        (class_ref, 0, CLASSES),
        (edge_ref, n_patch, n_patch),
    ):
        rows = slice(at, at + count)
        grad = ref[low : low + count, :]
        first = 0.5 * first_ref[rows, :] + 0.5 * grad
        second = 0.5 * second_ref[rows, :] + 0.5 * grad * grad
        first_new_ref[rows, :] = first
        second_new_ref[rows, :] = second
        new_ref[rows, :] = table_ref[rows, :] * (1.0 - LR_ADAM * WEIGHT_DECAY) - LR_ADAM * (
            first / fix_ref[0]
        ) / (jnp.sqrt(second / fix_ref[0]) + 1e-08)
        at += count


def update_tables(n_patch, bias_fix, edges, grad_time, grad_class, table, first, second):
    return pl.pallas_call(
        functools.partial(tables_kernel, n_patch),
        out_shape=[shape(table.shape, F32)] * 3,
        in_specs=[SMEM_SPEC] + [VMEM_SPEC] * 6,
        compiler_params=params(SCOPE),
        name="update_tables",
    )(bias_fix, edges, grad_time, grad_class, table, first, second)


def position_rows(first, rows):
    quarter = D // 4
    omega = jnp.exp(-math.log(10000.0) * jnp.arange(quarter, dtype=F32) / quarter)
    places = first + jnp.arange(rows, dtype=jnp.int32)
    rows_at = (places // GRID).astype(F32)[:, None] * omega[None]
    cols_at = (places % GRID).astype(F32)[:, None] * omega[None]
    return jnp.concatenate([jnp.sin(rows_at), jnp.cos(rows_at), jnp.sin(cols_at), jnp.cos(cols_at)], 1)


def time_features(timesteps):
    half_freq = FREQ // 2
    rates = jnp.exp(-math.log(10000.0) * jnp.arange(half_freq, dtype=F32) / half_freq)
    angles = timesteps.astype(F32)[:, None] * rates[None]
    return jnp.concatenate([jnp.cos(angles), jnp.sin(angles)], 1)


def shards(
    noisy_latents,
    noise_target,
    timesteps,
    labels,
    owners,
    step_count,
    master_bank,
    momentum_bank,
    embed_tables,
    embed_first,
    embed_second,
):
    n_lat, n_tok, n_patch = noisy_latents.shape
    n_slots, width, columns = master_bank.shape
    n_data = lax.axis_size("dp")
    my_data = lax.axis_index("dp")
    my_tensor = lax.axis_index("tensor")
    n_all = n_lat * n_data
    own_rows = n_lat * n_tok // 4
    count_all = float(n_all * n_tok * n_patch)
    depth = 2 if n_data <= 8 else 1
    steps = N_BIG + (n_data - 2) * depth

    kind = [2 + 2 * g + (b >= low + (3, 4)[g % 2]) for g, (low, high) in enumerate(GROUPS) for b in range(low, high)]
    slot_tables = np.stack(
        [
            BIG_OF,
            SMALL_OF,
            np.where(BIG_OF >= 0, np.array(kind)[BIG_OF], np.where(SMALL_OF == TIME_AT, 1, 0)),
            np.where(BIG_OF >= 0, SMALL_ROWS + BIG_OF, SMALL_OF),
        ]
    )
    tab, planned = plan(owners, slot_tables, n_slots, n_data, steps, depth, my_data)

    def flag(value):
        return jnp.asarray(value, jnp.int32).reshape(1)

    first_row = my_tensor * own_rows
    early = dict(
        slots=planned[:4, :n_slots],
        peers=planned[5, :n_data],
        chip=flag(my_tensor // 2),
        core=flag(my_tensor % 2),
        data=flag(my_data),
        bits=[flag((my_data // (1 << i)) % 2) for i in range((n_data - 1).bit_length())],
        time_mine=planned[4, 1:2],
        time_w2=lax.dynamic_index_in_dim(master_bank, planned[4, 0], 0, keepdims=False).astype(BF16),
        noisy=lax.dynamic_slice_in_dim(noisy_latents.reshape(n_lat * n_tok, n_patch), first_row, own_rows, 0),
        target=lax.dynamic_slice_in_dim(noise_target.reshape(n_lat * n_tok, n_patch), first_row, own_rows, 0),
        places=position_rows(first_row % n_tok, own_rows),
        ids=jnp.stack([timesteps, labels], 1),
        bias_fix=1.0 - jnp.power(0.5, step_count.astype(F32)),
        tab=tab,
        edge_cols=jnp.concatenate(
            [embed_tables[:n_patch], embed_tables[n_patch + FREQ + CLASSES :]], 0
        ).astype(BF16),
        time_w1=embed_tables[n_patch : n_patch + FREQ].astype(BF16),
        class_w=embed_tables[n_patch + FREQ : n_patch + FREQ + CLASSES].astype(BF16),
    )
    flat, tree = jax.tree.flatten(early)
    early = jax.tree.unflatten(tree, lax.optimization_barrier(tuple(flat)))
    chip, core, data, time_w2, noisy_own = (early[k] for k in ("chip", "core", "data", "time_w2", "noisy"))
    tab, peers = early["tab"], early["peers"]
    big_slots, small_slots, left_slots, right_slots = (early["slots"][i] for i in range(4))
    spread = Spreader(tab, spread_init(early["slots"], master_bank), n_data, steps, depth)
    spread.step()
    ring = Reducer(tab, n_data, steps, depth)

    def conditioning():
        ids, edge_rows = yield from together(
            dp_sum(own_latents(early["ids"], 0, data, n_data), n_data),
            gather_columns(early["edge_cols"], chip, core),
        )
        features = time_features(ids[:, 0]).astype(BF16)
        time_one = jnp.dot(features, early["time_w1"], preferred_element_type=F32)
        time_act = yield from gather_columns(jax.nn.silu(time_one).astype(BF16), chip, core)
        second = jnp.dot(time_act, time_w2, preferred_element_type=F32)
        second = yield from dp_sum(jnp.where(is_at(early["time_mine"], 1, 2), second, 0.0), n_data)
        onehot = ids[:, 1:2] == jnp.arange(CLASSES, dtype=jnp.int32)[None]
        condition = second + jnp.dot(onehot.astype(BF16), early["class_w"], preferred_element_type=F32)
        cond_in = yield from gather_columns(jax.nn.silu(condition).astype(BF16), chip, core)
        (mods,) = spread.work(modulations(small_slots, cond_in, master_bank), ISSUED)
        ISSUED.clear()
        bit = n_data // 2
        while bit:
            half = mods.shape[1] // 2
            sides = mods[:, :half], mods[:, half:]
            side = early["bits"][bit.bit_length() - 1]
            mods = pick(*sides, side) + (yield flip(pick(*sides, side, True), "dp", bit, n_data))
            bit //= 2
        latents = mods[:, 0], mods[:, 1]
        across = yield x_flip(pick(*latents, chip, True))
        own = pick(*latents, chip)
        pair = [pick(own, across, chip), pick(across, own, chip)]
        beside = core_flip(jnp.concatenate(pair, 1))
        beside = [beside[:, x * columns : (x + 1) * columns] for x in range(2)]
        blocks = [pick(one, two, core) for x in range(2) for one, two in ((pair[x], beside[x]), (beside[x], pair[x]))]
        return edge_rows, features, time_one, time_act, onehot, condition, cond_in, jnp.concatenate(blocks, 1)

    def forward():
        cond = yield from conditioning()
        edge_rows, mods = cond[0], cond[-1]
        stream, inner, normed, inv = enter(
            noisy_own, edge_rows[:n_patch], early["places"], mods, (small_at(0, 0), small_at(0, 1))
        )
        kept = []
        for layer in range(LAYERS):
            inner = yield from gather_tokens(inner)
            spread.prepare(2 * layer)
            qkv, mixed, keep, send = spread.work(attention(inner, columns, BIG * layer, n_lat))
            parts = yield from scatter_tokens(keep, send)
            attended, stream, inner_mid, normed_mid, inv_mid = residual(
                parts, stream, mods, tuple(small_at(layer, i) for i in (2, 3, 4))
            )
            inner_mid = yield from gather_tokens(inner_mid)
            spread.prepare(2 * layer + 1)
            hidden, active, keep, send = spread.work(mlp(inner_mid, columns, BIG * layer + 4))
            parts = yield from scatter_tokens(keep, send)
            kept.append([inner, normed, inv, qkv, mixed, attended, inner_mid, normed_mid, inv_mid, hidden, active])
            if layer + 1 < LAYERS:
                branch, stream, inner, normed, inv = residual(
                    parts,
                    stream,
                    mods,
                    (small_at(layer, 5), small_at(layer + 1, 0), small_at(layer + 1, 1)),
                )
                kept[-1].append(branch)
        return cond, kept, parts, stream

    cond, kept, parts_last, stream_last = drive(forward(), spread.step)
    edge_rows, features, time_one, time_act, onehot, condition, cond_in, mods = cond
    ring.held = spread.held

    def backward():
        grad, d_branch, rows, edge_head = leave(
            parts_last,
            stream_last,
            mods,
            edge_rows[n_patch:],
            early["target"],
            (small_at(LAYERS - 1, 5), SHIFT_F, SCALE_F),
            count_all,
        )
        lefts, rights = {}, {}
        for layer in reversed(range(LAYERS)):
            inner, normed, inv, qkv, mixed, attended, inner_mid, normed_mid, inv_mid, hidden, active = kept[layer][:11]
            d_branch = yield from gather_tokens(d_branch, 1 if layer == LAYERS - 1 else 2)
            d_hidden, keep, send = ring.work(mlp_back(d_branch, hidden, BIG * layer + 4))
            work = scatter_tokens(keep, send)
            flying = next(work)
            lefts[2 * layer + 1], rights[2 * layer + 1] = ring.work(
                weight_grads(BIG * layer + 4, [(inner_mid, d_hidden), (d_branch, active)], n_lat), ISSUED
            )
            ring.ready = BIG * layer + 4
            if layer == LAYERS - 1:
                ring.step((lefts[2 * layer + 1],))
            parts = finish(work, order(flying, (lefts[2 * layer + 1],) + ring.sent))
            grad, d_attended, rows = back(
                parts,
                normed_mid,
                inv_mid,
                grad,
                attended,
                mods,
                rows,
                small_at(layer, 4),
                small_at(layer, 2),
                small_at(layer, 3),
                [ring.held],
            )
            d_attended = yield from gather_tokens(d_attended, 2)
            d_qkv, keep, send = ring.work(attention_back(d_attended, qkv, BIG * layer, n_lat))
            work = scatter_tokens(keep, send)
            flying = next(work)
            lefts[2 * layer], rights[2 * layer] = ring.work(
                weight_grads(BIG * layer, [(inner, d_qkv), (d_attended, mixed[None])], n_lat), ISSUED
            )
            ring.ready = BIG * layer
            parts = finish(work, order(flying, (lefts[2 * layer],) + ring.sent))
            below = kept[layer - 1][11] if layer else normed
            grad, d_branch, rows = back(
                parts,
                normed,
                inv,
                grad,
                below,
                mods,
                rows,
                small_at(layer, 1),
                small_at(layer - 1, 5) if layer else None,
                small_at(layer, 0),
                [ring.held],
            )
        return (yield from cond_backward(rows, d_branch, edge_head, lefts, rights))

    def cond_backward(rows, d_stream, edge_head, lefts, rights):
        mine = core_columns_sum(rows, core)
        near, far = pick(*mine, chip), x_flip(pick(*mine, chip, True))
        own = [pick(near, far, chip).astype(BF16), pick(far, near, chip).astype(BF16)]
        if n_data == 8:
            first, *others = factor_rows(lefts, rights)
            one, two = jnp.concatenate(own + [first], 0), jnp.concatenate(others, 0)
            one, two = (jnp.pad(v, ((0, -len(v) % 96), (0, 0))) for v in (one, two))
            latents, others = yield from ring.gather(one, two)
            n_own, n_rows = n_lat * SMALL_ROWS, first.shape[0]
            factors = [v[n_own : n_own + n_rows] for v in latents] + [v[:n_rows] for v in others]
            factors = jnp.concatenate(factors, 0).reshape(n_all, n_rows, columns)
        else:
            latents = [(yield from dp_sum(own_latents(jnp.stack(own, 0), 0, data, n_data), n_data))]
        d_small, d_cond = ring.work(cond_back(small_slots, peers, latents, n_all, master_bank), ISSUED)
        ISSUED.clear()
        d_cond = yield from own_columns_sum(d_cond, chip, core)
        if n_data == 8:
            (parts,) = yield from ring.gather(jnp.concatenate(halves(d_cond), 0))
            (d_cond,) = ring.work(mail_sum(peers, parts))
        else:
            d_cond = yield from dp_sum(d_cond, n_data)
        unused, silu_pull = jax.vjp(jax.nn.silu, condition)
        d_condition = silu_pull(d_cond)[0]
        d_second = d_condition.astype(BF16)
        grad_class = lax.dot_general(
            onehot.astype(F32), d_condition, (((0,), (0,)), ((), ())), precision=HIGHEST_PREC
        )
        d_time_act = lax.dot_general(d_second, time_w2, (((1,), (1,)), ((), ())), preferred_element_type=F32)
        d_time_act = jnp.where(is_at(early["time_mine"], 1, 2), d_time_act, 0.0)
        grad_patch = lax.dot_general(noisy_own, d_stream, (((0,), (0,)), ((), ())), preferred_element_type=F32)
        sums = yield from own_columns_sum(jnp.concatenate([d_time_act, grad_patch, edge_head], 0), chip, core)
        ring.drain()
        if n_data != 8:
            factors = yield from dp_rows(jnp.stack(factor_rows(lefts, rights)), n_data)
        n_left = sum(v.shape[0] for v in lefts.values())
        a_rows = jnp.concatenate([factors[:, j * n_left : (j + 1) * n_left] for j in range(4)], 2).transpose(1, 0, 2)
        b_rows = factors[:, 4 * n_left : 4 * n_left + N_BIG].transpose(1, 0, 2)
        return d_small, d_second, grad_class, sums, a_rows, b_rows

    def factor_rows(lefts, rights):
        a_rows = jnp.concatenate([lefts[g] for g in range(len(GROUPS))], 0)
        b_rows = jnp.concatenate([rights[g] for g in range(len(GROUPS))], 0)
        parts = []
        for l in range(n_lat):
            part = [a_rows[:, l, j * columns : (j + 1) * columns] for j in range(4)] + [b_rows[:, l]]
            part = jnp.concatenate(part, 0).astype(BF16)
            parts.append(jnp.pad(part, ((0, -len(part) % 32), (0, 0))))
        return parts

    d_small, d_second, grad_class, sums, a_rows, b_rows = drive(backward(), ring.step)
    a_all = jnp.concatenate([cond_in[None], time_act[None], a_rows], 0)
    small_rows = jnp.where(
        jnp.arange(SMALL_ROWS)[:, None, None] == TIME_AT, d_second[None], d_small.transpose(1, 0, 2)
    )
    b_all = jnp.concatenate([small_rows, b_rows], 0)
    optimizer = Optimizer(
        (big_slots, left_slots, right_slots), tab, a_all, b_all, master_bank, momentum_bank, ring.held, ring.last()
    )
    adding = dp_sum(order(sums, ring.last()), n_data)
    flying = next(adding)
    try:
        while True:
            (mark,) = optimizer.step(ISSUED[-2:-1]) or (jnp.zeros((8, 128), F32),)
            flying = adding.send(flying + mark[:1, :1])
    except StopIteration as end:
        sums = end.value
    master_new, momentum_new = optimizer.all()
    d_time_act, edges = sums[:n_all], sums[n_all:]
    unused, time_pull = jax.vjp(jax.nn.silu, time_one)
    d_time_one = time_pull(d_time_act)[0].astype(BF16)
    grad_time_one = lax.dot_general(
        features, d_time_one, (((0,), (0,)), ((), ())), preferred_element_type=F32
    )
    loss = edges[2 * n_patch, 0]
    embed_new, first_new, second_new = update_tables(
        n_patch, early["bias_fix"], edges, grad_time_one, grad_class, embed_tables, embed_first, embed_second
    )
    return (loss, master_new, momentum_new, embed_new, first_new, second_new)


def solution(mesh):
    placed = (
        P("dp", None, None),
        P("dp", None, None),
        P("dp"),
        P("dp"),
        P(),
        P(),
        P("dp", None, "tensor"),
        P("dp", None, "tensor"),
        P(None, "tensor"),
        P(None, "tensor"),
        P(None, "tensor"),
    )
    return jax.shard_map(
        shards,
        mesh=mesh,
        in_specs=placed,
        out_specs=(
            P(),
            P("dp", None, "tensor"),
            P("dp", None, "tensor"),
            P(None, "tensor"),
            P(None, "tensor"),
            P(None, "tensor"),
        ),
        check_vma=False,
    )
```
